32 devices in a mesh: dp: 8 (over z, core), mp: 4 (over y, x).
Axes of the slice: x: 2, y: 2, z: 4, core: 2. Of those that a mesh axis runs over, the one named last changes fastest.
Arguments:
- tokens: bfloat16 [4, 4096, 768], P(None, ('dp', 'mp')), may hold values from -6 to 6
- first_values: bfloat16 [4, 4096, 384], P(None, ('dp', 'mp')), may hold values from -6 to 6
- out_cot: bfloat16 [4, 4096, 768], P(None, ('dp', 'mp')), may hold values from -6 to 6
- ln1_gain: bfloat16 [768], P(('dp', 'mp')), may hold values from 0.25 to 1.75
- ln1_bias: bfloat16 [768], P(('dp', 'mp')), may hold values from -3 to 3
- w_qkv: bfloat16 [768, 1920], P('dp', 'mp'), may hold values from -0.21875 to 0.21875
- q_bias: bfloat16 [768], P(('dp', 'mp')), may hold values from -3 to 3
- v_bias: bfloat16 [384], P(('dp', 'mp')), may hold values from -3 to 3
- w_out: bfloat16 [768, 768], P('dp', 'mp'), may hold values from -1.75 to 1.75
- out_bias: bfloat16 [768], P(('dp', 'mp')), may hold values from -3 to 3
- ln2_gain: bfloat16 [768], P(('dp', 'mp')), may hold values from 0.25 to 1.75
- ln2_bias: bfloat16 [768], P(('dp', 'mp')), may hold values from -3 to 3
- w_up: bfloat16 [768, 3072], P('dp', 'mp'), may hold values from -0.21875 to 0.21875
- up_bias: bfloat16 [3072], P(('dp', 'mp')), may hold values from -3 to 3
- w_down: bfloat16 [3072, 768], P('mp', 'dp'), may hold values from -0.109375 to 0.109375
- down_bias: bfloat16 [768], P(('dp', 'mp')), may hold values from -3 to 3
Outputs:
- layer_out: bfloat16 [4, 4096, 768], P(None, ('dp', 'mp'))
- input_grad: bfloat16 [4, 4096, 768], P(None, ('dp', 'mp'))
- first_grad: bfloat16 [4, 4096, 384], P(None, ('dp', 'mp'))
- ln1_gain_grad: float32 [768], P(('dp', 'mp'))
- ln1_bias_grad: float32 [768], P(('dp', 'mp'))
- qkv_grad: float32 [768, 1920], P('dp', 'mp')
- q_bias_grad: float32 [768], P(('dp', 'mp'))
- v_bias_grad: float32 [384], P(('dp', 'mp'))
- out_grad: float32 [768, 768], P('dp', 'mp')
- out_bias_grad: float32 [768], P(('dp', 'mp'))
- ln2_gain_grad: float32 [768], P(('dp', 'mp'))
- ln2_bias_grad: float32 [768], P(('dp', 'mp'))
- up_grad: float32 [768, 3072], P('dp', 'mp')
- up_bias_grad: float32 [3072], P(('dp', 'mp'))
- down_grad: float32 [3072, 768], P('mp', 'dp')
- down_bias_grad: float32 [768], P(('dp', 'mp'))
The draws below stay inside these ranges and needn't reach their ends.
All inputs are finite; a program needn't handle non-finite values.
Results may differ from the reference program's by a relative error of at most 0.02.
Values may be sent and summed in bfloat16 or wider, within the bound.
A program may use at most 192 MiB of HBM per device.

```python
import jax
import jax.numpy as jnp
from jax import lax

D = 768
HEADS = 12
HEAD = 64
FF = 3072
MICRO = 4
QKV = 1920
VFRESH = 384
VREUSE = 384
SEQ = 512
TOKENS_MB = 4096
N_DP = 8


def spiked(values, own_key, source, target, parts, factor):
    def block_of(dim):
        return (jnp.arange(values.shape[dim]) // (values.shape[dim] // parts)).reshape((-1,) + (1,) * (values.ndim - 1 - dim))

    near = jax.random.permutation(own_key, parts)[block_of(target)]
    other_side = (block_of(target) + parts // 2) % parts
    return jnp.where((block_of(source) == near) | (block_of(source) == other_side), factor * values, values)


def level_of(key, dims, shards, least, high):
    level = 1.0
    for axis_at, blocks in shards:
        draws = jax.random.uniform(jax.random.fold_in(jax.random.fold_in(key, 6), axis_at), (blocks,), jnp.float32, least / len(shards), high / len(shards))
        level = level * jnp.repeat(jnp.exp(draws), dims[axis_at] // blocks).reshape((-1,) + (1,) * (len(dims) - 1 - axis_at))
    return level


def noise(own_key, shape, width, most, pieces=(), kind=jnp.bfloat16):
    values = width * jax.random.normal(own_key, shape, jnp.float32)
    if pieces:
        values = values * level_of(own_key, shape, pieces, -0.22, 0.18)
    return jnp.clip(values, -most, most).astype(kind)


def noise_with(stream_key, shape, deviation, most, split, heavy, kind=jnp.bfloat16):
    array = deviation * jax.random.normal(stream_key, shape, jnp.float32)
    if split:
        array = array * level_of(stream_key, shape, split, -0.22, 0.18)
    return jnp.clip(spiked(array, jax.random.fold_in(stream_key, 3), *heavy), -most, most).astype(kind)


def setup_inputs(seed: int = 0) -> dict:
    splits = jax.random.split(jax.random.key(seed), 17)
    tokens = noise(splits[0], (MICRO, TOKENS_MB, D), 1.0, 6.0, ((1, 32),))
    first_values = noise(splits[1], (MICRO, TOKENS_MB, VREUSE), 1.0, 6.0, ((1, 32),))
    out_cot = noise_with(splits[2], (MICRO, TOKENS_MB, D), 1.0, 6.0, ((1, 32),), (1, 2, 32, 2.75))
    ln1_gain = jnp.clip(1.0 + 0.15 * jax.random.normal(splits[3], (D,), jnp.float32), 0.25, 1.75).astype(jnp.bfloat16)
    ln1_bias = noise(splits[4], (D,), 0.5, 3.0, ((0, 32),))
    w_qkv = noise(splits[5], (D, QKV), D ** -0.5, 0.21875, ((0, 8), (1, 4)))
    q_bias = noise(splits[6], (D,), 0.5, 3.0, ((0, 32),))
    v_bias = noise(splits[7], (VFRESH,), 0.5, 3.0, ((0, 32),))
    w_out = noise(splits[8], (D, D), (D // 64) ** -0.5, 1.75, ((0, 8), (1, 4)))
    out_bias = noise(splits[9], (D,), 0.5, 3.0, ((0, 32),))
    ln2_gain = jnp.clip(1.0 + 0.15 * jax.random.normal(splits[10], (D,), jnp.float32), 0.25, 1.75).astype(jnp.bfloat16)
    ln2_bias = noise(splits[11], (D,), 0.5, 3.0, ((0, 32),))
    w_up = noise(splits[12], (D, FF), D ** -0.5, 0.21875, ((0, 8), (1, 4)))
    up_bias = noise(splits[13], (FF,), 0.5, 3.0, ((0, 32),))
    w_down = noise(splits[14], (FF, D), FF ** -0.5, 0.109375, ((0, 4), (1, 8)))
    down_bias = noise(splits[15], (D,), 0.5, 3.0, ((0, 32),))
    return {"tokens": tokens, "first_values": first_values, "out_cot": out_cot, "ln1_gain": ln1_gain, "ln1_bias": ln1_bias, "w_qkv": w_qkv, "q_bias": q_bias, "v_bias": v_bias, "w_out": w_out, "out_bias": out_bias, "ln2_gain": ln2_gain, "ln2_bias": ln2_bias, "w_up": w_up, "up_bias": up_bias, "w_down": w_down, "down_bias": down_bias}


@jax.custom_vjp
def low(v):
    return lax.optimization_barrier(v.astype(jnp.bfloat16)).astype(jnp.float32)

@jax.custom_vjp
def low_back(v):
    return v

def low_keep(v):
    return (low(v), None)

def low_pass(kept, grad):
    return (grad,)

def back_keep(v):
    return (v, None)

def back_low(kept, grad):
    return (low(grad),)
low.defvjp(low_keep, low_pass)
low_back.defvjp(back_keep, back_low)
EPS = 1e-05
BIG = 1e+30
HIGH = lax.Precision.HIGHEST

def layer_norm(inputs, gain_vec, shift_vec):
    average = lax.optimization_barrier(jnp.mean(inputs, axis=-1, keepdims=True))
    centred = inputs - average
    variance = lax.optimization_barrier(jnp.mean(centred * centred, axis=-1, keepdims=True))
    return centred * lax.rsqrt(variance + EPS) * gain_vec + shift_vec

def gelu_tanh(inputs):
    return 0.5 * inputs * (1.0 + jnp.tanh(0.7978845608028654 * (inputs + 0.044715 * inputs * inputs * inputs)))

def attend(queries, key_vals, value_vals):
    length = queries.shape[0]
    block_rows = min(512, length)
    query_blocks = queries.reshape(length // block_rows, block_rows, HEADS, HEAD)
    key_heads = key_vals.reshape(length, HEADS, HEAD)
    value_heads = value_vals.reshape(length, HEADS, HEAD)
    key_pos = jnp.arange(length, dtype=jnp.int32)

    def one_block(element):
        query_block, offset = element
        scores = low_back(jnp.einsum('qhd,khd->hqk', query_block, key_heads, precision=HIGH) * HEAD ** (-0.5))
        query_pos = offset + jnp.arange(block_rows, dtype=jnp.int32)
        allowed = key_pos[None, :] <= query_pos[:, None]
        masked = jnp.where(allowed[None], scores, -BIG)
        shifted = jnp.exp(masked - lax.optimization_barrier(jnp.max(masked, axis=-1, keepdims=True)))
        weights = low(shifted / lax.optimization_barrier(jnp.sum(shifted, axis=-1, keepdims=True)))
        return jnp.einsum('hqk,khd->qhd', weights, value_heads, precision=HIGH)
    offsets = jnp.arange(length // block_rows, dtype=jnp.int32) * block_rows
    attended = lax.map(jax.checkpoint(one_block), (query_blocks, offsets))
    return attended.reshape(length, D)

def block_forward(inputs, firsts, params):
    gain_one, shift_one, qkv_proj, query_shift, value_shift, out_proj, out_shift, gain_two, shift_two, up_proj, up_shift, down_proj, down_shift = params
    normed = low(layer_norm(inputs, gain_one, shift_one))
    mixed_proj = jnp.dot(normed, qkv_proj, precision=HIGH)
    queries = low(low_back(mixed_proj[:, :D] + query_shift))
    key_vals = low(low_back(mixed_proj[:, D:2 * D]))
    value_vals = low(low_back(jnp.concatenate([mixed_proj[:, 2 * D:] + value_shift, firsts], axis=1)))
    attended = low(low_back(attend(queries, key_vals, value_vals)))
    middle = inputs + low_back(jnp.dot(attended, out_proj, precision=HIGH) + out_shift)
    normed_two = low(layer_norm(middle, gain_two, shift_two))
    hidden = low_back(jnp.dot(normed_two, up_proj, precision=HIGH) + up_shift)
    active = low(gelu_tanh(hidden))
    return middle + (jnp.dot(active, down_proj, precision=HIGH) + down_shift)

def reference(tokens, first_values, out_cot, ln1_gain, ln1_bias, w_qkv, q_bias, v_bias, w_out, out_bias, ln2_gain, ln2_bias, w_up, up_bias, w_down, down_bias):
    params = tuple((weight_arr.astype(jnp.float32) for weight_arr in (ln1_gain, ln1_bias, w_qkv, q_bias, v_bias, w_out, out_bias, ln2_gain, ln2_bias, w_up, up_bias, w_down, down_bias)))
    inputs = tokens.astype(jnp.float32)
    firsts = first_values.astype(jnp.float32)

    def whole(all_inputs, all_firsts, all_params):
        seq_inputs = all_inputs.reshape(MICRO * N_DP, SEQ, D)
        seq_firsts = all_firsts.reshape(MICRO * N_DP, SEQ, VREUSE)

        def one_seq(carried, seq_pair):
            return (carried, block_forward(seq_pair[0], seq_pair[1], all_params))
        ignored, outputs = lax.scan(one_seq, jnp.zeros((), jnp.float32), (seq_inputs, seq_firsts))
        return outputs.reshape(MICRO, TOKENS_MB, D)
    result, pullback = jax.vjp(whole, inputs, firsts, params)
    grad_inputs, grad_firsts, grad_params = pullback(out_cot.astype(jnp.float32))
    return (result.astype(jnp.bfloat16), grad_inputs.astype(jnp.bfloat16), grad_firsts.astype(jnp.bfloat16), grad_params[0], grad_params[1], grad_params[2], grad_params[3], grad_params[4], grad_params[5], grad_params[6], grad_params[7], grad_params[8], grad_params[9], grad_params[10], grad_params[11], grad_params[12])
```

```python
import functools

import jax
import jax.numpy as jnp
from jax import lax
from jax.experimental import pallas as pl
from jax.experimental.pallas import tpu as pltpu
from jax.sharding import PartitionSpec as P

D = 768
HEADS = 12
HEAD = 64
FF = 3072
MICRO = 4
QKV = 1920
SEQ = 512
VFRESH = 384

EPS = 1e-05
BIG = 1e30
GELU_C = 0.7978845608028654
GELU_A = 0.044715
MESH = pl.DeviceIdType.MESH
ANY = pl.BlockSpec(memory_space=pl.ANY)


class Plan:
    def __init__(self, mesh):
        self.n_dp = mesh.shape["dp"]
        self.n_mp = mesh.shape["mp"]
        self.n_z = self.n_dp // 2
        self.rows = D // self.n_dp
        self.cols = FF // self.n_mp
        self.qkv = QKV // self.n_mp
        self.out = D // self.n_mp
        self.out_at = -(-self.qkv // 128) * 128
        self.unit = 3 * self.rows + 16
        self.small = self.n_dp * self.n_mp
        self.per_seq = SEQ * MICRO // SEQ
        self.n_seq = self.n_mp // MICRO
        assert self.out_at + self.out <= self.cols and self.rows % 16 == 0
        assert self.n_seq * MICRO == self.n_mp

    def ring_at(self, i):
        half = self.n_mp // 2
        return i + (i // half) * (self.n_mp - 1 + half - 2 * i)


def where_am_i():
    return lax.axis_index("dp"), lax.axis_index("mp")


def greet(plan, dp, i, z, c):
    barrier = pltpu.get_barrier_semaphore()
    partners = [(dp + 1 - 2 * c, i)]
    partners += [(((z + k) % plan.n_z) * 2 + c, i) for k in range(1, plan.n_z)]
    partners += [(dp, (i + k) % plan.n_mp) for k in range(1, plan.n_mp)]
    for partner in partners:
        pl.semaphore_signal(barrier, inc=1, device_id=partner, device_id_type=MESH)
    pl.semaphore_wait(barrier, len(partners))


def push(src, dst, send, recv, device):
    copy = pltpu.make_async_remote_copy(
        src_ref=src, dst_ref=dst, send_sem=send, recv_sem=recv, device_id=device, device_id_type=MESH
    )
    return copy


def gather_kernel(plan, pk, tok, fv, cot, g, x, f, y, own_sem, zs, zr, rs, rr, ss, sr, xs, xr):
    dp, i = where_am_i()
    c, z = dp % 2, dp // 2
    n_mp, n_z = plan.n_mp, plan.n_z
    sib = (dp + 1 - 2 * c, i)
    p = plan.ring_at(i)
    device_at = lambda pos: plan.ring_at((pos + n_mp) % n_mp)
    greet(plan, dp, i, z, c)

    pairs = ((tok, x), (fv, f), (cot, y))
    q = plan.per_seq
    for a, (src, dst) in enumerate(pairs):
        for m in range(MICRO):
            target = m * plan.n_seq + i // q
            place = i % q

            @pl.when(target != i)
            def _():
                push(src.at[m], dst.at[place], xs.at[a, m], xr.at[a, place], (dp, target)).start()

            @pl.when(target == i)
            def _():
                pltpu.make_async_copy(src.at[m], dst.at[place], xs.at[a, m]).start()

    mine = pltpu.make_async_copy(pk, g.at[i, dp], own_sem)
    mine.start()
    unit_dp = [((z + n_z - k) % n_z) * 2 + c for k in range(n_z)]

    def source(k, origin):
        return g.at[origin, unit_dp[k]]

    sends = []

    def to_sibling(k, h, src, origin):
        cp = push(src, g.at[origin, unit_dp[k]], ss.at[k, h], sr.at[k, h], sib)
        cp.start()
        sends.append(cp)

    def to_ring(k, h, src):
        sign = 1 if k % 2 == 0 else -1
        origin = device_at(p - sign * h)
        cp = push(src, g.at[origin, unit_dp[k]], rs.at[k, h], rr.at[k, h], (dp, device_at(p + sign)))
        cp.start()
        sends.append(cp)

    to_ring(0, 0, pk)
    for k in range(1, n_z):
        cp = push(pk, g.at[i, dp], zs.at[k - 1], zr.at[k - 1], (((z + k) % n_z) * 2 + c, i))
        cp.start()
        sends.append(cp)
    to_sibling(0, 0, pk, i)
    for k in range(1, n_z):
        here = source(k, i)
        push(here, here, zs.at[k - 1], zr.at[k - 1], sib).wait_recv()
        to_ring(k, 0, here)
        to_sibling(k, 0, here, i)
    for h in range(n_mp - 1):
        for k in range(n_z):
            sign = 1 if k % 2 == 0 else -1
            origin = device_at(p - sign * (h + 1))
            here = source(k, origin)
            push(here, here, rs.at[k, h], rr.at[k, h], sib).wait_recv()
            if h < n_mp - 2:
                to_ring(k, h + 1, here)
            to_sibling(k, h + 1, here, origin)
    sib_dp = [((z + n_z - k) % n_z) * 2 + 1 - c for k in range(n_z)]
    for h in range(n_mp):
        for k in range(n_z):
            sign = 1 if k % 2 == 0 else -1
            here = g.at[device_at(p - sign * h), sib_dp[k]]
            push(here, here, ss.at[k, h], sr.at[k, h], sib).wait_recv()
    for cp in sends:
        cp.wait_send()
    mine.wait()
    for a, (src, dst) in enumerate(pairs):
        for m in range(MICRO):
            target = m * plan.n_seq + i // q
            place = i % q

            @pl.when(target != i)
            def _():
                push(src.at[m], dst.at[place], xs.at[a, m], xr.at[a, place], (dp, target)).wait_send()

            @pl.when(target == i)
            def _():
                pltpu.make_async_copy(src.at[m], dst.at[place], xs.at[a, m]).wait()

        for place in range(q):
            origin = (i % plan.n_seq) * q + place

            @pl.when(origin != i)
            def _():
                push(dst.at[place], dst.at[place], xs.at[a, 0], xr.at[a, place], sib).wait_recv()


def gather(plan, packed, tok, fv, cot):
    n_mp, n_z = plan.n_mp, plan.n_z
    bf = jnp.bfloat16
    dma = pltpu.SemaphoreType.DMA
    return pl.pallas_call(
        functools.partial(gather_kernel, plan),
        name="gather",
        out_shape=(
            jax.ShapeDtypeStruct((n_mp, plan.n_dp, plan.unit, plan.cols), bf),
            jax.ShapeDtypeStruct(tok.shape, bf),
            jax.ShapeDtypeStruct(fv.shape, bf),
            jax.ShapeDtypeStruct(cot.shape, bf),
        ),
        in_specs=[ANY] * 4,
        out_specs=(ANY,) * 4,
        scratch_shapes=[
            dma,
            dma((n_z - 1,)),
            dma((n_z - 1,)),
            dma((n_z, n_mp - 1)),
            dma((n_z, n_mp - 1)),
            dma((n_z, n_mp)),
            dma((n_z, n_mp)),
            dma((3, MICRO)),
            dma((3, plan.per_seq)),
        ],
        compiler_params=pltpu.CompilerParams(collective_id=0, has_side_effects=True),
    )(packed, tok, fv, cot)


def reduce_kernel(
    plan, grads, o1, o2, o3, total, r1, r2, r3,
    own, other, ring, last, own_sem, ss, sr, rs, rr, zs, zr, xs, xr,
):
    dp, i = where_am_i()
    c, z = dp % 2, dp // 2
    n_mp, n_z, R = plan.n_mp, plan.n_z, plan.rows
    sib = (dp + 1 - 2 * c, i)
    p = plan.ring_at(i)
    device_at = lambda pos: plan.ring_at((pos + n_mp) % n_mp)
    f32, bf = jnp.float32, jnp.bfloat16
    greet(plan, dp, i, z, c)

    pairs = ((o1, r1), (o2, r2), (o3, r3))
    q = plan.per_seq
    micro, part = i // plan.n_seq, i % plan.n_seq
    place = i % q

    def back(start):
        for a, (src, dst) in enumerate(pairs):
            for s in range(q):
                owner = part * q + s
                far = push(src.at[s], dst.at[micro], xs.at[a, s], xr.at[a, micro], (dp, owner))
                near = pltpu.make_async_copy(src.at[s], dst.at[micro], xs.at[a, s])

                @pl.when(owner != i)
                def _():
                    far.start() if start else far.wait_send()

                @pl.when(owner == i)
                def _():
                    near.start() if start else near.wait()

    bounds = ((0, R), (R, 2 * R), (2 * R, plan.unit))
    tiles = [pl.ds(lo, hi - lo) for lo, hi in bounds]
    unit_dp = [((z + n_z - k) % n_z) * 2 + c for k in range(n_z)]
    sib_dp = [((z + n_z - k) % n_z) * 2 + 1 - c for k in range(n_z)]
    order = [k for k in range(n_z - 1, -1, -1)]
    sends = []
    for k in order:
        for t in range(n_mp):
            cp = push(grads.at[t, sib_dp[k]], other.at[t, k], ss.at[k, t], sr.at[k, t], sib)
            cp.start()
            sends.append(cp)
            pltpu.make_async_copy(grads.at[t, unit_dp[k]], own.at[t, k], own_sem.at[k, t]).start()
    back(True)

    def add(t, k, tile, extra):
        own[t, k, tile, :] = (own[t, k, tile, :].astype(f32) + extra.astype(f32)).astype(bf)

    def chunk(k, step):
        sign = 1 if k % 2 == 0 else -1
        return device_at(p - sign * (1 + step))

    def ring_send(k, piece, step):
        sign = 1 if k % 2 == 0 else -1
        tile = tiles[piece]
        cp = push(
            own.at[chunk(k, step), k, tile],
            ring.at[k, step, tile],
            rs.at[k, piece, step],
            rr.at[k, piece, step],
            (dp, device_at(p + sign)),
        )
        cp.start()
        sends.append(cp)

    for k0 in range(n_z - 2, -1, -2):
        ks = (k0, k0 + 1)
        for k in ks:
            for t in range(n_mp):
                pltpu.make_async_copy(grads.at[t, unit_dp[k]], own.at[t, k], own_sem.at[k, t]).wait()
                push(other.at[t, k], other.at[t, k], ss.at[k, t], sr.at[k, t], sib).wait_recv()
        for step in range(n_mp):
            for piece in range(3):
                for k in ks:
                    tile = tiles[piece]
                    t = chunk(k, step)
                    if step > 0:
                        got = ring.at[k, step - 1, tile]
                        push(got, got, rs.at[k, piece, step - 1], rr.at[k, piece, step - 1], sib).wait_recv()
                        own[t, k, tile, :] = (
                            own[t, k, tile, :].astype(f32)
                            + other[t, k, tile, :].astype(f32)
                            + ring[k, step - 1, tile, :].astype(f32)
                        ).astype(bf)
                    else:
                        add(t, k, tile, other[t, k, tile, :])
                    if step < n_mp - 1:
                        ring_send(k, piece, step)
                    elif k > 0:
                        cp = push(
                            own.at[i, k, tile],
                            last.at[k - 1, tile],
                            zs.at[k - 1, piece],
                            zr.at[k - 1, piece],
                            (unit_dp[k], i),
                        )
                        cp.start()
                        sends.append(cp)
    for piece in range(3):
        tile = tiles[piece]
        for k in range(1, n_z):
            got = last.at[k - 1, tile]
            push(got, got, zs.at[k - 1, piece], zr.at[k - 1, piece], sib).wait_recv()
        value = own[i, 0, tile, :].astype(f32)
        for k in range(1, n_z):
            value = value + last[k - 1, tile, :].astype(f32)
        total[tile, :] = value
    for cp in sends:
        cp.wait_send()
    back(False)
    for a, (src, dst) in enumerate(pairs):
        for m in range(MICRO):
            origin = m * plan.n_seq + i // q

            @pl.when(origin != i)
            def _():
                push(dst.at[m], dst.at[m], xs.at[a, 0], xr.at[a, m], sib).wait_recv()


def reduce(plan, grads, o1, o2, o3):
    n_mp, n_z = plan.n_mp, plan.n_z
    bf, f32 = jnp.bfloat16, jnp.float32
    dma = pltpu.SemaphoreType.DMA
    block = (plan.unit, plan.cols)
    return pl.pallas_call(
        functools.partial(reduce_kernel, plan),
        name="reduce",
        out_shape=(
            jax.ShapeDtypeStruct(block, f32),
            jax.ShapeDtypeStruct(o1.shape, bf),
            jax.ShapeDtypeStruct(o2.shape, bf),
            jax.ShapeDtypeStruct(o3.shape, bf),
        ),
        in_specs=[ANY] * 4,
        out_specs=(pl.BlockSpec(memory_space=pltpu.VMEM), ANY, ANY, ANY),
        scratch_shapes=[
            pltpu.VMEM((n_mp, n_z) + block, bf),
            pltpu.VMEM((n_mp, n_z) + block, bf),
            pltpu.VMEM((n_z, n_mp - 1) + block, bf),
            pltpu.VMEM((n_z - 1,) + block, bf),
            dma((n_z, n_mp)),
            dma((n_z, n_mp)),
            dma((n_z, n_mp)),
            dma((n_z, 3, n_mp - 1)),
            dma((n_z, 3, n_mp - 1)),
            dma((n_z - 1, 3)),
            dma((n_z - 1, 3)),
            dma((3, plan.per_seq)),
            dma((3, MICRO)),
        ],
        compiler_params=pltpu.CompilerParams(
            collective_id=1, has_side_effects=True, vmem_limit_bytes=56 << 20
        ),
    )(grads, o1, o2, o3)


def layer_norm(inputs, gain_vec, shift_vec):
    average = jnp.mean(inputs, axis=-1, keepdims=True)
    centred = inputs - average
    variance = jnp.mean(centred * centred, axis=-1, keepdims=True)
    inv_std = lax.rsqrt(variance + EPS)
    scaled = centred * inv_std
    return (scaled * gain_vec + shift_vec, scaled, inv_std)


def norm_back(grad_out, scaled, inv_std, gain_vec):
    grad_scaled = grad_out * gain_vec
    first_term = jnp.mean(grad_scaled, axis=-1, keepdims=True)
    second_term = jnp.mean(grad_scaled * scaled, axis=-1, keepdims=True)
    grad_in = inv_std * (grad_scaled - first_term - scaled * second_term)
    return (grad_in, jnp.sum(grad_out * scaled, axis=0), jnp.sum(grad_out, axis=0))


def gelu_both(inputs):
    cubic_term = inputs + GELU_A * inputs * inputs * inputs
    tangent = jnp.tanh(GELU_C * cubic_term)
    gelu_out = 0.5 * inputs * (1.0 + tangent)
    gelu_slope = 0.5 * (1.0 + tangent) + 0.5 * inputs * (1.0 - tangent * tangent) * GELU_C * (
        1.0 + 3.0 * GELU_A * inputs * inputs
    )
    return (gelu_out, gelu_slope)


def mm(eq, a, b):
    return jnp.einsum(eq, a, b, preferred_element_type=jnp.float32)


def layer(x_low, first, cot, weights, vectors):
    w_qkv, w_out, w_up, w_downt = weights
    g1, b1, qb, vb, ob, g2, b2, ub, db_ = vectors
    bf, f32 = jnp.bfloat16, jnp.float32
    rows = x_low.shape[0]
    x = x_low.astype(f32)
    normed, scaled_one, inv_one = layer_norm(x, g1, b1)
    hl = normed.astype(bf)
    mixed = mm("rd,dc->rc", hl, w_qkv)
    heads = lambda t: t.reshape(rows, HEADS, HEAD).transpose(1, 0, 2)
    q = heads((mixed[:, :D] + qb).astype(bf))
    k = heads(mixed[:, D : 2 * D].astype(bf))
    v = heads(jnp.concatenate([(mixed[:, 2 * D :] + vb).astype(bf), first], axis=1))
    scale = HEAD**-0.5
    s = mm("hqd,hkd->hqk", q, k) * scale
    at = jnp.arange(rows, dtype=jnp.int32)
    allowed = (at[None, :] <= at[:, None])[None]
    s = jnp.where(allowed, s, -BIG)
    top = jnp.max(s, axis=-1, keepdims=True)
    e = jnp.exp(s - top)
    prob = e / jnp.sum(e, axis=-1, keepdims=True)
    prob_low = prob.astype(bf)
    flat = lambda t: t.transpose(1, 0, 2).reshape(rows, D)
    ol = flat(mm("hqk,hkd->hqd", prob_low, v)).astype(bf)
    middle = x + (mm("rd,de->re", ol, w_out) + ob)
    n2, scaled_two, inv_two = layer_norm(middle, g2, b2)
    h2 = n2.astype(bf)
    u = mm("rd,df->rf", h2, w_up) + ub
    act, slope = gelu_both(u)
    act = act.astype(bf)
    out = (middle + (mm("rf,df->rd", act, w_downt) + db_)).astype(bf)
    dy = cot.astype(f32)
    g_downt = mm("rd,rf->df", cot, act)
    du = (mm("rd,df->rf", cot, w_downt) * slope).astype(bf)
    g_up = mm("rd,rf->df", h2, du)
    g_ub = jnp.sum(du.astype(f32), axis=0)
    dh2 = mm("rf,df->rd", du, w_up)
    dr, g_g2, g_b2 = norm_back(dh2, scaled_two, inv_two, g2)
    dmid = dy + dr
    dbr = dmid.astype(bf)
    g_ob = jnp.sum(dbr.astype(f32), axis=0)
    g_out = mm("rd,re->de", ol, dbr)
    do = heads(mm("re,de->rd", dbr, w_out).astype(bf))
    dp = mm("hqd,hkd->hqk", do, v)
    delta = jnp.sum(prob * dp, axis=-1, keepdims=True)
    ds = (prob * (dp - delta)).astype(bf)
    dq = flat(mm("hqk,hkd->hqd", ds, k) * scale).astype(bf)
    dk = flat(mm("hqk,hqd->hkd", ds, q) * scale).astype(bf)
    dv = flat(mm("hqk,hqd->hkd", prob_low, do)).astype(bf)
    dm = jnp.concatenate([dq, dk, dv[:, :VFRESH]], axis=1)
    g_qb = jnp.sum(dq.astype(f32), axis=0)
    g_vb = jnp.sum(dv[:, :VFRESH].astype(f32), axis=0)
    g_qkv = mm("rd,rc->dc", hl, dm)
    dh = mm("rc,dc->rd", dm, w_qkv)
    dr1, g_g1, g_b1 = norm_back(dh, scaled_one, inv_one, g1)
    dx = (dmid + dr1).astype(bf)
    grads = (g_qkv, g_out, g_up, g_downt)
    small = (g_g1, g_b1, g_qb, g_vb, g_ob, g_g2, g_b2, g_ub, jnp.sum(dy, axis=0))
    return out, dx, dv[:, VFRESH:], grads, small


def shards(
    plan, tokens, first_values, out_cot, ln1_gain, ln1_bias, w_qkv, q_bias, v_bias, w_out, out_bias,
    ln2_gain, ln2_bias, w_up, up_bias, w_down, down_bias,
):
    bf, f32 = jnp.bfloat16, jnp.float32
    R, C, n_mp, n_dp = plan.rows, plan.cols, plan.n_mp, plan.n_dp
    small = (ln1_gain, ln1_bias, q_bias, v_bias, out_bias, ln2_gain, ln2_bias, up_bias, down_bias)
    widths = [s.shape[0] for s in small]
    gap = lambda a, w: jnp.pad(a, ((0, 0), (0, w - a.shape[1])))
    row = jnp.concatenate(small)[None]
    packed = jnp.concatenate(
        [
            jnp.concatenate([gap(w_qkv, plan.out_at), gap(w_out, C - plan.out_at)], axis=1),
            w_up,
            w_down.T,
            jnp.pad(row, ((0, 15), (0, C - row.shape[1]))),
        ],
        axis=0,
    )
    g, x, f, y = gather(plan, packed, tokens, first_values, out_cot)

    def wide(lo, at, width):
        part = g[:, :, lo : lo + R, at : at + width]
        return part.reshape(n_mp, D, width).transpose(1, 0, 2).reshape(D, n_mp * width)

    weights = (
        wide(0, 0, plan.qkv),
        wide(0, plan.out_at, plan.out),
        wide(R, 0, C),
        wide(2 * R, 0, C),
    )
    vecs = g[:, :, 3 * R, :].astype(f32).transpose(1, 0, 2)
    ends = [sum(widths[:n]) for n in range(len(widths) + 1)]
    vectors = [vecs[:, :, a:b].reshape(-1) for a, b in zip(ends[:-1], ends[1:])]
    out, dx, dfirst, grads, small_grads = layer(
        x.reshape(SEQ, D), f.reshape(SEQ, -1), y.reshape(SEQ, D), weights, vectors
    )
    split = lambda a: a.astype(bf).reshape(n_dp, R, n_mp, -1).transpose(2, 0, 1, 3)
    gap4 = lambda a, w: jnp.pad(a, ((0, 0), (0, 0), (0, 0), (0, w - a.shape[3])))
    rows = jnp.concatenate([v.astype(bf).reshape(n_dp, n_mp, 1, -1) for v in small_grads], axis=3)
    rows = rows.transpose(1, 0, 2, 3)
    full = jnp.concatenate(
        [
            jnp.concatenate(
                [gap4(split(grads[0]), plan.out_at), gap4(split(grads[1]), C - plan.out_at)], axis=3
            ),
            split(grads[2]),
            split(grads[3]),
            jnp.pad(rows, ((0, 0), (0, 0), (0, 15), (0, C - rows.shape[3]))),
        ],
        axis=2,
    )
    total, r1, r2, r3 = reduce(
        plan,
        full,
        out.reshape(tokens.shape),
        dx.reshape(tokens.shape),
        dfirst.reshape(first_values.shape),
    )
    s = [total[3 * R, a:b] for a, b in zip(ends[:-1], ends[1:])]
    return (
        r1, r2, r3,
        s[0], s[1],
        total[:R, : plan.qkv],
        s[2], s[3],
        total[:R, plan.out_at : plan.out_at + plan.out],
        s[4], s[5], s[6],
        total[R : 2 * R],
        s[7],
        total[2 * R : 3 * R].T,
        s[8],
    )


def solution(mesh):
    plan = Plan(mesh)
    line = P(("dp", "mp"))
    rows = P(None, ("dp", "mp"), None)
    block = P("dp", "mp")
    grads = (line, line, block, line, line, block, line, line, line, block, line, P("mp", "dp"), line)
    return jax.shard_map(
        functools.partial(shards, plan),
        mesh=mesh,
        in_specs=(rows, rows, rows) + grads,
        out_specs=(rows, rows, rows) + grads,
        check_vma=False,
    )
```

```python
import functools

import jax
import jax.numpy as jnp
import numpy as np
from jax import lax
from jax.experimental import pallas as pl
from jax.experimental.pallas import tpu as pltpu
from jax.sharding import PartitionSpec as P

D = 768
HEADS = 12
HEAD = 64
FF = 3072
MICRO = 4
QKV = 1920
SEQ = 512
VFRESH = 384

EPS = 1e-05
BIG = 1e30
GELU_C = 0.7978845608028654
GELU_A = 0.044715
MESH = pl.DeviceIdType.MESH
ANY = pl.BlockSpec(memory_space=pl.ANY)


class Plan:
    def __init__(self, mesh):
        self.n_dp = mesh.shape["dp"]
        self.n_mp = mesh.shape["mp"]
        self.n_z = self.n_dp // 2
        self.rows = D // self.n_dp
        self.cols = FF // self.n_mp
        self.qkv = QKV // self.n_mp
        self.out = D // self.n_mp
        self.out_at = -(-self.qkv // 128) * 128
        self.unit = 3 * self.rows + 16
        self.small = self.n_dp * self.n_mp
        self.per_seq = SEQ * MICRO // SEQ
        self.n_seq = self.n_mp // MICRO
        assert self.out_at + self.out <= self.cols and self.rows % 16 == 0
        assert self.n_seq * MICRO == self.n_mp

    def ring_at(self, i):
        half = self.n_mp // 2
        return i + (i // half) * (self.n_mp - 1 + half - 2 * i)


def where_am_i():
    return lax.axis_index("dp"), lax.axis_index("mp")


def greet(plan, dp, i, z, c):
    barrier = pltpu.get_barrier_semaphore()
    partners = [(dp + 1 - 2 * c, i)]
    partners += [(((z + k) % plan.n_z) * 2 + c, i) for k in range(1, plan.n_z)]
    partners += [(dp, (i + k) % plan.n_mp) for k in range(1, plan.n_mp)]
    for partner in partners:
        pl.semaphore_signal(barrier, inc=1, device_id=partner, device_id_type=MESH)
    pl.semaphore_wait(barrier, len(partners))


def push(src, dst, send, recv, device):
    copy = pltpu.make_async_remote_copy(
        src_ref=src, dst_ref=dst, send_sem=send, recv_sem=recv, device_id=device, device_id_type=MESH
    )
    return copy


def gather_kernel(plan, pk, tok, fv, cot, g, x, f, y, own_sem, zs, zr, rs, rr, ss, sr, xs, xr):
    dp, i = where_am_i()
    c, z = dp % 2, dp // 2
    n_mp, n_z = plan.n_mp, plan.n_z
    sib = (dp + 1 - 2 * c, i)
    p = plan.ring_at(i)
    device_at = lambda pos: plan.ring_at((pos + n_mp) % n_mp)
    greet(plan, dp, i, z, c)

    pairs = ((tok, x), (fv, f), (cot, y))
    q = plan.per_seq
    for a, (src, dst) in enumerate(pairs):
        for m in range(MICRO):
            target = m * plan.n_seq + i // q
            place = i % q

            @pl.when(target != i)
            def _():
                push(src.at[m], dst.at[place], xs.at[a, m], xr.at[a, place], (dp, target)).start()

            @pl.when(target == i)
            def _():
                pltpu.make_async_copy(src.at[m], dst.at[place], xs.at[a, m]).start()

    mine = pltpu.make_async_copy(pk, g.at[i, dp], own_sem)
    mine.start()
    unit_dp = [((z + n_z - k) % n_z) * 2 + c for k in range(n_z)]

    def source(k, origin):
        return g.at[origin, unit_dp[k]]

    sends = []

    def to_sibling(k, h, src, origin):
        cp = push(src, g.at[origin, unit_dp[k]], ss.at[k, h], sr.at[k, h], sib)
        cp.start()
        sends.append(cp)

    def to_ring(k, h, src):
        sign = 1 if k % 2 == 0 else -1
        origin = device_at(p - sign * h)
        cp = push(src, g.at[origin, unit_dp[k]], rs.at[k, h], rr.at[k, h], (dp, device_at(p + sign)))
        cp.start()
        sends.append(cp)

    to_ring(0, 0, pk)
    for k in range(1, n_z):
        cp = push(pk, g.at[i, dp], zs.at[k - 1], zr.at[k - 1], (((z + k) % n_z) * 2 + c, i))
        cp.start()
        sends.append(cp)
    to_sibling(0, 0, pk, i)
    for k in range(1, n_z):
        here = source(k, i)
        push(here, here, zs.at[k - 1], zr.at[k - 1], sib).wait_recv()
        to_ring(k, 0, here)
        to_sibling(k, 0, here, i)
    for h in range(n_mp - 1):
        for k in range(n_z):
            sign = 1 if k % 2 == 0 else -1
            origin = device_at(p - sign * (h + 1))
            here = source(k, origin)
            push(here, here, rs.at[k, h], rr.at[k, h], sib).wait_recv()
            if h < n_mp - 2:
                to_ring(k, h + 1, here)
            to_sibling(k, h + 1, here, origin)
    sib_dp = [((z + n_z - k) % n_z) * 2 + 1 - c for k in range(n_z)]
    for h in range(n_mp):
        for k in range(n_z):
            sign = 1 if k % 2 == 0 else -1
            here = g.at[device_at(p - sign * h), sib_dp[k]]
            push(here, here, ss.at[k, h], sr.at[k, h], sib).wait_recv()
    for cp in sends:
        cp.wait_send()
    mine.wait()
    for a, (src, dst) in enumerate(pairs):
        for m in range(MICRO):
            target = m * plan.n_seq + i // q
            place = i % q

            @pl.when(target != i)
            def _():
                push(src.at[m], dst.at[place], xs.at[a, m], xr.at[a, place], (dp, target)).wait_send()

            @pl.when(target == i)
            def _():
                pltpu.make_async_copy(src.at[m], dst.at[place], xs.at[a, m]).wait()

        for place in range(q):
            origin = (i % plan.n_seq) * q + place

            @pl.when(origin != i)
            def _():
                push(dst.at[place], dst.at[place], xs.at[a, 0], xr.at[a, place], sib).wait_recv()


def gather(plan, packed, tok, fv, cot):
    n_mp, n_z = plan.n_mp, plan.n_z
    bf = jnp.bfloat16
    dma = pltpu.SemaphoreType.DMA
    return pl.pallas_call(
        functools.partial(gather_kernel, plan),
        name="gather",
        out_shape=(
            jax.ShapeDtypeStruct((n_mp, plan.n_dp, plan.unit, plan.cols), bf),
            jax.ShapeDtypeStruct(tok.shape, bf),
            jax.ShapeDtypeStruct(fv.shape, bf),
            jax.ShapeDtypeStruct(cot.shape, bf),
        ),
        in_specs=[ANY] * 4,
        out_specs=(ANY,) * 4,
        scratch_shapes=[
            dma,
            dma((n_z - 1,)),
            dma((n_z - 1,)),
            dma((n_z, n_mp - 1)),
            dma((n_z, n_mp - 1)),
            dma((n_z, n_mp)),
            dma((n_z, n_mp)),
            dma((3, MICRO)),
            dma((3, plan.per_seq)),
        ],
        compiler_params=pltpu.CompilerParams(collective_id=0, has_side_effects=True),
    )(packed, tok, fv, cot)


def reduce_kernel(
    plan, grads, o1, o2, o3, total, r1, r2, r3,
    own, other, ring, last, own_sem, ss, sr, rs, rr, zs, zr, xs, xr,
):
    dp, i = where_am_i()
    c, z = dp % 2, dp // 2
    n_mp, n_z, R = plan.n_mp, plan.n_z, plan.rows
    sib = (dp + 1 - 2 * c, i)
    p = plan.ring_at(i)
    device_at = lambda pos: plan.ring_at((pos + n_mp) % n_mp)
    f32, bf = jnp.float32, jnp.bfloat16
    greet(plan, dp, i, z, c)

    pairs = ((o1, r1), (o2, r2), (o3, r3))
    q = plan.per_seq
    micro, part = i // plan.n_seq, i % plan.n_seq
    place = i % q

    def back(start):
        for a, (src, dst) in enumerate(pairs):
            for s in range(q):
                owner = part * q + s
                far = push(src.at[s], dst.at[micro], xs.at[a, s], xr.at[a, micro], (dp, owner))
                near = pltpu.make_async_copy(src.at[s], dst.at[micro], xs.at[a, s])

                @pl.when(owner != i)
                def _():
                    far.start() if start else far.wait_send()

                @pl.when(owner == i)
                def _():
                    near.start() if start else near.wait()

    bounds = ((0, R), (R, 2 * R), (2 * R, plan.unit))
    tiles = [pl.ds(lo, hi - lo) for lo, hi in bounds]
    unit_dp = [((z + n_z - k) % n_z) * 2 + c for k in range(n_z)]
    sib_dp = [((z + n_z - k) % n_z) * 2 + 1 - c for k in range(n_z)]
    order = [k for k in range(n_z - 1, -1, -1)]
    sends = []
    for k in order:
        for t in range(n_mp):
            cp = push(grads.at[t, sib_dp[k]], other.at[t, k], ss.at[k, t], sr.at[k, t], sib)
            cp.start()
            sends.append(cp)
            pltpu.make_async_copy(grads.at[t, unit_dp[k]], own.at[t, k], own_sem.at[k, t]).start()
    back(True)

    def add(t, k, tile, extra):
        own[t, k, tile, :] = (own[t, k, tile, :].astype(f32) + extra.astype(f32)).astype(bf)

    def chunk(k, step):
        sign = 1 if k % 2 == 0 else -1
        return device_at(p - sign * (1 + step))

    def ring_send(k, piece, step):
        sign = 1 if k % 2 == 0 else -1
        tile = tiles[piece]
        cp = push(
            own.at[chunk(k, step), k, tile],
            ring.at[k, step, tile],
            rs.at[k, piece, step],
            rr.at[k, piece, step],
            (dp, device_at(p + sign)),
        )
        cp.start()
        sends.append(cp)

    for k0 in range(n_z - 2, -1, -2):
        ks = (k0, k0 + 1)
        for k in ks:
            for t in range(n_mp):
                pltpu.make_async_copy(grads.at[t, unit_dp[k]], own.at[t, k], own_sem.at[k, t]).wait()
                push(other.at[t, k], other.at[t, k], ss.at[k, t], sr.at[k, t], sib).wait_recv()
        for step in range(n_mp):
            for piece in range(3):
                for k in ks:
                    tile = tiles[piece]
                    t = chunk(k, step)
                    if step > 0:
                        got = ring.at[k, step - 1, tile]
                        push(got, got, rs.at[k, piece, step - 1], rr.at[k, piece, step - 1], sib).wait_recv()
                        own[t, k, tile, :] = (
                            own[t, k, tile, :].astype(f32)
                            + other[t, k, tile, :].astype(f32)
                            + ring[k, step - 1, tile, :].astype(f32)
                        ).astype(bf)
                    else:
                        add(t, k, tile, other[t, k, tile, :])
                    if step < n_mp - 1:
                        ring_send(k, piece, step)
                    elif k > 0:
                        cp = push(
                            own.at[i, k, tile],
                            last.at[k - 1, tile],
                            zs.at[k - 1, piece],
                            zr.at[k - 1, piece],
                            (unit_dp[k], i),
                        )
                        cp.start()
                        sends.append(cp)
    for piece in range(3):
        tile = tiles[piece]
        for k in range(1, n_z):
            got = last.at[k - 1, tile]
            push(got, got, zs.at[k - 1, piece], zr.at[k - 1, piece], sib).wait_recv()
        value = own[i, 0, tile, :].astype(f32)
        for k in range(1, n_z):
            value = value + last[k - 1, tile, :].astype(f32)
        total[tile, :] = value
    for cp in sends:
        cp.wait_send()
    back(False)
    for a, (src, dst) in enumerate(pairs):
        for m in range(MICRO):
            origin = m * plan.n_seq + i // q

            @pl.when(origin != i)
            def _():
                push(dst.at[m], dst.at[m], xs.at[a, 0], xr.at[a, m], sib).wait_recv()


def reduce(plan, grads, o1, o2, o3):
    n_mp, n_z = plan.n_mp, plan.n_z
    bf, f32 = jnp.bfloat16, jnp.float32
    dma = pltpu.SemaphoreType.DMA
    block = (plan.unit, plan.cols)
    return pl.pallas_call(
        functools.partial(reduce_kernel, plan),
        name="reduce",
        out_shape=(
            jax.ShapeDtypeStruct(block, f32),
            jax.ShapeDtypeStruct(o1.shape, bf),
            jax.ShapeDtypeStruct(o2.shape, bf),
            jax.ShapeDtypeStruct(o3.shape, bf),
        ),
        in_specs=[ANY] * 4,
        out_specs=(pl.BlockSpec(memory_space=pltpu.VMEM), ANY, ANY, ANY),
        scratch_shapes=[
            pltpu.VMEM((n_mp, n_z) + block, bf),
            pltpu.VMEM((n_mp, n_z) + block, bf),
            pltpu.VMEM((n_z, n_mp - 1) + block, bf),
            pltpu.VMEM((n_z - 1,) + block, bf),
            dma((n_z, n_mp)),
            dma((n_z, n_mp)),
            dma((n_z, n_mp)),
            dma((n_z, 3, n_mp - 1)),
            dma((n_z, 3, n_mp - 1)),
            dma((n_z - 1, 3)),
            dma((n_z - 1, 3)),
            dma((3, plan.per_seq)),
            dma((3, MICRO)),
        ],
        compiler_params=pltpu.CompilerParams(
            collective_id=1, has_side_effects=True, vmem_limit_bytes=56 << 20
        ),
    )(grads, o1, o2, o3)


WIDE = (0, 1, 2, 4, 5, 6, 8)
V_BIAS, UP_BIAS = 3, 7
G1, B1, QB, OB, G2, B2, DB = WIDE


def dot(a, b):
    return jnp.dot(a, b, preferred_element_type=jnp.float32)


def dot_nt(a, b):
    return lax.dot_general(a, b, (((1,), (1,)), ((), ())), preferred_element_type=jnp.float32)


def chunks(rows, step, body):
    @pl.loop(0, rows // step)
    def _(at):
        body(pl.ds(pl.multiple_of(at * step, step), step))


def norm_stats(r):
    average = jnp.mean(r, axis=-1, keepdims=True)
    centred = r - average
    variance = jnp.mean(centred * centred, axis=-1, keepdims=True)
    inv_std = lax.rsqrt(variance + EPS)
    return centred * inv_std, inv_std


def norm_back(grad_out, scaled, inv_std, gain):
    e = grad_out * gain
    first = jnp.mean(e, axis=-1, keepdims=True)
    second = jnp.mean(e * scaled, axis=-1, keepdims=True)
    return inv_std * (e - first - scaled * second)


def layer_kernel(
    plan, tab, dev, x_ref, f_ref, y_ref, g_hbm, out_ref, dx_ref, df_ref, gr,
    w, wq, wo, sv, vec, ub, hl, hlt, qkv, ot, otb, lse, mid, n2, inv2, h2, h2t, yt,
    big, acc, act, du, do, dm, dv, dk, dqt, sums, ubg, sem,
):
    bf, f32 = jnp.bfloat16, jnp.float32
    R, C, n_mp, n_dp = plan.rows, plan.cols, plan.n_mp, plan.n_dp
    n = n_mp * n_dp
    spr = C // 128
    load = pltpu.make_async_copy(g_hbm, w, sem)
    load.start()
    load.wait()
    step = 64

    def panel(j, at):
        return w[j, :, at * R : (at + 1) * R, :].reshape(D, C)

    for r in range(-(-9 // spr)):
        for j in range(n_mp):
            for d in range(n_dp):
                at = j * n_dp + d
                sv[r, at : at + 1, :] = w[j, d, 3 * R + r : 3 * R + r + 1, :].astype(f32)
    rowdev = dev[:, 0:1]
    lanes = lambda v: slice((v % spr) * 128, (v % spr) * 128 + 128)
    onehot = lambda t, width: (lax.broadcasted_iota(jnp.int32, (128, width), 0) == tab[t : t + 1, :width]).astype(bf)

    def expand(v, e, owner):
        got = dot(sv[v // spr, :, lanes(v)].astype(bf), e)
        return jnp.sum(jnp.where(owner == rowdev, got, 0.0), axis=0, keepdims=True)

    e24 = onehot(0, D)
    for v in WIDE:
        vec[v : v + 1, :] = expand(v, e24, tab[1:2, :])
    vec[V_BIAS : V_BIAS + 1, :] = expand(V_BIAS, onehot(2, D), tab[3:4, :])
    e96 = onehot(4, C)
    for j in range(n_mp):
        ub[j : j + 1, :] = expand(UP_BIAS, e96, tab[5:6, :C] + j * n_dp)
    row = lambda v: vec[v : v + 1, :]

    for j in range(n_mp):
        for d in range(n_dp):
            rows = slice(d * R, (d + 1) * R)
            wq[rows, j * plan.qkv : (j + 1) * plan.qkv] = w[j, d, 0:R, 0 : plan.qkv]
            wo[rows, j * plan.out : (j + 1) * plan.out] = w[j, d, 0:R, plan.out_at : plan.out_at + plan.out]

    def first_norm(at):
        n1, _ = norm_stats(x_ref[at, :].astype(f32))
        hl[at, :] = (n1 * row(G1) + row(B1)).astype(bf)

    chunks(SEQ, step, first_norm)
    hlt[...] = hl[...].T
    yt[...] = y_ref[...].T

    def project(at):
        h = hl[at, :]
        q = dot(h, wq[:, 0:D]) + row(QB)
        qkv[at, 0:D] = q.astype(bf) * 0.125
        qkv[at, D : 2 * D] = dot(h, wq[:, D : 2 * D]).astype(bf)
        v = dot(h, wq[:, 2 * D : QKV]) + row(V_BIAS)[:, :VFRESH]
        qkv[at, 2 * D : QKV] = v.astype(bf)
        qkv[at, QKV : 3 * D] = f_ref[at, :]

    chunks(SEQ, 256, project)

    B = 256
    head_of = lax.broadcasted_iota(jnp.int32, (1, 128), 1) // HEAD
    keep = lax.broadcasted_iota(jnp.int32, (B, B), 0) <= lax.broadcasted_iota(jnp.int32, (B, B), 1)

    def scores(k2, qm, at):
        s = dot_nt(k2, qm)
        last = jnp.where(keep, s[at * B :, :], -BIG)
        return last if at == 0 else jnp.concatenate([s[: at * B, :], last], axis=0)

    @pl.loop(0, HEADS // 2)
    def _(t):
        cols = lambda base: pl.ds(pl.multiple_of(base + t * 128, 128), 128)
        vt = qkv[:, cols(2 * D)].T
        for e in range(2):
            mask = (head_of == e).astype(bf)
            for at in range(SEQ // B):
                kk = (at + 1) * B
                span = slice(at * B, kk)
                s = scores(qkv[0:kk, cols(D)], qkv[span, cols(0)] * mask, at)
                top = jnp.max(s, axis=0, keepdims=True)
                ex = jnp.exp(s - top)
                total = jnp.sum(ex, axis=0, keepdims=True)
                o = dot(vt[e * HEAD : (e + 1) * HEAD, 0:kk], ex.astype(bf)) / total
                ot[pl.ds(pl.multiple_of(t * 128 + e * HEAD, HEAD), HEAD), span] = o
                lse[t, e : e + 1, span] = top + jnp.log(total)

    otb[...] = ot[...].astype(bf)
    du[:, 0:D] = otb[...].T

    def second_norm(at):
        m = x_ref[at, :].astype(f32) + (dot(du[at, 0:D], wo[...]) + row(OB))
        mid[at, :] = m
        scaled, inv = norm_stats(m)
        n2[at, :] = scaled
        inv2[at, :] = jnp.broadcast_to(inv, (B, 128))
        h2[at, :] = (scaled * row(G2) + row(B2)).astype(bf)

    chunks(SEQ, B, second_norm)
    h2t[...] = h2[...].T
    acc[...] = jnp.zeros_like(acc)
    big[...] = jnp.zeros_like(big)

    @pl.loop(0, n_mp)
    def _(j):
        bias = ub[pl.ds(j, 1), :]

        def rows(at):
            up, down = panel(j, 1), panel(j, 2)
            u = dot(h2[at, :], up) + bias
            u2 = u * u
            tangent = jnp.tanh(GELU_C * (u + GELU_A * u2 * u))
            half = 0.5 * (1.0 + tangent)
            a = (u * half).astype(bf)
            slope = half + 0.5 * u * (1.0 - tangent * tangent) * GELU_C * (1.0 + 3.0 * GELU_A * u2)
            act[at, :] = a
            acc[at, :] += dot_nt(a, down)
            g = (dot(y_ref[at, :], down) * slope).astype(bf)
            du[at, 0:C] = g
            big[at, :] += dot_nt(g, up)

        chunks(SEQ, 128, rows)
        gr[j, :, 2 * R : 3 * R, :] = dot(yt[...], act[...]).astype(bf).reshape(n_dp, R, C)
        gr[j, :, R : 2 * R, :] = dot(h2t[...], du[:, 0:C]).astype(bf).reshape(n_dp, R, C)
        ubg[pl.ds(j, 1), :] = jnp.sum(du[:, 0:C].astype(f32), axis=0, keepdims=True)

    sums[...] = jnp.zeros_like(sums)

    def second_back(at):
        out_ref[at, :] = (mid[at, :] + (acc[at, :] + row(DB))).astype(bf)
        dh = big[at, :]
        dy = y_ref[at, :].astype(f32)
        scaled = n2[at, :]
        dr = norm_back(dh, scaled, inv2[at, 0:1], row(G2))
        dmid = dy + dr
        mid[at, :] = dmid
        low = dmid.astype(bf)
        du[at, 0:D] = low
        total = lambda a: jnp.sum(a, axis=0, keepdims=True)
        sums[G2 : G2 + 1, :] += total(dh * scaled)
        sums[B2 : B2 + 1, :] += total(dh)
        sums[OB : OB + 1, :] += total(low.astype(f32))
        sums[DB : DB + 1, :] += total(dy)

    chunks(SEQ, step, second_back)
    for j in range(n_mp):
        g = dot(otb[...], du[:, j * plan.out : (j + 1) * plan.out]).astype(bf)
        gr[j, :, 0:R, plan.out_at : plan.out_at + plan.out] = g.reshape(n_dp, R, plan.out)

    def out_back(at):
        do[at, :] = dot_nt(du[at, 0:D], wo[...]).astype(bf)

    chunks(SEQ, B, out_back)

    @pl.loop(0, HEADS // 2)
    def _(t):
        cols = lambda base: pl.ds(pl.multiple_of(base + t * 128, 128), 128)
        kt = qkv[:, cols(D)].T
        dot_ = do[:, cols(0)].astype(f32).T
        prod = dot_ * ot[cols(0), :]
        dv[...] = jnp.zeros_like(dv)
        dk[...] = jnp.zeros_like(dk)
        for e in range(2):
            mask = (head_of == e).astype(bf)
            delta = jnp.sum(prod[e * HEAD : (e + 1) * HEAD, :], axis=0, keepdims=True)
            for at in range(SEQ // B):
                kk = (at + 1) * B
                span = slice(at * B, kk)
                qm = qkv[span, cols(0)] * mask
                dom = do[span, cols(0)] * mask
                s = scores(qkv[0:kk, cols(D)], qm, at)
                p = jnp.exp(s - lse[t, e : e + 1, span])
                dp = dot_nt(qkv[0:kk, cols(2 * D)], dom)
                ds = (p * (dp - delta[:, span])).astype(bf)
                dv[0:kk, :] += dot(p.astype(bf), dom)
                dk[0:kk, :] += dot(ds, qm)
                dqt[e * HEAD : (e + 1) * HEAD, span] = dot(kt[e * HEAD : (e + 1) * HEAD, 0:kk], ds)
        dm[:, cols(0)] = (dqt[...].T * 0.125).astype(bf)
        dm[:, cols(D)] = dk[...].astype(bf)
        dm[:, cols(2 * D)] = dv[...].astype(bf)

    df_ref[...] = dm[:, QKV : 3 * D]
    for j in range(n_mp):
        g = dot(hlt[...], dm[:, j * plan.qkv : (j + 1) * plan.qkv]).astype(bf)
        gr[j, :, 0:R, 0 : plan.qkv] = g.reshape(n_dp, R, plan.qkv)

    def project_back(at):
        acc[at, :] = dot_nt(dm[at, 0:QKV], wq[...])

    chunks(SEQ, B, project_back)

    def first_back(at):
        n1, inv = norm_stats(x_ref[at, :].astype(f32))
        dh = acc[at, :]
        dr = norm_back(dh, n1, inv, row(G1))
        dx_ref[at, :] = (mid[at, :] + dr).astype(bf)
        total = lambda a: jnp.sum(a, axis=0, keepdims=True)
        sums[G1 : G1 + 1, :] += total(dh * n1)
        sums[B1 : B1 + 1, :] += total(dh)
        sums[QB : QB + 1, :] += total(dm[at, 0:D].astype(f32))
        sums[V_BIAS : V_BIAS + 1, 0:VFRESH] += total(dm[at, 2 * D : QKV].astype(f32))

    chunks(SEQ, step, first_back)

    def collect(g, e, owner):
        return dot_nt(jnp.where(owner == rowdev, g, 0.0).astype(bf), e)

    for v in WIDE:
        sv[v // spr, :, lanes(v)] = collect(sums[v : v + 1, :], e24, tab[1:2, :])
    sv[V_BIAS // spr, :, lanes(V_BIAS)] = collect(sums[V_BIAS : V_BIAS + 1, :], onehot(2, D), tab[3:4, :])
    got = collect(ubg[0:1, :], e96, tab[5:6, :C])
    for j in range(1, n_mp):
        got = got + collect(ubg[j : j + 1, :], e96, tab[5:6, :C] + j * n_dp)
    sv[UP_BIAS // spr, :, lanes(UP_BIAS)] = got
    at16 = lax.broadcasted_iota(jnp.int32, (16, C), 0)
    for j in range(n_mp):
        for d in range(n_dp):
            at = j * n_dp + d
            value = jnp.zeros((16, C), f32)
            for r in range(-(-9 // spr)):
                value = jnp.where(at16 == r, sv[r, at : at + 1, :], value)
            gr[j, d, 3 * R :, :] = value.astype(bf)


def layer(plan, g, x, f, y):
    R, C, n_mp, n_dp = plan.rows, plan.cols, plan.n_mp, plan.n_dp
    n = n_mp * n_dp
    bf, f32 = jnp.bfloat16, jnp.float32
    spr = C // 128
    count = np.arange(D, dtype=np.int32)
    tab = np.zeros((8, D), np.int32)
    for at, width in ((0, D // n), (2, VFRESH // n), (4, FF // n)):
        tab[at], tab[at + 1] = count % width, count // width
    r = np.arange(n, dtype=np.int32)
    dev = np.tile(((r % n_dp) * n_mp + r // n_dp)[:, None], (1, 128))
    vm = pltpu.VMEM
    vmem = pl.BlockSpec(memory_space=vm)
    wide = lambda t: vm((SEQ, D), t)
    tall = lambda t: vm((D, SEQ), t)
    return pl.pallas_call(
        functools.partial(layer_kernel, plan),
        name="layer",
        out_shape=(
            jax.ShapeDtypeStruct((SEQ, D), bf),
            jax.ShapeDtypeStruct((SEQ, D), bf),
            jax.ShapeDtypeStruct((SEQ, D // 2), bf),
            jax.ShapeDtypeStruct(g.shape, bf),
        ),
        in_specs=[vmem] * 5 + [ANY],
        out_specs=(vmem,) * 4,
        scratch_shapes=[
            vm(g.shape, bf), vm((D, QKV), bf), vm((D, D), bf),
            vm((-(-9 // spr), n, C), f32), vm((16, D), f32), vm((max(8, n_mp), C), f32),
            wide(bf), tall(bf), vm((SEQ, 3 * D), bf), tall(f32), tall(bf),
            vm((HEADS // 2, 8, SEQ), f32),
            wide(f32), wide(f32), vm((SEQ, 128), f32), wide(bf), tall(bf), tall(bf),
            wide(f32), wide(f32), vm((SEQ, C), bf), wide(bf), wide(bf), vm((SEQ, 3 * D), bf),
            vm((SEQ, 128), f32), vm((SEQ, 128), f32), vm((128, SEQ), f32),
            vm((16, D), f32), vm((max(8, n_mp), C), f32),
            pltpu.SemaphoreType.DMA,
        ],
        compiler_params=pltpu.CompilerParams(vmem_limit_bytes=63 << 20),
    )(jnp.asarray(tab), jnp.asarray(dev), x, f, y, g)


def shards(
    plan, tokens, first_values, out_cot, ln1_gain, ln1_bias, w_qkv, q_bias, v_bias, w_out, out_bias,
    ln2_gain, ln2_bias, w_up, up_bias, w_down, down_bias,
):
    R, C = plan.rows, plan.cols
    small = (ln1_gain, ln1_bias, q_bias, v_bias, out_bias, ln2_gain, ln2_bias, up_bias, down_bias)
    widths = [s.shape[0] for s in small]
    gap = lambda a, w: jnp.pad(a, ((0, 0), (0, w - a.shape[1])))
    spr = C // 128
    slots = jnp.concatenate([jnp.pad(s, (0, 128 - s.shape[0])) for s in small])
    slots = jnp.pad(slots, (0, 16 * C - slots.shape[0])).reshape(16, C)
    packed = jnp.concatenate(
        [
            jnp.concatenate([gap(w_qkv, plan.out_at), gap(w_out, C - plan.out_at)], axis=1),
            w_up,
            w_down.T,
            slots,
        ],
        axis=0,
    )
    g, x, f, y = gather(plan, packed, tokens, first_values, out_cot)
    out, dx, dfirst, full = layer(plan, g, x.reshape(SEQ, D), f.reshape(SEQ, -1), y.reshape(SEQ, D))
    total, r1, r2, r3 = reduce(
        plan,
        full,
        out.reshape(tokens.shape),
        dx.reshape(tokens.shape),
        dfirst.reshape(first_values.shape),
    )
    s = [total[3 * R + v // spr, (v % spr) * 128 : (v % spr) * 128 + w] for v, w in enumerate(widths)]
    return (
        r1, r2, r3,
        s[0], s[1],
        total[:R, : plan.qkv],
        s[2], s[3],
        total[:R, plan.out_at : plan.out_at + plan.out],
        s[4], s[5], s[6],
        total[R : 2 * R],
        s[7],
        total[2 * R : 3 * R].T,
        s[8],
    )


def solution(mesh):
    plan = Plan(mesh)
    line = P(("dp", "mp"))
    rows = P(None, ("dp", "mp"), None)
    block = P("dp", "mp")
    grads = (line, line, block, line, line, block, line, line, line, block, line, P("mp", "dp"), line)
    return jax.shard_map(
        functools.partial(shards, plan),
        mesh=mesh,
        in_specs=(rows, rows, rows) + grads,
        out_specs=(rows, rows, rows) + grads,
        check_vma=False,
    )
```

```python
import functools

import jax
import jax.numpy as jnp
import numpy as np
from jax import lax
from jax.experimental import pallas as pl
from jax.experimental.pallas import tpu as pltpu
from jax.sharding import PartitionSpec as P

D = 768
HEADS = 12
HEAD = 64
FF = 3072
MICRO = 4
QKV = 1920
SEQ = 512
VFRESH = 384

EPS = 1e-05
BIG = 1e30
GELU_C = 0.7978845608028654
GELU_A = 0.044715
MESH = pl.DeviceIdType.MESH
ANY = pl.BlockSpec(memory_space=pl.ANY)
IN_VMEM = pl.BlockSpec(memory_space=pltpu.VMEM)
BF, F32 = jnp.bfloat16, jnp.float32

WIDE = (0, 1, 2, 4, 5, 6, 8)
V_BIAS, UP_BIAS = 3, 7
G1, B1, QB, OB, G2, B2, DB = WIDE
N_VEC = 9


class Plan:
    def __init__(self, mesh):
        self.n_dp = mesh.shape["dp"]
        self.n_mp = mesh.shape["mp"]
        self.n = self.n_dp * self.n_mp
        self.n_z = self.n_dp // 2
        self.rows = D // self.n_dp
        self.cols = FF // self.n_mp
        self.qkv = QKV // self.n_mp
        self.out = D // self.n_mp
        self.qw = -(-self.qkv // 128) * 128
        self.group = self.cols // 3
        self.spr = self.qw // 128
        self.vec_rows = -(-N_VEC // self.spr)
        self.half = self.n_mp // 2
        self.per_seq = SEQ // (SEQ // MICRO)
        self.n_seq = self.n_mp // MICRO
        assert self.out <= self.group and self.rows % 48 == 0 and self.vec_rows <= 16
        assert self.n_seq * MICRO == self.n_mp and self.n_z % 2 == 0

    def ring_at(self, i):
        return i + (i // self.half) * (self.n_mp - 1 + self.half - 2 * i)

    def slots(self, d):
        if d == self.half:
            return 0, self.n_z // 2
        return self.n_z // 2 + (d - 1) * self.n_z, self.n_z


def dot(a, b):
    return jnp.dot(a, b, preferred_element_type=F32)


def dot_nt(a, b):
    return lax.dot_general(a, b, (((1,), (1,)), ((), ())), preferred_element_type=F32)


def chunks(rows, step, body):
    @pl.loop(0, rows // step)
    def _(at):
        body(pl.ds(pl.multiple_of(at * step, step), step))


def norm_stats(r):
    average = jnp.mean(r, axis=-1, keepdims=True)
    centred = r - average
    variance = jnp.mean(centred * centred, axis=-1, keepdims=True)
    inv_std = lax.rsqrt(variance + EPS)
    return centred * inv_std, inv_std


def norm_back(grad_out, scaled, inv_std, gain):
    e = grad_out * gain
    first = jnp.mean(e, axis=-1, keepdims=True)
    second = jnp.mean(e * scaled, axis=-1, keepdims=True)
    return inv_std * (e - first - scaled * second)


class Exchange:
    def __init__(self, plan):
        self.plan = plan
        dp, i = lax.axis_index("dp"), lax.axis_index("mp")
        self.dp, self.i, self.c, self.z = dp, i, dp % 2, dp // 2
        self.sib = (dp + 1 - 2 * self.c, i)
        self.p = plan.ring_at(i)

    def at(self, pos):
        return self.plan.ring_at((pos + 2 * self.plan.n_mp) % self.plan.n_mp)

    def z_peer(self, k):
        return ((self.z + k) % self.plan.n_z) * 2 + self.c

    def greet(self):
        plan = self.plan
        barrier = pltpu.get_barrier_semaphore()
        partners = [self.sib]
        partners += [(self.z_peer(k), self.i) for k in range(1, plan.n_z)]
        partners += [(self.dp, (self.i + k) % plan.n_mp) for k in range(1, plan.n_mp)]
        for partner in partners:
            pl.semaphore_signal(barrier, inc=1, device_id=partner, device_id_type=MESH)
        pl.semaphore_wait(barrier, len(partners))

    def push(self, src, dst, send, recv, device):
        return pltpu.make_async_remote_copy(
            src_ref=src, dst_ref=dst, send_sem=send, recv_sem=recv, device_id=device, device_id_type=MESH
        )


class Gather:
    def __init__(self, ex, ref, sems):
        self.ex, self.ref = ex, ref
        self.zs, self.zr, self.rs, self.rr, self.ss, self.sr = sems

    def units(self, s, d):
        plan = self.ex.plan
        return pl.ds(s * (plan.n_z // 2), plan.n_z // 2) if d == plan.half else pl.ds(0, plan.n_z)

    def own(self):
        return self.ref.at[self.ex.i, self.ex.z, self.ex.c]

    def z_copy(self, k):
        ex = self.ex
        return ex.push(self.own(), self.own(), self.zs.at[k - 1], self.zr.at[k - 1], (ex.z_peer(k), ex.i))

    def ring_copy(self, s, d):
        ex = self.ex
        sign = 1 - 2 * s
        view = self.ref.at[ex.at(ex.p - sign * (d - 1)), self.units(s, d), ex.c]
        return ex.push(view, view, self.rs.at[s, d - 1], self.rr.at[s, d - 1], (ex.dp, ex.at(ex.p + sign)))

    def sib_copy(self, offset):
        ex = self.ex
        at = (offset + ex.plan.n_mp) % ex.plan.n_mp
        view = self.ref.at[ex.at(ex.p + offset), :, ex.c]
        return ex.push(view, view, self.ss.at[at], self.sr.at[at], ex.sib)

    def start(self):
        for k in range(1, self.ex.plan.n_z):
            self.z_copy(k).start()

    def column(self):
        for k in range(1, self.ex.plan.n_z):
            self.z_copy(k).wait_recv()
        for s in range(2):
            self.ring_copy(s, 1).start()
        self.sib_copy(0).start()

    def hop(self, d):
        half = self.ex.plan.half
        for s in range(2):
            self.ring_copy(s, d).wait_recv()
            if d < half:
                self.ring_copy(s, d + 1).start()
                self.sib_copy(-d if s == 0 else d).start()
        if d == half:
            self.sib_copy(half).start()

    def wait_sib(self, offset):
        self.sib_copy(offset).wait_recv()

    def wait_sent(self, offset):
        half = self.ex.plan.half
        self.sib_copy(offset).wait_send()
        if offset == 0:
            for k in range(1, self.ex.plan.n_z):
                self.z_copy(k).wait_send()
            for s in range(2):
                self.ring_copy(s, 1).wait_send()
        elif abs(offset) < half:
            self.ring_copy(0 if offset < 0 else 1, abs(offset) + 1).wait_send()


class Reduce:
    def __init__(self, ex, ref, tile, other, ring, last, sems):
        self.ex, self.ref, self.tile = ex, ref, tile
        self.other, self.ring, self.last = other, ring, last
        self.ss, self.sr, self.rs, self.rr, self.zs, self.zr = sems

    def units(self, s, d):
        n_z = self.ex.plan.n_z
        return pl.ds(s * (n_z // 2), n_z // 2) if d == self.ex.plan.half else pl.ds(0, n_z)

    def sib_copy(self, offset):
        ex = self.ex
        at = (offset + ex.plan.n_mp) % ex.plan.n_mp
        view = self.ref.at[ex.at(ex.p + offset), :, 1 - ex.c, self.tile]
        return ex.push(view, self.other.at[at], self.ss.at[at], self.sr.at[at], ex.sib)

    def ring_copy(self, s, d, part=None):
        ex = self.ex
        plan = ex.plan
        sign = 1 - 2 * s
        at, count = plan.slots(d)
        if part is None:
            units, slot = self.units(s, d), pl.ds(at, count)
            sem = d - 1
        else:
            units, slot = pl.ds(part * (plan.n_z // 2), plan.n_z // 2), pl.ds(at + part * (plan.n_z // 2), plan.n_z // 2)
            sem = plan.half - 2 + 2 * part
        view = self.ref.at[ex.at(ex.p + sign * d), units, ex.c, self.tile]
        return ex.push(view, self.ring.at[s, slot], self.rs.at[s, sem], self.rr.at[s, sem], (ex.dp, ex.at(ex.p + sign)))

    def z_copy(self, k):
        ex = self.ex
        to = (ex.z + ex.plan.n_z - k) % ex.plan.n_z
        view = self.ref.at[ex.i, to, ex.c, self.tile]
        return ex.push(view, self.last.at[k - 1], self.zs.at[k - 1], self.zr.at[k - 1], (to * 2 + ex.c, ex.i))

    def to_sibling(self, offset):
        self.sib_copy(offset).start()

    def add(self, offset, first, count, *terms):
        j = self.ex.at(self.ex.p + offset)

        @pl.loop(0, count)
        def _(u):
            value = self.ref[j, first + u, self.ex.c, self.tile, :].astype(F32)
            for buf, at in terms:
                value = value + buf(at + u).astype(F32)
            self.ref[j, first + u, self.ex.c, self.tile, :] = value.astype(BF)

    def from_sibling(self, offset):
        at = (offset + self.ex.plan.n_mp) % self.ex.plan.n_mp
        self.sib_copy(offset).wait_recv()
        self.add(offset, 0, self.ex.plan.n_z, (lambda u: self.other[at, u], 0))

    def far(self):
        half = self.ex.plan.half
        self.from_sibling(half)
        for s in range(2):
            self.ring_copy(s, half).start()

    def free(self, s):
        half = self.ex.plan.half
        self.from_sibling((1 - 2 * s) * (half - 1))
        self.ring_copy(s, half - 1, 1 - s).start()

    def bound(self, s):
        plan = self.ex.plan
        half = plan.half
        self.ring_copy(s, half).wait_recv()
        at, count = plan.slots(half)
        self.add((1 - 2 * s) * (half - 1), s * count, count, (lambda u: self.ring[s, u], at))
        self.ring_copy(s, half - 1, s).start()

    def wait_ring(self, s, d):
        if d == self.ex.plan.half - 1:
            for part in range(2):
                self.ring_copy(s, d, part).wait_recv()
        else:
            self.ring_copy(s, d).wait_recv()

    def nearer(self):
        plan = self.ex.plan
        for d in range(plan.half - 2, 0, -1):
            for s in range(2):
                offset = (1 - 2 * s) * d
                self.from_sibling(offset)
                self.wait_ring(s, d + 1)
                self.add(offset, 0, plan.n_z, (lambda u: self.ring[s, u], plan.slots(d + 1)[0]))
                self.ring_copy(s, d).start()

    def home(self):
        plan = self.ex.plan
        for s in range(2):
            self.wait_ring(s, 1)
        self.sib_copy(0).wait_recv()
        at = plan.slots(1)[0]
        self.add(
            0, 0, plan.n_z,
            (lambda u: self.other[0, u], 0),
            (lambda u: self.ring[0, u], at),
            (lambda u: self.ring[1, u], at),
        )
        for k in range(1, plan.n_z):
            self.z_copy(k).start()

    def finish(self):
        ex = self.ex
        value = self.ref[ex.i, ex.z, ex.c, self.tile, :].astype(F32)
        for k in range(1, ex.plan.n_z):
            self.z_copy(k).wait_recv()
            value = value + self.last[k - 1].astype(F32)
        return value

    def wait_sent(self):
        plan = self.ex.plan
        for offset in range(plan.n_mp):
            self.sib_copy(offset).wait_send()
        for s in range(2):
            for d in range(1, plan.half + 1):
                if d == plan.half - 1:
                    for part in range(2):
                        self.ring_copy(s, d, part).wait_send()
                else:
                    self.ring_copy(s, d).wait_send()
        for k in range(1, plan.n_z):
            self.z_copy(k).wait_send()


class Rows:
    def __init__(self, ex, src, dst, send, recv, out):
        self.ex, self.src, self.dst, self.send, self.recv, self.out = ex, src, dst, send, recv, out

    def move(self, start):
        ex = self.ex
        plan, i = ex.plan, ex.i
        q = plan.per_seq
        for m in range(MICRO):
            if self.out:
                target, place = (i % plan.n_seq) * q + m, i // plan.n_seq
            else:
                target, place = m * plan.n_seq + i // q, i % q
            far = ex.push(self.src.at[m], self.dst.at[place], self.send.at[m], self.recv.at[place], (ex.dp, target))
            near = pltpu.make_async_copy(self.src.at[m], self.dst.at[place], self.send.at[m])

            @pl.when(target != i)
            def _():
                far.start() if start else far.wait_send()

            @pl.when(target == i)
            def _():
                near.start() if start else near.wait()

    def start(self):
        self.move(True)

    def wait_sent(self):
        self.move(False)

    def wait_here(self):
        ex = self.ex
        plan, i = ex.plan, ex.i
        q = plan.per_seq
        for m in range(MICRO):
            origin = m * plan.n_seq + i // q if self.out else (i % plan.n_seq) * q + m

            @pl.when(origin != i)
            def _():
                ex.push(self.dst.at[m], self.dst.at[m], self.send.at[0], self.recv.at[m], ex.sib).wait_recv()


def step_kernel(plan, n_in, *refs):
    (tab, dev, slots, w_qkv, w_out, w_up, w_down, tok, fv, cot) = refs[:n_in]
    (o_out, o_dx, o_df, o_q, o_s, o_o, o_f) = refs[n_in : n_in + 7]
    (
        gq, go, gf, x3, f3, y3, out3, dx3, df3,
        q_other, q_ring, q_last, s_other, s_ring, s_last, o_other, o_ring, o_last, f_other, f_ring, f_last,
        wq, wo, sv, vec, ub, hl, hlt, qkv, ot, otb, lse, mid, n2, inv2, h2, h2t, yt,
        big, acc, act, du, dv, dk, dqt, sums, ubg,
    ) = refs[n_in + 7 : n_in + 7 + 47]
    sems = refs[n_in + 7 + 47 :]
    R, C, n_mp, n_dp, n_z = plan.rows, plan.cols, plan.n_mp, plan.n_dp, plan.n_z
    step = 64
    ex = Exchange(plan)
    i, z, c = ex.i, ex.z, ex.c
    Q = Gather(ex, gq, sems[0:6])
    O = Gather(ex, go, sems[6:12])
    F = Gather(ex, gf, sems[12:18])
    RQ = Reduce(ex, gq, slice(0, R), q_other, q_ring, q_last, sems[18:24])
    RS = Reduce(ex, gq, slice(R, R + 16), s_other, s_ring, s_last, sems[24:30])
    RO = Reduce(ex, go, slice(0, R // 3), o_other, o_ring, o_last, sems[30:36])
    RF = Reduce(ex, gf, slice(0, 2 * R), f_other, f_ring, f_last, sems[36:42])
    a2a = sems[42:54]
    XT = Rows(ex, tok, x3, a2a[0], a2a[1], False)
    XF = Rows(ex, fv, f3, a2a[2], a2a[3], False)
    XY = Rows(ex, cot, y3, a2a[4], a2a[5], False)
    YO = Rows(ex, out3, o_out, a2a[6], a2a[7], True)
    YX = Rows(ex, dx3, o_dx, a2a[8], a2a[9], True)
    YF = Rows(ex, df3, o_df, a2a[10], a2a[11], True)

    third = R // 3
    gq[i, z, c, 0:R, 0 : plan.qkv] = w_qkv[...]
    gq[i, z, c, R:, :] = slots[...]
    for t in range(3):
        go[i, z, c, :, t * plan.group : t * plan.group + plan.out] = w_out[t * third : (t + 1) * third, :]
    gf[i, z, c, 0:R, :] = w_up[...]
    gf[i, z, c, R:, :] = w_down[...].T
    ex.greet()
    Q.start()
    O.start()
    XT.start()
    XF.start()
    F.start()
    Q.column()
    O.column()
    for d in range(1, plan.half):
        Q.hop(d)
        O.hop(d)
    F.column()
    XY.start()

    rowdev = dev[:, 0:1]
    row = lambda v: vec[v : v + 1, :]
    lanes = lambda v: slice((v % plan.spr) * 128, (v % plan.spr) * 128 + 128)
    onehot = lambda t, width: (lax.broadcasted_iota(jnp.int32, (128, width), 0) == tab[t : t + 1, :width]).astype(BF)
    e24 = onehot(0, D)
    e96 = onehot(4, C)

    def rows_of(ref3, at, step):
        part = SEQ // MICRO
        return ref3.at[at // (part // step), pl.ds(pl.multiple_of((at % (part // step)) * step, step), step)]

    def blocks(step, body):
        @pl.loop(0, SEQ // step)
        def _(at):
            body(at, pl.ds(pl.multiple_of(at * step, step), step))

    Q.hop(plan.half)
    O.hop(plan.half)
    for piece in (Q, O):
        for offset in range(-plan.half + 1, plan.half + 1):
            piece.wait_sib(offset)

    for j in range(n_mp):
        for d in range(n_dp):
            rows = slice(d * R, (d + 1) * R)
            wq[rows, j * plan.qkv : (j + 1) * plan.qkv] = gq[j, d // 2, d % 2, 0:R, 0 : plan.qkv]
            for t in range(3):
                rows = slice(d * R + t * third, d * R + (t + 1) * third)
                wo[rows, j * plan.out : (j + 1) * plan.out] = go[
                    j, d // 2, d % 2, :, t * plan.group : t * plan.group + plan.out
                ]
    for r in range(plan.vec_rows):
        for j in range(n_mp):
            for d in range(n_dp):
                at = j * n_dp + d
                sv[r, at : at + 1, :] = gq[j, d // 2, d % 2, R + r : R + r + 1, :].astype(F32)

    def expand(v, e, owner):
        got = dot(sv[v // plan.spr, :, lanes(v)].astype(BF), e)
        return jnp.sum(jnp.where(owner == rowdev, got, 0.0), axis=0, keepdims=True)

    for v in WIDE:
        vec[v : v + 1, :] = expand(v, e24, tab[1:2, :])
    vec[V_BIAS : V_BIAS + 1, :] = expand(V_BIAS, onehot(2, D), tab[3:4, :])
    for j in range(n_mp):
        ub[j : j + 1, :] = expand(UP_BIAS, e96, tab[5:6, :C] + j * n_dp)

    XT.wait_here()
    XT.wait_sent()

    def first_norm(at, rows):
        n1, _ = norm_stats(rows_of(x3, at, step)[...].astype(F32))
        hl[rows, :] = (n1 * row(G1) + row(B1)).astype(BF)

    blocks(step, first_norm)
    hlt[...] = hl[...].T
    XF.wait_here()
    XF.wait_sent()

    def project(at, rows):
        h = hl[rows, :]
        q = dot(h, wq[:, 0:D]) + row(QB)
        qkv[rows, 0:D] = q.astype(BF) * 0.125
        qkv[rows, D : 2 * D] = dot(h, wq[:, D : 2 * D]).astype(BF)
        v = dot(h, wq[:, 2 * D : QKV]) + row(V_BIAS)[:, :VFRESH]
        qkv[rows, 2 * D : QKV] = v.astype(BF)

    blocks(256, project)
    qkv[:, QKV : 3 * D] = f3[...].reshape(SEQ, D // 2)

    B = 256
    head_of = lax.broadcasted_iota(jnp.int32, (1, 128), 1) // HEAD
    keep = lax.broadcasted_iota(jnp.int32, (B, B), 0) <= lax.broadcasted_iota(jnp.int32, (B, B), 1)

    def scores(k2, qm, at):
        s = dot_nt(k2, qm)
        last = jnp.where(keep, s[at * B :, :], -BIG)
        return last if at == 0 else jnp.concatenate([s[: at * B, :], last], axis=0)

    @pl.loop(0, HEADS // 2)
    def _(t):
        cols = lambda base: pl.ds(pl.multiple_of(base + t * 128, 128), 128)
        vt = qkv[:, cols(2 * D)].T
        for e in range(2):
            mask = (head_of == e).astype(BF)
            for at in range(SEQ // B):
                kk = (at + 1) * B
                span = slice(at * B, kk)
                s = scores(qkv[0:kk, cols(D)], qkv[span, cols(0)] * mask, at)
                top = jnp.max(s, axis=0, keepdims=True)
                ex_ = jnp.exp(s - top)
                total = jnp.sum(ex_, axis=0, keepdims=True)
                o = dot(vt[e * HEAD : (e + 1) * HEAD, 0:kk], ex_.astype(BF)) / total
                ot[pl.ds(pl.multiple_of(t * 128 + e * HEAD, HEAD), HEAD), span] = o
                lse[t, e : e + 1, span] = top + jnp.log(total)

        for d in range(1, plan.half):

            @pl.when(t == 2 + d)
            def _():
                F.hop(d)

    otb[...] = ot[...].astype(BF)
    du[:, 0:D] = otb[...].T

    def second_norm(at, rows):
        m = rows_of(x3, at, 128)[...].astype(F32) + (dot(du[rows, 0:D], wo[...]) + row(OB))
        mid[rows, :] = m
        scaled, inv = norm_stats(m)
        n2[rows, :] = scaled
        inv2[rows, :] = jnp.broadcast_to(inv, (128, 128))
        h2[rows, :] = (scaled * row(G2) + row(B2)).astype(BF)

    blocks(128, second_norm)
    h2t[...] = h2[...].T
    XY.wait_here()
    XY.wait_sent()
    yt[...] = y3[...].reshape(SEQ, D).T
    acc[...] = jnp.zeros_like(acc)
    big[...] = jnp.zeros_like(big)

    offset_of = lambda q: (q + 1) // 2 * (1 - 2 * (q % 2))

    @pl.loop(0, n_mp)
    def _(q):
        j = ex.at(ex.p + offset_of(q))
        for s in range(n_mp):

            @pl.when(q == s)
            def _():
                if s == n_mp - 1:
                    F.hop(plan.half)
                F.wait_sib(plan.half if s == n_mp - 1 else offset_of(s))

        bias = ub[pl.ds(j, 1), :]

        def rows(at, rows):
            up = gf[j, :, :, 0:R, :].reshape(D, C)
            down = gf[j, :, :, R : 2 * R, :].reshape(D, C)
            u = dot(h2[rows, :], up) + bias
            u2 = u * u
            tangent = jnp.tanh(GELU_C * (u + GELU_A * u2 * u))
            half = 0.5 * (1.0 + tangent)
            a = (u * half).astype(BF)
            slope = half + 0.5 * u * (1.0 - tangent * tangent) * GELU_C * (1.0 + 3.0 * GELU_A * u2)
            act[rows, :] = a
            acc[rows, :] += dot_nt(a, down)
            g = (dot(rows_of(y3, at, 128)[...], down) * slope).astype(BF)
            du[rows, 0:C] = g
            big[rows, :] += dot_nt(g, up)

        blocks(128, rows)
        for s in range(n_mp):

            @pl.when(q == s)
            def _():
                F.wait_sent(plan.half if s == n_mp - 1 else offset_of(s))

        gf[j, :, :, R : 2 * R, :] = dot(yt[...], act[...]).astype(BF).reshape(n_z, 2, R, C)
        gf[j, :, :, 0:R, :] = dot(h2t[...], du[:, 0:C]).astype(BF).reshape(n_z, 2, R, C)
        ubg[pl.ds(j, 1), :] = jnp.sum(du[:, 0:C].astype(F32), axis=0, keepdims=True)
        for s in range(n_mp):

            @pl.when(q == s)
            def _():
                RF.to_sibling(plan.half if s == n_mp - 1 else offset_of(s))
                if s == n_mp - 1:
                    RF.free(1)
                    RF.free(0)

    sums[...] = jnp.zeros_like(sums)

    def second_back(at, rows):
        rows_of(out3, at, step)[...] = (mid[rows, :] + (acc[rows, :] + row(DB))).astype(BF)
        dh = big[rows, :]
        dy = rows_of(y3, at, step)[...].astype(F32)
        scaled = n2[rows, :]
        dr = norm_back(dh, scaled, inv2[rows, 0:1], row(G2))
        dmid = dy + dr
        mid[rows, :] = dmid
        low = dmid.astype(BF)
        du[rows, 0:D] = low
        total = lambda a: jnp.sum(a, axis=0, keepdims=True)
        sums[G2 : G2 + 1, :] += total(dh * scaled)
        sums[B2 : B2 + 1, :] += total(dh)
        sums[OB : OB + 1, :] += total(low.astype(F32))
        sums[DB : DB + 1, :] += total(dy)

    blocks(step, second_back)
    RF.far()
    YO.start()
    for offset in range(-plan.half + 1, plan.half + 1):
        O.wait_sent(offset)
        Q.wait_sent(offset)
    for j in range(n_mp):
        g = dot(otb[...], du[:, j * plan.out : (j + 1) * plan.out]).astype(BF).reshape(n_z, 2, 3, third, plan.out)
        for t in range(3):
            go[j, :, :, :, t * plan.group : t * plan.group + plan.out] = g[:, :, t]
    for offset in range(n_mp):
        RO.to_sibling(offset)
    do = hl

    def out_back(at, rows):
        do[rows, :] = dot_nt(du[rows, 0:D], wo[...]).astype(BF)

    blocks(256, out_back)
    RO.far()
    RO.free(0)
    RO.free(1)

    @pl.loop(0, HEADS // 2)
    def _(t):
        cols = lambda base: pl.ds(pl.multiple_of(base + t * 128, 128), 128)
        kt = qkv[:, cols(D)].T
        dot_ = do[:, cols(0)].astype(F32).T
        prod = dot_ * ot[cols(0), :]
        dv[...] = jnp.zeros_like(dv)
        dk[...] = jnp.zeros_like(dk)
        for e in range(2):
            mask = (head_of == e).astype(BF)
            delta = jnp.sum(prod[e * HEAD : (e + 1) * HEAD, :], axis=0, keepdims=True)
            for at in range(SEQ // B):
                kk = (at + 1) * B
                span = slice(at * B, kk)
                qm = qkv[span, cols(0)] * mask
                dom = do[span, cols(0)] * mask
                s = scores(qkv[0:kk, cols(D)], qm, at)
                p = jnp.exp(s - lse[t, e : e + 1, span])
                dp = dot_nt(qkv[0:kk, cols(2 * D)], dom)
                ds = (p * (dp - delta[:, span])).astype(BF)
                dv[0:kk, :] += dot(p.astype(BF), dom)
                dk[0:kk, :] += dot(ds, qm)
                dqt[e * HEAD : (e + 1) * HEAD, span] = dot(kt[e * HEAD : (e + 1) * HEAD, 0:kk], ds)
        qkv[:, cols(0)] = (dqt[...].T * 0.125).astype(BF)
        qkv[:, cols(D)] = dk[...].astype(BF)
        qkv[:, cols(2 * D)] = dv[...].astype(BF)

        @pl.when(t == 1)
        def _():
            for s in range(2):
                RF.bound(s)

        @pl.when(t == 3)
        def _():
            RF.nearer()
            for s in range(2):
                RO.bound(s)

        @pl.when(t == 5)
        def _():
            RO.nearer()

    df3[...] = qkv[:, QKV : 3 * D].reshape(df3.shape)
    YF.start()
    for j in range(n_mp):
        g = dot(hlt[...], qkv[:, j * plan.qkv : (j + 1) * plan.qkv]).astype(BF)
        gq[j, :, :, 0:R, 0 : plan.qkv] = g.reshape(n_z, 2, R, plan.qkv)
    for offset in (plan.half, *range(-plan.half + 1, plan.half)):
        RQ.to_sibling(offset)
    RF.home()
    RQ.far()
    RQ.free(0)
    RQ.free(1)
    RO.home()

    def project_back(at, rows):
        acc[rows, :] = dot_nt(qkv[rows, 0:QKV], wq[...])

    blocks(256, project_back)

    def first_back(at, rows):
        n1, inv = norm_stats(rows_of(x3, at, step)[...].astype(F32))
        dh = acc[rows, :]
        dr = norm_back(dh, n1, inv, row(G1))
        rows_of(dx3, at, step)[...] = (mid[rows, :] + dr).astype(BF)
        total = lambda a: jnp.sum(a, axis=0, keepdims=True)
        sums[G1 : G1 + 1, :] += total(dh * n1)
        sums[B1 : B1 + 1, :] += total(dh)
        sums[QB : QB + 1, :] += total(qkv[rows, 0:D].astype(F32))
        sums[V_BIAS : V_BIAS + 1, 0:VFRESH] += total(qkv[rows, 2 * D : QKV].astype(F32))

    blocks(step, first_back)
    YX.start()
    for s in range(2):
        RQ.bound(s)

    def collect(g, e, owner):
        return dot_nt(jnp.where(owner == rowdev, g, 0.0).astype(BF), e)

    for v in WIDE:
        sv[v // plan.spr, :, lanes(v)] = collect(sums[v : v + 1, :], e24, tab[1:2, :])
    sv[V_BIAS // plan.spr, :, lanes(V_BIAS)] = collect(sums[V_BIAS : V_BIAS + 1, :], onehot(2, D), tab[3:4, :])
    got = collect(ubg[0:1, :], e96, tab[5:6, :C])
    for j in range(1, n_mp):
        got = got + collect(ubg[j : j + 1, :], e96, tab[5:6, :C] + j * n_dp)
    sv[UP_BIAS // plan.spr, :, lanes(UP_BIAS)] = got
    at16 = lax.broadcasted_iota(jnp.int32, (16, plan.qw), 0)
    for j in range(n_mp):
        for d in range(n_dp):
            at = j * n_dp + d
            value = jnp.zeros((16, plan.qw), F32)
            for r in range(plan.vec_rows):
                value = jnp.where(at16 == r, sv[r, at : at + 1, :], value)
            gq[j, d // 2, d % 2, R:, :] = value.astype(BF)
    for offset in range(n_mp):
        RS.to_sibling(offset)
    o_f[...] = RF.finish()
    RS.far()
    RS.free(0)
    RS.free(1)
    RQ.nearer()
    o_o[...] = RO.finish()
    for s in range(2):
        RS.bound(s)
    RQ.home()
    RS.nearer()
    RS.home()
    o_q[...] = RQ.finish()
    o_s[...] = RS.finish()
    for r in (RF, RO, RQ, RS):
        r.wait_sent()
    for r in (YO, YF, YX):
        r.wait_sent()
        r.wait_here()


def step(plan, slots, w_qkv, w_out, w_up, w_down, tok, fv, cot):
    R, C, n_mp, n_z, n = plan.rows, plan.cols, plan.n_mp, plan.n_z, plan.n
    count = np.arange(D, dtype=np.int32)
    tab = np.zeros((8, D), np.int32)
    for at, width in ((0, D // n), (2, VFRESH // n), (4, FF // n)):
        tab[at], tab[at + 1] = count % width, count // width
    r = np.arange(n, dtype=np.int32)
    dev = np.tile(((r % plan.n_dp) * n_mp + r // plan.n_dp)[:, None], (1, 128))
    vm = pltpu.VMEM
    dma = pltpu.SemaphoreType.DMA
    wide = lambda t: vm((SEQ, D), t)
    tall = lambda t: vm((D, SEQ), t)
    panel = lambda rows, cols: vm((n_mp, n_z, 2, rows, cols), BF)

    def sums(rows, cols):
        ring = n_z // 2 + (plan.half - 1) * n_z
        return [
            vm((n_mp, n_z, rows, cols), BF),
            vm((2, ring, rows, cols), BF),
            vm((n_z - 1, rows, cols), BF),
        ]

    gather_sems = [dma((n_z - 1,))] * 2 + [dma((2, plan.half))] * 2 + [dma((n_mp,))] * 2
    reduce_sems = [dma((n_mp,))] * 2 + [dma((2, plan.half + 1))] * 2 + [dma((n_z - 1,))] * 2
    shape = jax.ShapeDtypeStruct
    ins = (jnp.asarray(tab), jnp.asarray(dev), slots, w_qkv, w_out, w_up, w_down, tok, fv, cot)
    return pl.pallas_call(
        functools.partial(step_kernel, plan, len(ins)),
        name="step",
        out_shape=(
            shape(tok.shape, BF),
            shape(tok.shape, BF),
            shape(fv.shape, BF),
            shape((R, plan.qw), F32),
            shape((16, plan.qw), F32),
            shape((R // 3, C), F32),
            shape((2 * R, C), F32),
        ),
        in_specs=[IN_VMEM] * 7 + [ANY] * 3,
        out_specs=(ANY,) * 3 + (IN_VMEM,) * 4,
        scratch_shapes=[
            panel(R + 16, plan.qw), panel(R // 3, C), panel(2 * R, C),
            vm(tok.shape, BF), vm(fv.shape, BF), vm(cot.shape, BF),
            vm(tok.shape, BF), vm(tok.shape, BF), vm(fv.shape, BF),
            *sums(R, plan.qw), *sums(16, plan.qw), *sums(R // 3, C), *sums(2 * R, C),
            vm((D, QKV), BF), vm((D, D), BF),
            vm((plan.vec_rows, n, plan.qw), F32), vm((16, D), F32), vm((max(8, n_mp), C), F32),
            wide(BF), tall(BF), vm((SEQ, 3 * D), BF), tall(F32), tall(BF),
            vm((HEADS // 2, 8, SEQ), F32),
            wide(F32), wide(F32), vm((SEQ, 128), F32), wide(BF), tall(BF), tall(BF),
            wide(F32), wide(F32), vm((SEQ, C), BF), wide(BF),
            vm((SEQ, 128), F32), vm((SEQ, 128), F32), vm((128, SEQ), F32),
            vm((16, D), F32), vm((max(8, n_mp), C), F32),
            *(gather_sems * 3),
            *(reduce_sems * 4),
            *([dma((MICRO,))] * 12),
        ],
        compiler_params=pltpu.CompilerParams(
            collective_id=0, has_side_effects=True, vmem_limit_bytes=63 << 20
        ),
    )(*ins)


def shards(
    plan, tokens, first_values, out_cot, ln1_gain, ln1_bias, w_qkv, q_bias, v_bias, w_out, out_bias,
    ln2_gain, ln2_bias, w_up, up_bias, w_down, down_bias,
):
    small = (ln1_gain, ln1_bias, q_bias, v_bias, out_bias, ln2_gain, ln2_bias, up_bias, down_bias)
    widths = [s.shape[0] for s in small]
    slots = jnp.concatenate([jnp.pad(s, (0, 128 - s.shape[0])) for s in small])
    slots = jnp.pad(slots, (0, 16 * plan.qw - slots.shape[0])).reshape(16, plan.qw)
    r1, r2, r3, t_q, t_s, t_o, t_f = step(
        plan, slots, w_qkv, w_out, w_up, w_down, tokens, first_values, out_cot
    )
    R, spr = plan.rows, plan.spr
    s = [t_s[v // spr, (v % spr) * 128 : (v % spr) * 128 + w] for v, w in enumerate(widths)]
    t_o = jnp.concatenate([t_o[:, t * plan.group : t * plan.group + plan.out] for t in range(3)], axis=0)
    return (
        r1, r2, r3,
        s[0], s[1],
        t_q[:, : plan.qkv],
        s[2], s[3],
        t_o,
        s[4], s[5], s[6],
        t_f[:R],
        s[7],
        t_f[R:].T,
        s[8],
    )


def solution(mesh):
    plan = Plan(mesh)
    line = P(("dp", "mp"))
    rows = P(None, ("dp", "mp"), None)
    block = P("dp", "mp")
    grads = (line, line, block, line, line, block, line, line, line, block, line, P("mp", "dp"), line)
    return jax.shard_map(
        functools.partial(shards, plan),
        mesh=mesh,
        in_specs=(rows, rows, rows) + grads,
        out_specs=(rows, rows, rows) + grads,
        check_vma=False,
    )
```

```python
import functools

import jax
import jax.numpy as jnp
import numpy as np
from jax import lax
from jax.experimental import pallas as pl
from jax.experimental.pallas import tpu as pltpu
from jax.sharding import PartitionSpec as P

D = 768
HEADS = 12
HEAD = 64
FF = 3072
MICRO = 4
QKV = 1920
SEQ = 512
VFRESH = 384

EPS = 1e-05
BIG = 1e30
GELU_C = 0.7978845608028654
GELU_A = 0.044715
MESH = pl.DeviceIdType.MESH
ANY = pl.BlockSpec(memory_space=pl.ANY)
IN_VMEM = pl.BlockSpec(memory_space=pltpu.VMEM)
BF, F32 = jnp.bfloat16, jnp.float32

WIDE = (0, 1, 2, 4, 5, 6, 8)
V_BIAS, UP_BIAS = 3, 7
G1, B1, QB, OB, G2, B2, DB = WIDE
N_VEC = 9


class Plan:
    def __init__(self, mesh):
        self.n_dp = mesh.shape["dp"]
        self.n_mp = mesh.shape["mp"]
        self.n = self.n_dp * self.n_mp
        self.n_z = self.n_dp // 2
        self.rows = D // self.n_dp
        self.cols = FF // self.n_mp
        self.qkv = QKV // self.n_mp
        self.out = D // self.n_mp
        self.qw = -(-self.qkv // 128) * 128
        self.group = self.cols // 3
        self.spr = self.qw // 128
        self.vec_rows = -(-N_VEC // self.spr)
        self.half = self.n_mp // 2
        self.per_seq = SEQ // (SEQ // MICRO)
        self.n_seq = self.n_mp // MICRO
        assert self.out <= self.group and self.rows % 48 == 0 and self.vec_rows <= 16
        self.bits = self.n_z.bit_length() - 1
        assert self.n_seq * MICRO == self.n_mp and self.n_z == 1 << self.bits and self.bits > 0

    def ring_at(self, i):
        return i + (i // self.half) * (self.n_mp - 1 + self.half - 2 * i)

    def row_half(self, s, rows):
        middle = -(-rows // 32) * 16 if rows > 16 else 8
        return slice(middle, rows) if s else slice(0, middle)

    def slots(self, d):
        if d == self.half:
            return 0, self.n_z // 2
        return self.n_z // 2 + (d - 1) * self.n_z, self.n_z


def dot(a, b):
    return jnp.dot(a, b, preferred_element_type=F32)


def dot_nt(a, b):
    return lax.dot_general(a, b, (((1,), (1,)), ((), ())), preferred_element_type=F32)


def chunks(rows, step, body):
    @pl.loop(0, rows // step)
    def _(at):
        body(pl.ds(pl.multiple_of(at * step, step), step))


def norm_stats(r):
    average = jnp.mean(r, axis=-1, keepdims=True)
    centred = r - average
    variance = jnp.mean(centred * centred, axis=-1, keepdims=True)
    inv_std = lax.rsqrt(variance + EPS)
    return centred * inv_std, inv_std


def norm_back(grad_out, scaled, inv_std, gain):
    e = grad_out * gain
    first = jnp.mean(e, axis=-1, keepdims=True)
    second = jnp.mean(e * scaled, axis=-1, keepdims=True)
    return inv_std * (e - first - scaled * second)


class Exchange:
    def __init__(self, plan):
        self.plan = plan
        dp, i = lax.axis_index("dp"), lax.axis_index("mp")
        self.dp, self.i, self.c, self.z = dp, i, dp % 2, dp // 2
        self.sib = (dp + 1 - 2 * self.c, i)
        self.p = plan.ring_at(i)

    def at(self, pos):
        return self.plan.ring_at((pos + 2 * self.plan.n_mp) % self.plan.n_mp)

    def across(self, b):
        return self.z + (1 << b) * (1 - 2 * (self.z // (1 << b) % 2))

    def z_units(self, b, far):
        n_z = self.plan.n_z
        base = self.across(b) if far else self.z
        return [(base + m * (2 << b)) % n_z for m in range(n_z // (2 << b))]

    def z_slot(self, b, m):
        return self.plan.n_z // (2 << b) - 1 + m

    def z_device(self, b):
        return (self.across(b) * 2 + self.c, self.i)

    def greet(self):
        plan = self.plan
        barrier = pltpu.get_barrier_semaphore()
        partners = [self.sib]
        partners += [self.z_device(b) for b in range(plan.bits)]
        partners += [(self.dp, (self.i + k) % plan.n_mp) for k in range(1, plan.n_mp)]
        for partner in partners:
            pl.semaphore_signal(barrier, inc=1, device_id=partner, device_id_type=MESH)
        pl.semaphore_wait(barrier, len(partners))

    def push(self, src, dst, send, recv, device):
        return pltpu.make_async_remote_copy(
            src_ref=src, dst_ref=dst, send_sem=send, recv_sem=recv, device_id=device, device_id_type=MESH
        )


class Gather:
    def __init__(self, ex, ref, sems):
        self.ex, self.ref = ex, ref
        self.zs, self.zr, self.rs, self.rr, self.ss, self.sr = sems

    def z_copy(self, b, m):
        ex = self.ex
        view = self.ref.at[ex.i, ex.z_units(b, False)[m], ex.c]
        at = ex.z_slot(b, m)
        return ex.push(view, view, self.zs.at[at], self.zr.at[at], ex.z_device(b))

    def ring_view(self, origin, s, d):
        n_z, half = self.ex.plan.n_z, self.ex.plan.half
        units = pl.ds(s * (n_z // 2), n_z // 2) if d == half else pl.ds(0, n_z)
        return self.ref.at[origin, units, self.ex.c]

    def ring_copy(self, s, d):
        ex = self.ex
        sign = 1 - 2 * s
        view = self.ring_view(ex.at(ex.p - sign * (d - 1)), s, d)
        return ex.push(view, view, self.rs.at[s, d - 1], self.rr.at[s, d - 1], (ex.dp, ex.at(ex.p + sign)))

    def sib_copy(self, offset):
        ex = self.ex
        at = (offset + ex.plan.n_mp) % ex.plan.n_mp
        view = self.ref.at[ex.at(ex.p + offset), :, ex.c]
        return ex.push(view, view, self.ss.at[at], self.sr.at[at], ex.sib)

    def start(self):
        for b in range(self.ex.plan.bits):
            self.z_copy(b, 0).start()

    def z_sizes(self):
        n_z = self.ex.plan.n_z
        return [(b, n_z // (2 << b)) for b in range(self.ex.plan.bits)]

    def spread(self):
        sizes = self.z_sizes()
        for b, count in reversed(sizes[:-1]):
            for m in range(sizes[b + 1][1]):
                self.z_copy(b + 1, m).wait_recv()
            for m in range(1, count):
                self.z_copy(b, m).start()

    def column(self):
        for m in range(self.z_sizes()[0][1]):
            self.z_copy(0, m).wait_recv()
        for s in range(2):
            self.ring_copy(s, 1).start()
        self.sib_copy(0).start()

    def hop(self, d):
        half = self.ex.plan.half
        for s in range(2):
            self.ring_copy(s, d).wait_recv()
            if d < half:
                self.ring_copy(s, d + 1).start()
                self.sib_copy(-d if s == 0 else d).start()
        if d == half:
            self.sib_copy(half).start()

    def wait_sib(self, offset):
        self.sib_copy(offset).wait_recv()

    def wait_sent(self, offset):
        half = self.ex.plan.half
        self.sib_copy(offset).wait_send()
        if offset == 0:
            for b, count in self.z_sizes():
                for m in range(count):
                    self.z_copy(b, m).wait_send()
            for s in range(2):
                self.ring_copy(s, 1).wait_send()
        elif abs(offset) < half:
            self.ring_copy(0 if offset < 0 else 1, abs(offset) + 1).wait_send()


class RingFirst(Gather):
    def ring_view(self, origin, s, d):
        ex = self.ex
        rows = ex.plan.row_half(s, self.ref.shape[3]) if d == ex.plan.half else slice(None)
        return self.ref.at[origin, ex.z, ex.c, rows]

    def panel_copy(self, offset, b, m):
        ex = self.ex
        view = self.ref.at[ex.at(ex.p + offset), ex.z_units(b, False)[m], ex.c]
        at = (offset + ex.plan.n_mp) % ex.plan.n_mp, ex.z_slot(b, m)
        return ex.push(view, view, self.zs.at[at], self.zr.at[at], ex.z_device(b))

    def begin(self, offset):
        for b in range(self.ex.plan.bits):
            self.panel_copy(offset, b, 0).start()

    def start(self):
        for s in range(2):
            self.ring_copy(s, 1).start()
        self.begin(0)

    def hop(self, d):
        half = self.ex.plan.half
        for s in range(2):
            self.ring_copy(s, d).wait_recv()
            if d < half:
                self.ring_copy(s, d + 1).start()
        if d < half:
            self.begin(-d)
            self.begin(d)
        else:
            self.begin(half)

    def spread(self, offset):
        sizes = self.z_sizes()
        for b, count in reversed(sizes[:-1]):
            for m in range(sizes[b + 1][1]):
                self.panel_copy(offset, b + 1, m).wait_recv()
            for m in range(1, count):
                self.panel_copy(offset, b, m).start()

    def column(self, offset):
        for m in range(self.z_sizes()[0][1]):
            self.panel_copy(offset, 0, m).wait_recv()
        self.sib_copy(offset).start()

    def wait_sent(self, offset):
        half = self.ex.plan.half
        self.sib_copy(offset).wait_send()
        for b, count in self.z_sizes():
            for m in range(count):
                self.panel_copy(offset, b, m).wait_send()
        if offset == 0:
            for s in range(2):
                self.ring_copy(s, 1).wait_send()
        elif abs(offset) < half:
            self.ring_copy(0 if offset < 0 else 1, abs(offset) + 1).wait_send()


class Reduce:
    def __init__(self, ex, ref, tile, other, ring, last, sems):
        self.ex, self.ref, self.tile = ex, ref, tile
        self.other, self.ring, self.last = other, ring, last
        self.ss, self.sr, self.rs, self.rr, self.zs, self.zr = sems

    def sib_copy(self, offset):
        ex = self.ex
        at = (offset + ex.plan.n_mp) % ex.plan.n_mp
        view = self.ref.at[ex.at(ex.p + offset), :, 1 - ex.c, self.tile]
        return ex.push(view, self.other.at[at], self.ss.at[at], self.sr.at[at], ex.sib)

    def ring_views(self, dest, s, d, part):
        plan = self.ex.plan
        at, count = plan.slots(d)
        first = 0
        if d == plan.half:
            first = s * count
        elif part is not None:
            count = plan.n_z // 2
            first, at = part * count, at + part * count
        return self.ref.at[dest, pl.ds(first, count), self.ex.c, self.tile], self.ring.at[s, pl.ds(at, count)]

    def ring_copy(self, s, d, part=None):
        ex = self.ex
        plan = ex.plan
        sign = 1 - 2 * s
        sem = d - 1 if part is None else plan.half - 2 + 2 * part
        view, there = self.ring_views(ex.at(ex.p + sign * d), s, d, part)
        return ex.push(view, there, self.rs.at[s, sem], self.rr.at[s, sem], (ex.dp, ex.at(ex.p + sign)))

    def ring_copies(self, s, d):
        if d == self.ex.plan.half - 1:
            return [self.ring_copy(s, d, part) for part in range(2)]
        return [self.ring_copy(s, d)]

    def z_copy(self, b, m):
        ex = self.ex
        view = self.ref.at[ex.i, ex.z_units(b, True)[m], ex.c, self.tile]
        at = ex.z_slot(b, m)
        return ex.push(view, self.last.at[at], self.zs.at[at], self.zr.at[at], ex.z_device(b))

    def z_sizes(self):
        n_z = self.ex.plan.n_z
        return [(b, n_z // (2 << b)) for b in range(self.ex.plan.bits)]

    def to_sibling(self, offset):
        self.sib_copy(offset).start()

    def add(self, offset, first, count, *terms):
        j = self.ex.at(self.ex.p + offset)

        @pl.loop(0, count)
        def _(u):
            value = self.ref[j, first + u, self.ex.c, self.tile, :].astype(F32)
            for buf, at in terms:
                value = value + buf(at + u).astype(F32)
            self.ref[j, first + u, self.ex.c, self.tile, :] = value.astype(BF)

    def from_sibling(self, offset):
        at = (offset + self.ex.plan.n_mp) % self.ex.plan.n_mp
        self.sib_copy(offset).wait_recv()
        self.add(offset, 0, self.ex.plan.n_z, (lambda u: self.other[at, u], 0))

    def far(self):
        half = self.ex.plan.half
        self.from_sibling(half)
        for s in range(2):
            self.ring_copy(s, half).start()

    def free(self, s):
        half = self.ex.plan.half
        self.from_sibling((1 - 2 * s) * (half - 1))
        self.ring_copy(s, half - 1, 1 - s).start()

    def bound(self, s):
        plan = self.ex.plan
        half = plan.half
        self.ring_copy(s, half).wait_recv()
        at, count = plan.slots(half)
        self.add((1 - 2 * s) * (half - 1), s * count, count, (lambda u: self.ring[s, u], at))
        self.ring_copy(s, half - 1, s).start()

    def wait_ring(self, s, d):
        for copy in self.ring_copies(s, d):
            copy.wait_recv()

    def nearer(self):
        plan = self.ex.plan
        for d in range(plan.half - 2, 0, -1):
            for s in range(2):
                offset = (1 - 2 * s) * d
                self.from_sibling(offset)
                self.wait_ring(s, d + 1)
                self.add(offset, 0, plan.n_z, (lambda u: self.ring[s, u], plan.slots(d + 1)[0]))
                self.ring_copy(s, d).start()

    def home(self):
        plan = self.ex.plan
        for s in range(2):
            self.wait_ring(s, 1)
        self.sib_copy(0).wait_recv()
        at = plan.slots(1)[0]
        self.add(
            0, 0, plan.n_z,
            (lambda u: self.other[0, u], 0),
            (lambda u: self.ring[0, u], at),
            (lambda u: self.ring[1, u], at),
        )
        for m in range(self.z_sizes()[0][1]):
            self.z_copy(0, m).start()

    def along(self):
        ex = self.ex
        for b, count in self.z_sizes()[:-1]:
            for m, unit in enumerate(ex.z_units(b, False)):
                self.z_copy(b, m).wait_recv()
                at = ex.z_slot(b, m)
                self.add(0, unit, 1, (lambda u: self.last[u], at))
            for m in range(count // 2):
                self.z_copy(b + 1, m).start()

    def finish(self):
        ex = self.ex
        self.z_copy(ex.plan.bits - 1, 0).wait_recv()
        return self.ref[ex.i, ex.z, ex.c, self.tile, :].astype(F32) + self.last[0].astype(F32)

    def wait_z_sent(self):
        for b, count in self.z_sizes():
            for m in range(count):
                self.z_copy(b, m).wait_send()

    def wait_sent(self):
        plan = self.ex.plan
        for offset in range(plan.n_mp):
            self.sib_copy(offset).wait_send()
        for s in range(2):
            for d in range(1, plan.half + 1):
                for copy in self.ring_copies(s, d):
                    copy.wait_send()
        self.wait_z_sent()


class RingLast(Reduce):
    def panel_copy(self, offset, b, m):
        ex = self.ex
        view = self.ref.at[ex.at(ex.p + offset), ex.z_units(b, True)[m], ex.c, self.tile]
        at = (offset + ex.plan.n_mp) % ex.plan.n_mp, ex.z_slot(b, m)
        return ex.push(view, self.last.at[at], self.zs.at[at], self.zr.at[at], ex.z_device(b))

    def begin(self, offset):
        self.from_sibling(offset)
        for m in range(self.z_sizes()[0][1]):
            self.panel_copy(offset, 0, m).start()

    def take(self, offset, b):
        ex = self.ex
        q = (offset + ex.plan.n_mp) % ex.plan.n_mp
        for m, unit in enumerate(ex.z_units(b, False)):
            self.panel_copy(offset, b, m).wait_recv()
            self.add(offset, unit, 1, (lambda u: self.last[q, u], ex.z_slot(b, m)))

    def along(self, offset):
        for b, count in self.z_sizes()[:-1]:
            self.take(offset, b)
            for m in range(count // 2):
                self.panel_copy(offset, b + 1, m).start()

    def end(self, offset):
        self.take(offset, self.ex.plan.bits - 1)

    def ring_views(self, dest, s, d, part):
        ex = self.ex
        rows = slice(None)
        if d == ex.plan.half:
            rows = ex.plan.row_half(s, ex.plan.rows)
        elif part is not None:
            rows = ex.plan.row_half(part, ex.plan.rows)
        return self.ref.at[dest, ex.z, ex.c, rows], self.ring.at[s, d - 1, rows]

    def add_rows(self, offset, rows, *terms):
        ex = self.ex
        j = ex.at(ex.p + offset)
        value = self.ref[j, ex.z, ex.c, rows, :].astype(F32)
        for term in terms:
            value = value + term.astype(F32)
        self.ref[j, ex.z, ex.c, rows, :] = value.astype(BF)

    def far(self):
        for s in range(2):
            self.ring_copy(s, self.ex.plan.half).start()

    def free(self, s):
        self.ring_copy(s, self.ex.plan.half - 1, 1 - s).start()

    def bound(self, s):
        plan = self.ex.plan
        half = plan.half
        self.ring_copy(s, half).wait_recv()
        rows = plan.row_half(s, plan.rows)
        self.add_rows((1 - 2 * s) * (half - 1), rows, self.ring[s, half - 1, rows, :])
        self.ring_copy(s, half - 1, s).start()

    def nearer(self):
        for d in range(self.ex.plan.half - 2, 0, -1):
            for s in range(2):
                self.wait_ring(s, d + 1)
                self.add_rows((1 - 2 * s) * d, slice(None), self.ring[s, d])
                self.ring_copy(s, d).start()

    def finish(self):
        ex = self.ex
        for s in range(2):
            self.wait_ring(s, 1)
        value = self.ref[ex.i, ex.z, ex.c].astype(F32)
        return value + self.ring[0, 0].astype(F32) + self.ring[1, 0].astype(F32)

    def wait_z_sent(self):
        for offset in range(self.ex.plan.n_mp):
            for b, count in self.z_sizes():
                for m in range(count):
                    self.panel_copy(offset, b, m).wait_send()


class Rows:
    def __init__(self, ex, src, dst, send, recv, out):
        self.ex, self.src, self.dst, self.send, self.recv, self.out = ex, src, dst, send, recv, out

    def move(self, start):
        ex = self.ex
        plan, i = ex.plan, ex.i
        q = plan.per_seq
        for m in range(MICRO):
            if self.out:
                target, place = (i % plan.n_seq) * q + m, i // plan.n_seq
            else:
                target, place = m * plan.n_seq + i // q, i % q
            far = ex.push(self.src.at[m], self.dst.at[place], self.send.at[m], self.recv.at[place], (ex.dp, target))
            near = pltpu.make_async_copy(self.src.at[m], self.dst.at[place], self.send.at[m])

            @pl.when(target != i)
            def _():
                far.start() if start else far.wait_send()

            @pl.when(target == i)
            def _():
                near.start() if start else near.wait()

    def start(self):
        self.move(True)

    def wait_sent(self):
        self.move(False)

    def wait_here(self):
        ex = self.ex
        plan, i = ex.plan, ex.i
        q = plan.per_seq
        for m in range(MICRO):
            origin = m * plan.n_seq + i // q if self.out else (i % plan.n_seq) * q + m

            @pl.when(origin != i)
            def _():
                ex.push(self.dst.at[m], self.dst.at[m], self.send.at[0], self.recv.at[m], ex.sib).wait_recv()


def step_kernel(plan, n_in, *refs):
    (tab, dev, w_qkv, w_out, w_up, w_down, tok, fv, cot), small = refs[:9], refs[9:n_in]
    (o_out, o_dx, o_df, o_q, o_s, o_o, o_u, o_d) = refs[n_in : n_in + 8]
    (
        gq, go, gu, gd, x3, f3, y3, out3, dx3, df3,
        q_other, q_ring, q_last, s_other, s_ring, s_last, o_other, o_ring, o_last, u_other, u_ring, u_last,
        d_other, d_ring, d_last,
        wq, wo, sv, vec, ub, hl, hlt, qkv, ot, otb, lse, mid, n2, inv2, h2, h2t, yt,
        big, acc, act, du, dv, dk, dqt, sums, ubg,
    ) = refs[n_in + 8 : n_in + 8 + 51]
    sems = refs[n_in + 8 + 51 :]
    R, C, n_mp, n_dp, n_z = plan.rows, plan.cols, plan.n_mp, plan.n_dp, plan.n_z
    step = 64
    ex = Exchange(plan)
    i, z, c = ex.i, ex.z, ex.c
    Q = Gather(ex, gq, sems[0:6])
    O = RingFirst(ex, go, sems[6:12])
    U = Gather(ex, gu, sems[12:18])
    W = RingFirst(ex, gd, sems[18:24])
    RQ = Reduce(ex, gq, slice(0, R), q_other, q_ring, q_last, sems[24:30])
    RS = Reduce(ex, gq, slice(R, R + 16), s_other, s_ring, s_last, sems[30:36])
    RO = Reduce(ex, go, slice(0, R // 3), o_other, o_ring, o_last, sems[36:42])
    RU = Reduce(ex, gu, slice(0, R), u_other, u_ring, u_last, sems[42:48])
    RD = RingLast(ex, gd, slice(0, R), d_other, d_ring, d_last, sems[48:54])
    a2a = sems[54:66]
    XT = Rows(ex, tok, x3, a2a[0], a2a[1], False)
    XF = Rows(ex, fv, f3, a2a[2], a2a[3], False)
    XY = Rows(ex, cot, y3, a2a[4], a2a[5], False)
    YO = Rows(ex, out3, o_out, a2a[6], a2a[7], True)
    YX = Rows(ex, dx3, o_dx, a2a[8], a2a[9], True)
    YF = Rows(ex, df3, o_df, a2a[10], a2a[11], True)
    near = range(-plan.half + 1, plan.half)

    third = R // 3
    gq[i, z, c, 0:R, 0 : plan.qkv] = w_qkv[...]
    sv[0, 0:16, :] = jnp.zeros((16, plan.qw), F32)
    for r in range(plan.vec_rows):
        pieces = [small[v][...] for v in range(r * plan.spr, min((r + 1) * plan.spr, N_VEC))]
        for k, piece in enumerate(pieces):
            sv[0, r : r + 1, k * 128 : k * 128 + piece.shape[0]] = piece.astype(F32)[None]
    gq[i, z, c, R:, :] = sv[0, 0:16, :].astype(BF)
    for t in range(3):
        go[i, z, c, :, t * plan.group : t * plan.group + plan.out] = w_out[t * third : (t + 1) * third, :]
    gu[i, z, c] = w_up[...]
    gd[i, z, c] = w_down[...]
    ex.greet()
    Q.start()
    O.start()
    XT.start()
    Q.spread()
    Q.column()
    U.start()
    W.start()
    O.hop(1)
    for d in range(2, plan.half + 1):
        O.hop(d)
    O.spread(0)
    XF.start()
    U.spread()
    Q.hop(1)
    W.hop(1)
    W.spread(0)
    for offset in (*near, plan.half):
        if offset:
            O.spread(offset)
        O.column(offset)
    XY.start()
    U.column()
    for d in range(2, plan.half + 1):
        Q.hop(d)
        W.hop(d)

    rowdev = dev[:, 0:1]
    row = lambda v: vec[v : v + 1, :]
    lanes = lambda v: slice((v % plan.spr) * 128, (v % plan.spr) * 128 + 128)
    onehot = lambda t, width: (lax.broadcasted_iota(jnp.int32, (128, width), 0) == tab[t : t + 1, :width]).astype(BF)
    e24 = onehot(0, D)
    e96 = onehot(4, C)

    def rows_of(ref3, at, step):
        part = SEQ // MICRO
        return ref3.at[at // (part // step), pl.ds(pl.multiple_of((at % (part // step)) * step, step), step)]

    def blocks(step, body):
        @pl.loop(0, SEQ // step)
        def _(at):
            body(at, pl.ds(pl.multiple_of(at * step, step), step))

    for piece in (Q, O):
        for offset in (*near, plan.half):
            piece.wait_sib(offset)

    for j in range(n_mp):
        for d in range(n_dp):
            rows = slice(d * R, (d + 1) * R)
            wq[rows, j * plan.qkv : (j + 1) * plan.qkv] = gq[j, d // 2, d % 2, 0:R, 0 : plan.qkv]
            for t in range(3):
                rows = slice(d * R + t * third, d * R + (t + 1) * third)
                wo[rows, j * plan.out : (j + 1) * plan.out] = go[
                    j, d // 2, d % 2, :, t * plan.group : t * plan.group + plan.out
                ]
    for r in range(plan.vec_rows):
        for j in range(n_mp):
            for d in range(n_dp):
                at = j * n_dp + d
                sv[r, at : at + 1, :] = gq[j, d // 2, d % 2, R + r : R + r + 1, :].astype(F32)

    def expand(v, e, owner):
        got = dot(sv[v // plan.spr, :, lanes(v)].astype(BF), e)
        return jnp.sum(jnp.where(owner == rowdev, got, 0.0), axis=0, keepdims=True)

    for v in WIDE:
        vec[v : v + 1, :] = expand(v, e24, tab[1:2, :])
    vec[V_BIAS : V_BIAS + 1, :] = expand(V_BIAS, onehot(2, D), tab[3:4, :])
    for j in range(n_mp):
        ub[j : j + 1, :] = expand(UP_BIAS, e96, tab[5:6, :C] + j * n_dp)

    XT.wait_here()
    XT.wait_sent()

    def first_norm(at, rows):
        n1, _ = norm_stats(rows_of(x3, at, step)[...].astype(F32))
        hl[rows, :] = (n1 * row(G1) + row(B1)).astype(BF)

    blocks(step, first_norm)
    hlt[...] = hl[...].T
    XF.wait_here()
    XF.wait_sent()

    def project(at, rows):
        h = hl[rows, :]
        q = dot(h, wq[:, 0:D]) + row(QB)
        qkv[rows, 0:D] = q.astype(BF) * 0.125
        qkv[rows, D : 2 * D] = dot(h, wq[:, D : 2 * D]).astype(BF)
        v = dot(h, wq[:, 2 * D : QKV]) + row(V_BIAS)[:, :VFRESH]
        qkv[rows, 2 * D : QKV] = v.astype(BF)

    blocks(256, project)
    qkv[:, QKV : 3 * D] = f3[...].reshape(SEQ, D // 2)

    B = 256
    head_of = lax.broadcasted_iota(jnp.int32, (1, 128), 1) // HEAD
    keep = lax.broadcasted_iota(jnp.int32, (B, B), 0) <= lax.broadcasted_iota(jnp.int32, (B, B), 1)

    def scores(k2, qm, at):
        s = dot_nt(k2, qm)
        last = jnp.where(keep, s[at * B :, :], -BIG)
        return last if at == 0 else jnp.concatenate([s[: at * B, :], last], axis=0)

    @pl.loop(0, HEADS // 2)
    def _(t):
        cols = lambda base: pl.ds(pl.multiple_of(base + t * 128, 128), 128)
        vt = qkv[:, cols(2 * D)].T
        for e in range(2):
            mask = (head_of == e).astype(BF)
            for at in range(SEQ // B):
                kk = (at + 1) * B
                span = slice(at * B, kk)
                s = scores(qkv[0:kk, cols(D)], qkv[span, cols(0)] * mask, at)
                top = jnp.max(s, axis=0, keepdims=True)
                ex_ = jnp.exp(s - top)
                total = jnp.sum(ex_, axis=0, keepdims=True)
                o = dot(vt[e * HEAD : (e + 1) * HEAD, 0:kk], ex_.astype(BF)) / total
                ot[pl.ds(pl.multiple_of(t * 128 + e * HEAD, HEAD), HEAD), span] = o
                lse[t, e : e + 1, span] = top + jnp.log(total)

        @pl.when(t == 0)
        def _():
            W.column(0)

        for d in range(1, plan.half):

            @pl.when(t == 2 * d)
            def _():
                W.spread(-d)
                W.spread(d)

    otb[...] = ot[...].astype(BF)
    du[:, 0:D] = otb[...].T

    def second_norm(at, rows):
        m = rows_of(x3, at, 128)[...].astype(F32) + (dot(du[rows, 0:D], wo[...]) + row(OB))
        mid[rows, :] = m
        scaled, inv = norm_stats(m)
        n2[rows, :] = scaled
        inv2[rows, :] = jnp.broadcast_to(inv, (128, 128))
        h2[rows, :] = (scaled * row(G2) + row(B2)).astype(BF)

    blocks(128, second_norm)
    W.spread(plan.half)
    for d in range(1, plan.half):
        U.hop(d)
    h2t[...] = h2[...].T
    XY.wait_here()
    XY.wait_sent()
    yt[...] = y3[...].reshape(SEQ, D).T
    acc[...] = jnp.zeros_like(acc)
    big[...] = jnp.zeros_like(big)

    order = [0, plan.half]
    for d in range(plan.half - 1, 0, -1):
        order += [-d, d]

    def nth(q):
        d = plan.half - q // 2
        return jnp.where(q == 0, 0, jnp.where(q == 1, plan.half, d * (2 * (q % 2) - 1)))

    def ring_turn(r, offset):
        if offset == plan.half:
            r.far()
        elif abs(offset) == plan.half - 1:
            r.free(0 if offset > 0 else 1)

    @pl.loop(0, n_mp)
    def _(q):
        j = ex.at(ex.p + nth(q))
        for s, offset in enumerate(order):

            @pl.when(q == s)
            def _():
                if s == 1:
                    U.hop(plan.half)
                    for other in (*near, plan.half):
                        if other:
                            W.column(other)
                U.wait_sib(offset)
                W.wait_sib(offset)

        up = gu[j].reshape(D, C)
        down = gd[j].reshape(D, C)
        u = dot(h2[...], up) + ub[pl.ds(j, 1), :]
        u2 = u * u
        tangent = jnp.tanh(GELU_C * (u + GELU_A * u2 * u))
        half = 0.5 * (1.0 + tangent)
        a = (u * half).astype(BF)
        slope = half + 0.5 * u * (1.0 - tangent * tangent) * GELU_C * (1.0 + 3.0 * GELU_A * u2)
        act[...] = a
        acc[...] += dot_nt(a, down)
        g = (dot(y3[...].reshape(SEQ, D), down) * slope).astype(BF)
        du[:, 0:C] = g
        big[...] += dot_nt(g, up)
        for s, offset in enumerate(order):

            @pl.when(q == s)
            def _():
                if s >= 1:
                    RD.begin(order[s - 1])
                    ring_turn(RU, order[s - 1])
                W.wait_sent(offset)
                U.wait_sent(offset)

        gd[j] = dot(yt[...], act[...]).astype(BF).reshape(n_z, 2, R, C)
        gu[j] = dot(h2t[...], du[:, 0:C]).astype(BF).reshape(n_z, 2, R, C)
        ubg[pl.ds(j, 1), :] = jnp.sum(du[:, 0:C].astype(F32), axis=0, keepdims=True)
        for s, offset in enumerate(order):

            @pl.when(q == s)
            def _():
                RD.to_sibling(offset)
                RU.to_sibling(offset)
                if s >= 3:
                    RD.along(order[s - 3])
                if s >= 4:
                    RD.end(order[s - 4])

    sums[...] = jnp.zeros_like(sums)

    def second_back(at, rows):
        rows_of(out3, at, step)[...] = (mid[rows, :] + (acc[rows, :] + row(DB))).astype(BF)
        dh = big[rows, :]
        dy = rows_of(y3, at, step)[...].astype(F32)
        scaled = n2[rows, :]
        dr = norm_back(dh, scaled, inv2[rows, 0:1], row(G2))
        dmid = dy + dr
        mid[rows, :] = dmid
        low = dmid.astype(BF)
        du[rows, 0:D] = low
        total = lambda a: jnp.sum(a, axis=0, keepdims=True)
        sums[G2 : G2 + 1, :] += total(dh * scaled)
        sums[B2 : B2 + 1, :] += total(dh)
        sums[OB : OB + 1, :] += total(low.astype(F32))
        sums[DB : DB + 1, :] += total(dy)

    blocks(step, second_back)
    RD.begin(order[-1])
    ring_turn(RU, order[-1])
    YO.start()
    RD.along(order[-3])
    for offset in (*near, plan.half):
        O.wait_sent(offset)
        Q.wait_sent(offset)
    for j in range(n_mp):
        g = dot(otb[...], du[:, j * plan.out : (j + 1) * plan.out]).astype(BF).reshape(n_z, 2, 3, third, plan.out)
        for t in range(3):
            go[j, :, :, :, t * plan.group : t * plan.group + plan.out] = g[:, :, t]
    for offset in range(n_mp):
        RO.to_sibling(offset)
    do = hl

    def out_back(at, rows):
        do[rows, :] = dot_nt(du[rows, 0:D], wo[...]).astype(BF)

    blocks(256, out_back)
    RO.far()
    RO.free(0)
    RO.free(1)

    @pl.loop(0, HEADS // 2)
    def _(t):
        cols = lambda base: pl.ds(pl.multiple_of(base + t * 128, 128), 128)
        kt = qkv[:, cols(D)].T
        dot_ = do[:, cols(0)].astype(F32).T
        prod = dot_ * ot[cols(0), :]
        dv[...] = jnp.zeros_like(dv)
        dk[...] = jnp.zeros_like(dk)
        for e in range(2):
            mask = (head_of == e).astype(BF)
            delta = jnp.sum(prod[e * HEAD : (e + 1) * HEAD, :], axis=0, keepdims=True)
            for at in range(SEQ // B):
                kk = (at + 1) * B
                span = slice(at * B, kk)
                qm = qkv[span, cols(0)] * mask
                dom = do[span, cols(0)] * mask
                s = scores(qkv[0:kk, cols(D)], qm, at)
                p = jnp.exp(s - lse[t, e : e + 1, span])
                dp = dot_nt(qkv[0:kk, cols(2 * D)], dom)
                ds = (p * (dp - delta[:, span])).astype(BF)
                dv[0:kk, :] += dot(p.astype(BF), dom)
                dk[0:kk, :] += dot(ds, qm)
                dqt[e * HEAD : (e + 1) * HEAD, span] = dot(kt[e * HEAD : (e + 1) * HEAD, 0:kk], ds)
        qkv[:, cols(0)] = (dqt[...].T * 0.125).astype(BF)
        qkv[:, cols(D)] = dk[...].astype(BF)
        qkv[:, cols(2 * D)] = dv[...].astype(BF)

        @pl.when(t == 0)
        def _():
            for s in range(2):
                RU.bound(s)
            RD.end(order[-4])

        @pl.when(t == 1)
        def _():
            RD.along(order[-2])

        @pl.when(t == 2)
        def _():
            RU.nearer()
            for s in range(2):
                RO.bound(s)

        @pl.when(t == 3)
        def _():
            RD.along(order[-1])
            RD.end(order[-3])
            RO.nearer()
            if plan.half == 2:
                RD.far()

        @pl.when(t == 4)
        def _():
            RU.home()

        @pl.when(t == 5)
        def _():
            RO.home()

    df3[...] = qkv[:, QKV : 3 * D].reshape(df3.shape)
    YF.start()
    for j in range(n_mp):
        g = dot(hlt[...], qkv[:, j * plan.qkv : (j + 1) * plan.qkv]).astype(BF)
        gq[j, :, :, 0:R, 0 : plan.qkv] = g.reshape(n_z, 2, R, plan.qkv)
    for offset in (plan.half, *near):
        RQ.to_sibling(offset)
    RQ.far()
    RQ.free(0)
    RQ.free(1)
    RD.end(order[-2])
    RD.end(order[-1])
    if plan.half != 2:
        RD.far()
    RD.free(0)
    RD.free(1)

    def project_back(at, rows):
        acc[rows, :] = dot_nt(qkv[rows, 0:QKV], wq[...])

    blocks(256, project_back)

    def first_back(at, rows):
        n1, inv = norm_stats(rows_of(x3, at, step)[...].astype(F32))
        dh = acc[rows, :]
        dr = norm_back(dh, n1, inv, row(G1))
        rows_of(dx3, at, step)[...] = (mid[rows, :] + dr).astype(BF)
        total = lambda a: jnp.sum(a, axis=0, keepdims=True)
        sums[G1 : G1 + 1, :] += total(dh * n1)
        sums[B1 : B1 + 1, :] += total(dh)
        sums[QB : QB + 1, :] += total(qkv[rows, 0:D].astype(F32))
        sums[V_BIAS : V_BIAS + 1, 0:VFRESH] += total(qkv[rows, 2 * D : QKV].astype(F32))

    blocks(step, first_back)
    YX.start()
    for s in range(2):
        RQ.bound(s)

    def collect(g, e, owner):
        return dot_nt(jnp.where(owner == rowdev, g, 0.0).astype(BF), e)

    for v in WIDE:
        sv[v // plan.spr, :, lanes(v)] = collect(sums[v : v + 1, :], e24, tab[1:2, :])
    sv[V_BIAS // plan.spr, :, lanes(V_BIAS)] = collect(sums[V_BIAS : V_BIAS + 1, :], onehot(2, D), tab[3:4, :])
    got = collect(ubg[0:1, :], e96, tab[5:6, :C])
    for j in range(1, n_mp):
        got = got + collect(ubg[j : j + 1, :], e96, tab[5:6, :C] + j * n_dp)
    sv[UP_BIAS // plan.spr, :, lanes(UP_BIAS)] = got
    at16 = lax.broadcasted_iota(jnp.int32, (16, plan.qw), 0)
    for j in range(n_mp):
        for d in range(n_dp):
            at = j * n_dp + d
            value = jnp.zeros((16, plan.qw), F32)
            for r in range(plan.vec_rows):
                value = jnp.where(at16 == r, sv[r, at : at + 1, :], value)
            gq[j, d // 2, d % 2, R:, :] = value.astype(BF)
    for offset in range(n_mp):
        RS.to_sibling(offset)
    RQ.nearer()
    RS.far()
    RS.free(0)
    RS.free(1)
    RU.along()
    RO.along()
    for s in range(2):
        RD.bound(s)
    RD.nearer()
    for s in range(2):
        RS.bound(s)
    RQ.home()
    RS.nearer()
    RS.home()
    o_u[...] = RU.finish()
    o_o[...] = RO.finish()
    RQ.along()
    RS.along()
    o_d[...] = RD.finish()
    o_q[...] = RQ.finish()
    o_s[...] = RS.finish()
    for r in (RU, RD, RO, RQ, RS):
        r.wait_sent()
    for r in (YO, YF, YX):
        r.wait_sent()
        r.wait_here()


def step(plan, w_qkv, w_out, w_up, w_down, tok, fv, cot, small):
    R, C, n_mp, n_z, n = plan.rows, plan.cols, plan.n_mp, plan.n_z, plan.n
    count = np.arange(D, dtype=np.int32)
    tab = np.zeros((8, D), np.int32)
    for at, width in ((0, D // n), (2, VFRESH // n), (4, FF // n)):
        tab[at], tab[at + 1] = count % width, count // width
    r = np.arange(n, dtype=np.int32)
    dev = np.tile(((r % plan.n_dp) * n_mp + r // plan.n_dp)[:, None], (1, 128))
    vm = pltpu.VMEM
    dma = pltpu.SemaphoreType.DMA
    wide = lambda t: vm((SEQ, D), t)
    tall = lambda t: vm((D, SEQ), t)
    panel = lambda rows, cols: vm((n_mp, n_z, 2, rows, cols), BF)

    def sums(rows, cols):
        ring = n_z // 2 + (plan.half - 1) * n_z
        return [
            vm((n_mp, n_z, rows, cols), BF),
            vm((2, ring, rows, cols), BF),
            vm((n_z - 1, rows, cols), BF),
        ]

    down_sums = [
        vm((n_mp, n_z, R, C), BF),
        vm((2, plan.half, R, C), BF),
        vm((n_mp, n_z - 1, R, C), BF),
    ]
    panel_z = [dma((n_mp, n_z - 1))] * 2
    gather_sems = [dma((n_z - 1,))] * 2 + [dma((2, plan.half))] * 2 + [dma((n_mp,))] * 2
    reduce_sems = [dma((n_mp,))] * 2 + [dma((2, plan.half + 1))] * 2 + [dma((n_z - 1,))] * 2
    shape = jax.ShapeDtypeStruct
    ins = (jnp.asarray(tab), jnp.asarray(dev), w_qkv, w_out, w_up, w_down, tok, fv, cot, *small)
    return pl.pallas_call(
        functools.partial(step_kernel, plan, len(ins)),
        name="step",
        out_shape=(
            shape(tok.shape, BF),
            shape(tok.shape, BF),
            shape(fv.shape, BF),
            shape((R, plan.qw), F32),
            shape((16, plan.qw), F32),
            shape((R // 3, C), F32),
            shape((R, C), F32),
            shape((R, C), F32),
        ),
        in_specs=[IN_VMEM] * 6 + [ANY] * 3 + [IN_VMEM] * N_VEC,
        out_specs=(ANY,) * 3 + (IN_VMEM,) * 5,
        scratch_shapes=[
            panel(R + 16, plan.qw), panel(R // 3, C), panel(R, C), panel(R, C),
            vm(tok.shape, BF), vm(fv.shape, BF), vm(cot.shape, BF),
            vm(tok.shape, BF), vm(tok.shape, BF), vm(fv.shape, BF),
            *sums(R, plan.qw), *sums(16, plan.qw), *sums(R // 3, C), *sums(R, C), *down_sums,
            vm((D, QKV), BF), vm((D, D), BF),
            vm((plan.vec_rows, n, plan.qw), F32), vm((16, D), F32), vm((max(8, n_mp), C), F32),
            wide(BF), tall(BF), vm((SEQ, 3 * D), BF), tall(F32), tall(BF),
            vm((HEADS // 2, 8, SEQ), F32),
            wide(F32), wide(F32), vm((SEQ, 128), F32), wide(BF), tall(BF), tall(BF),
            wide(F32), wide(F32), vm((SEQ, C), BF), wide(BF),
            vm((SEQ, 128), F32), vm((SEQ, 128), F32), vm((128, SEQ), F32),
            vm((16, D), F32), vm((max(8, n_mp), C), F32),
            *gather_sems,
            *(panel_z + gather_sems[2:]),
            *gather_sems,
            *(panel_z + gather_sems[2:]),
            *(reduce_sems * 4),
            *(reduce_sems[:4] + panel_z),
            *([dma((MICRO,))] * 12),
        ],
        compiler_params=pltpu.CompilerParams(
            collective_id=0, has_side_effects=True, vmem_limit_bytes=63 << 20
        ),
    )(*ins)


def unpack_kernel(plan, widths, *refs):
    (r1, r2, r3, t_q, t_s, t_o, t_u, t_d), outs, sem = refs[:8], refs[8:24], refs[24]
    moves = [pltpu.make_async_copy(src, dst, sem.at[k]) for k, (src, dst) in enumerate(zip((r1, r2, r3), outs[:3]))]
    for move in moves:
        move.start()
    outs[5][...] = t_q[:, 0 : plan.qkv]
    third = plan.rows // 3
    for t in range(3):
        outs[8][t * third : (t + 1) * third, :] = t_o[:, t * plan.group : t * plan.group + plan.out]
    outs[12][...] = t_u[...]
    outs[14][...] = t_d[...]
    for v, at in enumerate((3, 4, 6, 7, 9, 10, 11, 13, 15)):
        row, lane = v // plan.spr, (v % plan.spr) * 128
        outs[at][...] = t_s[row, lane : lane + widths[v]]
    for move in moves:
        move.wait()


def unpack(plan, summed, widths):
    shape = lambda *dims: jax.ShapeDtypeStruct(dims, F32)
    vec = [shape(w) for w in widths]
    R, C = plan.rows, plan.cols
    out_shape = [jax.ShapeDtypeStruct(r.shape, BF) for r in summed[:3]]
    out_shape += [vec[0], vec[1], shape(R, plan.qkv), vec[2], vec[3], shape(R, plan.out)]
    out_shape += [vec[4], vec[5], vec[6], shape(R, C), vec[7], shape(R, C), vec[8]]
    return pl.pallas_call(
        functools.partial(unpack_kernel, plan, widths),
        name="unpack",
        out_shape=tuple(out_shape),
        in_specs=[IN_VMEM] * 3 + [IN_VMEM] * 5,
        out_specs=(ANY,) * 3 + (IN_VMEM,) * 13,
        scratch_shapes=[pltpu.SemaphoreType.DMA((3,))],
    )(*summed)


def shards(
    plan, tokens, first_values, out_cot, ln1_gain, ln1_bias, w_qkv, q_bias, v_bias, w_out, out_bias,
    ln2_gain, ln2_bias, w_up, up_bias, w_down, down_bias,
):
    small = (ln1_gain, ln1_bias, q_bias, v_bias, out_bias, ln2_gain, ln2_bias, up_bias, down_bias)
    summed = step(plan, w_qkv, w_out, w_up, w_down.T, tokens, first_values, out_cot, small)
    outs = unpack(plan, summed, [s.shape[0] for s in small])
    return (*outs[:14], outs[14].T, outs[15])


def solution(mesh):
    plan = Plan(mesh)
    line = P(("dp", "mp"))
    rows = P(None, ("dp", "mp"), None)
    block = P("dp", "mp")
    grads = (line, line, block, line, line, block, line, line, line, block, line, P("mp", "dp"), line)
    return jax.shard_map(
        functools.partial(shards, plan),
        mesh=mesh,
        in_specs=(rows, rows, rows) + grads,
        out_specs=(rows, rows, rows) + grads,
        check_vma=False,
    )
```

```python
import functools

import jax
import jax.numpy as jnp
import numpy as np
from jax import lax
from jax.experimental import pallas as pl
from jax.experimental.pallas import tpu as pltpu
from jax.sharding import PartitionSpec as P

D = 768
HEADS = 12
HEAD = 64
FF = 3072
MICRO = 4
QKV = 1920
SEQ = 512
VFRESH = 384

EPS = 1e-05
BIG = 1e30
GELU_C = 0.7978845608028654
GELU_A = 0.044715
MESH = pl.DeviceIdType.MESH
ANY = pl.BlockSpec(memory_space=pl.ANY)
IN_VMEM = pl.BlockSpec(memory_space=pltpu.VMEM)
BF, F32 = jnp.bfloat16, jnp.float32

WIDE = (0, 1, 2, 4, 5, 6, 8)
V_BIAS, UP_BIAS = 3, 7
G1, B1, QB, OB, G2, B2, DB = WIDE
N_VEC = 9


class Plan:
    def __init__(self, mesh):
        self.n_dp = mesh.shape["dp"]
        self.n_mp = mesh.shape["mp"]
        self.n = self.n_dp * self.n_mp
        self.n_z = self.n_dp // 2
        self.rows = D // self.n_dp
        self.cols = FF // self.n_mp
        self.qkv = QKV // self.n_mp
        self.out = D // self.n_mp
        self.qw = -(-self.qkv // 128) * 128
        self.group = self.cols // 3
        self.spr = self.qw // 128
        self.vec_rows = -(-N_VEC // self.spr)
        self.half = self.n_mp // 2
        self.per_seq = SEQ // (SEQ // MICRO)
        self.n_seq = self.n_mp // MICRO
        assert self.out <= self.group and self.rows % 48 == 0 and self.vec_rows <= 16
        self.bits = self.n_z.bit_length() - 1
        assert self.n_seq * MICRO == self.n_mp and self.n_z == 1 << self.bits and self.bits > 0

    def ring_at(self, i):
        return i + (i // self.half) * (self.n_mp - 1 + self.half - 2 * i)

    def row_half(self, s, rows):
        middle = -(-rows // 32) * 16 if rows > 16 else 8
        return slice(middle, rows) if s else slice(0, middle)

    def slots(self, d):
        if d == self.half:
            return 0, self.n_z // 2
        return self.n_z // 2 + (d - 1) * self.n_z, self.n_z


def dot(a, b):
    return jnp.dot(a, b, preferred_element_type=F32)


def dot_nt(a, b):
    return lax.dot_general(a, b, (((1,), (1,)), ((), ())), preferred_element_type=F32)


def chunks(rows, step, body):
    @pl.loop(0, rows // step)
    def _(at):
        body(pl.ds(pl.multiple_of(at * step, step), step))


def norm_stats(r):
    average = jnp.mean(r, axis=-1, keepdims=True)
    centred = r - average
    variance = jnp.mean(centred * centred, axis=-1, keepdims=True)
    inv_std = lax.rsqrt(variance + EPS)
    return centred * inv_std, inv_std


def norm_back(grad_out, scaled, inv_std, gain):
    e = grad_out * gain
    first = jnp.mean(e, axis=-1, keepdims=True)
    second = jnp.mean(e * scaled, axis=-1, keepdims=True)
    return inv_std * (e - first - scaled * second)


class Exchange:
    def __init__(self, plan):
        self.plan = plan
        dp, i = lax.axis_index("dp"), lax.axis_index("mp")
        self.dp, self.i, self.c, self.z = dp, i, dp % 2, dp // 2
        self.sib = (dp + 1 - 2 * self.c, i)
        self.p = plan.ring_at(i)

    def at(self, pos):
        return self.plan.ring_at((pos + 2 * self.plan.n_mp) % self.plan.n_mp)

    def across(self, b):
        return self.z + (1 << b) * (1 - 2 * (self.z // (1 << b) % 2))

    def z_units(self, b, far):
        n_z = self.plan.n_z
        base = self.across(b) if far else self.z
        return [(base + m * (2 << b)) % n_z for m in range(n_z // (2 << b))]

    def z_slot(self, b, m):
        return self.plan.n_z // (2 << b) - 1 + m

    def z_device(self, b):
        return (self.across(b) * 2 + self.c, self.i)

    def greet(self):
        plan = self.plan
        barrier = pltpu.get_barrier_semaphore()
        partners = [self.sib]
        partners += [self.z_device(b) for b in range(plan.bits)]
        partners += [(self.dp, (self.i + k) % plan.n_mp) for k in range(1, plan.n_mp)]
        for partner in partners:
            pl.semaphore_signal(barrier, inc=1, device_id=partner, device_id_type=MESH)
        pl.semaphore_wait(barrier, len(partners))

    def push(self, src, dst, send, recv, device):
        return pltpu.make_async_remote_copy(
            src_ref=src, dst_ref=dst, send_sem=send, recv_sem=recv, device_id=device, device_id_type=MESH
        )


class Gather:
    def __init__(self, ex, ref, sems, tile=slice(None)):
        self.ex, self.ref, self.tile = ex, ref, tile
        self.zs, self.zr, self.rs, self.rr, self.ss, self.sr = sems

    def z_copy(self, b, m):
        ex = self.ex
        view = self.ref.at[ex.i, ex.z_units(b, False)[m], ex.c, self.tile]
        at = ex.z_slot(b, m)
        return ex.push(view, view, self.zs.at[at], self.zr.at[at], ex.z_device(b))

    def ring_view(self, origin, s, d):
        n_z, half = self.ex.plan.n_z, self.ex.plan.half
        units = pl.ds(s * (n_z // 2), n_z // 2) if d == half else pl.ds(0, n_z)
        return self.ref.at[origin, units, self.ex.c, self.tile]

    def ring_copy(self, s, d):
        ex = self.ex
        sign = 1 - 2 * s
        view = self.ring_view(ex.at(ex.p - sign * (d - 1)), s, d)
        return ex.push(view, view, self.rs.at[s, d - 1], self.rr.at[s, d - 1], (ex.dp, ex.at(ex.p + sign)))

    def sib_copy(self, offset):
        ex = self.ex
        at = (offset + ex.plan.n_mp) % ex.plan.n_mp
        view = self.ref.at[ex.at(ex.p + offset), :, ex.c, self.tile]
        return ex.push(view, view, self.ss.at[at], self.sr.at[at], ex.sib)

    def start(self):
        for b in range(self.ex.plan.bits):
            self.z_copy(b, 0).start()

    def z_sizes(self):
        n_z = self.ex.plan.n_z
        return [(b, n_z // (2 << b)) for b in range(self.ex.plan.bits)]

    def spread(self):
        sizes = self.z_sizes()
        for b, count in reversed(sizes[:-1]):
            for m in range(sizes[b + 1][1]):
                self.z_copy(b + 1, m).wait_recv()
            for m in range(1, count):
                self.z_copy(b, m).start()

    def column(self):
        for m in range(self.z_sizes()[0][1]):
            self.z_copy(0, m).wait_recv()
        for s in range(2):
            self.ring_copy(s, 1).start()
        self.sib_copy(0).start()

    def hop(self, d):
        half = self.ex.plan.half
        for s in range(2):
            self.ring_copy(s, d).wait_recv()
            if d < half:
                self.ring_copy(s, d + 1).start()
                self.sib_copy(-d if s == 0 else d).start()
        if d == half:
            self.sib_copy(half).start()

    def wait_sib(self, offset):
        self.sib_copy(offset).wait_recv()

    def wait_sent(self, offset):
        half = self.ex.plan.half
        self.sib_copy(offset).wait_send()
        if offset == 0:
            for b, count in self.z_sizes():
                for m in range(count):
                    self.z_copy(b, m).wait_send()
            for s in range(2):
                self.ring_copy(s, 1).wait_send()
        elif abs(offset) < half:
            self.ring_copy(0 if offset < 0 else 1, abs(offset) + 1).wait_send()


class RingFirst(Gather):
    def ring_view(self, origin, s, d):
        ex = self.ex
        rows = ex.plan.row_half(s, self.ref.shape[3]) if d == ex.plan.half else slice(None)
        return self.ref.at[origin, ex.z, ex.c, rows]

    def panel_copy(self, offset, b, m):
        ex = self.ex
        view = self.ref.at[ex.at(ex.p + offset), ex.z_units(b, False)[m], ex.c]
        at = (offset + ex.plan.n_mp) % ex.plan.n_mp, ex.z_slot(b, m)
        return ex.push(view, view, self.zs.at[at], self.zr.at[at], ex.z_device(b))

    def begin(self, offset):
        for b in range(self.ex.plan.bits):
            self.panel_copy(offset, b, 0).start()

    def circle(self):
        for s in range(2):
            self.ring_copy(s, 1).start()

    def hop(self, d):
        half = self.ex.plan.half
        for s in range(2):
            self.ring_copy(s, d).wait_recv()
            if d < half:
                self.ring_copy(s, d + 1).start()
        if d < half:
            self.begin(-d)
            self.begin(d)
        else:
            self.begin(half)

    def spread(self, offset):
        sizes = self.z_sizes()
        for b, count in reversed(sizes[:-1]):
            for m in range(sizes[b + 1][1]):
                self.panel_copy(offset, b + 1, m).wait_recv()
            for m in range(1, count):
                self.panel_copy(offset, b, m).start()

    def column(self, offset):
        for m in range(self.z_sizes()[0][1]):
            self.panel_copy(offset, 0, m).wait_recv()
        self.sib_copy(offset).start()

    def wait_sent(self, offset):
        half = self.ex.plan.half
        self.sib_copy(offset).wait_send()
        for b, count in self.z_sizes():
            for m in range(count):
                self.panel_copy(offset, b, m).wait_send()
        if offset == 0:
            for s in range(2):
                self.ring_copy(s, 1).wait_send()
        elif abs(offset) < half:
            self.ring_copy(0 if offset < 0 else 1, abs(offset) + 1).wait_send()


class Reduce:
    def __init__(self, ex, ref, tile, other, ring, last, sems):
        self.ex, self.ref, self.tile = ex, ref, tile
        self.other, self.ring, self.last = other, ring, last
        self.ss, self.sr, self.rs, self.rr, self.zs, self.zr = sems

    def sib_copy(self, offset):
        ex = self.ex
        at = (offset + ex.plan.n_mp) % ex.plan.n_mp
        view = self.ref.at[ex.at(ex.p + offset), :, 1 - ex.c, self.tile]
        return ex.push(view, self.other.at[at], self.ss.at[at], self.sr.at[at], ex.sib)

    def ring_views(self, dest, s, d, part):
        plan = self.ex.plan
        at, count = plan.slots(d)
        first = 0
        if d == plan.half:
            first = s * count
        elif part is not None:
            count = plan.n_z // 2
            first, at = part * count, at + part * count
        return self.ref.at[dest, pl.ds(first, count), self.ex.c, self.tile], self.ring.at[s, pl.ds(at, count)]

    def ring_copy(self, s, d, part=None):
        ex = self.ex
        plan = ex.plan
        sign = 1 - 2 * s
        sem = d - 1 if part is None else plan.half - 2 + 2 * part
        view, there = self.ring_views(ex.at(ex.p + sign * d), s, d, part)
        return ex.push(view, there, self.rs.at[s, sem], self.rr.at[s, sem], (ex.dp, ex.at(ex.p + sign)))

    def ring_copies(self, s, d):
        if d == self.ex.plan.half - 1:
            return [self.ring_copy(s, d, part) for part in range(2)]
        return [self.ring_copy(s, d)]

    def z_copy(self, b, m):
        ex = self.ex
        view = self.ref.at[ex.i, ex.z_units(b, True)[m], ex.c, self.tile]
        at = ex.z_slot(b, m)
        return ex.push(view, self.last.at[at], self.zs.at[at], self.zr.at[at], ex.z_device(b))

    def z_sizes(self):
        n_z = self.ex.plan.n_z
        return [(b, n_z // (2 << b)) for b in range(self.ex.plan.bits)]

    def to_sibling(self, offset):
        self.sib_copy(offset).start()

    def add(self, offset, first, count, *terms):
        j = self.ex.at(self.ex.p + offset)

        @pl.loop(0, count)
        def _(u):
            value = self.ref[j, first + u, self.ex.c, self.tile, :].astype(F32)
            for buf, at in terms:
                value = value + buf(at + u).astype(F32)
            self.ref[j, first + u, self.ex.c, self.tile, :] = value.astype(BF)

    def from_sibling(self, offset):
        at = (offset + self.ex.plan.n_mp) % self.ex.plan.n_mp
        self.sib_copy(offset).wait_recv()
        self.add(offset, 0, self.ex.plan.n_z, (lambda u: self.other[at, u], 0))

    def far(self):
        half = self.ex.plan.half
        self.from_sibling(half)
        for s in range(2):
            self.ring_copy(s, half).start()

    def free(self, s):
        half = self.ex.plan.half
        self.from_sibling((1 - 2 * s) * (half - 1))
        self.ring_copy(s, half - 1, 1 - s).start()

    def bound(self, s):
        plan = self.ex.plan
        half = plan.half
        self.ring_copy(s, half).wait_recv()
        at, count = plan.slots(half)
        self.add((1 - 2 * s) * (half - 1), s * count, count, (lambda u: self.ring[s, u], at))
        self.ring_copy(s, half - 1, s).start()

    def wait_ring(self, s, d):
        for copy in self.ring_copies(s, d):
            copy.wait_recv()

    def nearer(self):
        plan = self.ex.plan
        for d in range(plan.half - 2, 0, -1):
            for s in range(2):
                offset = (1 - 2 * s) * d
                self.from_sibling(offset)
                self.wait_ring(s, d + 1)
                self.add(offset, 0, plan.n_z, (lambda u: self.ring[s, u], plan.slots(d + 1)[0]))
                self.ring_copy(s, d).start()

    def home(self):
        plan = self.ex.plan
        for s in range(2):
            self.wait_ring(s, 1)
        self.sib_copy(0).wait_recv()
        at = plan.slots(1)[0]
        self.add(
            0, 0, plan.n_z,
            (lambda u: self.other[0, u], 0),
            (lambda u: self.ring[0, u], at),
            (lambda u: self.ring[1, u], at),
        )
        for m in range(self.z_sizes()[0][1]):
            self.z_copy(0, m).start()

    def along(self):
        ex = self.ex
        for b, count in self.z_sizes()[:-1]:
            for m, unit in enumerate(ex.z_units(b, False)):
                self.z_copy(b, m).wait_recv()
                at = ex.z_slot(b, m)
                self.add(0, unit, 1, (lambda u: self.last[u], at))
            for m in range(count // 2):
                self.z_copy(b + 1, m).start()

    def finish(self):
        ex = self.ex
        self.z_copy(ex.plan.bits - 1, 0).wait_recv()
        return self.ref[ex.i, ex.z, ex.c, self.tile, :].astype(F32) + self.last[0].astype(F32)

    def wait_z_sent(self):
        for b, count in self.z_sizes():
            for m in range(count):
                self.z_copy(b, m).wait_send()

    def wait_sent(self):
        plan = self.ex.plan
        for offset in range(plan.n_mp):
            self.sib_copy(offset).wait_send()
        for s in range(2):
            for d in range(1, plan.half + 1):
                for copy in self.ring_copies(s, d):
                    copy.wait_send()
        self.wait_z_sent()


class RingLast(Reduce):
    def half_rows(self, s):
        return self.ex.plan.row_half(s, self.ref.shape[3])

    def panel_copy(self, offset, b, m):
        ex = self.ex
        view = self.ref.at[ex.at(ex.p + offset), ex.z_units(b, True)[m], ex.c, self.tile]
        at = (offset + ex.plan.n_mp) % ex.plan.n_mp, ex.z_slot(b, m)
        return ex.push(view, self.last.at[at], self.zs.at[at], self.zr.at[at], ex.z_device(b))

    def begin(self, offset):
        self.from_sibling(offset)
        for m in range(self.z_sizes()[0][1]):
            self.panel_copy(offset, 0, m).start()

    def take(self, offset, b):
        ex = self.ex
        q = (offset + ex.plan.n_mp) % ex.plan.n_mp
        for m, unit in enumerate(ex.z_units(b, False)):
            self.panel_copy(offset, b, m).wait_recv()
            self.add(offset, unit, 1, (lambda u: self.last[q, u], ex.z_slot(b, m)))

    def along(self, offset):
        for b, count in self.z_sizes()[:-1]:
            self.take(offset, b)
            for m in range(count // 2):
                self.panel_copy(offset, b + 1, m).start()

    def end(self, offset):
        self.take(offset, self.ex.plan.bits - 1)

    def ring_views(self, dest, s, d, part):
        ex = self.ex
        rows = slice(None)
        if d == ex.plan.half:
            rows = self.half_rows(s)
        elif part is not None:
            rows = self.half_rows(part)
        return self.ref.at[dest, ex.z, ex.c, rows], self.ring.at[s, d - 1, rows]

    def add_rows(self, offset, rows, *terms):
        ex = self.ex
        j = ex.at(ex.p + offset)
        value = self.ref[j, ex.z, ex.c, rows, :].astype(F32)
        for term in terms:
            value = value + term.astype(F32)
        self.ref[j, ex.z, ex.c, rows, :] = value.astype(BF)

    def far(self):
        for s in range(2):
            self.ring_copy(s, self.ex.plan.half).start()

    def free(self, s):
        self.ring_copy(s, self.ex.plan.half - 1, 1 - s).start()

    def bound(self, s):
        plan = self.ex.plan
        half = plan.half
        self.ring_copy(s, half).wait_recv()
        rows = self.half_rows(s)
        self.add_rows((1 - 2 * s) * (half - 1), rows, self.ring[s, half - 1, rows, :])
        self.ring_copy(s, half - 1, s).start()

    def nearer(self):
        for d in range(self.ex.plan.half - 2, 0, -1):
            for s in range(2):
                self.wait_ring(s, d + 1)
                self.add_rows((1 - 2 * s) * d, slice(None), self.ring[s, d])
                self.ring_copy(s, d).start()

    def finish(self):
        ex = self.ex
        for s in range(2):
            self.wait_ring(s, 1)
        value = self.ref[ex.i, ex.z, ex.c].astype(F32)
        return value + self.ring[0, 0].astype(F32) + self.ring[1, 0].astype(F32)

    def wait_z_sent(self):
        for offset in range(self.ex.plan.n_mp):
            for b, count in self.z_sizes():
                for m in range(count):
                    self.panel_copy(offset, b, m).wait_send()


class Rows:
    def __init__(self, ex, src, dst, send, recv, out):
        self.ex, self.src, self.dst, self.send, self.recv, self.out = ex, src, dst, send, recv, out

    def move(self, start):
        ex = self.ex
        plan, i = ex.plan, ex.i
        q = plan.per_seq
        for m in range(MICRO):
            if self.out:
                target, place = (i % plan.n_seq) * q + m, i // plan.n_seq
            else:
                target, place = m * plan.n_seq + i // q, i % q
            far = ex.push(self.src.at[m], self.dst.at[place], self.send.at[m], self.recv.at[place], (ex.dp, target))
            near = pltpu.make_async_copy(self.src.at[m], self.dst.at[place], self.send.at[m])

            @pl.when(target != i)
            def _():
                far.start() if start else far.wait_send()

            @pl.when(target == i)
            def _():
                near.start() if start else near.wait()

    def start(self):
        self.move(True)

    def wait_sent(self):
        self.move(False)

    def wait_here(self):
        ex = self.ex
        plan, i = ex.plan, ex.i
        q = plan.per_seq
        for m in range(MICRO):
            origin = m * plan.n_seq + i // q if self.out else (i % plan.n_seq) * q + m

            @pl.when(origin != i)
            def _():
                ex.push(self.dst.at[m], self.dst.at[m], self.send.at[0], self.recv.at[m], ex.sib).wait_recv()


def step_kernel(plan, n_in, *refs):
    (tab, dev, w_qkv, w_out, w_up, w_down, tok, fv, cot), small = refs[:9], refs[9:n_in]
    (o_out, o_dx, o_df, o_q, o_s, o_o, o_u, o_d) = refs[n_in : n_in + 8]
    (
        gq, go, gu, gd, x3, f3, y3, out3, dx3, df3,
        q_other, q_ring, q_last, s_other, s_ring, s_last, o_other, o_ring, o_last, u_other, u_ring, u_last,
        d_other, d_ring, d_last,
        wq, wo, sv, vec, ub, hl, hlt, qkv, ot, otb, lse, mid, n2, inv2, h2, h2t, yt,
        big, acc, act, du, dv, dk, dqt, sums, ubg,
    ) = refs[n_in + 8 : n_in + 8 + 51]
    sems = refs[n_in + 8 + 51 :]
    R, C, n_mp, n_dp, n_z = plan.rows, plan.cols, plan.n_mp, plan.n_dp, plan.n_z
    step = 64
    ex = Exchange(plan)
    i, z, c = ex.i, ex.z, ex.c
    Q = Gather(ex, gq, sems[0:6])
    O = Gather(ex, go, sems[6:12])
    U1 = Gather(ex, gu, sems[12:18], plan.row_half(0, R))
    U2 = Gather(ex, gu, sems[18:24], plan.row_half(1, R))
    W = RingFirst(ex, gd, sems[24:30])
    RQ = Reduce(ex, gq, slice(0, R), q_other, q_ring, q_last, sems[30:36])
    RS = Reduce(ex, gq, slice(R, R + 16), s_other, s_ring, s_last, sems[36:42])
    RU = Reduce(ex, gu, slice(0, R), u_other, u_ring, u_last, sems[42:48])
    RO = RingLast(ex, go, slice(0, R // 3), o_other, o_ring, o_last, sems[48:54])
    RD = RingLast(ex, gd, slice(0, R), d_other, d_ring, d_last, sems[54:60])
    a2a = sems[60:72]
    XT = Rows(ex, tok, x3, a2a[0], a2a[1], False)
    XF = Rows(ex, fv, f3, a2a[2], a2a[3], False)
    XY = Rows(ex, cot, y3, a2a[4], a2a[5], False)
    YO = Rows(ex, out3, o_out, a2a[6], a2a[7], True)
    YX = Rows(ex, dx3, o_dx, a2a[8], a2a[9], True)
    YF = Rows(ex, df3, o_df, a2a[10], a2a[11], True)
    near = range(-plan.half + 1, plan.half)

    third = R // 3
    gq[i, z, c, 0:R, 0 : plan.qkv] = w_qkv[...]
    sv[0, 0:16, :] = jnp.zeros((16, plan.qw), F32)
    for r in range(plan.vec_rows):
        pieces = [small[v][...] for v in range(r * plan.spr, min((r + 1) * plan.spr, N_VEC))]
        for k, piece in enumerate(pieces):
            sv[0, r : r + 1, k * 128 : k * 128 + piece.shape[0]] = piece.astype(F32)[None]
    gq[i, z, c, R:, :] = sv[0, 0:16, :].astype(BF)
    for t in range(3):
        go[i, z, c, :, t * plan.group : t * plan.group + plan.out] = w_out[t * third : (t + 1) * third, :]
    gu[i, z, c] = w_up[...]
    gd[i, z, c] = w_down[...]
    ex.greet()
    Q.start()
    XT.start()
    Q.spread()
    Q.column()
    O.start()
    W.circle()
    W.begin(0)
    U1.start()
    U2.start()
    W.hop(1)
    O.spread()
    for d in range(2, plan.half + 1):
        W.hop(d)
    Q.hop(1)
    XF.start()
    U1.spread()
    U2.spread()
    O.column()
    for d in range(2, plan.half + 1):
        Q.hop(d)
    XY.start()
    for d in range(1, plan.half):
        O.hop(d)

    rowdev = dev[:, 0:1]
    row = lambda v: vec[v : v + 1, :]
    lanes = lambda v: slice((v % plan.spr) * 128, (v % plan.spr) * 128 + 128)
    onehot = lambda t, width: (lax.broadcasted_iota(jnp.int32, (128, width), 0) == tab[t : t + 1, :width]).astype(BF)
    e24 = onehot(0, D)
    e96 = onehot(4, C)

    def rows_of(ref3, at, step):
        part = SEQ // MICRO
        return ref3.at[at // (part // step), pl.ds(pl.multiple_of((at % (part // step)) * step, step), step)]

    def blocks(step, body):
        @pl.loop(0, SEQ // step)
        def _(at):
            body(at, pl.ds(pl.multiple_of(at * step, step), step))

    for offset in (*near, plan.half):
        Q.wait_sib(offset)

    for j in range(n_mp):
        for d in range(n_dp):
            rows = slice(d * R, (d + 1) * R)
            wq[rows, j * plan.qkv : (j + 1) * plan.qkv] = gq[j, d // 2, d % 2, 0:R, 0 : plan.qkv]
    for r in range(plan.vec_rows):
        for j in range(n_mp):
            for d in range(n_dp):
                at = j * n_dp + d
                sv[r, at : at + 1, :] = gq[j, d // 2, d % 2, R + r : R + r + 1, :].astype(F32)

    def expand(v, e, owner):
        got = dot(sv[v // plan.spr, :, lanes(v)].astype(BF), e)
        return jnp.sum(jnp.where(owner == rowdev, got, 0.0), axis=0, keepdims=True)

    for v in WIDE:
        vec[v : v + 1, :] = expand(v, e24, tab[1:2, :])
    vec[V_BIAS : V_BIAS + 1, :] = expand(V_BIAS, onehot(2, D), tab[3:4, :])
    for j in range(n_mp):
        ub[j : j + 1, :] = expand(UP_BIAS, e96, tab[5:6, :C] + j * n_dp)

    W.spread(0)
    U1.column()
    U2.column()
    XT.wait_here()
    XT.wait_sent()

    def first_norm(at, rows):
        n1, _ = norm_stats(rows_of(x3, at, step)[...].astype(F32))
        hl[rows, :] = (n1 * row(G1) + row(B1)).astype(BF)

    blocks(step, first_norm)
    hlt[...] = hl[...].T
    XF.wait_here()
    XF.wait_sent()

    q = dot(hl[...], wq[:, 0:D]) + row(QB)
    qkv[:, 0:D] = q.astype(BF) * 0.125
    qkv[:, D : 2 * D] = dot(hl[...], wq[:, D : 2 * D]).astype(BF)
    v = dot(hl[...], wq[:, 2 * D : QKV]) + row(V_BIAS)[:, :VFRESH]
    qkv[:, 2 * D : QKV] = v.astype(BF)
    for offset in near:
        if offset:
            W.spread(offset)
    qkv[:, QKV : 3 * D] = f3[...].reshape(SEQ, D // 2)

    B = 256
    head_of = lax.broadcasted_iota(jnp.int32, (1, 128), 1) // HEAD
    keep = lax.broadcasted_iota(jnp.int32, (B, B), 0) <= lax.broadcasted_iota(jnp.int32, (B, B), 1)

    def scores(k2, qm, at):
        s = dot_nt(k2, qm)
        last = jnp.where(keep, s[at * B :, :], -BIG)
        return last if at == 0 else jnp.concatenate([s[: at * B, :], last], axis=0)

    @pl.loop(0, HEADS // 2)
    def _(t):
        cols = lambda base: pl.ds(pl.multiple_of(base + t * 128, 128), 128)
        vt = qkv[:, cols(2 * D)].T
        for e in range(2):
            mask = (head_of == e).astype(BF)
            for at in range(SEQ // B):
                kk = (at + 1) * B
                span = slice(at * B, kk)
                s = scores(qkv[0:kk, cols(D)], qkv[span, cols(0)] * mask, at)
                top = jnp.max(s, axis=0, keepdims=True)
                ex_ = jnp.exp(s - top)
                total = jnp.sum(ex_, axis=0, keepdims=True)
                o = dot(vt[e * HEAD : (e + 1) * HEAD, 0:kk], ex_.astype(BF)) / total
                ot[pl.ds(pl.multiple_of(t * 128 + e * HEAD, HEAD), HEAD), span] = o
                lse[t, e : e + 1, span] = top + jnp.log(total)

        @pl.when(t == 0)
        def _():
            O.hop(plan.half)
            W.spread(plan.half)

        @pl.when(t == 4)
        def _():
            W.column(0)

    for offset in (*near, plan.half):
        O.wait_sib(offset)
    for j in range(n_mp):
        for d in range(n_dp):
            for t in range(3):
                rows = slice(d * R + t * third, d * R + (t + 1) * third)
                wo[rows, j * plan.out : (j + 1) * plan.out] = go[
                    j, d // 2, d % 2, :, t * plan.group : t * plan.group + plan.out
                ]
    otb[...] = ot[...].astype(BF)
    du[:, 0:D] = otb[...].T

    acc[...] = dot(du[:, 0:D], wo[...]) + row(OB)

    def second_norm(at, rows):
        m = rows_of(x3, at, step)[...].astype(F32) + acc[rows, :]
        mid[rows, :] = m
        scaled, inv = norm_stats(m)
        n2[rows, :] = scaled
        inv2[rows, :] = jnp.broadcast_to(inv, (step, 128))
        h2[rows, :] = (scaled * row(G2) + row(B2)).astype(BF)

    blocks(step, second_norm)
    W.column(plan.half)
    for offset in near:
        if offset:
            W.column(offset)
    for d in range(1, plan.half):
        U1.hop(d)
        U2.hop(d)
    h2t[...] = h2[...].T
    XY.wait_here()
    XY.wait_sent()
    yt[...] = y3[...].reshape(SEQ, D).T
    acc[...] = jnp.zeros_like(acc)
    big[...] = jnp.zeros_like(big)

    order = [0, plan.half]
    for d in range(plan.half - 1, 0, -1):
        order += [-d, d]

    def nth(q):
        d = plan.half - q // 2
        return jnp.where(q == 0, 0, jnp.where(q == 1, plan.half, d * (2 * (q % 2) - 1)))

    def ring_turn(r, offset):
        if offset == plan.half:
            r.far()
        elif abs(offset) == plan.half - 1:
            r.free(0 if offset > 0 else 1)

    @pl.loop(0, n_mp)
    def _(q):
        j = ex.at(ex.p + nth(q))
        for s, offset in enumerate(order):

            @pl.when(q == s)
            def _():
                if s == 1:
                    U1.hop(plan.half)
                    U2.hop(plan.half)
                    RD.begin(order[0])
                U1.wait_sib(offset)
                U2.wait_sib(offset)
                W.wait_sib(offset)

        up = gu[j].reshape(D, C)
        down = gd[j].reshape(D, C)
        u = dot(h2[...], up) + ub[pl.ds(j, 1), :]
        u2 = u * u
        tangent = jnp.tanh(GELU_C * (u + GELU_A * u2 * u))
        half = 0.5 * (1.0 + tangent)
        a = (u * half).astype(BF)
        slope = half + 0.5 * u * (1.0 - tangent * tangent) * GELU_C * (1.0 + 3.0 * GELU_A * u2)
        act[...] = a
        acc[...] += dot_nt(a, down)
        g = (dot(y3[...].reshape(SEQ, D), down) * slope).astype(BF)
        du[:, 0:C] = g
        big[...] += dot_nt(g, up)
        for s, offset in enumerate(order):

            @pl.when(q == s)
            def _():
                if s == 2:
                    RD.along(order[0])
                if s >= 3:
                    RD.begin(order[s - 1])
                    ring_turn(RU, order[s - 1])
                if s >= 4:
                    RD.along(order[s - 3])
                W.wait_sent(offset)
                U1.wait_sent(offset)
                U2.wait_sent(offset)

        gd[j] = dot(yt[...], act[...]).astype(BF).reshape(n_z, 2, R, C)
        gu[j] = dot(h2t[...], du[:, 0:C]).astype(BF).reshape(n_z, 2, R, C)
        ubg[pl.ds(j, 1), :] = jnp.sum(du[:, 0:C].astype(F32), axis=0, keepdims=True)
        for s, offset in enumerate(order):

            @pl.when(q == s)
            def _():
                RD.to_sibling(offset)
                RU.to_sibling(offset)
                if s == 2:
                    RD.begin(order[1])
                    ring_turn(RU, order[1])

    sums[...] = jnp.zeros_like(sums)

    def second_back(at, rows):
        rows_of(out3, at, step)[...] = (mid[rows, :] + (acc[rows, :] + row(DB))).astype(BF)
        dh = big[rows, :]
        dy = rows_of(y3, at, step)[...].astype(F32)
        scaled = n2[rows, :]
        dr = norm_back(dh, scaled, inv2[rows, 0:1], row(G2))
        dmid = dy + dr
        mid[rows, :] = dmid
        low = dmid.astype(BF)
        du[rows, 0:D] = low
        total = lambda a: jnp.sum(a, axis=0, keepdims=True)
        sums[G2 : G2 + 1, :] += total(dh * scaled)
        sums[B2 : B2 + 1, :] += total(dh)
        sums[OB : OB + 1, :] += total(low.astype(F32))
        sums[DB : DB + 1, :] += total(dy)

    blocks(step, second_back)
    for offset in order[:-3]:
        RD.end(offset)
    YO.start()
    for offset in (*near, plan.half):
        O.wait_sent(offset)
        Q.wait_sent(offset)
    for j in range(n_mp):
        g = dot(otb[...], du[:, j * plan.out : (j + 1) * plan.out]).astype(BF).reshape(n_z, 2, 3, third, plan.out)
        for t in range(3):
            go[j, :, :, :, t * plan.group : t * plan.group + plan.out] = g[:, :, t]
    for offset in order:
        RO.to_sibling(offset)
    RD.begin(order[-1])
    ring_turn(RU, order[-1])
    for side in range(2):
        RU.bound(side)
    RD.along(order[-3])
    for offset in order[1:] + order[:1]:
        RO.begin(offset)
    do = hl
    do[...] = dot_nt(du[:, 0:D], wo[...]).astype(BF)

    @pl.loop(0, HEADS // 2)
    def _(t):
        cols = lambda base: pl.ds(pl.multiple_of(base + t * 128, 128), 128)
        kt = qkv[:, cols(D)].T
        dot_ = do[:, cols(0)].astype(F32).T
        prod = dot_ * ot[cols(0), :]
        dv[...] = jnp.zeros_like(dv)
        dk[...] = jnp.zeros_like(dk)
        for e in range(2):
            mask = (head_of == e).astype(BF)
            delta = jnp.sum(prod[e * HEAD : (e + 1) * HEAD, :], axis=0, keepdims=True)
            for at in range(SEQ // B):
                kk = (at + 1) * B
                span = slice(at * B, kk)
                qm = qkv[span, cols(0)] * mask
                dom = do[span, cols(0)] * mask
                s = scores(qkv[0:kk, cols(D)], qm, at)
                p = jnp.exp(s - lse[t, e : e + 1, span])
                dp = dot_nt(qkv[0:kk, cols(2 * D)], dom)
                ds = (p * (dp - delta[:, span])).astype(BF)
                dv[0:kk, :] += dot(p.astype(BF), dom)
                dk[0:kk, :] += dot(ds, qm)
                dqt[e * HEAD : (e + 1) * HEAD, span] = dot(kt[e * HEAD : (e + 1) * HEAD, 0:kk], ds)
        qkv[:, cols(0)] = (dqt[...].T * 0.125).astype(BF)
        qkv[:, cols(D)] = dk[...].astype(BF)
        qkv[:, cols(2 * D)] = dv[...].astype(BF)

    df3[...] = qkv[:, QKV : 3 * D].reshape(df3.shape)
    YF.start()
    for j in range(n_mp):
        g = dot(hlt[...], qkv[:, j * plan.qkv : (j + 1) * plan.qkv]).astype(BF)
        gq[j, :, :, 0:R, 0 : plan.qkv] = g.reshape(n_z, 2, R, plan.qkv)
    for offset in (plan.half, *near):
        RQ.to_sibling(offset)
    acc[...] = dot_nt(qkv[:, 0:QKV], wq[...])
    RO.along(plan.half)
    RD.along(order[-2])
    for offset in near:
        RO.along(offset)

    def first_back(at, rows):
        n1, inv = norm_stats(rows_of(x3, at, step)[...].astype(F32))
        dh = acc[rows, :]
        dr = norm_back(dh, n1, inv, row(G1))
        rows_of(dx3, at, step)[...] = (mid[rows, :] + dr).astype(BF)
        total = lambda a: jnp.sum(a, axis=0, keepdims=True)
        sums[G1 : G1 + 1, :] += total(dh * n1)
        sums[B1 : B1 + 1, :] += total(dh)
        sums[QB : QB + 1, :] += total(qkv[rows, 0:D].astype(F32))
        sums[V_BIAS : V_BIAS + 1, 0:VFRESH] += total(qkv[rows, 2 * D : QKV].astype(F32))

    blocks(step, first_back)
    RQ.far()
    RQ.free(0)
    RQ.free(1)

    def collect(g, e, owner):
        return dot_nt(jnp.where(owner == rowdev, g, 0.0).astype(BF), e)

    for v in WIDE:
        sv[v // plan.spr, :, lanes(v)] = collect(sums[v : v + 1, :], e24, tab[1:2, :])
    sv[V_BIAS // plan.spr, :, lanes(V_BIAS)] = collect(sums[V_BIAS : V_BIAS + 1, :], onehot(2, D), tab[3:4, :])
    got = collect(ubg[0:1, :], e96, tab[5:6, :C])
    for j in range(1, n_mp):
        got = got + collect(ubg[j : j + 1, :], e96, tab[5:6, :C] + j * n_dp)
    sv[UP_BIAS // plan.spr, :, lanes(UP_BIAS)] = got
    at16 = lax.broadcasted_iota(jnp.int32, (16, plan.qw), 0)
    for j in range(n_mp):
        for d in range(n_dp):
            at = j * n_dp + d
            value = jnp.zeros((16, plan.qw), F32)
            for r in range(plan.vec_rows):
                value = jnp.where(at16 == r, sv[r, at : at + 1, :], value)
            gq[j, d // 2, d % 2, R:, :] = value.astype(BF)
    for offset in order:
        RS.to_sibling(offset)
    RS.far()
    RS.free(1)
    RS.free(0)
    RD.along(order[-1])
    RS.bound(1)
    RU.nearer()
    RU.home()
    RS.bound(0)
    RO.end(plan.half)
    RO.far()
    for offset in near:
        RO.end(offset)
    RO.free(1)
    RO.free(0)
    RQ.bound(1)
    RO.bound(1)
    RO.bound(0)
    RD.end(order[-3])
    RS.nearer()
    RS.home()
    RD.far()
    RQ.bound(0)
    RO.nearer()
    o_o[...] = RO.finish()
    RS.along()
    o_s[...] = RS.finish()
    RD.end(order[-2])
    RD.free(1)
    RD.bound(1)
    RQ.nearer()
    RQ.home()
    YX.start()
    RU.along()
    RD.end(order[-1])
    RD.free(0)
    RD.bound(0)
    RD.nearer()
    RQ.along()
    o_d[...] = RD.finish()
    o_u[...] = RU.finish()
    o_q[...] = RQ.finish()
    for r in (RU, RD, RO, RQ, RS):
        r.wait_sent()
    for r in (YO, YF, YX):
        r.wait_sent()
        r.wait_here()


def step(plan, w_qkv, w_out, w_up, w_down, tok, fv, cot, small):
    R, C, n_mp, n_z, n = plan.rows, plan.cols, plan.n_mp, plan.n_z, plan.n
    count = np.arange(D, dtype=np.int32)
    tab = np.zeros((8, D), np.int32)
    for at, width in ((0, D // n), (2, VFRESH // n), (4, FF // n)):
        tab[at], tab[at + 1] = count % width, count // width
    r = np.arange(n, dtype=np.int32)
    dev = np.tile(((r % plan.n_dp) * n_mp + r // plan.n_dp)[:, None], (1, 128))
    vm = pltpu.VMEM
    dma = pltpu.SemaphoreType.DMA
    wide = lambda t: vm((SEQ, D), t)
    tall = lambda t: vm((D, SEQ), t)
    panel = lambda rows, cols: vm((n_mp, n_z, 2, rows, cols), BF)

    def sums(rows, cols):
        ring = n_z // 2 + (plan.half - 1) * n_z
        return [
            vm((n_mp, n_z, rows, cols), BF),
            vm((2, ring, rows, cols), BF),
            vm((n_z - 1, rows, cols), BF),
        ]

    def ring_last(rows, cols):
        return [
            vm((n_mp, n_z, rows, cols), BF),
            vm((2, plan.half, rows, cols), BF),
            vm((n_mp, n_z - 1, rows, cols), BF),
        ]

    panel_z = [dma((n_mp, n_z - 1))] * 2
    gather_sems = [dma((n_z - 1,))] * 2 + [dma((2, plan.half))] * 2 + [dma((n_mp,))] * 2
    reduce_sems = [dma((n_mp,))] * 2 + [dma((2, plan.half + 1))] * 2 + [dma((n_z - 1,))] * 2
    shape = jax.ShapeDtypeStruct
    ins = (jnp.asarray(tab), jnp.asarray(dev), w_qkv, w_out, w_up, w_down, tok, fv, cot, *small)
    return pl.pallas_call(
        functools.partial(step_kernel, plan, len(ins)),
        name="step",
        out_shape=(
            shape(tok.shape, BF),
            shape(tok.shape, BF),
            shape(fv.shape, BF),
            shape((R, plan.qw), F32),
            shape((16, plan.qw), F32),
            shape((R // 3, C), F32),
            shape((R, C), F32),
            shape((R, C), F32),
        ),
        in_specs=[IN_VMEM] * 6 + [ANY] * 3 + [IN_VMEM] * N_VEC,
        out_specs=(ANY,) * 3 + (IN_VMEM,) * 5,
        scratch_shapes=[
            panel(R + 16, plan.qw), panel(R // 3, C), panel(R, C), panel(R, C),
            vm(tok.shape, BF), vm(fv.shape, BF), vm(cot.shape, BF),
            vm(tok.shape, BF), vm(tok.shape, BF), vm(fv.shape, BF),
            *sums(R, plan.qw), *sums(16, plan.qw), *ring_last(R // 3, C), *sums(R, C), *ring_last(R, C),
            vm((D, QKV), BF), vm((D, D), BF),
            vm((plan.vec_rows, n, plan.qw), F32), vm((16, D), F32), vm((max(8, n_mp), C), F32),
            wide(BF), tall(BF), vm((SEQ, 3 * D), BF), tall(F32), tall(BF),
            vm((HEADS // 2, 8, SEQ), F32),
            wide(F32), wide(F32), vm((SEQ, 128), F32), wide(BF), tall(BF), tall(BF),
            wide(F32), wide(F32), vm((SEQ, C), BF), wide(BF),
            vm((SEQ, 128), F32), vm((SEQ, 128), F32), vm((128, SEQ), F32),
            vm((16, D), F32), vm((max(8, n_mp), C), F32),
            *(gather_sems * 4),
            *(panel_z + gather_sems[2:]),
            *(reduce_sems * 3),
            *((reduce_sems[:4] + panel_z) * 2),
            *([dma((MICRO,))] * 12),
        ],
        compiler_params=pltpu.CompilerParams(
            collective_id=0, has_side_effects=True, vmem_limit_bytes=63 << 20
        ),
    )(*ins)


def unpack_kernel(plan, widths, *refs):
    (r1, r2, r3, t_q, t_s, t_o, t_u, t_d), outs, sem = refs[:8], refs[8:24], refs[24]
    moves = [pltpu.make_async_copy(src, dst, sem.at[k]) for k, (src, dst) in enumerate(zip((r1, r2, r3), outs[:3]))]
    for move in moves:
        move.start()
    outs[5][...] = t_q[:, 0 : plan.qkv]
    third = plan.rows // 3
    for t in range(3):
        outs[8][t * third : (t + 1) * third, :] = t_o[:, t * plan.group : t * plan.group + plan.out]
    outs[12][...] = t_u[...]
    outs[14][...] = t_d[...]
    for v, at in enumerate((3, 4, 6, 7, 9, 10, 11, 13, 15)):
        row, lane = v // plan.spr, (v % plan.spr) * 128
        outs[at][...] = t_s[row, lane : lane + widths[v]]
    for move in moves:
        move.wait()


def unpack(plan, summed, widths):
    shape = lambda *dims: jax.ShapeDtypeStruct(dims, F32)
    vec = [shape(w) for w in widths]
    R, C = plan.rows, plan.cols
    out_shape = [jax.ShapeDtypeStruct(r.shape, BF) for r in summed[:3]]
    out_shape += [vec[0], vec[1], shape(R, plan.qkv), vec[2], vec[3], shape(R, plan.out)]
    out_shape += [vec[4], vec[5], vec[6], shape(R, C), vec[7], shape(R, C), vec[8]]
    return pl.pallas_call(
        functools.partial(unpack_kernel, plan, widths),
        name="unpack",
        out_shape=tuple(out_shape),
        in_specs=[IN_VMEM] * 3 + [IN_VMEM] * 5,
        out_specs=(ANY,) * 3 + (IN_VMEM,) * 13,
        scratch_shapes=[pltpu.SemaphoreType.DMA((3,))],
    )(*summed)


def shards(
    plan, tokens, first_values, out_cot, ln1_gain, ln1_bias, w_qkv, q_bias, v_bias, w_out, out_bias,
    ln2_gain, ln2_bias, w_up, up_bias, w_down, down_bias,
):
    small = (ln1_gain, ln1_bias, q_bias, v_bias, out_bias, ln2_gain, ln2_bias, up_bias, down_bias)
    summed = step(plan, w_qkv, w_out, w_up, w_down.T, tokens, first_values, out_cot, small)
    outs = unpack(plan, summed, [s.shape[0] for s in small])
    return (*outs[:14], outs[14].T, outs[15])


def solution(mesh):
    plan = Plan(mesh)
    line = P(("dp", "mp"))
    rows = P(None, ("dp", "mp"), None)
    block = P("dp", "mp")
    grads = (line, line, block, line, line, block, line, line, line, block, line, P("mp", "dp"), line)
    return jax.shard_map(
        functools.partial(shards, plan),
        mesh=mesh,
        in_specs=(rows, rows, rows) + grads,
        out_specs=(rows, rows, rows) + grads,
        check_vma=False,
    )
```

```python
import functools

import jax
import jax.numpy as jnp
import numpy as np
from jax import lax
from jax.experimental import pallas as pl
from jax.experimental.pallas import tpu as pltpu
from jax.sharding import PartitionSpec as P

D = 768
HEADS = 12
HEAD = 64
FF = 3072
MICRO = 4
QKV = 1920
SEQ = 512
VFRESH = 384

EPS = 1e-05
BIG = 1e30
GELU_C = 0.7978845608028654
GELU_A = 0.044715
MESH = pl.DeviceIdType.MESH
ANY = pl.BlockSpec(memory_space=pl.ANY)
IN_VMEM = pl.BlockSpec(memory_space=pltpu.VMEM)
BF, F32 = jnp.bfloat16, jnp.float32

WIDE = (0, 1, 2, 4, 5, 6, 8)
V_BIAS, UP_BIAS = 3, 7
G1, B1, QB, OB, G2, B2, DB = WIDE
N_VEC = 9


class Plan:
    def __init__(self, mesh):
        self.n_dp = mesh.shape["dp"]
        self.n_mp = mesh.shape["mp"]
        self.n = self.n_dp * self.n_mp
        self.n_z = self.n_dp // 2
        self.rows = D // self.n_dp
        self.cols = FF // self.n_mp
        self.qkv = QKV // self.n_mp
        self.out = D // self.n_mp
        self.qw = -(-self.qkv // 128) * 128
        self.group = self.cols // 3
        self.spr = self.qw // 128
        self.vec_rows = -(-N_VEC // self.spr)
        self.half = self.n_mp // 2
        self.per_seq = SEQ // (SEQ // MICRO)
        self.n_seq = self.n_mp // MICRO
        assert self.out <= self.group and self.rows % 48 == 0 and self.vec_rows <= 8
        self.bits = self.n_z.bit_length() - 1
        assert self.n_seq * MICRO == self.n_mp and self.n_z == 1 << self.bits and self.bits > 0

    def ring_at(self, i):
        return i + (i // self.half) * (self.n_mp - 1 + self.half - 2 * i)

    def row_half(self, s, rows):
        middle = -(-rows // 32) * 16 if rows > 16 else 8
        return slice(middle, rows) if s else slice(0, middle)

    def slots(self, d):
        if d == self.half:
            return 0, self.n_z // 2
        return self.n_z // 2 + (d - 1) * self.n_z, self.n_z


def dot(a, b):
    return jnp.dot(a, b, preferred_element_type=F32)


def dot_nt(a, b):
    return lax.dot_general(a, b, (((1,), (1,)), ((), ())), preferred_element_type=F32)


def chunks(rows, step, body):
    @pl.loop(0, rows // step)
    def _(at):
        body(pl.ds(pl.multiple_of(at * step, step), step))


def norm_stats(r):
    average = jnp.mean(r, axis=-1, keepdims=True)
    centred = r - average
    variance = jnp.mean(centred * centred, axis=-1, keepdims=True)
    inv_std = lax.rsqrt(variance + EPS)
    return centred * inv_std, inv_std


def norm_back(grad_out, scaled, inv_std, gain):
    e = grad_out * gain
    first = jnp.mean(e, axis=-1, keepdims=True)
    second = jnp.mean(e * scaled, axis=-1, keepdims=True)
    return inv_std * (e - first - scaled * second)


class Exchange:
    def __init__(self, plan):
        self.plan = plan
        dp, i = lax.axis_index("dp"), lax.axis_index("mp")
        self.dp, self.i, self.c, self.z = dp, i, dp % 2, dp // 2
        self.sib = (dp + 1 - 2 * self.c, i)
        self.p = plan.ring_at(i)

    def at(self, pos):
        return self.plan.ring_at((pos + 2 * self.plan.n_mp) % self.plan.n_mp)

    def across(self, b):
        return self.z + (1 << b) * (1 - 2 * (self.z // (1 << b) % 2))

    def z_units(self, b, far):
        n_z = self.plan.n_z
        base = self.across(b) if far else self.z
        return [(base + m * (2 << b)) % n_z for m in range(n_z // (2 << b))]

    def z_slot(self, b, m):
        return self.plan.n_z // (2 << b) - 1 + m

    def z_device(self, b):
        return (self.across(b) * 2 + self.c, self.i)

    def greet(self):
        plan = self.plan
        barrier = pltpu.get_barrier_semaphore()
        partners = [self.sib]
        partners += [self.z_device(b) for b in range(plan.bits)]
        partners += [(self.dp, (self.i + k) % plan.n_mp) for k in range(1, plan.n_mp)]
        for partner in partners:
            pl.semaphore_signal(barrier, inc=1, device_id=partner, device_id_type=MESH)
        return lambda: pl.semaphore_wait(barrier, len(partners))

    def push(self, src, dst, send, recv, device):
        return pltpu.make_async_remote_copy(
            src_ref=src, dst_ref=dst, send_sem=send, recv_sem=recv, device_id=device, device_id_type=MESH
        )


class Gather:
    def __init__(self, ex, ref, sems, tile=slice(None)):
        self.ex, self.ref, self.tile = ex, ref, tile
        self.zs, self.zr, self.rs, self.rr, self.ss, self.sr = sems

    def z_copy(self, b, m):
        ex = self.ex
        view = self.ref.at[ex.i, ex.z_units(b, False)[m], ex.c, self.tile]
        at = ex.z_slot(b, m)
        return ex.push(view, view, self.zs.at[at], self.zr.at[at], ex.z_device(b))

    def ring_view(self, origin, s, d):
        n_z, half = self.ex.plan.n_z, self.ex.plan.half
        units = pl.ds(s * (n_z // 2), n_z // 2) if d == half else pl.ds(0, n_z)
        return self.ref.at[origin, units, self.ex.c, self.tile]

    def ring_copy(self, s, d):
        ex = self.ex
        sign = 1 - 2 * s
        view = self.ring_view(ex.at(ex.p - sign * (d - 1)), s, d)
        return ex.push(view, view, self.rs.at[s, d - 1], self.rr.at[s, d - 1], (ex.dp, ex.at(ex.p + sign)))

    def sib_copy(self, offset):
        ex = self.ex
        at = (offset + ex.plan.n_mp) % ex.plan.n_mp
        view = self.ref.at[ex.at(ex.p + offset), :, ex.c, self.tile]
        return ex.push(view, view, self.ss.at[at], self.sr.at[at], ex.sib)

    def start(self):
        for b in range(self.ex.plan.bits):
            self.z_copy(b, 0).start()

    def z_sizes(self):
        n_z = self.ex.plan.n_z
        return [(b, n_z // (2 << b)) for b in range(self.ex.plan.bits)]

    def spread(self):
        sizes = self.z_sizes()
        for b, count in reversed(sizes[:-1]):
            for m in range(sizes[b + 1][1]):
                self.z_copy(b + 1, m).wait_recv()
            for m in range(1, count):
                self.z_copy(b, m).start()

    def column(self):
        for m in range(self.z_sizes()[0][1]):
            self.z_copy(0, m).wait_recv()
        for s in range(2):
            self.ring_copy(s, 1).start()
        self.sib_copy(0).start()

    def hop(self, d):
        half = self.ex.plan.half
        for s in range(2):
            self.ring_copy(s, d).wait_recv()
            if d < half:
                self.ring_copy(s, d + 1).start()
                self.sib_copy(-d if s == 0 else d).start()
        if d == half:
            self.sib_copy(half).start()

    def wait_sib(self, offset):
        self.sib_copy(offset).wait_recv()

    def wait_sent(self, offset):
        half = self.ex.plan.half
        self.sib_copy(offset).wait_send()
        if offset == 0:
            for b, count in self.z_sizes():
                for m in range(count):
                    self.z_copy(b, m).wait_send()
            for s in range(2):
                self.ring_copy(s, 1).wait_send()
        elif abs(offset) < half:
            self.ring_copy(0 if offset < 0 else 1, abs(offset) + 1).wait_send()


class RingFirst(Gather):
    def ring_view(self, origin, s, d):
        ex = self.ex
        rows = ex.plan.row_half(s, self.ref.shape[3]) if d == ex.plan.half else slice(None)
        return self.ref.at[origin, ex.z, ex.c, rows]

    def panel_copy(self, offset, b, m):
        ex = self.ex
        view = self.ref.at[ex.at(ex.p + offset), ex.z_units(b, False)[m], ex.c]
        at = (offset + ex.plan.n_mp) % ex.plan.n_mp, ex.z_slot(b, m)
        return ex.push(view, view, self.zs.at[at], self.zr.at[at], ex.z_device(b))

    def begin(self, offset):
        for b in range(self.ex.plan.bits):
            self.panel_copy(offset, b, 0).start()

    def circle(self):
        for s in range(2):
            self.ring_copy(s, 1).start()

    def hop(self, d):
        half = self.ex.plan.half
        for s in range(2):
            self.ring_copy(s, d).wait_recv()
            if d < half:
                self.ring_copy(s, d + 1).start()
        if d < half:
            self.begin(-d)
            self.begin(d)
        else:
            self.begin(half)

    def spread(self, offset):
        sizes = self.z_sizes()
        for b, count in reversed(sizes[:-1]):
            for m in range(sizes[b + 1][1]):
                self.panel_copy(offset, b + 1, m).wait_recv()
            for m in range(1, count):
                self.panel_copy(offset, b, m).start()

    def column(self, offset):
        for m in range(self.z_sizes()[0][1]):
            self.panel_copy(offset, 0, m).wait_recv()
        self.sib_copy(offset).start()

    def wait_sent(self, offset):
        half = self.ex.plan.half
        self.sib_copy(offset).wait_send()
        for b, count in self.z_sizes():
            for m in range(count):
                self.panel_copy(offset, b, m).wait_send()
        if offset == 0:
            for s in range(2):
                self.ring_copy(s, 1).wait_send()
        elif abs(offset) < half:
            self.ring_copy(0 if offset < 0 else 1, abs(offset) + 1).wait_send()


class Reduce:
    def __init__(self, ex, ref, tile, other, ring, last, sems):
        self.ex, self.ref, self.tile = ex, ref, tile
        self.other, self.ring, self.last = other, ring, last
        self.ss, self.sr, self.rs, self.rr, self.zs, self.zr = sems

    def sib_copy(self, offset):
        ex = self.ex
        at = (offset + ex.plan.n_mp) % ex.plan.n_mp
        view = self.ref.at[ex.at(ex.p + offset), :, 1 - ex.c, self.tile]
        return ex.push(view, self.other.at[at], self.ss.at[at], self.sr.at[at], ex.sib)

    def ring_views(self, dest, s, d, part):
        plan = self.ex.plan
        at, count = plan.slots(d)
        first = 0
        if d == plan.half:
            first = s * count
        elif part is not None:
            count = plan.n_z // 2
            first, at = part * count, at + part * count
        return self.ref.at[dest, pl.ds(first, count), self.ex.c, self.tile], self.ring.at[s, pl.ds(at, count)]

    def ring_copy(self, s, d, part=None):
        ex = self.ex
        plan = ex.plan
        sign = 1 - 2 * s
        sem = d - 1 if part is None else plan.half - 2 + 2 * part
        view, there = self.ring_views(ex.at(ex.p + sign * d), s, d, part)
        return ex.push(view, there, self.rs.at[s, sem], self.rr.at[s, sem], (ex.dp, ex.at(ex.p + sign)))

    def ring_copies(self, s, d):
        if d == self.ex.plan.half - 1:
            return [self.ring_copy(s, d, part) for part in range(2)]
        return [self.ring_copy(s, d)]

    def z_copy(self, b, m):
        ex = self.ex
        view = self.ref.at[ex.i, ex.z_units(b, True)[m], ex.c, self.tile]
        at = ex.z_slot(b, m)
        return ex.push(view, self.last.at[at], self.zs.at[at], self.zr.at[at], ex.z_device(b))

    def z_sizes(self):
        n_z = self.ex.plan.n_z
        return [(b, n_z // (2 << b)) for b in range(self.ex.plan.bits)]

    def to_sibling(self, offset):
        self.sib_copy(offset).start()

    def add(self, offset, first, count, *terms):
        j = self.ex.at(self.ex.p + offset)

        @pl.loop(0, count)
        def _(u):
            value = self.ref[j, first + u, self.ex.c, self.tile, :].astype(F32)
            for buf, at in terms:
                value = value + buf(at + u).astype(F32)
            self.ref[j, first + u, self.ex.c, self.tile, :] = value.astype(BF)

    def from_sibling(self, offset):
        at = (offset + self.ex.plan.n_mp) % self.ex.plan.n_mp
        self.sib_copy(offset).wait_recv()
        self.add(offset, 0, self.ex.plan.n_z, (lambda u: self.other[at, u], 0))

    def far(self):
        half = self.ex.plan.half
        self.from_sibling(half)
        for s in range(2):
            self.ring_copy(s, half).start()

    def free(self, s):
        half = self.ex.plan.half
        self.from_sibling((1 - 2 * s) * (half - 1))
        self.ring_copy(s, half - 1, 1 - s).start()

    def bound(self, s):
        plan = self.ex.plan
        half = plan.half
        self.ring_copy(s, half).wait_recv()
        at, count = plan.slots(half)
        self.add((1 - 2 * s) * (half - 1), s * count, count, (lambda u: self.ring[s, u], at))
        self.ring_copy(s, half - 1, s).start()

    def wait_ring(self, s, d):
        for copy in self.ring_copies(s, d):
            copy.wait_recv()

    def nearer(self):
        plan = self.ex.plan
        for d in range(plan.half - 2, 0, -1):
            for s in range(2):
                offset = (1 - 2 * s) * d
                self.from_sibling(offset)
                self.wait_ring(s, d + 1)
                self.add(offset, 0, plan.n_z, (lambda u: self.ring[s, u], plan.slots(d + 1)[0]))
                self.ring_copy(s, d).start()

    def home(self):
        plan = self.ex.plan
        for s in range(2):
            self.wait_ring(s, 1)
        self.sib_copy(0).wait_recv()
        at = plan.slots(1)[0]
        self.add(
            0, 0, plan.n_z,
            (lambda u: self.other[0, u], 0),
            (lambda u: self.ring[0, u], at),
            (lambda u: self.ring[1, u], at),
        )
        for m in range(self.z_sizes()[0][1]):
            self.z_copy(0, m).start()

    def along(self):
        ex = self.ex
        for b, count in self.z_sizes()[:-1]:
            for m, unit in enumerate(ex.z_units(b, False)):
                self.z_copy(b, m).wait_recv()
                at = ex.z_slot(b, m)
                self.add(0, unit, 1, (lambda u: self.last[u], at))
            for m in range(count // 2):
                self.z_copy(b + 1, m).start()

    def finish(self):
        ex = self.ex
        self.z_copy(ex.plan.bits - 1, 0).wait_recv()
        return self.ref[ex.i, ex.z, ex.c, self.tile, :].astype(F32) + self.last[0].astype(F32)

    def wait_z_sent(self):
        for b, count in self.z_sizes():
            for m in range(count):
                self.z_copy(b, m).wait_send()

    def wait_sent(self):
        plan = self.ex.plan
        for offset in range(plan.n_mp):
            self.sib_copy(offset).wait_send()
        for s in range(2):
            for d in range(1, plan.half + 1):
                for copy in self.ring_copies(s, d):
                    copy.wait_send()
        self.wait_z_sent()


class RingLast(Reduce):
    def half_rows(self, s):
        return self.ex.plan.row_half(s, self.ref.shape[3])

    def panel_copy(self, offset, b, m):
        ex = self.ex
        view = self.ref.at[ex.at(ex.p + offset), ex.z_units(b, True)[m], ex.c, self.tile]
        at = (offset + ex.plan.n_mp) % ex.plan.n_mp, ex.z_slot(b, m)
        return ex.push(view, self.last.at[at], self.zs.at[at], self.zr.at[at], ex.z_device(b))

    def begin(self, offset):
        self.from_sibling(offset)
        for m in range(self.z_sizes()[0][1]):
            self.panel_copy(offset, 0, m).start()

    def take(self, offset, b):
        ex = self.ex
        q = (offset + ex.plan.n_mp) % ex.plan.n_mp
        for m, unit in enumerate(ex.z_units(b, False)):
            self.panel_copy(offset, b, m).wait_recv()
            self.add(offset, unit, 1, (lambda u: self.last[q, u], ex.z_slot(b, m)))

    def along(self, offset):
        for b, count in self.z_sizes()[:-1]:
            self.take(offset, b)
            for m in range(count // 2):
                self.panel_copy(offset, b + 1, m).start()

    def end(self, offset):
        self.take(offset, self.ex.plan.bits - 1)

    def ring_views(self, dest, s, d, part):
        ex = self.ex
        rows = slice(None)
        if d == ex.plan.half:
            rows = self.half_rows(s)
        elif part is not None:
            rows = self.half_rows(part)
        return self.ref.at[dest, ex.z, ex.c, rows], self.ring.at[s, d - 1, rows]

    def add_rows(self, offset, rows, *terms):
        ex = self.ex
        j = ex.at(ex.p + offset)
        value = self.ref[j, ex.z, ex.c, rows, :].astype(F32)
        for term in terms:
            value = value + term.astype(F32)
        self.ref[j, ex.z, ex.c, rows, :] = value.astype(BF)

    def far(self):
        for s in range(2):
            self.ring_copy(s, self.ex.plan.half).start()

    def free(self, s):
        self.ring_copy(s, self.ex.plan.half - 1, 1 - s).start()

    def bound(self, s):
        plan = self.ex.plan
        half = plan.half
        self.ring_copy(s, half).wait_recv()
        rows = self.half_rows(s)
        self.add_rows((1 - 2 * s) * (half - 1), rows, self.ring[s, half - 1, rows, :])
        self.ring_copy(s, half - 1, s).start()

    def nearer(self):
        for d in range(self.ex.plan.half - 2, 0, -1):
            for s in range(2):
                self.wait_ring(s, d + 1)
                self.add_rows((1 - 2 * s) * d, slice(None), self.ring[s, d])
                self.ring_copy(s, d).start()

    def finish(self):
        ex = self.ex
        for s in range(2):
            self.wait_ring(s, 1)
        value = self.ref[ex.i, ex.z, ex.c].astype(F32)
        return value + self.ring[0, 0].astype(F32) + self.ring[1, 0].astype(F32)

    def wait_z_sent(self):
        for offset in range(self.ex.plan.n_mp):
            for b, count in self.z_sizes():
                for m in range(count):
                    self.panel_copy(offset, b, m).wait_send()


class Rows:
    def __init__(self, ex, src, dst, send, recv, out):
        self.ex, self.src, self.dst, self.send, self.recv, self.out = ex, src, dst, send, recv, out

    def move(self, start):
        ex = self.ex
        plan, i = ex.plan, ex.i
        q = plan.per_seq
        for m in range(MICRO):
            if self.out:
                target, place = (i % plan.n_seq) * q + m, i // plan.n_seq
            else:
                target, place = m * plan.n_seq + i // q, i % q
            far = ex.push(self.src.at[m], self.dst.at[place], self.send.at[m], self.recv.at[place], (ex.dp, target))
            near = pltpu.make_async_copy(self.src.at[m], self.dst.at[place], self.send.at[m])

            @pl.when(target != i)
            def _():
                far.start() if start else far.wait_send()

            @pl.when(target == i)
            def _():
                near.start() if start else near.wait()

    def start(self):
        self.move(True)

    def wait_sent(self):
        self.move(False)

    def wait_here(self):
        ex = self.ex
        plan, i = ex.plan, ex.i
        q = plan.per_seq
        for m in range(MICRO):
            origin = m * plan.n_seq + i // q if self.out else (i % plan.n_seq) * q + m

            @pl.when(origin != i)
            def _():
                ex.push(self.dst.at[m], self.dst.at[m], self.send.at[0], self.recv.at[m], ex.sib).wait_recv()


def step_kernel(plan, n_in, *refs):
    (tab, dev, w_qkv, w_out, w_up, w_down, tok, fv, cot), small = refs[:9], refs[9:n_in]
    (o_out, o_dx, o_df, o_q, o_s, o_o, o_u, o_d) = refs[n_in : n_in + 8]
    (
        gq, go, gu, gd, x3, f3, y3, out3,
        q_other, q_ring, q_last, s_other, s_ring, s_last, o_other, o_ring, o_last, u_other, u_ring, u_last,
        d_other, d_ring, d_last,
        wq, wo, sv, vec, ub, hlt, qkv, otb, lse, mid, h2, h2t, yt,
        big, acc, act, slope, du, dv, dk, dqt, sums, ubg,
    ) = refs[n_in + 8 : n_in + 8 + 46]
    sems = refs[n_in + 8 + 46 :]
    dx3, df3 = y3, f3
    R, C, n_mp, n_dp, n_z = plan.rows, plan.cols, plan.n_mp, plan.n_dp, plan.n_z
    step = 64
    ex = Exchange(plan)
    i, z, c = ex.i, ex.z, ex.c
    Q = Gather(ex, gq, sems[0:6])
    O = Gather(ex, go, sems[6:12])
    U1 = Gather(ex, gu, sems[12:18], plan.row_half(0, R))
    U2 = Gather(ex, gu, sems[18:24], plan.row_half(1, R))
    W = RingFirst(ex, gd, sems[24:30])
    RQ = Reduce(ex, gq, slice(0, R), q_other, q_ring, q_last, sems[30:36])
    RS = Reduce(ex, gq, slice(R, R + 8), s_other, s_ring, s_last, sems[36:42])
    RU = Reduce(ex, gu, slice(0, R), u_other, u_ring, u_last, sems[42:48])
    RO = Reduce(ex, go, slice(0, R // 3), o_other, o_ring, o_last, sems[48:54])
    RD = RingLast(ex, gd, slice(0, R), d_other, d_ring, d_last, sems[54:60])
    a2a = sems[60:72]
    XT = Rows(ex, tok, x3, a2a[0], a2a[1], False)
    XF = Rows(ex, fv, f3, a2a[2], a2a[3], False)
    XY = Rows(ex, cot, y3, a2a[4], a2a[5], False)
    YO = Rows(ex, out3, o_out, a2a[6], a2a[7], True)
    YX = Rows(ex, dx3, o_dx, a2a[8], a2a[9], True)
    YF = Rows(ex, df3, o_df, a2a[10], a2a[11], True)
    near = range(-plan.half + 1, plan.half)

    all_here = ex.greet()
    third = R // 3
    gq[i, z, c, 0:R, 0 : plan.qkv] = w_qkv[...]
    sv[0, 0:8, :] = jnp.zeros((8, plan.qw), F32)
    for r in range(plan.vec_rows):
        pieces = [small[v][...] for v in range(r * plan.spr, min((r + 1) * plan.spr, N_VEC))]
        for k, piece in enumerate(pieces):
            sv[0, r : r + 1, k * 128 : k * 128 + piece.shape[0]] = piece.astype(F32)[None]
    gq[i, z, c, R:, :] = sv[0, 0:8, :].astype(BF)
    for t in range(3):
        go[i, z, c, :, t * plan.group : t * plan.group + plan.out] = w_out[t * third : (t + 1) * third, :]
    gu[i, z, c] = w_up[...]
    gd[i, z, c] = w_down[...]
    all_here()
    Q.start()
    XT.start()
    Q.spread()
    Q.column()
    U1.start()
    U2.start()
    W.begin(0)
    Q.hop(1)
    U1.spread()
    XF.start()
    U2.spread()
    O.start()
    W.circle()
    W.spread(0)
    O.spread()
    U1.column()
    U2.column()
    O.column()
    W.column(0)
    W.hop(1)
    for d in range(2, plan.half + 1):
        Q.hop(d)

    rowdev = dev[:, 0:1]
    row = lambda v: vec[v : v + 1, :]
    lanes = lambda v: slice((v % plan.spr) * 128, (v % plan.spr) * 128 + 128)
    onehot = lambda t, width: (lax.broadcasted_iota(jnp.int32, (128, width), 0) == tab[t : t + 1, :width]).astype(BF)
    e24 = onehot(0, D)
    e96 = onehot(4, C)

    def rows_of(ref3, at, step):
        part = SEQ // MICRO
        return ref3.at[at // (part // step), pl.ds(pl.multiple_of((at % (part // step)) * step, step), step)]

    def blocks(step, body):
        @pl.loop(0, SEQ // step)
        def _(at):
            body(at, pl.ds(pl.multiple_of(at * step, step), step))

    for offset in (*near, plan.half):
        Q.wait_sib(offset)

    for j in range(n_mp):
        for d in range(n_dp):
            rows = slice(d * R, (d + 1) * R)
            wq[rows, j * plan.qkv : (j + 1) * plan.qkv] = gq[j, d // 2, d % 2, 0:R, 0 : plan.qkv]
    for r in range(plan.vec_rows):
        for j in range(n_mp):
            for d in range(n_dp):
                at = j * n_dp + d
                sv[r, at : at + 1, :] = gq[j, d // 2, d % 2, R + r : R + r + 1, :].astype(F32)

    def expand(v, e, owner):
        got = dot(sv[v // plan.spr, :, lanes(v)].astype(BF), e)
        return jnp.sum(jnp.where(owner == rowdev, got, 0.0), axis=0, keepdims=True)

    for v in WIDE:
        vec[v : v + 1, :] = expand(v, e24, tab[1:2, :])
    vec[V_BIAS : V_BIAS + 1, :] = expand(V_BIAS, onehot(2, D), tab[3:4, :])
    for j in range(n_mp):
        ub[j : j + 1, :] = expand(UP_BIAS, e96, tab[5:6, :C] + j * n_dp)

    XT.wait_here()
    XT.wait_sent()

    def first_norm(at, rows):
        n1, _ = norm_stats(rows_of(x3, at, step)[...].astype(F32))
        rows_of(out3, at, step)[...] = (n1 * row(G1) + row(B1)).astype(BF)

    blocks(step, first_norm)
    for d in range(2, plan.half + 1):
        W.hop(d)
    hl = out3[...].reshape(SEQ, D)
    hlt[...] = hl.T
    XF.wait_here()
    XF.wait_sent()

    q = dot(hl, wq[:, 0:D]) + row(QB)
    qkv[:, 0:D] = q.astype(BF) * 0.125
    qkv[:, D : 2 * D] = dot(hl, wq[:, D : 2 * D]).astype(BF)
    v = dot(hl, wq[:, 2 * D : QKV]) + row(V_BIAS)[:, :VFRESH]
    qkv[:, 2 * D : QKV] = v.astype(BF)
    qkv[:, QKV : 3 * D] = f3[...].reshape(SEQ, D // 2)

    B = 256
    head_of = lax.broadcasted_iota(jnp.int32, (1, 128), 1) // HEAD
    keep = lax.broadcasted_iota(jnp.int32, (B, B), 0) <= lax.broadcasted_iota(jnp.int32, (B, B), 1)

    def scores(k2, qm, at):
        s = dot_nt(k2, qm)
        last = jnp.where(keep, s[at * B :, :], -BIG)
        return last if at == 0 else jnp.concatenate([s[: at * B, :], last], axis=0)

    @pl.loop(0, HEADS // 2)
    def _(t):
        cols = lambda base: pl.ds(pl.multiple_of(base + t * 128, 128), 128)
        vt = qkv[:, cols(2 * D)].T
        for e in range(2):
            mask = (head_of == e).astype(BF)
            for at in range(SEQ // B):
                kk = (at + 1) * B
                span = slice(at * B, kk)
                s = scores(qkv[0:kk, cols(D)], qkv[span, cols(0)] * mask, at)
                top = jnp.max(s, axis=0, keepdims=True)
                ex_ = jnp.exp(s - top)
                total = jnp.sum(ex_, axis=0, keepdims=True)
                o = dot(vt[e * HEAD : (e + 1) * HEAD, 0:kk], ex_.astype(BF)) / total
                otb[pl.ds(pl.multiple_of(t * 128 + e * HEAD, HEAD), HEAD), span] = o.astype(BF)
                lse[t, e : e + 1, span] = top + jnp.log(total)

        @pl.when(t == 0)
        def _():
            for d in range(1, plan.half):
                O.hop(d)

        @pl.when(t == 1)
        def _():
            for d in range(1, plan.half):
                U1.hop(d)
                U2.hop(d)
            for offset in near:
                if offset:
                    W.spread(offset)
            XY.start()

        @pl.when(t == 3)
        def _():
            O.hop(plan.half)

        @pl.when(t == 5)
        def _():
            W.spread(plan.half)

    for offset in (*near, plan.half):
        O.wait_sib(offset)
    for j in range(n_mp):
        for d in range(n_dp):
            for t in range(3):
                rows = slice(d * R + t * third, d * R + (t + 1) * third)
                wo[rows, j * plan.out : (j + 1) * plan.out] = go[
                    j, d // 2, d % 2, :, t * plan.group : t * plan.group + plan.out
                ]
    du[:, 0:D] = otb[...].T

    acc[...] = dot(du[:, 0:D], wo[...]) + row(OB)

    def second_norm(at, rows):
        m = rows_of(x3, at, step)[...].astype(F32) + acc[rows, :]
        mid[rows, :] = m
        scaled, _ = norm_stats(m)
        h2[rows, :] = (scaled * row(G2) + row(B2)).astype(BF)

    blocks(step, second_norm)
    for offset in near:
        if offset:
            W.column(offset)
    h2t[...] = h2[...].T
    acc[...] = jnp.zeros_like(acc)
    big[...] = jnp.zeros_like(big)

    offset_of = lambda q: (q + 1) // 2 * (1 - 2 * (q % 2))

    @pl.loop(0, n_mp)
    def _(q):
        j = ex.at(ex.p + offset_of(q))
        for s in range(n_mp):
            offset = plan.half if s == n_mp - 1 else offset_of(s)

            @pl.when(q == s)
            def _():
                if s == n_mp - 2:
                    W.column(plan.half)
                    U1.hop(plan.half)
                    U2.hop(plan.half)
                U1.wait_sib(offset)
                U2.wait_sib(offset)
                W.wait_sib(offset)

        u = dot(h2[...], gu[j].reshape(D, C)) + ub[pl.ds(j, 1), :]
        u2 = u * u
        tangent = jnp.tanh(GELU_C * (u + GELU_A * u2 * u))
        half = 0.5 * (1.0 + tangent)
        a = (u * half).astype(BF)
        act[j] = a
        slope[j] = (
            half + 0.5 * u * (1.0 - tangent * tangent) * GELU_C * (1.0 + 3.0 * GELU_A * u2)
        ).astype(BF)
        acc[...] += dot_nt(a, gd[j].reshape(D, C))

    def finish_out(at, rows):
        rows_of(out3, at, step)[...] = (mid[rows, :] + (acc[rows, :] + row(DB))).astype(BF)

    blocks(step, finish_out)
    YO.start()
    XY.wait_here()
    XY.wait_sent()
    yt[...] = y3[...].reshape(SEQ, D).T

    order = [plan.half]
    for d in range(plan.half - 1, 0, -1):
        order += [-d, d]
    order += [0]

    def nth(q):
        d = plan.half - (q + 1) // 2
        return jnp.where(q == 0, plan.half, jnp.where(q == n_mp - 1, 0, d * (1 - 2 * (q % 2))))

    def leave(offset):
        RD.begin(offset)
        if offset == plan.half:
            RU.far()
        elif abs(offset) == plan.half - 1:
            RU.free(0 if offset > 0 else 1)

    @pl.loop(0, n_mp)
    def _(q):
        j = ex.at(ex.p + nth(q))
        g = (dot(y3[...].reshape(SEQ, D), gd[j].reshape(D, C)) * slope[j].astype(F32)).astype(BF)
        du[:, 0:C] = g
        big[...] += dot_nt(g, gu[j].reshape(D, C))
        for s, offset in enumerate(order):

            @pl.when(q == s)
            def _():
                if s >= 3:
                    leave(order[s - 1])
                W.wait_sent(offset)
                U1.wait_sent(offset)
                U2.wait_sent(offset)

        gd[j] = dot(yt[...], act[j]).astype(BF).reshape(n_z, 2, R, C)
        gu[j] = dot(h2t[...], du[:, 0:C]).astype(BF).reshape(n_z, 2, R, C)
        ubg[pl.ds(j, 1), :] = jnp.sum(du[:, 0:C].astype(F32), axis=0, keepdims=True)
        for s, offset in enumerate(order):

            @pl.when(q == s)
            def _():
                RD.to_sibling(offset)
                RU.to_sibling(offset)
                if s == 2:
                    leave(order[0])
                    leave(order[1])

    sums[...] = jnp.zeros_like(sums)

    def second_back(at, rows):
        dh = big[rows, :]
        dy = rows_of(y3, at, step)[...].astype(F32)
        scaled, inv = norm_stats(mid[rows, :])
        dr = norm_back(dh, scaled, inv, row(G2))
        dmid = dy + dr
        mid[rows, :] = dmid
        low = dmid.astype(BF)
        du[rows, 0:D] = low
        total = lambda a: jnp.sum(a, axis=0, keepdims=True)
        sums[G2 : G2 + 1, :] += total(dh * scaled)
        sums[B2 : B2 + 1, :] += total(dh)
        sums[OB : OB + 1, :] += total(low.astype(F32))
        sums[DB : DB + 1, :] += total(dy)

    blocks(step, second_back)
    for offset in order[:-4]:
        RD.along(offset)
        RD.end(offset)
    for offset in (*near, plan.half):
        O.wait_sent(offset)
        Q.wait_sent(offset)
    for j in range(n_mp):
        g = dot(otb[...], du[:, j * plan.out : (j + 1) * plan.out]).astype(BF).reshape(n_z, 2, 3, third, plan.out)
        for t in range(3):
            go[j, :, :, :, t * plan.group : t * plan.group + plan.out] = g[:, :, t]
    for offset in order:
        RO.to_sibling(offset)
    do = h2
    do[...] = dot_nt(du[:, 0:D], wo[...]).astype(BF)
    RD.begin(0)
    RU.bound(0)
    RO.far()
    RO.free(0)
    RO.free(1)
    RU.bound(1)

    @pl.loop(0, HEADS // 2)
    def _(t):
        cols = lambda base: pl.ds(pl.multiple_of(base + t * 128, 128), 128)
        kt = qkv[:, cols(D)].T
        dot_ = do[:, cols(0)].astype(F32).T
        prod = dot_ * otb[cols(0), :].astype(F32)
        dv[...] = jnp.zeros_like(dv)
        dk[...] = jnp.zeros_like(dk)
        for e in range(2):
            mask = (head_of == e).astype(BF)
            delta = jnp.sum(prod[e * HEAD : (e + 1) * HEAD, :], axis=0, keepdims=True)
            for at in range(SEQ // B):
                kk = (at + 1) * B
                span = slice(at * B, kk)
                qm = qkv[span, cols(0)] * mask
                dom = do[span, cols(0)] * mask
                s = scores(qkv[0:kk, cols(D)], qm, at)
                p = jnp.exp(s - lse[t, e : e + 1, span])
                dp = dot_nt(qkv[0:kk, cols(2 * D)], dom)
                ds = (p * (dp - delta[:, span])).astype(BF)
                dv[0:kk, :] += dot(p.astype(BF), dom)
                dk[0:kk, :] += dot(ds, qm)
                dqt[e * HEAD : (e + 1) * HEAD, span] = dot(kt[e * HEAD : (e + 1) * HEAD, 0:kk], ds)
        qkv[:, cols(0)] = (dqt[...].T * 0.125).astype(BF)
        qkv[:, cols(D)] = dk[...].astype(BF)
        qkv[:, cols(2 * D)] = dv[...].astype(BF)

        @pl.when(t == 3)
        def _():
            RD.along(order[-4])

    df3[...] = qkv[:, QKV : 3 * D].reshape(df3.shape)
    YF.start()
    RO.bound(1)
    for j in range(n_mp):
        g = dot(hlt[...], qkv[:, j * plan.qkv : (j + 1) * plan.qkv]).astype(BF)
        gq[j, :, :, 0:R, 0 : plan.qkv] = g.reshape(n_z, 2, R, plan.qkv)
    for offset in order:
        RQ.to_sibling(offset)
    RO.bound(0)
    RD.along(order[-3])
    acc[...] = dot_nt(qkv[:, 0:QKV], wq[...])
    RD.along(order[-2])

    def first_back(at, rows):
        n1, inv = norm_stats(rows_of(x3, at, step)[...].astype(F32))
        dh = acc[rows, :]
        dr = norm_back(dh, n1, inv, row(G1))
        rows_of(dx3, at, step)[...] = (mid[rows, :] + dr).astype(BF)
        total = lambda a: jnp.sum(a, axis=0, keepdims=True)
        sums[G1 : G1 + 1, :] += total(dh * n1)
        sums[B1 : B1 + 1, :] += total(dh)
        sums[QB : QB + 1, :] += total(qkv[rows, 0:D].astype(F32))
        sums[V_BIAS : V_BIAS + 1, 0:VFRESH] += total(qkv[rows, 2 * D : QKV].astype(F32))

    blocks(step, first_back)
    RQ.far()
    RQ.free(0)
    RQ.free(1)

    def collect(g, e, owner):
        return dot_nt(jnp.where(owner == rowdev, g, 0.0).astype(BF), e)

    for v in WIDE:
        sv[v // plan.spr, :, lanes(v)] = collect(sums[v : v + 1, :], e24, tab[1:2, :])
    sv[V_BIAS // plan.spr, :, lanes(V_BIAS)] = collect(sums[V_BIAS : V_BIAS + 1, :], onehot(2, D), tab[3:4, :])
    got = collect(ubg[0:1, :], e96, tab[5:6, :C])
    for j in range(1, n_mp):
        got = got + collect(ubg[j : j + 1, :], e96, tab[5:6, :C] + j * n_dp)
    sv[UP_BIAS // plan.spr, :, lanes(UP_BIAS)] = got
    at8 = lax.broadcasted_iota(jnp.int32, (8, plan.qw), 0)
    for j in range(n_mp):
        for d in range(n_dp):
            at = j * n_dp + d
            value = jnp.zeros((8, plan.qw), F32)
            for r in range(plan.vec_rows):
                value = jnp.where(at8 == r, sv[r, at : at + 1, :], value)
            gq[j, d // 2, d % 2, R:, :] = value.astype(BF)
    for offset in order:
        RS.to_sibling(offset)
    RD.along(order[-1])
    RS.far()
    RS.free(0)
    RS.free(1)
    RO.nearer()
    RO.home()
    RU.nearer()
    RU.home()
    RS.bound(1)
    RS.bound(0)
    RS.nearer()
    RS.home()
    RD.end(order[-4])
    RD.far()
    RQ.bound(1)
    RS.along()
    RQ.bound(0)
    RO.along()
    o_s[...] = RS.finish()
    RD.end(order[-3])
    RD.free(1)
    RD.bound(1)
    RQ.nearer()
    RQ.home()
    YX.start()
    RD.end(order[-2])
    RD.free(0)
    RD.bound(0)
    o_o[...] = RO.finish()
    RU.along()
    RD.end(order[-1])
    RD.nearer()
    RQ.along()
    o_d[...] = RD.finish()
    o_u[...] = RU.finish()
    o_q[...] = RQ.finish()
    for r in (RU, RD, RO, RQ, RS):
        r.wait_sent()
    for r in (YO, YF, YX):
        r.wait_sent()
        r.wait_here()


def step(plan, w_qkv, w_out, w_up, w_down, tok, fv, cot, small):
    R, C, n_mp, n_z, n = plan.rows, plan.cols, plan.n_mp, plan.n_z, plan.n
    count = np.arange(D, dtype=np.int32)
    tab = np.zeros((8, D), np.int32)
    for at, width in ((0, D // n), (2, VFRESH // n), (4, FF // n)):
        tab[at], tab[at + 1] = count % width, count // width
    r = np.arange(n, dtype=np.int32)
    dev = np.tile(((r % plan.n_dp) * n_mp + r // plan.n_dp)[:, None], (1, 128))
    vm = pltpu.VMEM
    dma = pltpu.SemaphoreType.DMA
    wide = lambda t: vm((SEQ, D), t)
    tall = lambda t: vm((D, SEQ), t)
    panel = lambda rows, cols: vm((n_mp, n_z, 2, rows, cols), BF)

    def sums(rows, cols):
        ring = n_z // 2 + (plan.half - 1) * n_z
        return [
            vm((n_mp, n_z, rows, cols), BF),
            vm((2, ring, rows, cols), BF),
            vm((n_z - 1, rows, cols), BF),
        ]

    def ring_last(rows, cols):
        return [
            vm((n_mp, n_z, rows, cols), BF),
            vm((2, plan.half, rows, cols), BF),
            vm((n_mp, n_z - 1, rows, cols), BF),
        ]

    panel_z = [dma((n_mp, n_z - 1))] * 2
    gather_sems = [dma((n_z - 1,))] * 2 + [dma((2, plan.half))] * 2 + [dma((n_mp,))] * 2
    reduce_sems = [dma((n_mp,))] * 2 + [dma((2, plan.half + 1))] * 2 + [dma((n_z - 1,))] * 2
    shape = jax.ShapeDtypeStruct
    ins = (jnp.asarray(tab), jnp.asarray(dev), w_qkv, w_out, w_up, w_down, tok, fv, cot, *small)
    return pl.pallas_call(
        functools.partial(step_kernel, plan, len(ins)),
        name="step",
        out_shape=(
            shape(tok.shape, BF),
            shape(tok.shape, BF),
            shape(fv.shape, BF),
            shape((R, plan.qw), F32),
            shape((8, plan.qw), F32),
            shape((R // 3, C), F32),
            shape((R, C), F32),
            shape((R, C), F32),
        ),
        in_specs=[IN_VMEM] * 6 + [ANY] * 3 + [IN_VMEM] * N_VEC,
        out_specs=(ANY,) * 3 + (IN_VMEM,) * 5,
        scratch_shapes=[
            panel(R + 8, plan.qw), panel(R // 3, C), panel(R, C), panel(R, C),
            vm(tok.shape, BF), vm(fv.shape, BF), vm(cot.shape, BF),
            vm(tok.shape, BF),
            *sums(R, plan.qw), *sums(8, plan.qw), *sums(R // 3, C), *sums(R, C), *ring_last(R, C),
            vm((D, QKV), BF), vm((D, D), BF),
            vm((plan.vec_rows, n, plan.qw), F32), vm((16, D), F32), vm((max(8, n_mp), C), F32),
            tall(BF), vm((SEQ, 3 * D), BF), tall(BF),
            vm((HEADS // 2, 8, SEQ), F32),
            wide(F32), wide(BF), tall(BF), tall(BF),
            wide(F32), wide(F32), vm((n_mp, SEQ, C), BF), vm((n_mp, SEQ, C), BF), wide(BF),
            vm((SEQ, 128), F32), vm((SEQ, 128), F32), vm((128, SEQ), F32),
            vm((16, D), F32), vm((max(8, n_mp), C), F32),
            *(gather_sems * 4),
            *(panel_z + gather_sems[2:]),
            *(reduce_sems * 4),
            *(reduce_sems[:4] + panel_z),
            *([dma((MICRO,))] * 12),
        ],
        compiler_params=pltpu.CompilerParams(
            collective_id=0, has_side_effects=True, vmem_limit_bytes=63 << 20
        ),
    )(*ins)


def unpack_kernel(plan, widths, *refs):
    (r1, r2, r3, t_q, t_s, t_o, t_u, t_d), outs, sem = refs[:8], refs[8:24], refs[24]
    moves = [pltpu.make_async_copy(src, dst, sem.at[k]) for k, (src, dst) in enumerate(zip((r1, r2, r3), outs[:3]))]
    for move in moves:
        move.start()
    outs[5][...] = t_q[:, 0 : plan.qkv]
    third = plan.rows // 3
    for t in range(3):
        outs[8][t * third : (t + 1) * third, :] = t_o[:, t * plan.group : t * plan.group + plan.out]
    outs[12][...] = t_u[...]
    outs[14][...] = t_d[...]
    for v, at in enumerate((3, 4, 6, 7, 9, 10, 11, 13, 15)):
        row, lane = v // plan.spr, (v % plan.spr) * 128
        outs[at][...] = t_s[row, lane : lane + widths[v]]
    for move in moves:
        move.wait()


def unpack(plan, summed, widths):
    shape = lambda *dims: jax.ShapeDtypeStruct(dims, F32)
    vec = [shape(w) for w in widths]
    R, C = plan.rows, plan.cols
    out_shape = [jax.ShapeDtypeStruct(r.shape, BF) for r in summed[:3]]
    out_shape += [vec[0], vec[1], shape(R, plan.qkv), vec[2], vec[3], shape(R, plan.out)]
    out_shape += [vec[4], vec[5], vec[6], shape(R, C), vec[7], shape(R, C), vec[8]]
    return pl.pallas_call(
        functools.partial(unpack_kernel, plan, widths),
        name="unpack",
        out_shape=tuple(out_shape),
        in_specs=[IN_VMEM] * 3 + [IN_VMEM] * 5,
        out_specs=(ANY,) * 3 + (IN_VMEM,) * 13,
        scratch_shapes=[pltpu.SemaphoreType.DMA((3,))],
    )(*summed)


def shards(
    plan, tokens, first_values, out_cot, ln1_gain, ln1_bias, w_qkv, q_bias, v_bias, w_out, out_bias,
    ln2_gain, ln2_bias, w_up, up_bias, w_down, down_bias,
):
    small = (ln1_gain, ln1_bias, q_bias, v_bias, out_bias, ln2_gain, ln2_bias, up_bias, down_bias)
    summed = step(plan, w_qkv, w_out, w_up, w_down.T, tokens, first_values, out_cot, small)
    outs = unpack(plan, summed, [s.shape[0] for s in small])
    return (*outs[:14], outs[14].T, outs[15])


def solution(mesh):
    plan = Plan(mesh)
    line = P(("dp", "mp"))
    rows = P(None, ("dp", "mp"), None)
    block = P("dp", "mp")
    grads = (line, line, block, line, line, block, line, line, line, block, line, P("mp", "dp"), line)
    return jax.shard_map(
        functools.partial(shards, plan),
        mesh=mesh,
        in_specs=(rows, rows, rows) + grads,
        out_specs=(rows, rows, rows) + grads,
        check_vma=False,
    )
```

```python
import functools

import jax
import jax.numpy as jnp
import numpy as np
from jax import lax
from jax.experimental import pallas as pl
from jax.experimental.pallas import tpu as pltpu
from jax.sharding import PartitionSpec as P

D = 768
HEADS = 12
HEAD = 64
FF = 3072
MICRO = 4
QKV = 1920
SEQ = 512
VFRESH = 384

EPS = 1e-05
BIG = 1e30
GELU_C = 0.7978845608028654
GELU_A = 0.044715
MESH = pl.DeviceIdType.MESH
ANY = pl.BlockSpec(memory_space=pl.ANY)
IN_VMEM = pl.BlockSpec(memory_space=pltpu.VMEM)
BF, F32 = jnp.bfloat16, jnp.float32

WIDE = (0, 1, 2, 4, 5, 6, 8)
V_BIAS, UP_BIAS = 3, 7
G1, B1, QB, OB, G2, B2, DB = WIDE
N_VEC = 9


class Plan:
    def __init__(self, mesh):
        self.n_dp = mesh.shape["dp"]
        self.n_mp = mesh.shape["mp"]
        self.n = self.n_dp * self.n_mp
        self.n_z = self.n_dp // 2
        self.rows = D // self.n_dp
        self.cols = FF // self.n_mp
        self.qkv = QKV // self.n_mp
        self.out = D // self.n_mp
        self.qw = -(-self.qkv // 128) * 128
        self.parts = self.cols // self.out
        self.spr = self.qw // 128
        self.vec_rows = -(-N_VEC // self.spr)
        self.half = self.n_mp // 2
        self.per_seq = SEQ // (SEQ // MICRO)
        self.n_seq = self.n_mp // MICRO
        assert self.parts * self.out == self.cols and self.rows % (8 * self.parts) == 0 and self.vec_rows <= 8
        self.bits = self.n_z.bit_length() - 1
        assert self.n_seq * MICRO == self.n_mp and self.n_z == 1 << self.bits and self.bits > 0

    def ring_at(self, i):
        return i + (i // self.half) * (self.n_mp - 1 + self.half - 2 * i)

    def row_half(self, s, rows):
        middle = -(-rows // 32) * 16 if rows > 16 else 8
        return slice(middle, rows) if s else slice(0, middle)

    def slots(self, d):
        if d == self.half:
            return 0, self.n_z // 2
        return self.n_z // 2 + (d - 1) * self.n_z, self.n_z


def dot(a, b):
    return jnp.dot(a, b, preferred_element_type=F32)


def dot_nt(a, b):
    return lax.dot_general(a, b, (((1,), (1,)), ((), ())), preferred_element_type=F32)


def chunks(rows, step, body):
    @pl.loop(0, rows // step)
    def _(at):
        body(pl.ds(pl.multiple_of(at * step, step), step))


def norm_stats(r):
    average = jnp.mean(r, axis=-1, keepdims=True)
    centred = r - average
    variance = jnp.mean(centred * centred, axis=-1, keepdims=True)
    inv_std = lax.rsqrt(variance + EPS)
    return centred * inv_std, inv_std


def norm_back(grad_out, scaled, inv_std, gain):
    e = grad_out * gain
    first = jnp.mean(e, axis=-1, keepdims=True)
    second = jnp.mean(e * scaled, axis=-1, keepdims=True)
    return inv_std * (e - first - scaled * second)


class Exchange:
    def __init__(self, plan):
        self.plan = plan
        dp, i = lax.axis_index("dp"), lax.axis_index("mp")
        self.dp, self.i, self.c, self.z = dp, i, dp % 2, dp // 2
        self.sib = (dp + 1 - 2 * self.c, i)
        self.p = plan.ring_at(i)

    def at(self, pos):
        return self.plan.ring_at((pos + 2 * self.plan.n_mp) % self.plan.n_mp)

    def across(self, b):
        return self.z + (1 << b) * (1 - 2 * (self.z // (1 << b) % 2))

    def z_units(self, b, far):
        n_z = self.plan.n_z
        base = self.across(b) if far else self.z
        return [(base + m * (2 << b)) % n_z for m in range(n_z // (2 << b))]

    def z_slot(self, b, m):
        return self.plan.n_z // (2 << b) - 1 + m

    def z_device(self, b):
        return (self.across(b) * 2 + self.c, self.i)

    def greet(self):
        plan = self.plan
        barrier = pltpu.get_barrier_semaphore()
        partners = [self.sib]
        partners += [self.z_device(b) for b in range(plan.bits)]
        partners += [(self.dp, (self.i + k) % plan.n_mp) for k in range(1, plan.n_mp)]
        for partner in partners:
            pl.semaphore_signal(barrier, inc=1, device_id=partner, device_id_type=MESH)
        return lambda: pl.semaphore_wait(barrier, len(partners))

    def push(self, src, dst, send, recv, device):
        return pltpu.make_async_remote_copy(
            src_ref=src, dst_ref=dst, send_sem=send, recv_sem=recv, device_id=device, device_id_type=MESH
        )


class Gather:
    def __init__(self, ex, ref, sems, tile=slice(None)):
        self.ex, self.ref, self.tile = ex, ref, tile
        self.zs, self.zr, self.rs, self.rr, self.ss, self.sr = sems

    def z_copy(self, b, m):
        ex = self.ex
        view = self.ref.at[ex.i, ex.z_units(b, False)[m], ex.c, self.tile]
        at = ex.z_slot(b, m)
        return ex.push(view, view, self.zs.at[at], self.zr.at[at], ex.z_device(b))

    def ring_view(self, origin, s, d):
        n_z, half = self.ex.plan.n_z, self.ex.plan.half
        units = pl.ds(s * (n_z // 2), n_z // 2) if d == half else pl.ds(0, n_z)
        return self.ref.at[origin, units, self.ex.c, self.tile]

    def ring_copy(self, s, d):
        ex = self.ex
        sign = 1 - 2 * s
        view = self.ring_view(ex.at(ex.p - sign * (d - 1)), s, d)
        return ex.push(view, view, self.rs.at[s, d - 1], self.rr.at[s, d - 1], (ex.dp, ex.at(ex.p + sign)))

    def sib_copy(self, offset):
        ex = self.ex
        at = (offset + ex.plan.n_mp) % ex.plan.n_mp
        view = self.ref.at[ex.at(ex.p + offset), :, ex.c, self.tile]
        return ex.push(view, view, self.ss.at[at], self.sr.at[at], ex.sib)

    def start(self):
        for b in range(self.ex.plan.bits):
            self.z_copy(b, 0).start()

    def z_sizes(self):
        n_z = self.ex.plan.n_z
        return [(b, n_z // (2 << b)) for b in range(self.ex.plan.bits)]

    def spread(self):
        sizes = self.z_sizes()
        for b, count in reversed(sizes[:-1]):
            for m in range(sizes[b + 1][1]):
                self.z_copy(b + 1, m).wait_recv()
            for m in range(1, count):
                self.z_copy(b, m).start()

    def column(self):
        for m in range(self.z_sizes()[0][1]):
            self.z_copy(0, m).wait_recv()
        for s in range(2):
            self.ring_copy(s, 1).start()
        self.sib_copy(0).start()

    def hop(self, d):
        half = self.ex.plan.half
        for s in range(2):
            self.ring_copy(s, d).wait_recv()
            if d < half:
                self.ring_copy(s, d + 1).start()
                self.sib_copy(-d if s == 0 else d).start()
        if d == half:
            self.sib_copy(half).start()

    def wait_sib(self, offset):
        self.sib_copy(offset).wait_recv()

    def wait_sent(self, offset):
        half = self.ex.plan.half
        self.sib_copy(offset).wait_send()
        if offset == 0:
            for b, count in self.z_sizes():
                for m in range(count):
                    self.z_copy(b, m).wait_send()
            for s in range(2):
                self.ring_copy(s, 1).wait_send()
        elif abs(offset) < half:
            self.ring_copy(0 if offset < 0 else 1, abs(offset) + 1).wait_send()


class RingFirst(Gather):
    def ring_view(self, origin, s, d):
        ex = self.ex
        rows = ex.plan.row_half(s, self.ref.shape[3]) if d == ex.plan.half else slice(None)
        return self.ref.at[origin, ex.z, ex.c, rows]

    def panel_copy(self, offset, b, m):
        ex = self.ex
        view = self.ref.at[ex.at(ex.p + offset), ex.z_units(b, False)[m], ex.c]
        at = (offset + ex.plan.n_mp) % ex.plan.n_mp, ex.z_slot(b, m)
        return ex.push(view, view, self.zs.at[at], self.zr.at[at], ex.z_device(b))

    def begin(self, offset):
        for b in range(self.ex.plan.bits):
            self.panel_copy(offset, b, 0).start()

    def circle(self):
        for s in range(2):
            self.ring_copy(s, 1).start()

    def hop(self, d):
        half = self.ex.plan.half
        for s in range(2):
            self.ring_copy(s, d).wait_recv()
            if d < half:
                self.ring_copy(s, d + 1).start()
        if d < half:
            self.begin(-d)
            self.begin(d)
        else:
            self.begin(half)

    def spread(self, offset):
        sizes = self.z_sizes()
        for b, count in reversed(sizes[:-1]):
            for m in range(sizes[b + 1][1]):
                self.panel_copy(offset, b + 1, m).wait_recv()
            for m in range(1, count):
                self.panel_copy(offset, b, m).start()

    def column(self, offset):
        for m in range(self.z_sizes()[0][1]):
            self.panel_copy(offset, 0, m).wait_recv()
        self.sib_copy(offset).start()

    def wait_sent(self, offset):
        half = self.ex.plan.half
        self.sib_copy(offset).wait_send()
        for b, count in self.z_sizes():
            for m in range(count):
                self.panel_copy(offset, b, m).wait_send()
        if offset == 0:
            for s in range(2):
                self.ring_copy(s, 1).wait_send()
        elif abs(offset) < half:
            self.ring_copy(0 if offset < 0 else 1, abs(offset) + 1).wait_send()


class Reduce:
    def __init__(self, ex, ref, tile, other, ring, last, sems):
        self.ex, self.ref, self.tile = ex, ref, tile
        self.other, self.ring, self.last = other, ring, last
        self.ss, self.sr, self.rs, self.rr, self.zs, self.zr = sems

    def sib_copy(self, offset):
        ex = self.ex
        at = (offset + ex.plan.n_mp) % ex.plan.n_mp
        view = self.ref.at[ex.at(ex.p + offset), :, 1 - ex.c, self.tile]
        return ex.push(view, self.other.at[at], self.ss.at[at], self.sr.at[at], ex.sib)

    def ring_views(self, dest, s, d, part):
        plan = self.ex.plan
        at, count = plan.slots(d)
        first = 0
        if d == plan.half:
            first = s * count
        elif part is not None:
            count = plan.n_z // 2
            first, at = part * count, at + part * count
        return self.ref.at[dest, pl.ds(first, count), self.ex.c, self.tile], self.ring.at[s, pl.ds(at, count)]

    def ring_copy(self, s, d, part=None):
        ex = self.ex
        plan = ex.plan
        sign = 1 - 2 * s
        sem = d - 1 if part is None else plan.half - 2 + 2 * part
        view, there = self.ring_views(ex.at(ex.p + sign * d), s, d, part)
        return ex.push(view, there, self.rs.at[s, sem], self.rr.at[s, sem], (ex.dp, ex.at(ex.p + sign)))

    def ring_copies(self, s, d):
        if d == self.ex.plan.half - 1:
            return [self.ring_copy(s, d, part) for part in range(2)]
        return [self.ring_copy(s, d)]

    def z_copy(self, b, m):
        ex = self.ex
        view = self.ref.at[ex.i, ex.z_units(b, True)[m], ex.c, self.tile]
        at = ex.z_slot(b, m)
        return ex.push(view, self.last.at[at], self.zs.at[at], self.zr.at[at], ex.z_device(b))

    def z_sizes(self):
        n_z = self.ex.plan.n_z
        return [(b, n_z // (2 << b)) for b in range(self.ex.plan.bits)]

    def to_sibling(self, offset):
        self.sib_copy(offset).start()

    def add(self, offset, first, count, *terms):
        j = self.ex.at(self.ex.p + offset)

        @pl.loop(0, count)
        def _(u):
            value = self.ref[j, first + u, self.ex.c, self.tile, :].astype(F32)
            for buf, at in terms:
                value = value + buf(at + u).astype(F32)
            self.ref[j, first + u, self.ex.c, self.tile, :] = value.astype(BF)

    def from_sibling(self, offset):
        at = (offset + self.ex.plan.n_mp) % self.ex.plan.n_mp
        self.sib_copy(offset).wait_recv()
        self.add(offset, 0, self.ex.plan.n_z, (lambda u: self.other[at, u], 0))

    def far(self):
        half = self.ex.plan.half
        self.from_sibling(half)
        for s in range(2):
            self.ring_copy(s, half).start()

    def free(self, s):
        half = self.ex.plan.half
        self.from_sibling((1 - 2 * s) * (half - 1))
        self.ring_copy(s, half - 1, 1 - s).start()

    def bound(self, s):
        plan = self.ex.plan
        half = plan.half
        self.ring_copy(s, half).wait_recv()
        at, count = plan.slots(half)
        self.add((1 - 2 * s) * (half - 1), s * count, count, (lambda u: self.ring[s, u], at))
        self.ring_copy(s, half - 1, s).start()

    def wait_ring(self, s, d):
        for copy in self.ring_copies(s, d):
            copy.wait_recv()

    def nearer(self):
        plan = self.ex.plan
        for d in range(plan.half - 2, 0, -1):
            for s in range(2):
                offset = (1 - 2 * s) * d
                self.from_sibling(offset)
                self.wait_ring(s, d + 1)
                self.add(offset, 0, plan.n_z, (lambda u: self.ring[s, u], plan.slots(d + 1)[0]))
                self.ring_copy(s, d).start()

    def home(self):
        plan = self.ex.plan
        for s in range(2):
            self.wait_ring(s, 1)
        self.sib_copy(0).wait_recv()
        at = plan.slots(1)[0]
        self.add(
            0, 0, plan.n_z,
            (lambda u: self.other[0, u], 0),
            (lambda u: self.ring[0, u], at),
            (lambda u: self.ring[1, u], at),
        )
        for m in range(self.z_sizes()[0][1]):
            self.z_copy(0, m).start()

    def along(self):
        ex = self.ex
        for b, count in self.z_sizes()[:-1]:
            for m, unit in enumerate(ex.z_units(b, False)):
                self.z_copy(b, m).wait_recv()
                at = ex.z_slot(b, m)
                self.add(0, unit, 1, (lambda u: self.last[u], at))
            for m in range(count // 2):
                self.z_copy(b + 1, m).start()

    def finish(self):
        ex = self.ex
        self.z_copy(ex.plan.bits - 1, 0).wait_recv()
        return self.ref[ex.i, ex.z, ex.c, self.tile, :].astype(F32) + self.last[0].astype(F32)

    def wait_z_sent(self):
        for b, count in self.z_sizes():
            for m in range(count):
                self.z_copy(b, m).wait_send()

    def wait_sent(self):
        plan = self.ex.plan
        for offset in range(plan.n_mp):
            self.sib_copy(offset).wait_send()
        for s in range(2):
            for d in range(1, plan.half + 1):
                for copy in self.ring_copies(s, d):
                    copy.wait_send()
        self.wait_z_sent()


class RingLast(Reduce):
    def half_rows(self, s):
        return self.ex.plan.row_half(s, self.ref.shape[3])

    def panel_copy(self, offset, b, m):
        ex = self.ex
        view = self.ref.at[ex.at(ex.p + offset), ex.z_units(b, True)[m], ex.c, self.tile]
        at = (offset + ex.plan.n_mp) % ex.plan.n_mp, ex.z_slot(b, m)
        return ex.push(view, self.last.at[at], self.zs.at[at], self.zr.at[at], ex.z_device(b))

    def begin(self, offset):
        self.from_sibling(offset)
        for m in range(self.z_sizes()[0][1]):
            self.panel_copy(offset, 0, m).start()

    def take(self, offset, b):
        ex = self.ex
        q = (offset + ex.plan.n_mp) % ex.plan.n_mp
        for m, unit in enumerate(ex.z_units(b, False)):
            self.panel_copy(offset, b, m).wait_recv()
            self.add(offset, unit, 1, (lambda u: self.last[q, u], ex.z_slot(b, m)))

    def along(self, offset):
        for b, count in self.z_sizes()[:-1]:
            self.take(offset, b)
            for m in range(count // 2):
                self.panel_copy(offset, b + 1, m).start()

    def end(self, offset):
        self.take(offset, self.ex.plan.bits - 1)

    def ring_views(self, dest, s, d, part):
        ex = self.ex
        rows = slice(None)
        if d == ex.plan.half:
            rows = self.half_rows(s)
        elif part is not None:
            rows = self.half_rows(part)
        return self.ref.at[dest, ex.z, ex.c, rows], self.ring.at[s, d - 1, rows]

    def add_rows(self, offset, rows, *terms):
        ex = self.ex
        j = ex.at(ex.p + offset)
        value = self.ref[j, ex.z, ex.c, rows, :].astype(F32)
        for term in terms:
            value = value + term.astype(F32)
        self.ref[j, ex.z, ex.c, rows, :] = value.astype(BF)

    def far(self):
        for s in range(2):
            self.ring_copy(s, self.ex.plan.half).start()

    def free(self, s):
        self.ring_copy(s, self.ex.plan.half - 1, 1 - s).start()

    def bound(self, s):
        plan = self.ex.plan
        half = plan.half
        self.ring_copy(s, half).wait_recv()
        rows = self.half_rows(s)
        self.add_rows((1 - 2 * s) * (half - 1), rows, self.ring[s, half - 1, rows, :])
        self.ring_copy(s, half - 1, s).start()

    def nearer(self):
        for d in range(self.ex.plan.half - 2, 0, -1):
            for s in range(2):
                self.wait_ring(s, d + 1)
                self.add_rows((1 - 2 * s) * d, slice(None), self.ring[s, d])
                self.ring_copy(s, d).start()

    def finish(self):
        ex = self.ex
        for s in range(2):
            self.wait_ring(s, 1)
        value = self.ref[ex.i, ex.z, ex.c].astype(F32)
        return value + self.ring[0, 0].astype(F32) + self.ring[1, 0].astype(F32)

    def wait_z_sent(self):
        for offset in range(self.ex.plan.n_mp):
            for b, count in self.z_sizes():
                for m in range(count):
                    self.panel_copy(offset, b, m).wait_send()


class Rows:
    def __init__(self, ex, src, dst, send, recv, out):
        self.ex, self.src, self.dst, self.send, self.recv, self.out = ex, src, dst, send, recv, out

    def move(self, start):
        ex = self.ex
        plan, i = ex.plan, ex.i
        q = plan.per_seq
        for m in range(MICRO):
            if self.out:
                target, place = (i % plan.n_seq) * q + m, i // plan.n_seq
            else:
                target, place = m * plan.n_seq + i // q, i % q
            far = ex.push(self.src.at[m], self.dst.at[place], self.send.at[m], self.recv.at[place], (ex.dp, target))
            near = pltpu.make_async_copy(self.src.at[m], self.dst.at[place], self.send.at[m])

            @pl.when(target != i)
            def _():
                far.start() if start else far.wait_send()

            @pl.when(target == i)
            def _():
                near.start() if start else near.wait()

    def start(self):
        self.move(True)

    def wait_sent(self):
        self.move(False)

    def wait_here(self):
        ex = self.ex
        plan, i = ex.plan, ex.i
        q = plan.per_seq
        for m in range(MICRO):
            origin = m * plan.n_seq + i // q if self.out else (i % plan.n_seq) * q + m

            @pl.when(origin != i)
            def _():
                ex.push(self.dst.at[m], self.dst.at[m], self.send.at[0], self.recv.at[m], ex.sib).wait_recv()


def step_kernel(plan, n_in, *refs):
    (tab, dev, w_qkv, w_out, w_up, w_down, tok, fv, cot), small = refs[:9], refs[9:n_in]
    (o_out, o_dx, o_df, o_q, o_s, o_o, o_u, o_d) = refs[n_in : n_in + 8]
    (
        gq, go, gu, gd, x3, f3, y3, out3,
        q_other, q_ring, q_last, s_other, s_ring, s_last, o_other, o_ring, o_last, u_other, u_ring, u_last,
        d_other, d_ring, d_last,
        wq, wo, sv, vec, ub, hlt, qkv, otb, lse, mid, h2, h2t, yt,
        big, acc, act, slope, du, dv, dk, dqt, sums, ubg,
    ) = refs[n_in + 8 : n_in + 8 + 46]
    sems = refs[n_in + 8 + 46 :]
    dx3, df3 = y3, f3
    R, C, n_mp, n_dp, n_z = plan.rows, plan.cols, plan.n_mp, plan.n_dp, plan.n_z
    step = 64
    part = R // plan.parts
    ex = Exchange(plan)
    i, z, c = ex.i, ex.z, ex.c
    Q = Gather(ex, gq, sems[0:6])
    O = Gather(ex, go, sems[6:12])
    U1 = Gather(ex, gu, sems[12:18], plan.row_half(0, R))
    U2 = Gather(ex, gu, sems[18:24], plan.row_half(1, R))
    W = RingFirst(ex, gd, sems[24:30])
    RQ = Reduce(ex, gq, slice(0, R), q_other, q_ring, q_last, sems[30:36])
    RS = Reduce(ex, gq, slice(R, R + 8), s_other, s_ring, s_last, sems[36:42])
    RU = Reduce(ex, gu, slice(0, R), u_other, u_ring, u_last, sems[42:48])
    RO = Reduce(ex, go, slice(0, part), o_other, o_ring, o_last, sems[48:54])
    RD = RingLast(ex, gd, slice(0, R), d_other, d_ring, d_last, sems[54:60])
    a2a = sems[60:72]
    XT = Rows(ex, tok, x3, a2a[0], a2a[1], False)
    XF = Rows(ex, fv, f3, a2a[2], a2a[3], False)
    XY = Rows(ex, cot, y3, a2a[4], a2a[5], False)
    YO = Rows(ex, out3, o_out, a2a[6], a2a[7], True)
    YX = Rows(ex, dx3, o_dx, a2a[8], a2a[9], True)
    YF = Rows(ex, df3, o_df, a2a[10], a2a[11], True)
    near = range(-plan.half + 1, plan.half)

    all_here = ex.greet()
    gq[i, z, c, 0:R, 0 : plan.qkv] = w_qkv[...]
    sv[0, 0:8, :] = jnp.zeros((8, plan.qw), F32)
    for r in range(plan.vec_rows):
        pieces = [small[v][...] for v in range(r * plan.spr, min((r + 1) * plan.spr, N_VEC))]
        for k, piece in enumerate(pieces):
            sv[0, r : r + 1, k * 128 : k * 128 + piece.shape[0]] = piece.astype(F32)[None]
    gq[i, z, c, R:, :] = sv[0, 0:8, :].astype(BF)
    def rows_of(ref3, at, step):
        part = SEQ // MICRO
        return ref3.at[at // (part // step), pl.ds(pl.multiple_of((at % (part // step)) * step, step), step)]

    def blocks(step, body):
        @pl.loop(0, SEQ // step)
        def _(at):
            body(at, pl.ds(pl.multiple_of(at * step, step), step))

    all_here()
    Q.start()
    XT.start()
    for t in range(plan.parts):
        go[i, z, c, :, t * plan.out : (t + 1) * plan.out] = w_out[t * part : (t + 1) * part, :]
    gu[i, z, c] = w_up[...]
    gd[i, z, c] = w_down[...]
    Q.spread()
    Q.column()
    U1.start()
    U2.start()
    W.begin(0)
    XT.wait_here()
    XT.wait_sent()

    def first_stats(at, rows):
        acc[rows, :], _ = norm_stats(rows_of(x3, at, step)[...].astype(F32))

    blocks(step, first_stats)
    Q.hop(1)
    U1.spread()
    XF.start()
    U2.spread()
    O.start()
    W.circle()
    W.spread(0)
    O.spread()
    U1.column()
    U2.column()
    O.column()
    W.column(0)
    W.hop(1)
    for d in range(2, plan.half + 1):
        Q.hop(d)

    rowdev = dev[:, 0:1]
    row = lambda v: vec[v : v + 1, :]
    lanes = lambda v: slice((v % plan.spr) * 128, (v % plan.spr) * 128 + 128)
    onehot = lambda t, width: (lax.broadcasted_iota(jnp.int32, (128, width), 0) == tab[t : t + 1, :width]).astype(BF)
    e24 = onehot(0, D)
    e96 = onehot(4, C)

    for offset in (*near, plan.half):
        Q.wait_sib(offset)

    for j in range(n_mp):
        for d in range(n_dp):
            rows = slice(d * R, (d + 1) * R)
            wq[rows, j * plan.qkv : (j + 1) * plan.qkv] = gq[j, d // 2, d % 2, 0:R, 0 : plan.qkv]
    for r in range(plan.vec_rows):
        for j in range(n_mp):
            for d in range(n_dp):
                at = j * n_dp + d
                sv[r, at : at + 1, :] = gq[j, d // 2, d % 2, R + r : R + r + 1, :].astype(F32)

    def expand(v, e, owner):
        got = dot(sv[v // plan.spr, :, lanes(v)].astype(BF), e)
        return jnp.sum(jnp.where(owner == rowdev, got, 0.0), axis=0, keepdims=True)

    for v in WIDE:
        vec[v : v + 1, :] = expand(v, e24, tab[1:2, :])
    vec[V_BIAS : V_BIAS + 1, :] = expand(V_BIAS, onehot(2, D), tab[3:4, :])
    for j in range(n_mp):
        ub[j : j + 1, :] = expand(UP_BIAS, e96, tab[5:6, :C] + j * n_dp)

    def first_norm(at, rows):
        rows_of(out3, at, step)[...] = (acc[rows, :] * row(G1) + row(B1)).astype(BF)

    blocks(step, first_norm)
    for d in range(2, plan.half + 1):
        W.hop(d)
    hl = out3[...].reshape(SEQ, D)
    hlt[...] = hl.T
    XF.wait_here()
    XF.wait_sent()

    q = dot(hl, wq[:, 0:D]) + row(QB)
    qkv[:, 0:D] = q.astype(BF) * 0.125
    qkv[:, D : 2 * D] = dot(hl, wq[:, D : 2 * D]).astype(BF)
    v = dot(hl, wq[:, 2 * D : QKV]) + row(V_BIAS)[:, :VFRESH]
    qkv[:, 2 * D : QKV] = v.astype(BF)
    qkv[:, QKV : 3 * D] = f3[...].reshape(SEQ, D // 2)

    B = 256
    head_of = lax.broadcasted_iota(jnp.int32, (1, 128), 1) // HEAD
    keep = lax.broadcasted_iota(jnp.int32, (B, B), 0) <= lax.broadcasted_iota(jnp.int32, (B, B), 1)

    def scores(k2, qm, at):
        s = dot_nt(k2, qm)
        last = jnp.where(keep, s[at * B :, :], -BIG)
        return last if at == 0 else jnp.concatenate([s[: at * B, :], last], axis=0)

    @pl.loop(0, HEADS // 2)
    def _(t):
        cols = lambda base: pl.ds(pl.multiple_of(base + t * 128, 128), 128)
        vt = qkv[:, cols(2 * D)].T
        for e in range(2):
            mask = (head_of == e).astype(BF)
            for at in range(SEQ // B):
                kk = (at + 1) * B
                span = slice(at * B, kk)
                s = scores(qkv[0:kk, cols(D)], qkv[span, cols(0)] * mask, at)
                top = jnp.max(s, axis=0, keepdims=True)
                ex_ = jnp.exp(s - top)
                total = jnp.sum(ex_, axis=0, keepdims=True)
                o = dot(vt[e * HEAD : (e + 1) * HEAD, 0:kk], ex_.astype(BF)) / total
                otb[pl.ds(pl.multiple_of(t * 128 + e * HEAD, HEAD), HEAD), span] = o.astype(BF)
                lse[t, e : e + 1, span] = top + jnp.log(total)

        @pl.when(t == 0)
        def _():
            for d in range(1, plan.half):
                O.hop(d)

        @pl.when(t == 1)
        def _():
            for d in range(1, plan.half):
                U1.hop(d)
                U2.hop(d)
            for offset in near:
                if offset:
                    W.spread(offset)
            XY.start()

        @pl.when(t == 3)
        def _():
            O.hop(plan.half)

        @pl.when(t == 5)
        def _():
            W.spread(plan.half)

    for offset in (*near, plan.half):
        O.wait_sib(offset)
    for j in range(n_mp):
        for d in range(n_dp):
            for t in range(plan.parts):
                rows = slice(d * R + t * part, d * R + (t + 1) * part)
                wo[rows, j * plan.out : (j + 1) * plan.out] = go[
                    j, d // 2, d % 2, :, t * plan.out : (t + 1) * plan.out
                ]
    du[:, 0:D] = otb[...].T

    acc[...] = dot(du[:, 0:D], wo[...]) + row(OB)

    def second_norm(at, rows):
        m = rows_of(x3, at, step)[...].astype(F32) + acc[rows, :]
        mid[rows, :] = m
        scaled, _ = norm_stats(m)
        h2[rows, :] = (scaled * row(G2) + row(B2)).astype(BF)

    blocks(step, second_norm)
    for offset in near:
        if offset:
            W.column(offset)
    h2t[...] = h2[...].T
    acc[...] = jnp.zeros_like(acc)
    big[...] = jnp.zeros_like(big)

    offset_of = lambda q: (q + 1) // 2 * (1 - 2 * (q % 2))

    @pl.loop(0, n_mp)
    def _(q):
        j = ex.at(ex.p + offset_of(q))
        for s in range(n_mp):
            offset = plan.half if s == n_mp - 1 else offset_of(s)

            @pl.when(q == s)
            def _():
                if s == n_mp - 2:
                    W.column(plan.half)
                    U1.hop(plan.half)
                    U2.hop(plan.half)
                U1.wait_sib(offset)
                U2.wait_sib(offset)
                W.wait_sib(offset)

        u = dot(h2[...], gu[j].reshape(D, C)) + ub[pl.ds(j, 1), :]
        u2 = u * u
        tangent = jnp.tanh(GELU_C * (u + GELU_A * u2 * u))
        half = 0.5 * (1.0 + tangent)
        a = (u * half).astype(BF)
        act[j] = a
        slope[j] = (
            half + 0.5 * u * (1.0 - tangent * tangent) * GELU_C * (1.0 + 3.0 * GELU_A * u2)
        ).astype(BF)
        acc[...] += dot_nt(a, gd[j].reshape(D, C))

    def finish_out(at, rows):
        rows_of(out3, at, step)[...] = (mid[rows, :] + (acc[rows, :] + row(DB))).astype(BF)

    blocks(step, finish_out)
    YO.start()
    XY.wait_here()
    XY.wait_sent()
    yt[...] = y3[...].reshape(SEQ, D).T

    order = [plan.half]
    for d in range(plan.half - 1, 0, -1):
        order += [-d, d]
    order += [0]

    def nth(q):
        d = plan.half - (q + 1) // 2
        return jnp.where(q == 0, plan.half, jnp.where(q == n_mp - 1, 0, d * (1 - 2 * (q % 2))))

    def up_leaves(offset):
        if offset == plan.half:
            RU.far()
        elif abs(offset) == plan.half - 1:
            RU.free(0 if offset > 0 else 1)

    @pl.loop(0, n_mp)
    def _(q):
        j = ex.at(ex.p + nth(q))
        g = (dot(y3[...].reshape(SEQ, D), gd[j].reshape(D, C)) * slope[j].astype(F32)).astype(BF)
        du[:, 0:C] = g
        big[...] += dot_nt(g, gu[j].reshape(D, C))
        for s, offset in enumerate(order):

            @pl.when(q == s)
            def _():
                if s >= 1:
                    up_leaves(order[s - 1])
                if s >= 2:
                    RD.begin(order[s - 2])
                W.wait_sent(offset)
                U1.wait_sent(offset)
                U2.wait_sent(offset)

        gu[j] = dot(h2t[...], du[:, 0:C]).astype(BF).reshape(n_z, 2, R, C)
        for s, offset in enumerate(order):

            @pl.when(q == s)
            def _():
                RU.to_sibling(offset)

        gd[j] = dot(yt[...], act[j]).astype(BF).reshape(n_z, 2, R, C)
        ubg[pl.ds(j, 1), :] = jnp.sum(du[:, 0:C].astype(F32), axis=0, keepdims=True)
        for s, offset in enumerate(order):

            @pl.when(q == s)
            def _():
                RD.to_sibling(offset)

    RD.begin(order[-2])
    sums[...] = jnp.zeros_like(sums)

    def second_back(at, rows):
        dh = big[rows, :]
        dy = rows_of(y3, at, step)[...].astype(F32)
        scaled, inv = norm_stats(mid[rows, :])
        dr = norm_back(dh, scaled, inv, row(G2))
        dmid = dy + dr
        mid[rows, :] = dmid
        low = dmid.astype(BF)
        du[rows, 0:D] = low
        total = lambda a: jnp.sum(a, axis=0, keepdims=True)
        sums[G2 : G2 + 1, :] += total(dh * scaled)
        sums[B2 : B2 + 1, :] += total(dh)
        sums[OB : OB + 1, :] += total(low.astype(F32))
        sums[DB : DB + 1, :] += total(dy)

    blocks(step, second_back)
    for offset in order[:-4]:
        RD.along(offset)
        RD.end(offset)
    for offset in (*near, plan.half):
        O.wait_sent(offset)
        Q.wait_sent(offset)
    for j in range(n_mp):
        g = dot(otb[...], du[:, j * plan.out : (j + 1) * plan.out]).reshape(n_z, 2, plan.parts, part, plan.out)
        for t in range(plan.parts):
            go[j, :, :, :, t * plan.out : (t + 1) * plan.out] = g[:, :, t].astype(BF)
    for offset in order:
        RO.to_sibling(offset)
    do = h2
    do[...] = dot_nt(du[:, 0:D], wo[...]).astype(BF)
    RD.begin(0)
    RU.bound(0)
    RO.far()
    RO.free(0)
    RO.free(1)
    RU.bound(1)

    @pl.loop(0, HEADS // 2)
    def _(t):
        cols = lambda base: pl.ds(pl.multiple_of(base + t * 128, 128), 128)
        kt = qkv[:, cols(D)].T
        dot_ = do[:, cols(0)].astype(F32).T
        prod = dot_ * otb[cols(0), :].astype(F32)
        dv[...] = jnp.zeros_like(dv)
        dk[...] = jnp.zeros_like(dk)
        for e in range(2):
            mask = (head_of == e).astype(BF)
            delta = jnp.sum(prod[e * HEAD : (e + 1) * HEAD, :], axis=0, keepdims=True)
            for at in range(SEQ // B):
                kk = (at + 1) * B
                span = slice(at * B, kk)
                qm = qkv[span, cols(0)] * mask
                dom = do[span, cols(0)] * mask
                s = scores(qkv[0:kk, cols(D)], qm, at)
                p = jnp.exp(s - lse[t, e : e + 1, span])
                dp = dot_nt(qkv[0:kk, cols(2 * D)], dom)
                ds = (p * (dp - delta[:, span])).astype(BF)
                dv[0:kk, :] += dot(p.astype(BF), dom)
                dk[0:kk, :] += dot(ds, qm)
                dqt[e * HEAD : (e + 1) * HEAD, span] = dot(kt[e * HEAD : (e + 1) * HEAD, 0:kk], ds)
        qkv[:, cols(0)] = (dqt[...].T * 0.125).astype(BF)
        qkv[:, cols(D)] = dk[...].astype(BF)
        qkv[:, cols(2 * D)] = dv[...].astype(BF)

        @pl.when(t == 3)
        def _():
            RD.along(order[-4])

    df3[...] = qkv[:, QKV : 3 * D].reshape(df3.shape)
    YF.start()
    RO.bound(1)
    for j in range(n_mp):
        g = dot(hlt[...], qkv[:, j * plan.qkv : (j + 1) * plan.qkv]).astype(BF)
        gq[j, :, :, 0:R, 0 : plan.qkv] = g.reshape(n_z, 2, R, plan.qkv)
    for offset in order:
        RQ.to_sibling(offset)
    RO.bound(0)
    RD.along(order[-3])
    acc[...] = dot_nt(qkv[:, 0:QKV], wq[...])
    RD.along(order[-2])

    def first_back(at, rows):
        n1, inv = norm_stats(rows_of(x3, at, step)[...].astype(F32))
        dh = acc[rows, :]
        dr = norm_back(dh, n1, inv, row(G1))
        rows_of(dx3, at, step)[...] = (mid[rows, :] + dr).astype(BF)
        total = lambda a: jnp.sum(a, axis=0, keepdims=True)
        sums[G1 : G1 + 1, :] += total(dh * n1)
        sums[B1 : B1 + 1, :] += total(dh)
        sums[QB : QB + 1, :] += total(qkv[rows, 0:D].astype(F32))
        sums[V_BIAS : V_BIAS + 1, 0:VFRESH] += total(qkv[rows, 2 * D : QKV].astype(F32))

    blocks(step, first_back)
    RQ.far()
    RQ.free(0)
    RQ.free(1)

    def collect(g, e, owner):
        return dot_nt(jnp.where(owner == rowdev, g, 0.0).astype(BF), e)

    for v in WIDE:
        sv[v // plan.spr, :, lanes(v)] = collect(sums[v : v + 1, :], e24, tab[1:2, :])
    sv[V_BIAS // plan.spr, :, lanes(V_BIAS)] = collect(sums[V_BIAS : V_BIAS + 1, :], onehot(2, D), tab[3:4, :])
    got = collect(ubg[0:1, :], e96, tab[5:6, :C])
    for j in range(1, n_mp):
        got = got + collect(ubg[j : j + 1, :], e96, tab[5:6, :C] + j * n_dp)
    sv[UP_BIAS // plan.spr, :, lanes(UP_BIAS)] = got
    at8 = lax.broadcasted_iota(jnp.int32, (8, plan.qw), 0)
    for j in range(n_mp):
        for d in range(n_dp):
            at = j * n_dp + d
            value = jnp.zeros((8, plan.qw), F32)
            for r in range(plan.vec_rows):
                value = jnp.where(at8 == r, sv[r, at : at + 1, :], value)
            gq[j, d // 2, d % 2, R:, :] = value.astype(BF)
    for offset in order:
        RS.to_sibling(offset)
    RD.along(order[-1])
    RS.far()
    RS.free(0)
    RS.free(1)
    RO.nearer()
    RO.home()
    RU.nearer()
    RU.home()
    RS.bound(1)
    RS.bound(0)
    RS.nearer()
    RS.home()
    RD.end(order[-4])
    RD.far()
    RQ.bound(1)
    RS.along()
    RQ.bound(0)
    RO.along()
    o_s[...] = RS.finish()
    RD.end(order[-3])
    RD.free(1)
    RD.bound(1)
    RQ.nearer()
    RQ.home()
    YX.start()
    RD.end(order[-2])
    RD.free(0)
    RD.bound(0)
    o_o[...] = RO.finish()
    RU.along()
    RD.end(order[-1])
    RD.nearer()
    RQ.along()
    o_d[...] = RD.finish()
    o_u[...] = RU.finish()
    o_q[...] = RQ.finish()
    for r in (RU, RD, RO, RQ, RS):
        r.wait_sent()
    for r in (YO, YF, YX):
        r.wait_sent()
        r.wait_here()


def step(plan, w_qkv, w_out, w_up, w_down, tok, fv, cot, small):
    R, C, n_mp, n_z, n = plan.rows, plan.cols, plan.n_mp, plan.n_z, plan.n
    count = np.arange(D, dtype=np.int32)
    tab = np.zeros((8, D), np.int32)
    for at, width in ((0, D // n), (2, VFRESH // n), (4, FF // n)):
        tab[at], tab[at + 1] = count % width, count // width
    r = np.arange(n, dtype=np.int32)
    dev = np.tile(((r % plan.n_dp) * n_mp + r // plan.n_dp)[:, None], (1, 128))
    vm = pltpu.VMEM
    dma = pltpu.SemaphoreType.DMA
    wide = lambda t: vm((SEQ, D), t)
    tall = lambda t: vm((D, SEQ), t)
    panel = lambda rows, cols: vm((n_mp, n_z, 2, rows, cols), BF)

    def sums(rows, cols):
        ring = n_z // 2 + (plan.half - 1) * n_z
        return [
            vm((n_mp, n_z, rows, cols), BF),
            vm((2, ring, rows, cols), BF),
            vm((n_z - 1, rows, cols), BF),
        ]

    def ring_last(rows, cols):
        return [
            vm((n_mp, n_z, rows, cols), BF),
            vm((2, plan.half, rows, cols), BF),
            vm((n_mp, n_z - 1, rows, cols), BF),
        ]

    panel_z = [dma((n_mp, n_z - 1))] * 2
    gather_sems = [dma((n_z - 1,))] * 2 + [dma((2, plan.half))] * 2 + [dma((n_mp,))] * 2
    reduce_sems = [dma((n_mp,))] * 2 + [dma((2, plan.half + 1))] * 2 + [dma((n_z - 1,))] * 2
    shape = jax.ShapeDtypeStruct
    ins = (jnp.asarray(tab), jnp.asarray(dev), w_qkv, w_out, w_up, w_down, tok, fv, cot, *small)
    return pl.pallas_call(
        functools.partial(step_kernel, plan, len(ins)),
        name="step",
        out_shape=(
            shape(tok.shape, BF),
            shape(tok.shape, BF),
            shape(fv.shape, BF),
            shape((R, plan.qw), F32),
            shape((8, plan.qw), F32),
            shape((R // plan.parts, C), F32),
            shape((R, C), F32),
            shape((R, C), F32),
        ),
        in_specs=[IN_VMEM] * 6 + [ANY] * 3 + [IN_VMEM] * N_VEC,
        out_specs=(ANY,) * 3 + (IN_VMEM,) * 5,
        scratch_shapes=[
            panel(R + 8, plan.qw), panel(R // plan.parts, C), panel(R, C), panel(R, C),
            vm(tok.shape, BF), vm(fv.shape, BF), vm(cot.shape, BF),
            vm(tok.shape, BF),
            *sums(R, plan.qw), *sums(8, plan.qw), *sums(R // plan.parts, C), *sums(R, C), *ring_last(R, C),
            vm((D, QKV), BF), vm((D, D), BF),
            vm((plan.vec_rows, n, plan.qw), F32), vm((16, D), F32), vm((max(8, n_mp), C), F32),
            tall(BF), vm((SEQ, 3 * D), BF), tall(BF),
            vm((HEADS // 2, 8, SEQ), F32),
            wide(F32), wide(BF), tall(BF), tall(BF),
            wide(F32), wide(F32), vm((n_mp, SEQ, C), BF), vm((n_mp, SEQ, C), BF), wide(BF),
            vm((SEQ, 128), F32), vm((SEQ, 128), F32), vm((128, SEQ), F32),
            vm((16, D), F32), vm((max(8, n_mp), C), F32),
            *(gather_sems * 4),
            *(panel_z + gather_sems[2:]),
            *(reduce_sems * 4),
            *(reduce_sems[:4] + panel_z),
            *([dma((MICRO,))] * 12),
        ],
        compiler_params=pltpu.CompilerParams(
            collective_id=0, has_side_effects=True, vmem_limit_bytes=63 << 20
        ),
    )(*ins)


def unpack_kernel(plan, widths, *refs):
    (r1, r2, r3, t_q, t_s, t_o, t_u, t_d), outs, sem = refs[:8], refs[8:24], refs[24]
    moves = [pltpu.make_async_copy(src, dst, sem.at[k]) for k, (src, dst) in enumerate(zip((r1, r2, r3), outs[:3]))]
    for move in moves:
        move.start()
    outs[5][...] = t_q[:, 0 : plan.qkv]
    part = plan.rows // plan.parts
    for t in range(plan.parts):
        outs[8][t * part : (t + 1) * part, :] = t_o[:, t * plan.out : (t + 1) * plan.out]
    outs[12][...] = t_u[...]
    outs[14][...] = t_d[...]
    for v, at in enumerate((3, 4, 6, 7, 9, 10, 11, 13, 15)):
        row, lane = v // plan.spr, (v % plan.spr) * 128
        outs[at][...] = t_s[row, lane : lane + widths[v]]
    for move in moves:
        move.wait()


def unpack(plan, summed, widths):
    shape = lambda *dims: jax.ShapeDtypeStruct(dims, F32)
    vec = [shape(w) for w in widths]
    R, C = plan.rows, plan.cols
    out_shape = [jax.ShapeDtypeStruct(r.shape, BF) for r in summed[:3]]
    out_shape += [vec[0], vec[1], shape(R, plan.qkv), vec[2], vec[3], shape(R, plan.out)]
    out_shape += [vec[4], vec[5], vec[6], shape(R, C), vec[7], shape(R, C), vec[8]]
    return pl.pallas_call(
        functools.partial(unpack_kernel, plan, widths),
        name="unpack",
        out_shape=tuple(out_shape),
        in_specs=[IN_VMEM] * 3 + [IN_VMEM] * 5,
        out_specs=(ANY,) * 3 + (IN_VMEM,) * 13,
        scratch_shapes=[pltpu.SemaphoreType.DMA((3,))],
    )(*summed)


def shards(
    plan, tokens, first_values, out_cot, ln1_gain, ln1_bias, w_qkv, q_bias, v_bias, w_out, out_bias,
    ln2_gain, ln2_bias, w_up, up_bias, w_down, down_bias,
):
    small = (ln1_gain, ln1_bias, q_bias, v_bias, out_bias, ln2_gain, ln2_bias, up_bias, down_bias)
    assert tokens.shape[1] * plan.n_mp == SEQ
    summed = step(plan, w_qkv, w_out, w_up, w_down.T, tokens, first_values, out_cot, small)
    outs = unpack(plan, summed, [s.shape[0] for s in small])
    return (*outs[:14], outs[14].T, outs[15])


def layer_norm(inputs, gain_vec, shift_vec):
    average = jnp.mean(inputs, axis=-1, keepdims=True)
    centred = inputs - average
    variance = jnp.mean(centred * centred, axis=-1, keepdims=True)
    inv_std = lax.rsqrt(variance + EPS)
    scaled = centred * inv_std
    return (scaled * gain_vec + shift_vec, scaled, inv_std)


def norm_back_all(grad_out, scaled, inv_std, gain_vec):
    grad_scaled = grad_out * gain_vec
    first_term = jnp.mean(grad_scaled, axis=-1, keepdims=True)
    second_term = jnp.mean(grad_scaled * scaled, axis=-1, keepdims=True)
    grad_in = inv_std * (grad_scaled - first_term - scaled * second_term)
    return (grad_in, jnp.sum(grad_out * scaled, axis=0), jnp.sum(grad_out, axis=0))


def gelu_both(inputs):
    cubic_term = inputs + GELU_A * inputs * inputs * inputs
    tangent = jnp.tanh(GELU_C * cubic_term)
    gelu_out = 0.5 * inputs * (1.0 + tangent)
    gelu_slope = 0.5 * (1.0 + tangent) + 0.5 * inputs * (1.0 - tangent * tangent) * GELU_C * (
        1.0 + 3.0 * GELU_A * inputs * inputs
    )
    return (gelu_out, gelu_slope)


def split_heads(matrix):
    return matrix.reshape(matrix.shape[0], HEADS, HEAD)


def block_scores(query_heads, key_block, row_first, key_first):
    key_heads = split_heads(key_block)
    scores = jnp.einsum(
        "qhd,khd->hqk", query_heads, key_heads, preferred_element_type=jnp.float32
    ) * HEAD ** (-0.5)
    query_pos = row_first + jnp.arange(query_heads.shape[0], dtype=jnp.int32)
    key_pos = key_first + jnp.arange(key_block.shape[0], dtype=jnp.int32)
    allowed = key_pos[None, :] <= query_pos[:, None]
    return (jnp.where(allowed[None], scores, -BIG), allowed, key_heads)


def block_length():
    return 512


def fold_blocks(function, carried, key_block, value_block, key_first):
    row_count = key_block.shape[0]
    block_rows = block_length()
    if block_rows == row_count:
        return function(carried, key_block, value_block, key_first)
    key_parts = key_block.reshape(row_count // block_rows, block_rows, key_block.shape[1])
    value_parts = value_block.reshape(row_count // block_rows, block_rows, value_block.shape[1])
    offsets = key_first + jnp.arange(row_count // block_rows, dtype=jnp.int32) * block_rows

    def step_once(inner_state, element):
        return (function(inner_state, element[0], element[1], element[2]), None)

    result, ignored = lax.scan(step_once, carried, (key_parts, value_parts, offsets))
    return result


def map_blocks(function, key_block, value_block, key_first):
    row_count = key_block.shape[0]
    block_rows = block_length()
    if block_rows == row_count:
        return function(key_block, value_block, key_first)
    key_parts = key_block.reshape(row_count // block_rows, block_rows, key_block.shape[1])
    value_parts = value_block.reshape(row_count // block_rows, block_rows, value_block.shape[1])
    offsets = key_first + jnp.arange(row_count // block_rows, dtype=jnp.int32) * block_rows

    def apply_once(element):
        return function(element[0], element[1], element[2])

    outputs = lax.map(apply_once, (key_parts, value_parts, offsets))
    return outputs.reshape(row_count, outputs.shape[-1])


def attention_forward(queries, keys_low, values_low, row_first):
    query_heads = split_heads(queries)
    row_total = queries.shape[0]

    def online_step(fold_state, key_block, value_block, key_first):
        running_top, running_sum, running_acc = fold_state
        masked, allowed, ignored = block_scores(query_heads, key_block, row_first, key_first)
        new_top = jnp.maximum(running_top, jnp.max(masked, axis=-1))
        weights = jnp.exp(masked - new_top[:, :, None]) * allowed[None]
        shrink = jnp.exp(running_top - new_top)
        running_sum = running_sum * shrink + jnp.sum(weights, axis=-1)
        running_acc = running_acc * shrink[:, :, None] + jnp.einsum(
            "hqk,khd->hqd",
            weights.astype(jnp.bfloat16),
            split_heads(value_block),
            preferred_element_type=jnp.float32,
        )
        return (new_top, running_sum, running_acc)

    start_state = (
        jnp.full((HEADS, row_total), -BIG, jnp.float32),
        jnp.zeros((HEADS, row_total), jnp.float32),
        jnp.zeros((HEADS, row_total, HEAD), jnp.float32),
    )
    running_top, running_sum, running_acc = fold_blocks(
        online_step,
        start_state,
        lax.all_gather(keys_low, "mp", axis=0, tiled=True),
        lax.all_gather(values_low, "mp", axis=0, tiled=True),
        jnp.int32(0),
    )
    attended = (running_acc / running_sum[:, :, None]).transpose(1, 0, 2).reshape(row_total, D)
    return (attended, running_top + jnp.log(running_sum))


def attention_backward(queries, keys_low, values_low, grad_out, attended, log_total, row_first):
    query_heads = split_heads(queries)
    grad_heads = split_heads(grad_out)
    row_total = queries.shape[0]
    score_scale = HEAD ** (-0.5)
    row_delta = jnp.sum(grad_heads.astype(jnp.float32) * split_heads(attended), axis=-1).T
    keys_all, values_all = (
        lax.all_gather(keys_low, "mp", axis=0, tiled=True),
        lax.all_gather(values_low, "mp", axis=0, tiled=True),
    )

    def soft_grads(key_block, value_block, key_first):
        masked, allowed, key_heads = block_scores(query_heads, key_block, row_first, key_first)
        probabilities = jnp.exp(masked - log_total[:, :, None])
        grad_probs = jnp.einsum(
            "qhd,khd->hqk", grad_heads, split_heads(value_block), preferred_element_type=jnp.float32
        )
        grad_scores = (probabilities * (grad_probs - row_delta[:, :, None])).astype(jnp.bfloat16)
        return (probabilities, grad_scores, key_heads)

    def query_step(accum, key_block, value_block, key_first):
        probabilities, grad_scores, key_heads = soft_grads(key_block, value_block, key_first)
        return (
            accum
            + jnp.einsum("hqk,khd->qhd", grad_scores, key_heads, preferred_element_type=jnp.float32)
            * score_scale
        )

    grad_query = fold_blocks(
        query_step, jnp.zeros((row_total, HEADS, HEAD), jnp.float32), keys_all, values_all, 0
    )

    def key_step(key_block, value_block, key_first):
        probabilities, grad_scores, key_heads = soft_grads(key_block, value_block, key_first)
        grad_value = jnp.einsum(
            "hqk,qhd->khd",
            probabilities.astype(jnp.bfloat16),
            grad_heads,
            preferred_element_type=jnp.float32,
        )
        grad_key = (
            jnp.einsum("hqk,qhd->khd", grad_scores, query_heads, preferred_element_type=jnp.float32)
            * score_scale
        )
        return jnp.concatenate(
            [grad_key.reshape(key_block.shape[0], D), grad_value.reshape(key_block.shape[0], D)],
            axis=1,
        )

    key_block = keys_all
    value_block = values_all
    grad_kv = lax.psum_scatter(
        map_blocks(key_step, key_block, value_block, jnp.int32(0)).astype(jnp.bfloat16),
        "mp",
        scatter_dimension=0,
        tiled=True,
    ).astype(jnp.float32)
    return (grad_query.reshape(row_total, D), grad_kv)


def reduce_grads(local_grads):
    row_parts = (
        lax.psum_scatter(
            local_grads[0].astype(jnp.bfloat16), "dp", scatter_dimension=0, tiled=True
        ).astype(jnp.float32),
        lax.psum_scatter(
            local_grads[1].astype(jnp.bfloat16), "dp", scatter_dimension=0, tiled=True
        ).astype(jnp.float32),
        lax.psum_scatter(
            local_grads[2].astype(jnp.bfloat16), "dp", scatter_dimension=0, tiled=True
        ).astype(jnp.float32),
        lax.psum_scatter(
            local_grads[3].astype(jnp.bfloat16), "dp", scatter_dimension=0, tiled=True
        ).astype(jnp.float32),
        lax.psum_scatter(
            local_grads[4].astype(jnp.bfloat16), "dp", scatter_dimension=0, tiled=True
        ).astype(jnp.float32),
        lax.psum_scatter(
            local_grads[5].astype(jnp.bfloat16), "dp", scatter_dimension=0, tiled=True
        ).astype(jnp.float32),
        lax.psum_scatter(
            local_grads[6].astype(jnp.bfloat16), "dp", scatter_dimension=0, tiled=True
        ).astype(jnp.float32),
        lax.psum_scatter(
            local_grads[7].astype(jnp.bfloat16), "dp", scatter_dimension=0, tiled=True
        ).astype(jnp.float32),
        lax.psum_scatter(
            local_grads[8].astype(jnp.bfloat16), "dp", scatter_dimension=0, tiled=True
        ).astype(jnp.float32),
        lax.psum_scatter(
            local_grads[9].astype(jnp.bfloat16), "dp", scatter_dimension=0, tiled=True
        ).astype(jnp.float32),
        lax.psum_scatter(
            local_grads[10].astype(jnp.bfloat16), "dp", scatter_dimension=0, tiled=True
        ).astype(jnp.float32),
        lax.psum_scatter(
            local_grads[11].astype(jnp.bfloat16), "dp", scatter_dimension=1, tiled=True
        ).astype(jnp.float32),
        lax.psum_scatter(
            local_grads[12].astype(jnp.bfloat16), "dp", scatter_dimension=0, tiled=True
        ).astype(jnp.float32),
    )
    row_parts = tuple(row_parts)
    col_parts = tuple(
        (
            lax.psum_scatter(
                row_parts[0].astype(jnp.bfloat16), "mp", scatter_dimension=0, tiled=True
            ).astype(jnp.float32),
            lax.psum_scatter(
                row_parts[1].astype(jnp.bfloat16), "mp", scatter_dimension=0, tiled=True
            ).astype(jnp.float32),
            lax.psum_scatter(
                row_parts[2].astype(jnp.bfloat16), "mp", scatter_dimension=1, tiled=True
            ).astype(jnp.float32),
            lax.psum_scatter(
                row_parts[3].astype(jnp.bfloat16), "mp", scatter_dimension=0, tiled=True
            ).astype(jnp.float32),
            lax.psum_scatter(
                row_parts[4].astype(jnp.bfloat16), "mp", scatter_dimension=0, tiled=True
            ).astype(jnp.float32),
            lax.psum_scatter(
                row_parts[5].astype(jnp.bfloat16), "mp", scatter_dimension=1, tiled=True
            ).astype(jnp.float32),
            lax.psum_scatter(
                row_parts[6].astype(jnp.bfloat16), "mp", scatter_dimension=0, tiled=True
            ).astype(jnp.float32),
            lax.psum_scatter(
                row_parts[7].astype(jnp.bfloat16), "mp", scatter_dimension=0, tiled=True
            ).astype(jnp.float32),
            lax.psum_scatter(
                row_parts[8].astype(jnp.bfloat16), "mp", scatter_dimension=0, tiled=True
            ).astype(jnp.float32),
            lax.psum_scatter(
                row_parts[10].astype(jnp.bfloat16), "mp", scatter_dimension=0, tiled=True
            ).astype(jnp.float32),
            lax.psum_scatter(
                row_parts[12].astype(jnp.bfloat16), "mp", scatter_dimension=0, tiled=True
            ).astype(jnp.float32),
        )
    )
    return col_parts[:9] + (row_parts[9], col_parts[9], row_parts[11], col_parts[10])


def general_shards(
    tokens,
    first_values,
    out_cot,
    ln1_gain,
    ln1_bias,
    w_qkv,
    q_bias,
    v_bias,
    w_out,
    out_bias,
    ln2_gain,
    ln2_bias,
    w_up,
    up_bias,
    w_down,
    down_bias,
):
    near_blocks = tuple(
        (
            lax.all_gather(ln1_gain, "mp", axis=0, tiled=True),
            lax.all_gather(ln1_bias, "mp", axis=0, tiled=True),
            lax.all_gather(w_qkv, "mp", axis=1, tiled=True),
            lax.all_gather(q_bias, "mp", axis=0, tiled=True),
            lax.all_gather(v_bias, "mp", axis=0, tiled=True),
            lax.all_gather(w_out, "mp", axis=1, tiled=True),
            lax.all_gather(out_bias, "mp", axis=0, tiled=True),
            lax.all_gather(ln2_gain, "mp", axis=0, tiled=True),
            lax.all_gather(ln2_bias, "mp", axis=0, tiled=True),
            lax.all_gather(up_bias, "mp", axis=0, tiled=True),
            lax.all_gather(down_bias, "mp", axis=0, tiled=True),
        )
    )
    near_blocks = near_blocks[:9] + (w_up, near_blocks[9], w_down, near_blocks[10])
    params = tuple(
        (
            lax.all_gather(near_blocks[0], "dp", axis=0, tiled=True),
            lax.all_gather(near_blocks[1], "dp", axis=0, tiled=True),
            lax.all_gather(near_blocks[2], "dp", axis=0, tiled=True),
            lax.all_gather(near_blocks[3], "dp", axis=0, tiled=True),
            lax.all_gather(near_blocks[4], "dp", axis=0, tiled=True),
            lax.all_gather(near_blocks[5], "dp", axis=0, tiled=True),
            lax.all_gather(near_blocks[6], "dp", axis=0, tiled=True),
            lax.all_gather(near_blocks[7], "dp", axis=0, tiled=True),
            lax.all_gather(near_blocks[8], "dp", axis=0, tiled=True),
            lax.all_gather(near_blocks[9], "dp", axis=0, tiled=True),
            lax.all_gather(near_blocks[10], "dp", axis=0, tiled=True),
            lax.all_gather(near_blocks[11], "dp", axis=1, tiled=True),
            lax.all_gather(near_blocks[12], "dp", axis=0, tiled=True),
        )
    )
    gain_one = params[0].astype(jnp.float32)
    shift_one = params[1].astype(jnp.float32)
    qkv_full = params[2]
    query_shift = params[3].astype(jnp.float32)
    value_shift = params[4].astype(jnp.float32)
    out_full = params[5]
    out_shift = params[6].astype(jnp.float32)
    gain_two = params[7].astype(jnp.float32)
    shift_two = params[8].astype(jnp.float32)
    up_full = params[9]
    up_shift_all = params[10].astype(jnp.float32)
    down_full = params[11]
    down_shift = params[12].astype(jnp.float32)
    up_cols = up_full.shape[1]
    up_start = 0
    up_start = lax.axis_index("mp") * up_cols
    up_used = lax.dynamic_slice_in_dim(up_shift_all, up_start, up_cols, 0)
    row_total = tokens.shape[1]
    row_first = lax.axis_index("mp") * row_total
    fresh_cols = value_shift.shape[0]
    outputs = []
    grad_inputs = []
    grad_firsts = []
    summed = None
    for micro_index in range(MICRO):
        cot_low = out_cot[micro_index]
        inputs = tokens[micro_index].astype(jnp.float32)
        normed, scaled_one, inv_one = layer_norm(inputs, gain_one, shift_one)
        normed_low = normed.astype(jnp.bfloat16)
        mixed_proj = jnp.dot(normed_low, qkv_full, preferred_element_type=jnp.float32)
        queries = (mixed_proj[:, :D] + query_shift).astype(jnp.bfloat16)
        keys_low = mixed_proj[:, D : 2 * D].astype(jnp.bfloat16)
        values_low = jnp.concatenate(
            [
                (mixed_proj[:, 2 * D :] + value_shift).astype(jnp.bfloat16),
                first_values[micro_index],
            ],
            axis=1,
        )
        attended, log_total = attention_forward(queries, keys_low, values_low, row_first)
        attended_low = attended.astype(jnp.bfloat16)
        middle = inputs + (
            jnp.dot(attended_low, out_full, preferred_element_type=jnp.float32) + out_shift
        )
        normed_two, scaled_two, inv_two = layer_norm(middle, gain_two, shift_two)
        normed_two_low = normed_two.astype(jnp.bfloat16)
        cot_float = cot_low.astype(jnp.float32)
        row_piece = lax.all_gather(normed_two_low, "mp", axis=0, tiled=True)
        hidden = jnp.dot(row_piece, up_full, preferred_element_type=jnp.float32) + up_used
        gelu_out, gelu_slope = gelu_both(hidden)
        active_all = gelu_out.astype(jnp.bfloat16)
        down_part = lax.psum_scatter(
            jnp.dot(active_all, down_full, preferred_element_type=jnp.float32).astype(jnp.bfloat16),
            "mp",
            scatter_dimension=0,
            tiled=True,
        ).astype(jnp.float32)
        result = middle + (down_part + down_shift)
        back_row_piece = lax.all_gather(cot_low, "mp", axis=0, tiled=True)
        grad_active = jnp.einsum(
            "rd,fd->rf", back_row_piece, down_full, preferred_element_type=jnp.float32
        )
        back_gelu_out, back_gelu_slope = gelu_both(hidden)
        grad_hidden = (grad_active * back_gelu_slope).astype(jnp.bfloat16)
        grad_normed_two = lax.psum_scatter(
            jnp.einsum(
                "rf,df->rd", grad_hidden, up_full, preferred_element_type=jnp.float32
            ).astype(jnp.bfloat16),
            "mp",
            scatter_dimension=0,
            tiled=True,
        ).astype(jnp.float32)
        grad_down = jnp.einsum(
            "rf,rd->fd", active_all, back_row_piece, preferred_element_type=jnp.float32
        )
        grad_up = jnp.einsum(
            "rd,rf->df", row_piece, grad_hidden, preferred_element_type=jnp.float32
        )
        up_piece = jnp.sum(grad_hidden.astype(jnp.float32), axis=0)
        grad_up_shift = lax.dynamic_update_slice_in_dim(
            jnp.zeros((FF,), jnp.float32), up_piece, up_start, 0
        )
        grad_norm_two, grad_gain_two, grad_shift_two = norm_back_all(
            grad_normed_two, scaled_two, inv_two, gain_two
        )
        grad_middle = cot_float + grad_norm_two
        grad_branch = grad_middle.astype(jnp.bfloat16)
        grad_out_shift = jnp.sum(grad_branch.astype(jnp.float32), axis=0)
        grad_out_proj = jnp.einsum(
            "rd,re->de", attended_low, grad_branch, preferred_element_type=jnp.float32
        )
        grad_attended = jnp.einsum(
            "re,de->rd", grad_branch, out_full, preferred_element_type=jnp.float32
        ).astype(jnp.bfloat16)
        grad_query, grad_kv = attention_backward(
            queries, keys_low, values_low, grad_attended, attended, log_total, row_first
        )
        grad_query_low = grad_query.astype(jnp.bfloat16)
        grad_kv_low = grad_kv.astype(jnp.bfloat16)
        grad_mixed = jnp.concatenate([grad_query_low, grad_kv_low[:, : D + fresh_cols]], axis=1)
        grad_query_shift = jnp.sum(grad_query_low.astype(jnp.float32), axis=0)
        grad_value_shift = jnp.sum(grad_kv_low[:, D : D + fresh_cols].astype(jnp.float32), axis=0)
        grad_qkv = jnp.einsum(
            "rd,rc->dc", normed_low, grad_mixed, preferred_element_type=jnp.float32
        )
        grad_normed = jnp.einsum(
            "rc,dc->rd", grad_mixed, qkv_full, preferred_element_type=jnp.float32
        )
        grad_norm_one, grad_gain_one, grad_shift_one = norm_back_all(
            grad_normed, scaled_one, inv_one, gain_one
        )
        grad_input = grad_middle + grad_norm_one
        local_grads = (
            grad_gain_one,
            grad_shift_one,
            grad_qkv,
            grad_query_shift,
            grad_value_shift,
            grad_out_proj,
            grad_out_shift,
            grad_gain_two,
            grad_shift_two,
            grad_up,
            grad_up_shift,
            grad_down,
            jnp.sum(cot_float, axis=0),
        )
        result, grad_input, grad_first, local_grads = (
            result.astype(jnp.bfloat16),
            grad_input.astype(jnp.bfloat16),
            grad_kv_low[:, D + fresh_cols :],
            local_grads,
        )
        outputs.append(result)
        grad_inputs.append(grad_input)
        grad_firsts.append(grad_first)
        local_grads = reduce_grads(local_grads)
        summed = local_grads if summed is None else jax.tree.map(jnp.add, summed, local_grads)
    return (
        jnp.stack(outputs),
        jnp.stack(grad_inputs),
        jnp.stack(grad_firsts),
        summed[0],
        summed[1],
        summed[2],
        summed[3],
        summed[4],
        summed[5],
        summed[6],
        summed[7],
        summed[8],
        summed[9],
        summed[10],
        summed[11],
        summed[12],
    )


def solution(mesh):
    whole_sequences = mesh.shape["mp"] == MICRO
    body = functools.partial(shards, Plan(mesh)) if whole_sequences else general_shards
    line = P(("dp", "mp"))
    rows = P(None, ("dp", "mp"), None)
    block = P("dp", "mp")
    grads = (line, line, block, line, line, block, line, line, line, block, line, P("mp", "dp"), line)
    return jax.shard_map(
        body,
        mesh=mesh,
        in_specs=(rows, rows, rows) + grads,
        out_specs=(rows, rows, rows) + grads,
        check_vma=False,
    )
```

```python
import functools

import jax
import jax.numpy as jnp
import numpy as np
from jax import lax
from jax.experimental import pallas as pl
from jax.experimental.pallas import tpu as pltpu
from jax.sharding import PartitionSpec as P

D = 768
HEADS = 12
HEAD = 64
FF = 3072
MICRO = 4
QKV = 1920
SEQ = 512
VFRESH = 384

EPS = 1e-05
BIG = 1e30
GELU_C = 0.7978845608028654
GELU_A = 0.044715
MESH = pl.DeviceIdType.MESH
ANY = pl.BlockSpec(memory_space=pl.ANY)
IN_VMEM = pl.BlockSpec(memory_space=pltpu.VMEM)
BF, F32 = jnp.bfloat16, jnp.float32

WIDE = (0, 1, 2, 4, 5, 6, 8)
V_BIAS, UP_BIAS = 3, 7
G1, B1, QB, OB, G2, B2, DB = WIDE
N_VEC = 9
LANES = 32
UP_ROWS = (UP_BIAS, N_VEC, N_VEC + 1)


class Plan:
    def __init__(self, mesh):
        self.n_dp = mesh.shape["dp"]
        self.n_mp = mesh.shape["mp"]
        self.n = self.n_dp * self.n_mp
        self.n_z = self.n_dp // 2
        self.rows = D // self.n_dp
        self.cols = FF // self.n_mp
        self.qkv = QKV // self.n_mp
        self.out = D // self.n_mp
        self.qw = -(-self.qkv // 128) * 128
        self.parts = self.cols // self.out
        self.spr = self.qw // 128
        self.vec_rows = -(-N_VEC // self.spr)
        self.half = self.n_mp // 2
        self.per_seq = SEQ // (SEQ // MICRO)
        self.n_seq = self.n_mp // MICRO
        assert self.qkv + LANES <= self.qw and D // self.n <= LANES and FF // self.n <= 3 * LANES
        assert self.parts * self.out == self.cols and self.rows % (8 * self.parts) == 0 and self.vec_rows <= 8
        self.bits = self.n_z.bit_length() - 1
        assert self.n_seq * MICRO == self.n_mp and self.n_z == 1 << self.bits and self.bits > 0

    def ring_at(self, i):
        return i + (i // self.half) * (self.n_mp - 1 + self.half - 2 * i)

    def row_half(self, s, rows):
        middle = -(-rows // 32) * 16 if rows > 16 else 8
        return slice(middle, rows) if s else slice(0, middle)

    def slots(self, d):
        if d == self.half:
            return 0, self.n_z // 2
        return self.n_z // 2 + (d - 1) * self.n_z, self.n_z


def dot(a, b):
    return jnp.dot(a, b, preferred_element_type=F32)


def dot_nt(a, b):
    return lax.dot_general(a, b, (((1,), (1,)), ((), ())), preferred_element_type=F32)


def chunks(rows, step, body):
    @pl.loop(0, rows // step)
    def _(at):
        body(pl.ds(pl.multiple_of(at * step, step), step))


def norm_stats(r):
    average = jnp.mean(r, axis=-1, keepdims=True)
    centred = r - average
    variance = jnp.mean(centred * centred, axis=-1, keepdims=True)
    inv_std = lax.rsqrt(variance + EPS)
    return centred * inv_std, inv_std


def norm_back(grad_out, scaled, inv_std, gain):
    e = grad_out * gain
    first = jnp.mean(e, axis=-1, keepdims=True)
    second = jnp.mean(e * scaled, axis=-1, keepdims=True)
    return inv_std * (e - first - scaled * second)


class Exchange:
    def __init__(self, plan):
        self.plan = plan
        dp, i = lax.axis_index("dp"), lax.axis_index("mp")
        self.dp, self.i, self.c, self.z = dp, i, dp % 2, dp // 2
        self.sib = (dp + 1 - 2 * self.c, i)
        self.p = plan.ring_at(i)

    def at(self, pos):
        return self.plan.ring_at((pos + 2 * self.plan.n_mp) % self.plan.n_mp)

    def across(self, b):
        return self.z + (1 << b) * (1 - 2 * (self.z // (1 << b) % 2))

    def z_units(self, b, far):
        n_z = self.plan.n_z
        base = self.across(b) if far else self.z
        return [(base + m * (2 << b)) % n_z for m in range(n_z // (2 << b))]

    def z_slot(self, b, m):
        return self.plan.n_z // (2 << b) - 1 + m

    def z_device(self, b):
        return (self.across(b) * 2 + self.c, self.i)

    def greet(self):
        plan = self.plan
        barrier = pltpu.get_barrier_semaphore()
        partners = [self.sib]
        partners += [self.z_device(b) for b in range(plan.bits)]
        partners += [(self.dp, (self.i + k) % plan.n_mp) for k in range(1, plan.n_mp)]
        for partner in partners:
            pl.semaphore_signal(barrier, inc=1, device_id=partner, device_id_type=MESH)
        return lambda: pl.semaphore_wait(barrier, len(partners))

    def push(self, src, dst, send, recv, device):
        return pltpu.make_async_remote_copy(
            src_ref=src, dst_ref=dst, send_sem=send, recv_sem=recv, device_id=device, device_id_type=MESH
        )


class Gather:
    def __init__(self, ex, ref, sems, tile=slice(None)):
        self.ex, self.ref, self.tile = ex, ref, tile
        self.zs, self.zr, self.rs, self.rr, self.ss, self.sr = sems

    def z_copy(self, b, m):
        ex = self.ex
        view = self.ref.at[ex.i, ex.z_units(b, False)[m], ex.c, self.tile]
        at = ex.z_slot(b, m)
        return ex.push(view, view, self.zs.at[at], self.zr.at[at], ex.z_device(b))

    def ring_view(self, origin, s, d):
        n_z, half = self.ex.plan.n_z, self.ex.plan.half
        units = pl.ds(s * (n_z // 2), n_z // 2) if d == half else pl.ds(0, n_z)
        return self.ref.at[origin, units, self.ex.c, self.tile]

    def ring_copy(self, s, d):
        ex = self.ex
        sign = 1 - 2 * s
        view = self.ring_view(ex.at(ex.p - sign * (d - 1)), s, d)
        return ex.push(view, view, self.rs.at[s, d - 1], self.rr.at[s, d - 1], (ex.dp, ex.at(ex.p + sign)))

    def sib_copy(self, offset):
        ex = self.ex
        at = (offset + ex.plan.n_mp) % ex.plan.n_mp
        view = self.ref.at[ex.at(ex.p + offset), :, ex.c, self.tile]
        return ex.push(view, view, self.ss.at[at], self.sr.at[at], ex.sib)

    def start(self):
        for b in range(self.ex.plan.bits):
            self.z_copy(b, 0).start()

    def z_sizes(self):
        n_z = self.ex.plan.n_z
        return [(b, n_z // (2 << b)) for b in range(self.ex.plan.bits)]

    def spread(self):
        sizes = self.z_sizes()
        for b, count in reversed(sizes[:-1]):
            for m in range(sizes[b + 1][1]):
                self.z_copy(b + 1, m).wait_recv()
            for m in range(1, count):
                self.z_copy(b, m).start()

    def column(self):
        for m in range(self.z_sizes()[0][1]):
            self.z_copy(0, m).wait_recv()
        for s in range(2):
            self.ring_copy(s, 1).start()
        self.sib_copy(0).start()

    def hop(self, d):
        half = self.ex.plan.half
        for s in range(2):
            self.ring_copy(s, d).wait_recv()
            if d < half:
                self.ring_copy(s, d + 1).start()
                self.sib_copy(-d if s == 0 else d).start()
        if d == half:
            self.sib_copy(half).start()

    def wait_sib(self, offset):
        self.sib_copy(offset).wait_recv()

    def wait_sent(self, offset):
        half = self.ex.plan.half
        self.sib_copy(offset).wait_send()
        if offset == 0:
            for b, count in self.z_sizes():
                for m in range(count):
                    self.z_copy(b, m).wait_send()
            for s in range(2):
                self.ring_copy(s, 1).wait_send()
        elif abs(offset) < half:
            self.ring_copy(0 if offset < 0 else 1, abs(offset) + 1).wait_send()


class RingFirst(Gather):
    def ring_view(self, origin, s, d):
        ex = self.ex
        rows = ex.plan.row_half(s, self.ref.shape[3]) if d == ex.plan.half else slice(None)
        return self.ref.at[origin, ex.z, ex.c, rows]

    def panel_copy(self, offset, b, m):
        ex = self.ex
        view = self.ref.at[ex.at(ex.p + offset), ex.z_units(b, False)[m], ex.c]
        at = (offset + ex.plan.n_mp) % ex.plan.n_mp, ex.z_slot(b, m)
        return ex.push(view, view, self.zs.at[at], self.zr.at[at], ex.z_device(b))

    def begin(self, offset):
        for b in range(self.ex.plan.bits):
            self.panel_copy(offset, b, 0).start()

    def circle(self):
        for s in range(2):
            self.ring_copy(s, 1).start()

    def hop(self, d):
        half = self.ex.plan.half
        for s in range(2):
            self.ring_copy(s, d).wait_recv()
            if d < half:
                self.ring_copy(s, d + 1).start()
        if d < half:
            self.begin(-d)
            self.begin(d)
        else:
            self.begin(half)

    def spread(self, offset):
        sizes = self.z_sizes()
        for b, count in reversed(sizes[:-1]):
            for m in range(sizes[b + 1][1]):
                self.panel_copy(offset, b + 1, m).wait_recv()
            for m in range(1, count):
                self.panel_copy(offset, b, m).start()

    def column(self, offset):
        for m in range(self.z_sizes()[0][1]):
            self.panel_copy(offset, 0, m).wait_recv()
        self.sib_copy(offset).start()

    def wait_sent(self, offset):
        half = self.ex.plan.half
        self.sib_copy(offset).wait_send()
        for b, count in self.z_sizes():
            for m in range(count):
                self.panel_copy(offset, b, m).wait_send()
        if offset == 0:
            for s in range(2):
                self.ring_copy(s, 1).wait_send()
        elif abs(offset) < half:
            self.ring_copy(0 if offset < 0 else 1, abs(offset) + 1).wait_send()


class Reduce:
    def __init__(self, ex, ref, tile, other, ring, last, sems):
        self.ex, self.ref, self.tile = ex, ref, tile
        self.other, self.ring, self.last = other, ring, last
        self.ss, self.sr, self.rs, self.rr, self.zs, self.zr = sems

    def sib_copy(self, offset):
        ex = self.ex
        at = (offset + ex.plan.n_mp) % ex.plan.n_mp
        view = self.ref.at[ex.at(ex.p + offset), :, 1 - ex.c, self.tile]
        return ex.push(view, self.other.at[at], self.ss.at[at], self.sr.at[at], ex.sib)

    def ring_views(self, dest, s, d, part):
        plan = self.ex.plan
        at, count = plan.slots(d)
        first = 0
        if d == plan.half:
            first = s * count
        elif part is not None:
            count = plan.n_z // 2
            first, at = part * count, at + part * count
        return self.ref.at[dest, pl.ds(first, count), self.ex.c, self.tile], self.ring.at[s, pl.ds(at, count)]

    def ring_copy(self, s, d, part=None):
        ex = self.ex
        plan = ex.plan
        sign = 1 - 2 * s
        sem = d - 1 if part is None else plan.half - 2 + 2 * part
        view, there = self.ring_views(ex.at(ex.p + sign * d), s, d, part)
        return ex.push(view, there, self.rs.at[s, sem], self.rr.at[s, sem], (ex.dp, ex.at(ex.p + sign)))

    def ring_copies(self, s, d):
        if d == self.ex.plan.half - 1:
            return [self.ring_copy(s, d, part) for part in range(2)]
        return [self.ring_copy(s, d)]

    def z_copy(self, b, m):
        ex = self.ex
        view = self.ref.at[ex.i, ex.z_units(b, True)[m], ex.c, self.tile]
        at = ex.z_slot(b, m)
        return ex.push(view, self.last.at[at], self.zs.at[at], self.zr.at[at], ex.z_device(b))

    def z_sizes(self):
        n_z = self.ex.plan.n_z
        return [(b, n_z // (2 << b)) for b in range(self.ex.plan.bits)]

    def to_sibling(self, offset):
        self.sib_copy(offset).start()

    def add(self, offset, first, count, *terms):
        j = self.ex.at(self.ex.p + offset)

        @pl.loop(0, count)
        def _(u):
            value = self.ref[j, first + u, self.ex.c, self.tile, :].astype(F32)
            for buf, at in terms:
                value = value + buf(at + u).astype(F32)
            self.ref[j, first + u, self.ex.c, self.tile, :] = value.astype(BF)

    def from_sibling(self, offset):
        at = (offset + self.ex.plan.n_mp) % self.ex.plan.n_mp
        self.sib_copy(offset).wait_recv()
        self.add(offset, 0, self.ex.plan.n_z, (lambda u: self.other[at, u], 0))

    def far(self):
        half = self.ex.plan.half
        self.from_sibling(half)
        for s in range(2):
            self.ring_copy(s, half).start()

    def free(self, s):
        half = self.ex.plan.half
        self.from_sibling((1 - 2 * s) * (half - 1))
        self.ring_copy(s, half - 1, 1 - s).start()

    def bound(self, s):
        plan = self.ex.plan
        half = plan.half
        self.ring_copy(s, half).wait_recv()
        at, count = plan.slots(half)
        self.add((1 - 2 * s) * (half - 1), s * count, count, (lambda u: self.ring[s, u], at))
        self.ring_copy(s, half - 1, s).start()

    def wait_ring(self, s, d):
        for copy in self.ring_copies(s, d):
            copy.wait_recv()

    def nearer(self):
        plan = self.ex.plan
        for d in range(plan.half - 2, 0, -1):
            for s in range(2):
                offset = (1 - 2 * s) * d
                self.from_sibling(offset)
                self.wait_ring(s, d + 1)
                self.add(offset, 0, plan.n_z, (lambda u: self.ring[s, u], plan.slots(d + 1)[0]))
                self.ring_copy(s, d).start()

    def home(self):
        plan = self.ex.plan
        for s in range(2):
            self.wait_ring(s, 1)
        self.sib_copy(0).wait_recv()
        at = plan.slots(1)[0]
        self.add(
            0, 0, plan.n_z,
            (lambda u: self.other[0, u], 0),
            (lambda u: self.ring[0, u], at),
            (lambda u: self.ring[1, u], at),
        )
        for m in range(self.z_sizes()[0][1]):
            self.z_copy(0, m).start()

    def along(self):
        ex = self.ex
        for b, count in self.z_sizes()[:-1]:
            for m, unit in enumerate(ex.z_units(b, False)):
                self.z_copy(b, m).wait_recv()
                at = ex.z_slot(b, m)
                self.add(0, unit, 1, (lambda u: self.last[u], at))
            for m in range(count // 2):
                self.z_copy(b + 1, m).start()

    def finish(self):
        ex = self.ex
        self.z_copy(ex.plan.bits - 1, 0).wait_recv()
        return self.ref[ex.i, ex.z, ex.c, self.tile, :].astype(F32) + self.last[0].astype(F32)

    def wait_z_sent(self):
        for b, count in self.z_sizes():
            for m in range(count):
                self.z_copy(b, m).wait_send()

    def wait_sent(self):
        plan = self.ex.plan
        for offset in range(plan.n_mp):
            self.sib_copy(offset).wait_send()
        for s in range(2):
            for d in range(1, plan.half + 1):
                for copy in self.ring_copies(s, d):
                    copy.wait_send()
        self.wait_z_sent()


class RingLast(Reduce):
    def half_rows(self, s):
        return self.ex.plan.row_half(s, self.ref.shape[3])

    def panel_copy(self, offset, b, m):
        ex = self.ex
        view = self.ref.at[ex.at(ex.p + offset), ex.z_units(b, True)[m], ex.c, self.tile]
        at = (offset + ex.plan.n_mp) % ex.plan.n_mp, ex.z_slot(b, m)
        return ex.push(view, self.last.at[at], self.zs.at[at], self.zr.at[at], ex.z_device(b))

    def begin(self, offset):
        self.from_sibling(offset)
        for m in range(self.z_sizes()[0][1]):
            self.panel_copy(offset, 0, m).start()

    def take(self, offset, b):
        ex = self.ex
        q = (offset + ex.plan.n_mp) % ex.plan.n_mp
        for m, unit in enumerate(ex.z_units(b, False)):
            self.panel_copy(offset, b, m).wait_recv()
            self.add(offset, unit, 1, (lambda u: self.last[q, u], ex.z_slot(b, m)))

    def along(self, offset):
        for b, count in self.z_sizes()[:-1]:
            self.take(offset, b)
            for m in range(count // 2):
                self.panel_copy(offset, b + 1, m).start()

    def end(self, offset):
        self.take(offset, self.ex.plan.bits - 1)

    def ring_views(self, dest, s, d, part):
        ex = self.ex
        rows = slice(None)
        if d == ex.plan.half:
            rows = self.half_rows(s)
        elif part is not None:
            rows = self.half_rows(part)
        return self.ref.at[dest, ex.z, ex.c, rows], self.ring.at[s, d - 1, rows]

    def add_rows(self, offset, rows, *terms):
        ex = self.ex
        j = ex.at(ex.p + offset)
        value = self.ref[j, ex.z, ex.c, rows, :].astype(F32)
        for term in terms:
            value = value + term.astype(F32)
        self.ref[j, ex.z, ex.c, rows, :] = value.astype(BF)

    def far(self):
        for s in range(2):
            self.ring_copy(s, self.ex.plan.half).start()

    def free(self, s):
        self.ring_copy(s, self.ex.plan.half - 1, 1 - s).start()

    def bound(self, s):
        plan = self.ex.plan
        half = plan.half
        self.ring_copy(s, half).wait_recv()
        rows = self.half_rows(s)
        self.add_rows((1 - 2 * s) * (half - 1), rows, self.ring[s, half - 1, rows, :])
        self.ring_copy(s, half - 1, s).start()

    def nearer(self):
        for d in range(self.ex.plan.half - 2, 0, -1):
            for s in range(2):
                self.wait_ring(s, d + 1)
                self.add_rows((1 - 2 * s) * d, slice(None), self.ring[s, d])
                self.ring_copy(s, d).start()

    def finish(self):
        ex = self.ex
        for s in range(2):
            self.wait_ring(s, 1)
        value = self.ref[ex.i, ex.z, ex.c].astype(F32)
        return value + self.ring[0, 0].astype(F32) + self.ring[1, 0].astype(F32)

    def wait_z_sent(self):
        for offset in range(self.ex.plan.n_mp):
            for b, count in self.z_sizes():
                for m in range(count):
                    self.panel_copy(offset, b, m).wait_send()


class Rows:
    def __init__(self, ex, src, dst, send, recv, out):
        self.ex, self.src, self.dst, self.send, self.recv, self.out = ex, src, dst, send, recv, out

    def move(self, start):
        ex = self.ex
        plan, i = ex.plan, ex.i
        q = plan.per_seq
        for m in range(MICRO):
            if self.out:
                target, place = (i % plan.n_seq) * q + m, i // plan.n_seq
            else:
                target, place = m * plan.n_seq + i // q, i % q
            far = ex.push(self.src.at[m], self.dst.at[place], self.send.at[m], self.recv.at[place], (ex.dp, target))
            near = pltpu.make_async_copy(self.src.at[m], self.dst.at[place], self.send.at[m])

            @pl.when(target != i)
            def _():
                far.start() if start else far.wait_send()

            @pl.when(target == i)
            def _():
                near.start() if start else near.wait()

    def start(self):
        self.move(True)

    def wait_sent(self):
        self.move(False)

    def wait_here(self):
        ex = self.ex
        plan, i = ex.plan, ex.i
        q = plan.per_seq
        for m in range(MICRO):
            origin = m * plan.n_seq + i // q if self.out else (i % plan.n_seq) * q + m

            @pl.when(origin != i)
            def _():
                ex.push(self.dst.at[m], self.dst.at[m], self.send.at[0], self.recv.at[m], ex.sib).wait_recv()


def step_kernel(plan, n_in, *refs):
    (tab, dev, w_qkv, w_out, w_up, w_down, tok, fv, cot), small = refs[:9], refs[9:n_in]
    (o_out, o_dx, o_df, o_q, o_s, o_o, o_u, o_d) = refs[n_in : n_in + 8]
    (
        gq, go, gu, gd, x3, f3, y3, out3,
        q_other, q_ring, q_last, s_other, s_ring, s_last, o_other, o_ring, o_last, u_other, u_ring, u_last,
        d_other, d_ring, d_last,
        wq, wo, sv, tail, vec, ub, hlt, qkv, otb, lse, mid, h2, h2t, yt,
        big, acc, act, slope, du, dv, dk, dqt, sums, ubg,
    ) = refs[n_in + 8 : n_in + 8 + 47]
    sems = refs[n_in + 8 + 47 :]
    dx3, df3 = y3, f3
    R, C, n_mp, n_dp, n_z = plan.rows, plan.cols, plan.n_mp, plan.n_dp, plan.n_z
    step = 64
    part = R // plan.parts
    ex = Exchange(plan)
    i, z, c = ex.i, ex.z, ex.c
    Q = Gather(ex, gq, sems[0:6], slice(0, R))
    O = Gather(ex, go, sems[6:12])
    U1 = Gather(ex, gu, sems[12:18], plan.row_half(0, R))
    U2 = Gather(ex, gu, sems[18:24], plan.row_half(1, R))
    W = RingFirst(ex, gd, sems[24:30])
    RQ = Reduce(ex, gq, slice(0, R), q_other, q_ring, q_last, sems[30:36])
    RS = Reduce(ex, gq, slice(R, R + 8), s_other, s_ring, s_last, sems[36:42])
    RU = Reduce(ex, gu, slice(0, R), u_other, u_ring, u_last, sems[42:48])
    RO = Reduce(ex, go, slice(0, part), o_other, o_ring, o_last, sems[48:54])
    RD = RingLast(ex, gd, slice(0, R), d_other, d_ring, d_last, sems[54:60])
    a2a = sems[60:72]
    XT = Rows(ex, tok, x3, a2a[0], a2a[1], False)
    XF = Rows(ex, fv, f3, a2a[2], a2a[3], False)
    XY = Rows(ex, cot, y3, a2a[4], a2a[5], False)
    YO = Rows(ex, out3, o_out, a2a[6], a2a[7], True)
    YX = Rows(ex, dx3, o_dx, a2a[8], a2a[9], True)
    YF = Rows(ex, df3, o_df, a2a[10], a2a[11], True)
    near = range(-plan.half + 1, plan.half)

    all_here = ex.greet()
    gq[i, z, c, 0:R, 0 : plan.qkv] = w_qkv[...]
    sv[0, 0:16, 0:128] = jnp.zeros((16, 128), F32)
    sv[1, 0:1, 0 : 3 * LANES] = jnp.zeros((1, 3 * LANES), F32)
    sv[1, 0:1, 0 : small[UP_BIAS].shape[0]] = small[UP_BIAS][...].astype(F32)[None]
    for v in range(N_VEC):
        if v != UP_BIAS:
            sv[0, v : v + 1, 0 : small[v].shape[0]] = small[v][...].astype(F32)[None]
    for k, r in enumerate(UP_ROWS):
        sv[0, r : r + 1, 0:LANES] = sv[1, 0:1, k * LANES : (k + 1) * LANES]
    gq[i, z, c, 0:16, plan.qw - LANES :] = sv[0, 0:16, 0:LANES].astype(BF)
    def rows_of(ref3, at, step):
        part = SEQ // MICRO
        return ref3.at[at // (part // step), pl.ds(pl.multiple_of((at % (part // step)) * step, step), step)]

    def blocks(step, body):
        @pl.loop(0, SEQ // step)
        def _(at):
            body(at, pl.ds(pl.multiple_of(at * step, step), step))

    all_here()
    Q.start()
    XT.start()
    for t in range(plan.parts):
        go[i, z, c, :, t * plan.out : (t + 1) * plan.out] = w_out[t * part : (t + 1) * part, :]
    gu[i, z, c] = w_up[...]
    gd[i, z, c] = w_down[...]
    Q.spread()
    Q.column()
    W.circle()
    U1.start()
    U2.start()
    W.begin(0)
    XT.wait_here()
    XT.wait_sent()

    def first_stats(at, rows):
        acc[rows, :], _ = norm_stats(rows_of(x3, at, step)[...].astype(F32))

    blocks(step, first_stats)
    Q.hop(1)
    U1.spread()
    XF.start()
    U2.spread()
    O.start()
    W.spread(0)
    O.spread()
    U1.column()
    U2.column()
    O.column()
    W.column(0)
    W.hop(1)
    for d in range(2, plan.half + 1):
        Q.hop(d)

    rowdev = dev[:, 0:1]
    row = lambda v: vec[v : v + 1, :]
    lanes = lambda v: slice((v % plan.spr) * 128, (v % plan.spr) * 128 + 128)
    onehot = lambda t, width: (lax.broadcasted_iota(jnp.int32, (128, width), 0) == tab[t : t + 1, :width]).astype(BF)
    e24 = onehot(0, D)
    e96 = onehot(4, C)

    for offset in (*near, plan.half):
        Q.wait_sib(offset)

    for j in range(n_mp):
        for d in range(n_dp):
            rows = slice(d * R, (d + 1) * R)
            wq[rows, j * plan.qkv : (j + 1) * plan.qkv] = gq[j, d // 2, d % 2, 0:R, 0 : plan.qkv]
    for j in range(n_mp):
        for d in range(n_dp):
            tail[j * n_dp + d] = gq[j, d // 2, d % 2, 0:16, plan.qw - 128 :].astype(F32)
    skip = 128 - LANES
    shifted = lambda t, width, back: (
        lax.broadcasted_iota(jnp.int32, (128, width), 0) - skip == tab[t : t + 1, :width] - back
    ) & (lax.broadcasted_iota(jnp.int32, (128, width), 0) >= skip)

    def expand(r, e, owner):
        got = dot(tail[:, r, :].astype(BF), e.astype(BF))
        return jnp.sum(jnp.where(owner == rowdev, got, 0.0), axis=0, keepdims=True)

    for v in WIDE:
        vec[v : v + 1, :] = expand(v, shifted(0, D, 0), tab[1:2, :])
    vec[V_BIAS : V_BIAS + 1, :] = expand(V_BIAS, shifted(2, D, 0), tab[3:4, :])
    for j in range(n_mp):
        owner = tab[5:6, :C] + j * n_dp
        ub[j : j + 1, :] = sum(expand(r, shifted(4, C, k * LANES), owner) for k, r in enumerate(UP_ROWS))

    def first_norm(at, rows):
        rows_of(out3, at, step)[...] = (acc[rows, :] * row(G1) + row(B1)).astype(BF)

    blocks(step, first_norm)
    for d in range(2, plan.half + 1):
        W.hop(d)
    hl = out3[...].reshape(SEQ, D)
    hlt[...] = hl.T
    XF.wait_here()
    XF.wait_sent()

    q = dot(hl, wq[:, 0:D]) + row(QB)
    qkv[:, 0:D] = q.astype(BF) * 0.125
    qkv[:, D : 2 * D] = dot(hl, wq[:, D : 2 * D]).astype(BF)
    v = dot(hl, wq[:, 2 * D : QKV]) + row(V_BIAS)[:, :VFRESH]
    qkv[:, 2 * D : QKV] = v.astype(BF)
    qkv[:, QKV : 3 * D] = f3[...].reshape(SEQ, D // 2)

    B = 256
    head_of = lax.broadcasted_iota(jnp.int32, (1, 128), 1) // HEAD
    keep = lax.broadcasted_iota(jnp.int32, (B, B), 0) <= lax.broadcasted_iota(jnp.int32, (B, B), 1)

    def scores(k2, qm, at):
        s = dot_nt(k2, qm)
        last = jnp.where(keep, s[at * B :, :], -BIG)
        return last if at == 0 else jnp.concatenate([s[: at * B, :], last], axis=0)

    @pl.loop(0, HEADS // 2)
    def _(t):
        cols = lambda base: pl.ds(pl.multiple_of(base + t * 128, 128), 128)
        vt = qkv[:, cols(2 * D)].T
        for e in range(2):
            mask = (head_of == e).astype(BF)
            for at in range(SEQ // B):
                kk = (at + 1) * B
                span = slice(at * B, kk)
                s = scores(qkv[0:kk, cols(D)], qkv[span, cols(0)] * mask, at)
                top = jnp.max(s, axis=0, keepdims=True)
                ex_ = jnp.exp(s - top)
                total = jnp.sum(ex_, axis=0, keepdims=True)
                o = dot(vt[e * HEAD : (e + 1) * HEAD, 0:kk], ex_.astype(BF)) / total
                otb[pl.ds(pl.multiple_of(t * 128 + e * HEAD, HEAD), HEAD), span] = o.astype(BF)
                lse[t, e : e + 1, span] = top + jnp.log(total)

        @pl.when(t == 0)
        def _():
            for d in range(1, plan.half):
                O.hop(d)

        @pl.when(t == 1)
        def _():
            for d in range(1, plan.half):
                U1.hop(d)
                U2.hop(d)
            for offset in near:
                if offset:
                    W.spread(offset)
            XY.start()

        @pl.when(t == 3)
        def _():
            O.hop(plan.half)

        @pl.when(t == 5)
        def _():
            W.spread(plan.half)

    for offset in (*near, plan.half):
        O.wait_sib(offset)
    for j in range(n_mp):
        for d in range(n_dp):
            for t in range(plan.parts):
                rows = slice(d * R + t * part, d * R + (t + 1) * part)
                wo[rows, j * plan.out : (j + 1) * plan.out] = go[
                    j, d // 2, d % 2, :, t * plan.out : (t + 1) * plan.out
                ]
    du[:, 0:D] = otb[...].T

    acc[...] = dot(du[:, 0:D], wo[...]) + row(OB)

    def second_norm(at, rows):
        m = rows_of(x3, at, step)[...].astype(F32) + acc[rows, :]
        mid[rows, :] = m
        scaled, _ = norm_stats(m)
        h2[rows, :] = (scaled * row(G2) + row(B2)).astype(BF)

    blocks(step, second_norm)
    for offset in near:
        if offset:
            W.column(offset)
    h2t[...] = h2[...].T
    acc[...] = jnp.zeros_like(acc)
    big[...] = jnp.zeros_like(big)

    offset_of = lambda q: (q + 1) // 2 * (1 - 2 * (q % 2))

    @pl.loop(0, n_mp)
    def _(q):
        j = ex.at(ex.p + offset_of(q))
        for s in range(n_mp):
            offset = plan.half if s == n_mp - 1 else offset_of(s)

            @pl.when(q == s)
            def _():
                if s == n_mp - 2:
                    W.column(plan.half)
                    U1.hop(plan.half)
                    U2.hop(plan.half)
                U1.wait_sib(offset)
                U2.wait_sib(offset)
                W.wait_sib(offset)

        u = dot(h2[...], gu[j].reshape(D, C)) + ub[pl.ds(j, 1), :]
        u2 = u * u
        tangent = jnp.tanh(GELU_C * (u + GELU_A * u2 * u))
        half = 0.5 * (1.0 + tangent)
        a = (u * half).astype(BF)
        act[j] = a
        slope[j] = (
            half + 0.5 * u * (1.0 - tangent * tangent) * GELU_C * (1.0 + 3.0 * GELU_A * u2)
        ).astype(BF)
        acc[...] += dot_nt(a, gd[j].reshape(D, C))

    def finish_out(at, rows):
        rows_of(out3, at, step)[...] = (mid[rows, :] + (acc[rows, :] + row(DB))).astype(BF)

    blocks(step, finish_out)
    YO.start()
    XY.wait_here()
    XY.wait_sent()
    yt[...] = y3[...].reshape(SEQ, D).T

    order = [plan.half]
    for d in range(plan.half - 1, 0, -1):
        order += [-d, d]
    order += [0]

    def nth(q):
        d = plan.half - (q + 1) // 2
        return jnp.where(q == 0, plan.half, jnp.where(q == n_mp - 1, 0, d * (1 - 2 * (q % 2))))

    def up_leaves(offset):
        if offset == plan.half:
            RU.far()
        elif abs(offset) == plan.half - 1:
            RU.free(0 if offset > 0 else 1)

    @pl.loop(0, n_mp)
    def _(q):
        j = ex.at(ex.p + nth(q))
        g = (dot(y3[...].reshape(SEQ, D), gd[j].reshape(D, C)) * slope[j].astype(F32)).astype(BF)
        du[:, 0:C] = g
        big[...] += dot_nt(g, gu[j].reshape(D, C))
        for s, offset in enumerate(order):

            @pl.when(q == s)
            def _():
                if s >= 1:
                    up_leaves(order[s - 1])
                if s >= 2:
                    RD.begin(order[s - 2])
                W.wait_sent(offset)
                U1.wait_sent(offset)
                U2.wait_sent(offset)

        gu[j] = dot(h2t[...], du[:, 0:C]).astype(BF).reshape(n_z, 2, R, C)
        for s, offset in enumerate(order):

            @pl.when(q == s)
            def _():
                RU.to_sibling(offset)

        gd[j] = dot(yt[...], act[j]).astype(BF).reshape(n_z, 2, R, C)
        ubg[pl.ds(j, 1), :] = jnp.sum(du[:, 0:C].astype(F32), axis=0, keepdims=True)
        for s, offset in enumerate(order):

            @pl.when(q == s)
            def _():
                RD.to_sibling(offset)

    RD.begin(order[-2])
    sums[...] = jnp.zeros_like(sums)

    def second_back(at, rows):
        dh = big[rows, :]
        dy = rows_of(y3, at, step)[...].astype(F32)
        scaled, inv = norm_stats(mid[rows, :])
        dr = norm_back(dh, scaled, inv, row(G2))
        dmid = dy + dr
        mid[rows, :] = dmid
        low = dmid.astype(BF)
        du[rows, 0:D] = low
        total = lambda a: jnp.sum(a, axis=0, keepdims=True)
        sums[G2 : G2 + 1, :] += total(dh * scaled)
        sums[B2 : B2 + 1, :] += total(dh)
        sums[OB : OB + 1, :] += total(low.astype(F32))
        sums[DB : DB + 1, :] += total(dy)

    blocks(step, second_back)
    for offset in order[:-4]:
        RD.along(offset)
        RD.end(offset)
    for offset in (*near, plan.half):
        O.wait_sent(offset)
        Q.wait_sent(offset)
    for j in range(n_mp):
        g = dot(otb[...], du[:, j * plan.out : (j + 1) * plan.out]).reshape(n_z, 2, plan.parts, part, plan.out)
        for t in range(plan.parts):
            go[j, :, :, :, t * plan.out : (t + 1) * plan.out] = g[:, :, t].astype(BF)
    for offset in order:
        RO.to_sibling(offset)
    do = h2
    do[...] = dot_nt(du[:, 0:D], wo[...]).astype(BF)
    RD.begin(0)
    RU.bound(0)
    RO.far()
    RO.free(0)
    RO.free(1)
    RU.bound(1)

    @pl.loop(0, HEADS // 2)
    def _(t):
        cols = lambda base: pl.ds(pl.multiple_of(base + t * 128, 128), 128)
        kt = qkv[:, cols(D)].T
        dot_ = do[:, cols(0)].astype(F32).T
        prod = dot_ * otb[cols(0), :].astype(F32)
        dv[...] = jnp.zeros_like(dv)
        dk[...] = jnp.zeros_like(dk)
        for e in range(2):
            mask = (head_of == e).astype(BF)
            delta = jnp.sum(prod[e * HEAD : (e + 1) * HEAD, :], axis=0, keepdims=True)
            for at in range(SEQ // B):
                kk = (at + 1) * B
                span = slice(at * B, kk)
                qm = qkv[span, cols(0)] * mask
                dom = do[span, cols(0)] * mask
                s = scores(qkv[0:kk, cols(D)], qm, at)
                p = jnp.exp(s - lse[t, e : e + 1, span])
                dp = dot_nt(qkv[0:kk, cols(2 * D)], dom)
                ds = (p * (dp - delta[:, span])).astype(BF)
                dv[0:kk, :] += dot(p.astype(BF), dom)
                dk[0:kk, :] += dot(ds, qm)
                dqt[e * HEAD : (e + 1) * HEAD, span] = dot(kt[e * HEAD : (e + 1) * HEAD, 0:kk], ds)
        qkv[:, cols(0)] = (dqt[...].T * 0.125).astype(BF)
        qkv[:, cols(D)] = dk[...].astype(BF)
        qkv[:, cols(2 * D)] = dv[...].astype(BF)

        @pl.when(t == 3)
        def _():
            RD.along(order[-4])

    df3[...] = qkv[:, QKV : 3 * D].reshape(df3.shape)
    YF.start()
    RO.bound(1)
    for j in range(n_mp):
        g = dot(hlt[...], qkv[:, j * plan.qkv : (j + 1) * plan.qkv]).astype(BF)
        gq[j, :, :, 0:R, 0 : plan.qkv] = g.reshape(n_z, 2, R, plan.qkv)
    for offset in order:
        RQ.to_sibling(offset)
    RO.bound(0)
    RD.along(order[-3])
    acc[...] = dot_nt(qkv[:, 0:QKV], wq[...])
    RD.along(order[-2])

    def first_back(at, rows):
        n1, inv = norm_stats(rows_of(x3, at, step)[...].astype(F32))
        dh = acc[rows, :]
        dr = norm_back(dh, n1, inv, row(G1))
        rows_of(dx3, at, step)[...] = (mid[rows, :] + dr).astype(BF)
        total = lambda a: jnp.sum(a, axis=0, keepdims=True)
        sums[G1 : G1 + 1, :] += total(dh * n1)
        sums[B1 : B1 + 1, :] += total(dh)
        sums[QB : QB + 1, :] += total(qkv[rows, 0:D].astype(F32))
        sums[V_BIAS : V_BIAS + 1, 0:VFRESH] += total(qkv[rows, 2 * D : QKV].astype(F32))

    blocks(step, first_back)
    RQ.far()
    RQ.free(0)
    RQ.free(1)

    def collect(g, e, owner):
        return dot_nt(jnp.where(owner == rowdev, g, 0.0).astype(BF), e)

    for v in WIDE:
        sv[v // plan.spr, :, lanes(v)] = collect(sums[v : v + 1, :], e24, tab[1:2, :])
    sv[V_BIAS // plan.spr, :, lanes(V_BIAS)] = collect(sums[V_BIAS : V_BIAS + 1, :], onehot(2, D), tab[3:4, :])
    got = collect(ubg[0:1, :], e96, tab[5:6, :C])
    for j in range(1, n_mp):
        got = got + collect(ubg[j : j + 1, :], e96, tab[5:6, :C] + j * n_dp)
    sv[UP_BIAS // plan.spr, :, lanes(UP_BIAS)] = got
    at8 = lax.broadcasted_iota(jnp.int32, (8, plan.qw), 0)
    for j in range(n_mp):
        for d in range(n_dp):
            at = j * n_dp + d
            value = jnp.zeros((8, plan.qw), F32)
            for r in range(plan.vec_rows):
                value = jnp.where(at8 == r, sv[r, at : at + 1, :], value)
            gq[j, d // 2, d % 2, R:, :] = value.astype(BF)
    for offset in order:
        RS.to_sibling(offset)
    RD.along(order[-1])
    RS.far()
    RS.free(0)
    RS.free(1)
    RO.nearer()
    RO.home()
    RU.nearer()
    RU.home()
    RS.bound(1)
    RS.bound(0)
    RS.nearer()
    RS.home()
    RD.end(order[-4])
    RD.far()
    RQ.bound(1)
    RS.along()
    RQ.bound(0)
    RO.along()
    o_s[...] = RS.finish()
    RD.end(order[-3])
    RD.free(1)
    RD.bound(1)
    RQ.nearer()
    RQ.home()
    YX.start()
    RD.end(order[-2])
    RD.free(0)
    RD.bound(0)
    o_o[...] = RO.finish()
    RU.along()
    RD.end(order[-1])
    RD.nearer()
    RQ.along()
    o_d[...] = RD.finish()
    o_u[...] = RU.finish()
    o_q[...] = RQ.finish()
    for r in (RU, RD, RO, RQ, RS):
        r.wait_sent()
    for r in (YO, YF, YX):
        r.wait_sent()
        r.wait_here()


def step(plan, w_qkv, w_out, w_up, w_down, tok, fv, cot, small):
    R, C, n_mp, n_z, n = plan.rows, plan.cols, plan.n_mp, plan.n_z, plan.n
    count = np.arange(D, dtype=np.int32)
    tab = np.zeros((8, D), np.int32)
    for at, width in ((0, D // n), (2, VFRESH // n), (4, FF // n)):
        tab[at], tab[at + 1] = count % width, count // width
    r = np.arange(n, dtype=np.int32)
    dev = np.tile(((r % plan.n_dp) * n_mp + r // plan.n_dp)[:, None], (1, 128))
    vm = pltpu.VMEM
    dma = pltpu.SemaphoreType.DMA
    wide = lambda t: vm((SEQ, D), t)
    tall = lambda t: vm((D, SEQ), t)
    panel = lambda rows, cols: vm((n_mp, n_z, 2, rows, cols), BF)

    def sums(rows, cols):
        ring = n_z // 2 + (plan.half - 1) * n_z
        return [
            vm((n_mp, n_z, rows, cols), BF),
            vm((2, ring, rows, cols), BF),
            vm((n_z - 1, rows, cols), BF),
        ]

    def ring_last(rows, cols):
        return [
            vm((n_mp, n_z, rows, cols), BF),
            vm((2, plan.half, rows, cols), BF),
            vm((n_mp, n_z - 1, rows, cols), BF),
        ]

    panel_z = [dma((n_mp, n_z - 1))] * 2
    gather_sems = [dma((n_z - 1,))] * 2 + [dma((2, plan.half))] * 2 + [dma((n_mp,))] * 2
    reduce_sems = [dma((n_mp,))] * 2 + [dma((2, plan.half + 1))] * 2 + [dma((n_z - 1,))] * 2
    shape = jax.ShapeDtypeStruct
    ins = (jnp.asarray(tab), jnp.asarray(dev), w_qkv, w_out, w_up, w_down, tok, fv, cot, *small)
    return pl.pallas_call(
        functools.partial(step_kernel, plan, len(ins)),
        name="step",
        out_shape=(
            shape(tok.shape, BF),
            shape(tok.shape, BF),
            shape(fv.shape, BF),
            shape((R, plan.qw), F32),
            shape((8, plan.qw), F32),
            shape((R // plan.parts, C), F32),
            shape((R, C), F32),
            shape((R, C), F32),
        ),
        in_specs=[IN_VMEM] * 6 + [ANY] * 3 + [IN_VMEM] * N_VEC,
        out_specs=(ANY,) * 3 + (IN_VMEM,) * 5,
        scratch_shapes=[
            panel(R + 8, plan.qw), panel(R // plan.parts, C), panel(R, C), panel(R, C),
            vm(tok.shape, BF), vm(fv.shape, BF), vm(cot.shape, BF),
            vm(tok.shape, BF),
            *sums(R, plan.qw), *sums(8, plan.qw), *sums(R // plan.parts, C), *sums(R, C), *ring_last(R, C),
            vm((D, QKV), BF), vm((D, D), BF),
            vm((plan.vec_rows, n, plan.qw), F32), vm((n, 16, 128), F32), vm((16, D), F32), vm((max(8, n_mp), C), F32),
            tall(BF), vm((SEQ, 3 * D), BF), tall(BF),
            vm((HEADS // 2, 8, SEQ), F32),
            wide(F32), wide(BF), tall(BF), tall(BF),
            wide(F32), wide(F32), vm((n_mp, SEQ, C), BF), vm((n_mp, SEQ, C), BF), wide(BF),
            vm((SEQ, 128), F32), vm((SEQ, 128), F32), vm((128, SEQ), F32),
            vm((16, D), F32), vm((max(8, n_mp), C), F32),
            *(gather_sems * 4),
            *(panel_z + gather_sems[2:]),
            *(reduce_sems * 4),
            *(reduce_sems[:4] + panel_z),
            *([dma((MICRO,))] * 12),
        ],
        compiler_params=pltpu.CompilerParams(
            collective_id=0, has_side_effects=True, vmem_limit_bytes=63 << 20
        ),
    )(*ins)


def unpack_kernel(plan, widths, *refs):
    (r1, r2, r3, t_q, t_s, t_o, t_u, t_d), outs, sem = refs[:8], refs[8:24], refs[24]
    moves = [pltpu.make_async_copy(src, dst, sem.at[k]) for k, (src, dst) in enumerate(zip((r1, r2, r3), outs[:3]))]
    for move in moves:
        move.start()
    outs[5][...] = t_q[:, 0 : plan.qkv]
    part = plan.rows // plan.parts
    for t in range(plan.parts):
        outs[8][t * part : (t + 1) * part, :] = t_o[:, t * plan.out : (t + 1) * plan.out]
    outs[12][...] = t_u[...]
    outs[14][...] = t_d[...]
    for v, at in enumerate((3, 4, 6, 7, 9, 10, 11, 13, 15)):
        row, lane = v // plan.spr, (v % plan.spr) * 128
        outs[at][...] = t_s[row, lane : lane + widths[v]]
    for move in moves:
        move.wait()


def unpack(plan, summed, widths):
    shape = lambda *dims: jax.ShapeDtypeStruct(dims, F32)
    vec = [shape(w) for w in widths]
    R, C = plan.rows, plan.cols
    out_shape = [jax.ShapeDtypeStruct(r.shape, BF) for r in summed[:3]]
    out_shape += [vec[0], vec[1], shape(R, plan.qkv), vec[2], vec[3], shape(R, plan.out)]
    out_shape += [vec[4], vec[5], vec[6], shape(R, C), vec[7], shape(R, C), vec[8]]
    return pl.pallas_call(
        functools.partial(unpack_kernel, plan, widths),
        name="unpack",
        out_shape=tuple(out_shape),
        in_specs=[IN_VMEM] * 3 + [IN_VMEM] * 5,
        out_specs=(ANY,) * 3 + (IN_VMEM,) * 13,
        scratch_shapes=[pltpu.SemaphoreType.DMA((3,))],
    )(*summed)


def shards(
    plan, tokens, first_values, out_cot, ln1_gain, ln1_bias, w_qkv, q_bias, v_bias, w_out, out_bias,
    ln2_gain, ln2_bias, w_up, up_bias, w_down, down_bias,
):
    small = (ln1_gain, ln1_bias, q_bias, v_bias, out_bias, ln2_gain, ln2_bias, up_bias, down_bias)
    assert tokens.shape[1] * plan.n_mp == SEQ
    summed = step(plan, w_qkv, w_out, w_up, w_down.T, tokens, first_values, out_cot, small)
    outs = unpack(plan, summed, [s.shape[0] for s in small])
    return (*outs[:14], outs[14].T, outs[15])


def layer_norm(inputs, gain_vec, shift_vec):
    average = jnp.mean(inputs, axis=-1, keepdims=True)
    centred = inputs - average
    variance = jnp.mean(centred * centred, axis=-1, keepdims=True)
    inv_std = lax.rsqrt(variance + EPS)
    scaled = centred * inv_std
    return (scaled * gain_vec + shift_vec, scaled, inv_std)


def norm_back_all(grad_out, scaled, inv_std, gain_vec):
    grad_scaled = grad_out * gain_vec
    first_term = jnp.mean(grad_scaled, axis=-1, keepdims=True)
    second_term = jnp.mean(grad_scaled * scaled, axis=-1, keepdims=True)
    grad_in = inv_std * (grad_scaled - first_term - scaled * second_term)
    return (grad_in, jnp.sum(grad_out * scaled, axis=0), jnp.sum(grad_out, axis=0))


def gelu_both(inputs):
    cubic_term = inputs + GELU_A * inputs * inputs * inputs
    tangent = jnp.tanh(GELU_C * cubic_term)
    gelu_out = 0.5 * inputs * (1.0 + tangent)
    gelu_slope = 0.5 * (1.0 + tangent) + 0.5 * inputs * (1.0 - tangent * tangent) * GELU_C * (
        1.0 + 3.0 * GELU_A * inputs * inputs
    )
    return (gelu_out, gelu_slope)


def split_heads(matrix):
    return matrix.reshape(matrix.shape[0], HEADS, HEAD)


def block_scores(query_heads, key_block, row_first, key_first):
    key_heads = split_heads(key_block)
    scores = jnp.einsum(
        "qhd,khd->hqk", query_heads, key_heads, preferred_element_type=jnp.float32
    ) * HEAD ** (-0.5)
    query_pos = row_first + jnp.arange(query_heads.shape[0], dtype=jnp.int32)
    key_pos = key_first + jnp.arange(key_block.shape[0], dtype=jnp.int32)
    allowed = key_pos[None, :] <= query_pos[:, None]
    return (jnp.where(allowed[None], scores, -BIG), allowed, key_heads)


def block_length():
    return 512


def fold_blocks(function, carried, key_block, value_block, key_first):
    row_count = key_block.shape[0]
    block_rows = block_length()
    if block_rows == row_count:
        return function(carried, key_block, value_block, key_first)
    key_parts = key_block.reshape(row_count // block_rows, block_rows, key_block.shape[1])
    value_parts = value_block.reshape(row_count // block_rows, block_rows, value_block.shape[1])
    offsets = key_first + jnp.arange(row_count // block_rows, dtype=jnp.int32) * block_rows

    def step_once(inner_state, element):
        return (function(inner_state, element[0], element[1], element[2]), None)

    result, ignored = lax.scan(step_once, carried, (key_parts, value_parts, offsets))
    return result


def map_blocks(function, key_block, value_block, key_first):
    row_count = key_block.shape[0]
    block_rows = block_length()
    if block_rows == row_count:
        return function(key_block, value_block, key_first)
    key_parts = key_block.reshape(row_count // block_rows, block_rows, key_block.shape[1])
    value_parts = value_block.reshape(row_count // block_rows, block_rows, value_block.shape[1])
    offsets = key_first + jnp.arange(row_count // block_rows, dtype=jnp.int32) * block_rows

    def apply_once(element):
        return function(element[0], element[1], element[2])

    outputs = lax.map(apply_once, (key_parts, value_parts, offsets))
    return outputs.reshape(row_count, outputs.shape[-1])


def attention_forward(queries, keys_low, values_low, row_first):
    query_heads = split_heads(queries)
    row_total = queries.shape[0]

    def online_step(fold_state, key_block, value_block, key_first):
        running_top, running_sum, running_acc = fold_state
        masked, allowed, ignored = block_scores(query_heads, key_block, row_first, key_first)
        new_top = jnp.maximum(running_top, jnp.max(masked, axis=-1))
        weights = jnp.exp(masked - new_top[:, :, None]) * allowed[None]
        shrink = jnp.exp(running_top - new_top)
        running_sum = running_sum * shrink + jnp.sum(weights, axis=-1)
        running_acc = running_acc * shrink[:, :, None] + jnp.einsum(
            "hqk,khd->hqd",
            weights.astype(jnp.bfloat16),
            split_heads(value_block),
            preferred_element_type=jnp.float32,
        )
        return (new_top, running_sum, running_acc)

    start_state = (
        jnp.full((HEADS, row_total), -BIG, jnp.float32),
        jnp.zeros((HEADS, row_total), jnp.float32),
        jnp.zeros((HEADS, row_total, HEAD), jnp.float32),
    )
    running_top, running_sum, running_acc = fold_blocks(
        online_step,
        start_state,
        lax.all_gather(keys_low, "mp", axis=0, tiled=True),
        lax.all_gather(values_low, "mp", axis=0, tiled=True),
        jnp.int32(0),
    )
    attended = (running_acc / running_sum[:, :, None]).transpose(1, 0, 2).reshape(row_total, D)
    return (attended, running_top + jnp.log(running_sum))


def attention_backward(queries, keys_low, values_low, grad_out, attended, log_total, row_first):
    query_heads = split_heads(queries)
    grad_heads = split_heads(grad_out)
    row_total = queries.shape[0]
    score_scale = HEAD ** (-0.5)
    row_delta = jnp.sum(grad_heads.astype(jnp.float32) * split_heads(attended), axis=-1).T
    keys_all, values_all = (
        lax.all_gather(keys_low, "mp", axis=0, tiled=True),
        lax.all_gather(values_low, "mp", axis=0, tiled=True),
    )

    def soft_grads(key_block, value_block, key_first):
        masked, allowed, key_heads = block_scores(query_heads, key_block, row_first, key_first)
        probabilities = jnp.exp(masked - log_total[:, :, None])
        grad_probs = jnp.einsum(
            "qhd,khd->hqk", grad_heads, split_heads(value_block), preferred_element_type=jnp.float32
        )
        grad_scores = (probabilities * (grad_probs - row_delta[:, :, None])).astype(jnp.bfloat16)
        return (probabilities, grad_scores, key_heads)

    def query_step(accum, key_block, value_block, key_first):
        probabilities, grad_scores, key_heads = soft_grads(key_block, value_block, key_first)
        return (
            accum
            + jnp.einsum("hqk,khd->qhd", grad_scores, key_heads, preferred_element_type=jnp.float32)
            * score_scale
        )

    grad_query = fold_blocks(
        query_step, jnp.zeros((row_total, HEADS, HEAD), jnp.float32), keys_all, values_all, 0
    )

    def key_step(key_block, value_block, key_first):
        probabilities, grad_scores, key_heads = soft_grads(key_block, value_block, key_first)
        grad_value = jnp.einsum(
            "hqk,qhd->khd",
            probabilities.astype(jnp.bfloat16),
            grad_heads,
            preferred_element_type=jnp.float32,
        )
        grad_key = (
            jnp.einsum("hqk,qhd->khd", grad_scores, query_heads, preferred_element_type=jnp.float32)
            * score_scale
        )
        return jnp.concatenate(
            [grad_key.reshape(key_block.shape[0], D), grad_value.reshape(key_block.shape[0], D)],
            axis=1,
        )

    key_block = keys_all
    value_block = values_all
    grad_kv = lax.psum_scatter(
        map_blocks(key_step, key_block, value_block, jnp.int32(0)).astype(jnp.bfloat16),
        "mp",
        scatter_dimension=0,
        tiled=True,
    ).astype(jnp.float32)
    return (grad_query.reshape(row_total, D), grad_kv)


def reduce_grads(local_grads):
    row_parts = (
        lax.psum_scatter(
            local_grads[0].astype(jnp.bfloat16), "dp", scatter_dimension=0, tiled=True
        ).astype(jnp.float32),
        lax.psum_scatter(
            local_grads[1].astype(jnp.bfloat16), "dp", scatter_dimension=0, tiled=True
        ).astype(jnp.float32),
        lax.psum_scatter(
            local_grads[2].astype(jnp.bfloat16), "dp", scatter_dimension=0, tiled=True
        ).astype(jnp.float32),
        lax.psum_scatter(
            local_grads[3].astype(jnp.bfloat16), "dp", scatter_dimension=0, tiled=True
        ).astype(jnp.float32),
        lax.psum_scatter(
            local_grads[4].astype(jnp.bfloat16), "dp", scatter_dimension=0, tiled=True
        ).astype(jnp.float32),
        lax.psum_scatter(
            local_grads[5].astype(jnp.bfloat16), "dp", scatter_dimension=0, tiled=True
        ).astype(jnp.float32),
        lax.psum_scatter(
            local_grads[6].astype(jnp.bfloat16), "dp", scatter_dimension=0, tiled=True
        ).astype(jnp.float32),
        lax.psum_scatter(
            local_grads[7].astype(jnp.bfloat16), "dp", scatter_dimension=0, tiled=True
        ).astype(jnp.float32),
        lax.psum_scatter(
            local_grads[8].astype(jnp.bfloat16), "dp", scatter_dimension=0, tiled=True
        ).astype(jnp.float32),
        lax.psum_scatter(
            local_grads[9].astype(jnp.bfloat16), "dp", scatter_dimension=0, tiled=True
        ).astype(jnp.float32),
        lax.psum_scatter(
            local_grads[10].astype(jnp.bfloat16), "dp", scatter_dimension=0, tiled=True
        ).astype(jnp.float32),
        lax.psum_scatter(
            local_grads[11].astype(jnp.bfloat16), "dp", scatter_dimension=1, tiled=True
        ).astype(jnp.float32),
        lax.psum_scatter(
            local_grads[12].astype(jnp.bfloat16), "dp", scatter_dimension=0, tiled=True
        ).astype(jnp.float32),
    )
    row_parts = tuple(row_parts)
    col_parts = tuple(
        (
            lax.psum_scatter(
                row_parts[0].astype(jnp.bfloat16), "mp", scatter_dimension=0, tiled=True
            ).astype(jnp.float32),
            lax.psum_scatter(
                row_parts[1].astype(jnp.bfloat16), "mp", scatter_dimension=0, tiled=True
            ).astype(jnp.float32),
            lax.psum_scatter(
                row_parts[2].astype(jnp.bfloat16), "mp", scatter_dimension=1, tiled=True
            ).astype(jnp.float32),
            lax.psum_scatter(
                row_parts[3].astype(jnp.bfloat16), "mp", scatter_dimension=0, tiled=True
            ).astype(jnp.float32),
            lax.psum_scatter(
                row_parts[4].astype(jnp.bfloat16), "mp", scatter_dimension=0, tiled=True
            ).astype(jnp.float32),
            lax.psum_scatter(
                row_parts[5].astype(jnp.bfloat16), "mp", scatter_dimension=1, tiled=True
            ).astype(jnp.float32),
            lax.psum_scatter(
                row_parts[6].astype(jnp.bfloat16), "mp", scatter_dimension=0, tiled=True
            ).astype(jnp.float32),
            lax.psum_scatter(
                row_parts[7].astype(jnp.bfloat16), "mp", scatter_dimension=0, tiled=True
            ).astype(jnp.float32),
            lax.psum_scatter(
                row_parts[8].astype(jnp.bfloat16), "mp", scatter_dimension=0, tiled=True
            ).astype(jnp.float32),
            lax.psum_scatter(
                row_parts[10].astype(jnp.bfloat16), "mp", scatter_dimension=0, tiled=True
            ).astype(jnp.float32),
            lax.psum_scatter(
                row_parts[12].astype(jnp.bfloat16), "mp", scatter_dimension=0, tiled=True
            ).astype(jnp.float32),
        )
    )
    return col_parts[:9] + (row_parts[9], col_parts[9], row_parts[11], col_parts[10])


def general_shards(
    tokens,
    first_values,
    out_cot,
    ln1_gain,
    ln1_bias,
    w_qkv,
    q_bias,
    v_bias,
    w_out,
    out_bias,
    ln2_gain,
    ln2_bias,
    w_up,
    up_bias,
    w_down,
    down_bias,
):
    near_blocks = tuple(
        (
            lax.all_gather(ln1_gain, "mp", axis=0, tiled=True),
            lax.all_gather(ln1_bias, "mp", axis=0, tiled=True),
            lax.all_gather(w_qkv, "mp", axis=1, tiled=True),
            lax.all_gather(q_bias, "mp", axis=0, tiled=True),
            lax.all_gather(v_bias, "mp", axis=0, tiled=True),
            lax.all_gather(w_out, "mp", axis=1, tiled=True),
            lax.all_gather(out_bias, "mp", axis=0, tiled=True),
            lax.all_gather(ln2_gain, "mp", axis=0, tiled=True),
            lax.all_gather(ln2_bias, "mp", axis=0, tiled=True),
            lax.all_gather(up_bias, "mp", axis=0, tiled=True),
            lax.all_gather(down_bias, "mp", axis=0, tiled=True),
        )
    )
    near_blocks = near_blocks[:9] + (w_up, near_blocks[9], w_down, near_blocks[10])
    params = tuple(
        (
            lax.all_gather(near_blocks[0], "dp", axis=0, tiled=True),
            lax.all_gather(near_blocks[1], "dp", axis=0, tiled=True),
            lax.all_gather(near_blocks[2], "dp", axis=0, tiled=True),
            lax.all_gather(near_blocks[3], "dp", axis=0, tiled=True),
            lax.all_gather(near_blocks[4], "dp", axis=0, tiled=True),
            lax.all_gather(near_blocks[5], "dp", axis=0, tiled=True),
            lax.all_gather(near_blocks[6], "dp", axis=0, tiled=True),
            lax.all_gather(near_blocks[7], "dp", axis=0, tiled=True),
            lax.all_gather(near_blocks[8], "dp", axis=0, tiled=True),
            lax.all_gather(near_blocks[9], "dp", axis=0, tiled=True),
            lax.all_gather(near_blocks[10], "dp", axis=0, tiled=True),
            lax.all_gather(near_blocks[11], "dp", axis=1, tiled=True),
            lax.all_gather(near_blocks[12], "dp", axis=0, tiled=True),
        )
    )
    gain_one = params[0].astype(jnp.float32)
    shift_one = params[1].astype(jnp.float32)
    qkv_full = params[2]
    query_shift = params[3].astype(jnp.float32)
    value_shift = params[4].astype(jnp.float32)
    out_full = params[5]
    out_shift = params[6].astype(jnp.float32)
    gain_two = params[7].astype(jnp.float32)
    shift_two = params[8].astype(jnp.float32)
    up_full = params[9]
    up_shift_all = params[10].astype(jnp.float32)
    down_full = params[11]
    down_shift = params[12].astype(jnp.float32)
    up_cols = up_full.shape[1]
    up_start = 0
    up_start = lax.axis_index("mp") * up_cols
    up_used = lax.dynamic_slice_in_dim(up_shift_all, up_start, up_cols, 0)
    row_total = tokens.shape[1]
    row_first = lax.axis_index("mp") * row_total
    fresh_cols = value_shift.shape[0]
    outputs = []
    grad_inputs = []
    grad_firsts = []
    summed = None
    for micro_index in range(MICRO):
        cot_low = out_cot[micro_index]
        inputs = tokens[micro_index].astype(jnp.float32)
        normed, scaled_one, inv_one = layer_norm(inputs, gain_one, shift_one)
        normed_low = normed.astype(jnp.bfloat16)
        mixed_proj = jnp.dot(normed_low, qkv_full, preferred_element_type=jnp.float32)
        queries = (mixed_proj[:, :D] + query_shift).astype(jnp.bfloat16)
        keys_low = mixed_proj[:, D : 2 * D].astype(jnp.bfloat16)
        values_low = jnp.concatenate(
            [
                (mixed_proj[:, 2 * D :] + value_shift).astype(jnp.bfloat16),
                first_values[micro_index],
            ],
            axis=1,
        )
        attended, log_total = attention_forward(queries, keys_low, values_low, row_first)
        attended_low = attended.astype(jnp.bfloat16)
        middle = inputs + (
            jnp.dot(attended_low, out_full, preferred_element_type=jnp.float32) + out_shift
        )
        normed_two, scaled_two, inv_two = layer_norm(middle, gain_two, shift_two)
        normed_two_low = normed_two.astype(jnp.bfloat16)
        cot_float = cot_low.astype(jnp.float32)
        row_piece = lax.all_gather(normed_two_low, "mp", axis=0, tiled=True)
        hidden = jnp.dot(row_piece, up_full, preferred_element_type=jnp.float32) + up_used
        gelu_out, gelu_slope = gelu_both(hidden)
        active_all = gelu_out.astype(jnp.bfloat16)
        down_part = lax.psum_scatter(
            jnp.dot(active_all, down_full, preferred_element_type=jnp.float32).astype(jnp.bfloat16),
            "mp",
            scatter_dimension=0,
            tiled=True,
        ).astype(jnp.float32)
        result = middle + (down_part + down_shift)
        back_row_piece = lax.all_gather(cot_low, "mp", axis=0, tiled=True)
        grad_active = jnp.einsum(
            "rd,fd->rf", back_row_piece, down_full, preferred_element_type=jnp.float32
        )
        back_gelu_out, back_gelu_slope = gelu_both(hidden)
        grad_hidden = (grad_active * back_gelu_slope).astype(jnp.bfloat16)
        grad_normed_two = lax.psum_scatter(
            jnp.einsum(
                "rf,df->rd", grad_hidden, up_full, preferred_element_type=jnp.float32
            ).astype(jnp.bfloat16),
            "mp",
            scatter_dimension=0,
            tiled=True,
        ).astype(jnp.float32)
        grad_down = jnp.einsum(
            "rf,rd->fd", active_all, back_row_piece, preferred_element_type=jnp.float32
        )
        grad_up = jnp.einsum(
            "rd,rf->df", row_piece, grad_hidden, preferred_element_type=jnp.float32
        )
        up_piece = jnp.sum(grad_hidden.astype(jnp.float32), axis=0)
        grad_up_shift = lax.dynamic_update_slice_in_dim(
            jnp.zeros((FF,), jnp.float32), up_piece, up_start, 0
        )
        grad_norm_two, grad_gain_two, grad_shift_two = norm_back_all(
            grad_normed_two, scaled_two, inv_two, gain_two
        )
        grad_middle = cot_float + grad_norm_two
        grad_branch = grad_middle.astype(jnp.bfloat16)
        grad_out_shift = jnp.sum(grad_branch.astype(jnp.float32), axis=0)
        grad_out_proj = jnp.einsum(
            "rd,re->de", attended_low, grad_branch, preferred_element_type=jnp.float32
        )
        grad_attended = jnp.einsum(
            "re,de->rd", grad_branch, out_full, preferred_element_type=jnp.float32
        ).astype(jnp.bfloat16)
        grad_query, grad_kv = attention_backward(
            queries, keys_low, values_low, grad_attended, attended, log_total, row_first
        )
        grad_query_low = grad_query.astype(jnp.bfloat16)
        grad_kv_low = grad_kv.astype(jnp.bfloat16)
        grad_mixed = jnp.concatenate([grad_query_low, grad_kv_low[:, : D + fresh_cols]], axis=1)
        grad_query_shift = jnp.sum(grad_query_low.astype(jnp.float32), axis=0)
        grad_value_shift = jnp.sum(grad_kv_low[:, D : D + fresh_cols].astype(jnp.float32), axis=0)
        grad_qkv = jnp.einsum(
            "rd,rc->dc", normed_low, grad_mixed, preferred_element_type=jnp.float32
        )
        grad_normed = jnp.einsum(
            "rc,dc->rd", grad_mixed, qkv_full, preferred_element_type=jnp.float32
        )
        grad_norm_one, grad_gain_one, grad_shift_one = norm_back_all(
            grad_normed, scaled_one, inv_one, gain_one
        )
        grad_input = grad_middle + grad_norm_one
        local_grads = (
            grad_gain_one,
            grad_shift_one,
            grad_qkv,
            grad_query_shift,
            grad_value_shift,
            grad_out_proj,
            grad_out_shift,
            grad_gain_two,
            grad_shift_two,
            grad_up,
            grad_up_shift,
            grad_down,
            jnp.sum(cot_float, axis=0),
        )
        result, grad_input, grad_first, local_grads = (
            result.astype(jnp.bfloat16),
            grad_input.astype(jnp.bfloat16),
            grad_kv_low[:, D + fresh_cols :],
            local_grads,
        )
        outputs.append(result)
        grad_inputs.append(grad_input)
        grad_firsts.append(grad_first)
        local_grads = reduce_grads(local_grads)
        summed = local_grads if summed is None else jax.tree.map(jnp.add, summed, local_grads)
    return (
        jnp.stack(outputs),
        jnp.stack(grad_inputs),
        jnp.stack(grad_firsts),
        summed[0],
        summed[1],
        summed[2],
        summed[3],
        summed[4],
        summed[5],
        summed[6],
        summed[7],
        summed[8],
        summed[9],
        summed[10],
        summed[11],
        summed[12],
    )


def solution(mesh):
    whole_sequences = mesh.shape["mp"] == MICRO
    body = functools.partial(shards, Plan(mesh)) if whole_sequences else general_shards
    line = P(("dp", "mp"))
    rows = P(None, ("dp", "mp"), None)
    block = P("dp", "mp")
    grads = (line, line, block, line, line, block, line, line, line, block, line, P("mp", "dp"), line)
    return jax.shard_map(
        body,
        mesh=mesh,
        in_specs=(rows, rows, rows) + grads,
        out_specs=(rows, rows, rows) + grads,
        check_vma=False,
    )
```

```python
import functools

import jax
import jax.numpy as jnp
import numpy as np
from jax import lax
from jax.experimental import pallas as pl
from jax.experimental.pallas import tpu as pltpu
from jax.sharding import PartitionSpec as P

D = 768
HEADS = 12
HEAD = 64
FF = 3072
MICRO = 4
QKV = 1920
SEQ = 512
VFRESH = 384

EPS = 1e-05
BIG = 1e30
GELU_C = 0.7978845608028654
GELU_A = 0.044715
MESH = pl.DeviceIdType.MESH
ANY = pl.BlockSpec(memory_space=pl.ANY)
IN_VMEM = pl.BlockSpec(memory_space=pltpu.VMEM)
BF, F32 = jnp.bfloat16, jnp.float32

WIDE = (0, 1, 2, 4, 5, 6, 8)
V_BIAS, UP_BIAS = 3, 7
G1, B1, QB, OB, G2, B2, DB = WIDE
N_VEC = 9
LANES = 32
UP_ROWS = (UP_BIAS, N_VEC, N_VEC + 1)


class Plan:
    def __init__(self, mesh):
        self.n_dp = mesh.shape["dp"]
        self.n_mp = mesh.shape["mp"]
        self.n = self.n_dp * self.n_mp
        self.n_z = self.n_dp // 2
        self.rows = D // self.n_dp
        self.cols = FF // self.n_mp
        self.qkv = QKV // self.n_mp
        self.out = D // self.n_mp
        self.qw = -(-self.qkv // 128) * 128
        self.parts = self.cols // self.out
        self.spr = self.qw // 128
        self.vec_rows = -(-N_VEC // self.spr)
        self.half = self.n_mp // 2
        self.per_seq = SEQ // (SEQ // MICRO)
        self.n_seq = self.n_mp // MICRO
        assert self.qkv + LANES <= self.qw and D // self.n <= LANES and FF // self.n <= 3 * LANES
        assert self.parts * self.out == self.cols and self.rows % (8 * self.parts) == 0 and self.vec_rows <= 8
        self.bits = self.n_z.bit_length() - 1
        assert self.n_seq * MICRO == self.n_mp and self.n_z == 1 << self.bits and self.bits > 0

    def ring_at(self, i):
        return i + (i // self.half) * (self.n_mp - 1 + self.half - 2 * i)

    def row_half(self, s, rows):
        middle = -(-rows // 32) * 16 if rows > 16 else 8
        return slice(middle, rows) if s else slice(0, middle)

    def slots(self, d):
        if d == self.half:
            return 0, self.n_z // 2
        return self.n_z // 2 + (d - 1) * self.n_z, self.n_z


def dot(a, b):
    return jnp.dot(a, b, preferred_element_type=F32)


def dot_nt(a, b):
    return lax.dot_general(a, b, (((1,), (1,)), ((), ())), preferred_element_type=F32)


def chunks(rows, step, body):
    @pl.loop(0, rows // step)
    def _(at):
        body(pl.ds(pl.multiple_of(at * step, step), step))


def norm_stats(r):
    average = jnp.mean(r, axis=-1, keepdims=True)
    centred = r - average
    variance = jnp.mean(centred * centred, axis=-1, keepdims=True)
    inv_std = lax.rsqrt(variance + EPS)
    return centred * inv_std, inv_std


def norm_back(grad_out, scaled, inv_std, gain):
    e = grad_out * gain
    first = jnp.mean(e, axis=-1, keepdims=True)
    second = jnp.mean(e * scaled, axis=-1, keepdims=True)
    return inv_std * (e - first - scaled * second)


class Exchange:
    def __init__(self, plan):
        self.plan = plan
        dp, i = lax.axis_index("dp"), lax.axis_index("mp")
        self.dp, self.i, self.c, self.z = dp, i, dp % 2, dp // 2
        self.sib = (dp + 1 - 2 * self.c, i)
        self.p = plan.ring_at(i)

    def at(self, pos):
        return self.plan.ring_at((pos + 2 * self.plan.n_mp) % self.plan.n_mp)

    def across(self, b):
        return self.z + (1 << b) * (1 - 2 * (self.z // (1 << b) % 2))

    def z_units(self, b, far):
        n_z = self.plan.n_z
        base = self.across(b) if far else self.z
        return [(base + m * (2 << b)) % n_z for m in range(n_z // (2 << b))]

    def z_slot(self, b, m):
        return self.plan.n_z // (2 << b) - 1 + m

    def z_device(self, b):
        return (self.across(b) * 2 + self.c, self.i)

    def greet(self):
        plan = self.plan
        barrier = pltpu.get_barrier_semaphore()
        partners = [self.sib]
        partners += [self.z_device(b) for b in range(plan.bits)]
        partners += [(self.dp, (self.i + k) % plan.n_mp) for k in range(1, plan.n_mp)]
        for partner in partners:
            pl.semaphore_signal(barrier, inc=1, device_id=partner, device_id_type=MESH)
        return lambda: pl.semaphore_wait(barrier, len(partners))

    def push(self, src, dst, send, recv, device):
        return pltpu.make_async_remote_copy(
            src_ref=src, dst_ref=dst, send_sem=send, recv_sem=recv, device_id=device, device_id_type=MESH
        )


class Gather:
    def __init__(self, ex, ref, sems, tile=slice(None)):
        self.ex, self.ref, self.tile = ex, ref, tile
        self.zs, self.zr, self.rs, self.rr, self.ss, self.sr = sems

    def z_copy(self, b, m):
        ex = self.ex
        view = self.ref.at[ex.i, ex.z_units(b, False)[m], ex.c, self.tile]
        at = ex.z_slot(b, m)
        return ex.push(view, view, self.zs.at[at], self.zr.at[at], ex.z_device(b))

    def ring_view(self, origin, s, d):
        n_z, half = self.ex.plan.n_z, self.ex.plan.half
        units = pl.ds(s * (n_z // 2), n_z // 2) if d == half else pl.ds(0, n_z)
        return self.ref.at[origin, units, self.ex.c, self.tile]

    def ring_copy(self, s, d):
        ex = self.ex
        sign = 1 - 2 * s
        view = self.ring_view(ex.at(ex.p - sign * (d - 1)), s, d)
        return ex.push(view, view, self.rs.at[s, d - 1], self.rr.at[s, d - 1], (ex.dp, ex.at(ex.p + sign)))

    def sib_copy(self, offset):
        ex = self.ex
        at = (offset + ex.plan.n_mp) % ex.plan.n_mp
        view = self.ref.at[ex.at(ex.p + offset), :, ex.c, self.tile]
        return ex.push(view, view, self.ss.at[at], self.sr.at[at], ex.sib)

    def start(self):
        for b in range(self.ex.plan.bits):
            self.z_copy(b, 0).start()

    def z_sizes(self):
        n_z = self.ex.plan.n_z
        return [(b, n_z // (2 << b)) for b in range(self.ex.plan.bits)]

    def spread(self):
        sizes = self.z_sizes()
        for b, count in reversed(sizes[:-1]):
            for m in range(sizes[b + 1][1]):
                self.z_copy(b + 1, m).wait_recv()
            for m in range(1, count):
                self.z_copy(b, m).start()

    def column(self):
        for m in range(self.z_sizes()[0][1]):
            self.z_copy(0, m).wait_recv()
        for s in range(2):
            self.ring_copy(s, 1).start()
        self.sib_copy(0).start()

    def hop(self, d):
        half = self.ex.plan.half
        for s in range(2):
            self.ring_copy(s, d).wait_recv()
            if d < half:
                self.ring_copy(s, d + 1).start()
                self.sib_copy(-d if s == 0 else d).start()
        if d == half:
            self.sib_copy(half).start()

    def wait_sib(self, offset):
        self.sib_copy(offset).wait_recv()

    def wait_sent(self, offset):
        half = self.ex.plan.half
        self.sib_copy(offset).wait_send()
        if offset == 0:
            for b, count in self.z_sizes():
                for m in range(count):
                    self.z_copy(b, m).wait_send()
            for s in range(2):
                self.ring_copy(s, 1).wait_send()
        elif abs(offset) < half:
            self.ring_copy(0 if offset < 0 else 1, abs(offset) + 1).wait_send()


class RingFirst(Gather):
    def ring_view(self, origin, s, d):
        ex = self.ex
        rows = ex.plan.row_half(s, self.ref.shape[3]) if d == ex.plan.half else slice(None)
        return self.ref.at[origin, ex.z, ex.c, rows]

    def panel_copy(self, offset, b, m):
        ex = self.ex
        view = self.ref.at[ex.at(ex.p + offset), ex.z_units(b, False)[m], ex.c]
        at = (offset + ex.plan.n_mp) % ex.plan.n_mp, ex.z_slot(b, m)
        return ex.push(view, view, self.zs.at[at], self.zr.at[at], ex.z_device(b))

    def begin(self, offset):
        for b in range(self.ex.plan.bits):
            self.panel_copy(offset, b, 0).start()

    def circle(self):
        for s in range(2):
            self.ring_copy(s, 1).start()

    def hop(self, d):
        half = self.ex.plan.half
        for s in range(2):
            self.ring_copy(s, d).wait_recv()
            if d < half:
                self.ring_copy(s, d + 1).start()
        if d < half:
            self.begin(-d)
            self.begin(d)
        else:
            self.begin(half)

    def spread(self, offset):
        sizes = self.z_sizes()
        for b, count in reversed(sizes[:-1]):
            for m in range(sizes[b + 1][1]):
                self.panel_copy(offset, b + 1, m).wait_recv()
            for m in range(1, count):
                self.panel_copy(offset, b, m).start()

    def column(self, offset):
        for m in range(self.z_sizes()[0][1]):
            self.panel_copy(offset, 0, m).wait_recv()
        self.sib_copy(offset).start()

    def wait_sent(self, offset):
        half = self.ex.plan.half
        self.sib_copy(offset).wait_send()
        for b, count in self.z_sizes():
            for m in range(count):
                self.panel_copy(offset, b, m).wait_send()
        if offset == 0:
            for s in range(2):
                self.ring_copy(s, 1).wait_send()
        elif abs(offset) < half:
            self.ring_copy(0 if offset < 0 else 1, abs(offset) + 1).wait_send()


class Reduce:
    def __init__(self, ex, ref, tile, other, ring, last, sems):
        self.ex, self.ref, self.tile = ex, ref, tile
        self.other, self.ring, self.last = other, ring, last
        self.ss, self.sr, self.rs, self.rr, self.zs, self.zr = sems

    def sib_copy(self, offset):
        ex = self.ex
        at = (offset + ex.plan.n_mp) % ex.plan.n_mp
        view = self.ref.at[ex.at(ex.p + offset), :, 1 - ex.c, self.tile]
        return ex.push(view, self.other.at[at], self.ss.at[at], self.sr.at[at], ex.sib)

    def ring_views(self, dest, s, d, part):
        plan = self.ex.plan
        at, count = plan.slots(d)
        first = 0
        if d == plan.half:
            first = s * count
        elif part is not None:
            count = plan.n_z // 2
            first, at = part * count, at + part * count
        return self.ref.at[dest, pl.ds(first, count), self.ex.c, self.tile], self.ring.at[s, pl.ds(at, count)]

    def ring_copy(self, s, d, part=None):
        ex = self.ex
        plan = ex.plan
        sign = 1 - 2 * s
        sem = d - 1 if part is None else plan.half - 2 + 2 * part
        view, there = self.ring_views(ex.at(ex.p + sign * d), s, d, part)
        return ex.push(view, there, self.rs.at[s, sem], self.rr.at[s, sem], (ex.dp, ex.at(ex.p + sign)))

    def ring_copies(self, s, d):
        if d == self.ex.plan.half - 1:
            return [self.ring_copy(s, d, part) for part in range(2)]
        return [self.ring_copy(s, d)]

    def z_copy(self, b, m):
        ex = self.ex
        view = self.ref.at[ex.i, ex.z_units(b, True)[m], ex.c, self.tile]
        at = ex.z_slot(b, m)
        return ex.push(view, self.last.at[at], self.zs.at[at], self.zr.at[at], ex.z_device(b))

    def z_sizes(self):
        n_z = self.ex.plan.n_z
        return [(b, n_z // (2 << b)) for b in range(self.ex.plan.bits)]

    def to_sibling(self, offset):
        self.sib_copy(offset).start()

    def add(self, offset, first, count, *terms):
        j = self.ex.at(self.ex.p + offset)

        @pl.loop(0, count)
        def _(u):
            value = self.ref[j, first + u, self.ex.c, self.tile, :].astype(F32)
            for buf, at in terms:
                value = value + buf(at + u).astype(F32)
            self.ref[j, first + u, self.ex.c, self.tile, :] = value.astype(BF)

    def from_sibling(self, offset):
        at = (offset + self.ex.plan.n_mp) % self.ex.plan.n_mp
        self.sib_copy(offset).wait_recv()
        self.add(offset, 0, self.ex.plan.n_z, (lambda u: self.other[at, u], 0))

    def far(self):
        half = self.ex.plan.half
        self.from_sibling(half)
        for s in range(2):
            self.ring_copy(s, half).start()

    def free(self, s):
        half = self.ex.plan.half
        self.from_sibling((1 - 2 * s) * (half - 1))
        self.ring_copy(s, half - 1, 1 - s).start()

    def bound(self, s):
        plan = self.ex.plan
        half = plan.half
        self.ring_copy(s, half).wait_recv()
        at, count = plan.slots(half)
        self.add((1 - 2 * s) * (half - 1), s * count, count, (lambda u: self.ring[s, u], at))
        self.ring_copy(s, half - 1, s).start()

    def wait_ring(self, s, d):
        for copy in self.ring_copies(s, d):
            copy.wait_recv()

    def nearer(self):
        plan = self.ex.plan
        for d in range(plan.half - 2, 0, -1):
            for s in range(2):
                offset = (1 - 2 * s) * d
                self.from_sibling(offset)
                self.wait_ring(s, d + 1)
                self.add(offset, 0, plan.n_z, (lambda u: self.ring[s, u], plan.slots(d + 1)[0]))
                self.ring_copy(s, d).start()

    def home(self):
        plan = self.ex.plan
        for s in range(2):
            self.wait_ring(s, 1)
        self.sib_copy(0).wait_recv()
        at = plan.slots(1)[0]
        self.add(
            0, 0, plan.n_z,
            (lambda u: self.other[0, u], 0),
            (lambda u: self.ring[0, u], at),
            (lambda u: self.ring[1, u], at),
        )
        for m in range(self.z_sizes()[0][1]):
            self.z_copy(0, m).start()

    def along(self):
        ex = self.ex
        for b, count in self.z_sizes()[:-1]:
            for m, unit in enumerate(ex.z_units(b, False)):
                self.z_copy(b, m).wait_recv()
                at = ex.z_slot(b, m)
                self.add(0, unit, 1, (lambda u: self.last[u], at))
            for m in range(count // 2):
                self.z_copy(b + 1, m).start()

    def finish(self):
        ex = self.ex
        self.z_copy(ex.plan.bits - 1, 0).wait_recv()
        return self.ref[ex.i, ex.z, ex.c, self.tile, :].astype(F32) + self.last[0].astype(F32)

    def wait_z_sent(self):
        for b, count in self.z_sizes():
            for m in range(count):
                self.z_copy(b, m).wait_send()

    def wait_sent(self):
        plan = self.ex.plan
        for offset in range(plan.n_mp):
            self.sib_copy(offset).wait_send()
        for s in range(2):
            for d in range(1, plan.half + 1):
                for copy in self.ring_copies(s, d):
                    copy.wait_send()
        self.wait_z_sent()


class RingLast(Reduce):
    def half_rows(self, s):
        return self.ex.plan.row_half(s, self.ref.shape[3])

    def panel_copy(self, offset, b, m):
        ex = self.ex
        view = self.ref.at[ex.at(ex.p + offset), ex.z_units(b, True)[m], ex.c, self.tile]
        at = (offset + ex.plan.n_mp) % ex.plan.n_mp, ex.z_slot(b, m)
        return ex.push(view, self.last.at[at], self.zs.at[at], self.zr.at[at], ex.z_device(b))

    def begin(self, offset):
        self.from_sibling(offset)
        for m in range(self.z_sizes()[0][1]):
            self.panel_copy(offset, 0, m).start()

    def take(self, offset, b):
        ex = self.ex
        q = (offset + ex.plan.n_mp) % ex.plan.n_mp
        for m, unit in enumerate(ex.z_units(b, False)):
            self.panel_copy(offset, b, m).wait_recv()
            self.add(offset, unit, 1, (lambda u: self.last[q, u], ex.z_slot(b, m)))

    def along(self, offset):
        for b, count in self.z_sizes()[:-1]:
            self.take(offset, b)
            for m in range(count // 2):
                self.panel_copy(offset, b + 1, m).start()

    def end(self, offset):
        self.take(offset, self.ex.plan.bits - 1)

    def ring_views(self, dest, s, d, part):
        ex = self.ex
        rows = slice(None)
        if d == ex.plan.half:
            rows = self.half_rows(s)
        elif part is not None:
            rows = self.half_rows(part)
        return self.ref.at[dest, ex.z, ex.c, rows], self.ring.at[s, d - 1, rows]

    def add_rows(self, offset, rows, *terms):
        ex = self.ex
        j = ex.at(ex.p + offset)
        value = self.ref[j, ex.z, ex.c, rows, :].astype(F32)
        for term in terms:
            value = value + term.astype(F32)
        self.ref[j, ex.z, ex.c, rows, :] = value.astype(BF)

    def far(self):
        for s in range(2):
            self.ring_copy(s, self.ex.plan.half).start()

    def free(self, s):
        self.ring_copy(s, self.ex.plan.half - 1, 1 - s).start()

    def bound(self, s):
        plan = self.ex.plan
        half = plan.half
        self.ring_copy(s, half).wait_recv()
        rows = self.half_rows(s)
        self.add_rows((1 - 2 * s) * (half - 1), rows, self.ring[s, half - 1, rows, :])
        self.ring_copy(s, half - 1, s).start()

    def nearer(self):
        for d in range(self.ex.plan.half - 2, 0, -1):
            for s in range(2):
                self.wait_ring(s, d + 1)
                self.add_rows((1 - 2 * s) * d, slice(None), self.ring[s, d])
                self.ring_copy(s, d).start()

    def finish(self):
        ex = self.ex
        for s in range(2):
            self.wait_ring(s, 1)
        value = self.ref[ex.i, ex.z, ex.c].astype(F32)
        return value + self.ring[0, 0].astype(F32) + self.ring[1, 0].astype(F32)

    def wait_z_sent(self):
        for offset in range(self.ex.plan.n_mp):
            for b, count in self.z_sizes():
                for m in range(count):
                    self.panel_copy(offset, b, m).wait_send()


class Rows:
    def __init__(self, ex, src, dst, send, recv, out):
        self.ex, self.src, self.dst, self.send, self.recv, self.out = ex, src, dst, send, recv, out

    def move(self, start):
        ex = self.ex
        plan, i = ex.plan, ex.i
        q = plan.per_seq
        for m in range(MICRO):
            if self.out:
                target, place = (i % plan.n_seq) * q + m, i // plan.n_seq
            else:
                target, place = m * plan.n_seq + i // q, i % q
            far = ex.push(self.src.at[m], self.dst.at[place], self.send.at[m], self.recv.at[place], (ex.dp, target))
            near = pltpu.make_async_copy(self.src.at[m], self.dst.at[place], self.send.at[m])

            @pl.when(target != i)
            def _():
                far.start() if start else far.wait_send()

            @pl.when(target == i)
            def _():
                near.start() if start else near.wait()

    def start(self):
        self.move(True)

    def wait_sent(self):
        self.move(False)

    def wait_here(self):
        ex = self.ex
        plan, i = ex.plan, ex.i
        q = plan.per_seq
        for m in range(MICRO):
            origin = m * plan.n_seq + i // q if self.out else (i % plan.n_seq) * q + m

            @pl.when(origin != i)
            def _():
                ex.push(self.dst.at[m], self.dst.at[m], self.send.at[0], self.recv.at[m], ex.sib).wait_recv()


def step_kernel(plan, n_in, *refs):
    (tab, dev, w_qkv, w_out, w_up, w_down, tok, fv, cot), small = refs[:9], refs[9:n_in]
    (o_out, o_dx, o_df, o_q, o_s, o_o, o_u, o_d) = refs[n_in : n_in + 8]
    (
        gq, go, gu, gd, x3, f3, y3, out3,
        q_other, q_ring, q_last, s_other, s_ring, s_last, o_other, o_ring, o_last, u_other, u_ring, u_last,
        d_other, d_ring, d_last,
        wq, wo, sv, tail, vec, ub, hlt, qkv, otb, lse, mid, h2, h2t, yt,
        big, acc, act, slope, du, dv, dk, dqt, sums, ubg,
    ) = refs[n_in + 8 : n_in + 8 + 47]
    sems = refs[n_in + 8 + 47 :]
    dx3, df3 = y3, f3
    R, C, n_mp, n_dp, n_z = plan.rows, plan.cols, plan.n_mp, plan.n_dp, plan.n_z
    step = 64
    part = R // plan.parts
    ex = Exchange(plan)
    i, z, c = ex.i, ex.z, ex.c
    Q = Gather(ex, gq, sems[0:6], slice(0, R))
    O = Gather(ex, go, sems[6:12])
    U1 = Gather(ex, gu, sems[12:18], plan.row_half(0, R))
    U2 = Gather(ex, gu, sems[18:24], plan.row_half(1, R))
    W = RingFirst(ex, gd, sems[24:30])
    RQ = Reduce(ex, gq, slice(0, R), q_other, q_ring, q_last, sems[30:36])
    RS = Reduce(ex, gq, slice(R, R + 8), s_other, s_ring, s_last, sems[36:42])
    RU = Reduce(ex, gu, slice(0, R), u_other, u_ring, u_last, sems[42:48])
    RO = Reduce(ex, go, slice(0, part), o_other, o_ring, o_last, sems[48:54])
    RD = RingLast(ex, gd, slice(0, R), d_other, d_ring, d_last, sems[54:60])
    a2a = sems[60:72]
    XT = Rows(ex, tok, x3, a2a[0], a2a[1], False)
    XF = Rows(ex, fv, f3, a2a[2], a2a[3], False)
    XY = Rows(ex, cot, y3, a2a[4], a2a[5], False)
    YO = Rows(ex, out3, o_out, a2a[6], a2a[7], True)
    YX = Rows(ex, dx3, o_dx, a2a[8], a2a[9], True)
    YF = Rows(ex, df3, o_df, a2a[10], a2a[11], True)
    near = range(-plan.half + 1, plan.half)

    all_here = ex.greet()
    gq[i, z, c, 0:R, 0 : plan.qkv] = w_qkv[...]
    sv[0, 0:16, 0:128] = jnp.zeros((16, 128), F32)
    sv[1, 0:1, 0 : 3 * LANES] = jnp.zeros((1, 3 * LANES), F32)
    sv[1, 0:1, 0 : small[UP_BIAS].shape[0]] = small[UP_BIAS][...].astype(F32)[None]
    for v in range(N_VEC):
        if v != UP_BIAS:
            sv[0, v : v + 1, 0 : small[v].shape[0]] = small[v][...].astype(F32)[None]
    for k, r in enumerate(UP_ROWS):
        sv[0, r : r + 1, 0:LANES] = sv[1, 0:1, k * LANES : (k + 1) * LANES]
    gq[i, z, c, 0:16, plan.qw - LANES :] = sv[0, 0:16, 0:LANES].astype(BF)
    def rows_of(ref3, at, step):
        part = SEQ // MICRO
        return ref3.at[at // (part // step), pl.ds(pl.multiple_of((at % (part // step)) * step, step), step)]

    def blocks(step, body):
        @pl.loop(0, SEQ // step)
        def _(at):
            body(at, pl.ds(pl.multiple_of(at * step, step), step))

    all_here()
    Q.start()
    XT.start()
    for t in range(plan.parts):
        go[i, z, c, :, t * plan.out : (t + 1) * plan.out] = w_out[t * part : (t + 1) * part, :]
    gu[i, z, c] = w_up[...]
    gd[i, z, c] = w_down[...]
    Q.spread()
    Q.column()
    W.circle()
    U1.start()
    U2.start()
    W.begin(0)
    XT.wait_here()
    XT.wait_sent()

    def first_stats(at, rows):
        acc[rows, :], _ = norm_stats(rows_of(x3, at, step)[...].astype(F32))

    blocks(step, first_stats)
    Q.hop(1)
    U1.spread()
    XF.start()
    U2.spread()
    O.start()
    W.spread(0)
    O.spread()
    U1.column()
    U2.column()
    O.column()
    W.column(0)
    W.hop(1)
    for d in range(2, plan.half + 1):
        Q.hop(d)

    rowdev = dev[:, 0:1]
    row = lambda v: vec[v : v + 1, :]
    lanes = lambda v: slice((v % plan.spr) * 128, (v % plan.spr) * 128 + 128)
    onehot = lambda t, width: (lax.broadcasted_iota(jnp.int32, (128, width), 0) == tab[t : t + 1, :width]).astype(BF)
    e24 = onehot(0, D)
    e96 = onehot(4, C)

    for offset in (*near, plan.half):
        Q.wait_sib(offset)

    for j in range(n_mp):
        for d in range(n_dp):
            rows = slice(d * R, (d + 1) * R)
            wq[rows, j * plan.qkv : (j + 1) * plan.qkv] = gq[j, d // 2, d % 2, 0:R, 0 : plan.qkv]
    for j in range(n_mp):
        for d in range(n_dp):
            tail[j * n_dp + d] = gq[j, d // 2, d % 2, 0:16, plan.qw - 128 :].astype(F32)
    skip = 128 - LANES
    shifted = lambda t, width, back: (
        lax.broadcasted_iota(jnp.int32, (128, width), 0) - skip == tab[t : t + 1, :width] - back
    ) & (lax.broadcasted_iota(jnp.int32, (128, width), 0) >= skip)

    def expand(r, e, owner):
        got = dot(tail[:, r, :].astype(BF), e.astype(BF))
        return jnp.sum(jnp.where(owner == rowdev, got, 0.0), axis=0, keepdims=True)

    for v in WIDE:
        vec[v : v + 1, :] = expand(v, shifted(0, D, 0), tab[1:2, :])
    vec[V_BIAS : V_BIAS + 1, :] = expand(V_BIAS, shifted(2, D, 0), tab[3:4, :])
    for j in range(n_mp):
        owner = tab[5:6, :C] + j * n_dp
        ub[j : j + 1, :] = sum(expand(r, shifted(4, C, k * LANES), owner) for k, r in enumerate(UP_ROWS))

    def first_norm(at, rows):
        rows_of(out3, at, step)[...] = (acc[rows, :] * row(G1) + row(B1)).astype(BF)

    blocks(step, first_norm)
    for d in range(2, plan.half + 1):
        W.hop(d)
    hl = out3[...].reshape(SEQ, D)
    hlt[...] = hl.T
    XF.wait_here()
    XF.wait_sent()

    q = dot(hl, wq[:, 0:D]) + row(QB)
    qkv[:, 0:D] = q.astype(BF) * 0.125
    qkv[:, D : 2 * D] = dot(hl, wq[:, D : 2 * D]).astype(BF)
    v = dot(hl, wq[:, 2 * D : QKV]) + row(V_BIAS)[:, :VFRESH]
    qkv[:, 2 * D : QKV] = v.astype(BF)
    qkv[:, QKV : 3 * D] = f3[...].reshape(SEQ, D // 2)

    B = 256
    head_of = lax.broadcasted_iota(jnp.int32, (1, 128), 1) // HEAD
    keep = lax.broadcasted_iota(jnp.int32, (B, B), 0) <= lax.broadcasted_iota(jnp.int32, (B, B), 1)

    def scores(k2, qm, at):
        s = dot_nt(k2, qm)
        last = jnp.where(keep, s[at * B :, :], -BIG)
        return last if at == 0 else jnp.concatenate([s[: at * B, :], last], axis=0)

    @pl.loop(0, HEADS // 2)
    def _(t):
        cols = lambda base: pl.ds(pl.multiple_of(base + t * 128, 128), 128)
        vt = qkv[:, cols(2 * D)].T
        for e in range(2):
            mask = (head_of == e).astype(BF)
            for at in range(SEQ // B):
                kk = (at + 1) * B
                span = slice(at * B, kk)
                s = scores(qkv[0:kk, cols(D)], qkv[span, cols(0)] * mask, at)
                top = jnp.max(s, axis=0, keepdims=True)
                ex_ = jnp.exp(s - top)
                total = jnp.sum(ex_, axis=0, keepdims=True)
                o = dot(vt[e * HEAD : (e + 1) * HEAD, 0:kk], ex_.astype(BF)) / total
                otb[pl.ds(pl.multiple_of(t * 128 + e * HEAD, HEAD), HEAD), span] = o.astype(BF)
                lse[t, e : e + 1, span] = top + jnp.log(total)

        @pl.when(t == 0)
        def _():
            for d in range(1, plan.half):
                O.hop(d)

        @pl.when(t == 1)
        def _():
            for d in range(1, plan.half):
                U1.hop(d)
                U2.hop(d)
            for offset in near:
                if offset:
                    W.spread(offset)
            XY.start()

        @pl.when(t == 3)
        def _():
            O.hop(plan.half)

        @pl.when(t == 5)
        def _():
            W.spread(plan.half)

    for offset in (*near, plan.half):
        O.wait_sib(offset)
    for j in range(n_mp):
        for d in range(n_dp):
            for t in range(plan.parts):
                rows = slice(d * R + t * part, d * R + (t + 1) * part)
                wo[rows, j * plan.out : (j + 1) * plan.out] = go[
                    j, d // 2, d % 2, :, t * plan.out : (t + 1) * plan.out
                ]
    du[:, 0:D] = otb[...].T

    acc[...] = dot(du[:, 0:D], wo[...]) + row(OB)

    def second_norm(at, rows):
        m = rows_of(x3, at, step)[...].astype(F32) + acc[rows, :]
        mid[rows, :] = m
        scaled, _ = norm_stats(m)
        h2[rows, :] = (scaled * row(G2) + row(B2)).astype(BF)

    blocks(step, second_norm)
    for offset in near:
        if offset:
            W.column(offset)
    h2t[...] = h2[...].T
    acc[...] = jnp.zeros_like(acc)
    big[...] = jnp.zeros_like(big)

    offset_of = lambda q: (q + 1) // 2 * (1 - 2 * (q % 2))

    @pl.loop(0, n_mp)
    def _(q):
        j = ex.at(ex.p + offset_of(q))
        for s in range(n_mp):
            offset = plan.half if s == n_mp - 1 else offset_of(s)

            @pl.when(q == s)
            def _():
                if s == 1:
                    W.column(plan.half)
                    U1.hop(plan.half)
                    U2.hop(plan.half)
                U1.wait_sib(offset)
                U2.wait_sib(offset)
                W.wait_sib(offset)

        u = dot(h2[...], gu[j].reshape(D, C)) + ub[pl.ds(j, 1), :]
        u2 = u * u
        tangent = jnp.tanh(GELU_C * (u + GELU_A * u2 * u))
        half = 0.5 * (1.0 + tangent)
        a = (u * half).astype(BF)
        act[j] = a
        slope[j] = (
            half + 0.5 * u * (1.0 - tangent * tangent) * GELU_C * (1.0 + 3.0 * GELU_A * u2)
        ).astype(BF)
        acc[...] += dot_nt(a, gd[j].reshape(D, C))

    def finish_out(at, rows):
        rows_of(out3, at, step)[...] = (mid[rows, :] + (acc[rows, :] + row(DB))).astype(BF)

    blocks(step, finish_out)
    YO.start()
    XY.wait_here()
    XY.wait_sent()
    yt[...] = y3[...].reshape(SEQ, D).T

    order = [plan.half]
    for d in range(plan.half - 1, 0, -1):
        order += [-d, d]
    order += [0]

    def nth(q):
        d = plan.half - (q + 1) // 2
        return jnp.where(q == 0, plan.half, jnp.where(q == n_mp - 1, 0, d * (1 - 2 * (q % 2))))

    def up_leaves(offset):
        if offset == plan.half:
            RU.far()
        elif abs(offset) == plan.half - 1:
            RU.free(0 if offset > 0 else 1)

    @pl.loop(0, n_mp)
    def _(q):
        j = ex.at(ex.p + nth(q))
        g = (dot(y3[...].reshape(SEQ, D), gd[j].reshape(D, C)) * slope[j].astype(F32)).astype(BF)
        du[:, 0:C] = g
        big[...] += dot_nt(g, gu[j].reshape(D, C))
        for s, offset in enumerate(order):

            @pl.when(q == s)
            def _():
                if s >= 1:
                    up_leaves(order[s - 1])
                if s >= 2:
                    RD.begin(order[s - 2])
                W.wait_sent(offset)
                U1.wait_sent(offset)
                U2.wait_sent(offset)

        gu[j] = dot(h2t[...], du[:, 0:C]).astype(BF).reshape(n_z, 2, R, C)
        for s, offset in enumerate(order):

            @pl.when(q == s)
            def _():
                RU.to_sibling(offset)

        gd[j] = dot(yt[...], act[j]).astype(BF).reshape(n_z, 2, R, C)
        ubg[pl.ds(j, 1), :] = jnp.sum(du[:, 0:C].astype(F32), axis=0, keepdims=True)
        for s, offset in enumerate(order):

            @pl.when(q == s)
            def _():
                RD.to_sibling(offset)

    RD.begin(order[-2])
    sums[...] = jnp.zeros_like(sums)

    def second_back(at, rows):
        dh = big[rows, :]
        dy = rows_of(y3, at, step)[...].astype(F32)
        scaled, inv = norm_stats(mid[rows, :])
        dr = norm_back(dh, scaled, inv, row(G2))
        dmid = dy + dr
        mid[rows, :] = dmid
        low = dmid.astype(BF)
        du[rows, 0:D] = low
        total = lambda a: jnp.sum(a, axis=0, keepdims=True)
        sums[G2 : G2 + 1, :] += total(dh * scaled)
        sums[B2 : B2 + 1, :] += total(dh)
        sums[OB : OB + 1, :] += total(low.astype(F32))
        sums[DB : DB + 1, :] += total(dy)

    blocks(step, second_back)
    for offset in order[:-4]:
        RD.along(offset)
        RD.end(offset)
    for offset in (*near, plan.half):
        O.wait_sent(offset)
        Q.wait_sent(offset)
    for j in range(n_mp):
        g = dot(otb[...], du[:, j * plan.out : (j + 1) * plan.out]).reshape(n_z, 2, plan.parts, part, plan.out)
        for t in range(plan.parts):
            go[j, :, :, :, t * plan.out : (t + 1) * plan.out] = g[:, :, t].astype(BF)
    for offset in order:
        RO.to_sibling(offset)
    do = h2
    do[...] = dot_nt(du[:, 0:D], wo[...]).astype(BF)
    RD.begin(0)
    RU.bound(0)
    RO.far()
    RO.free(0)
    RO.free(1)
    RU.bound(1)

    @pl.loop(0, HEADS // 2)
    def _(t):
        cols = lambda base: pl.ds(pl.multiple_of(base + t * 128, 128), 128)
        kt = qkv[:, cols(D)].T
        dot_ = do[:, cols(0)].astype(F32).T
        prod = dot_ * otb[cols(0), :].astype(F32)
        dv[...] = jnp.zeros_like(dv)
        dk[...] = jnp.zeros_like(dk)
        for e in range(2):
            mask = (head_of == e).astype(BF)
            delta = jnp.sum(prod[e * HEAD : (e + 1) * HEAD, :], axis=0, keepdims=True)
            for at in range(SEQ // B):
                kk = (at + 1) * B
                span = slice(at * B, kk)
                qm = qkv[span, cols(0)] * mask
                dom = do[span, cols(0)] * mask
                s = scores(qkv[0:kk, cols(D)], qm, at)
                p = jnp.exp(s - lse[t, e : e + 1, span])
                dp = dot_nt(qkv[0:kk, cols(2 * D)], dom)
                ds = (p * (dp - delta[:, span])).astype(BF)
                dv[0:kk, :] += dot(p.astype(BF), dom)
                dk[0:kk, :] += dot(ds, qm)
                dqt[e * HEAD : (e + 1) * HEAD, span] = dot(kt[e * HEAD : (e + 1) * HEAD, 0:kk], ds)
        qkv[:, cols(0)] = (dqt[...].T * 0.125).astype(BF)
        qkv[:, cols(D)] = dk[...].astype(BF)
        qkv[:, cols(2 * D)] = dv[...].astype(BF)

        @pl.when(t == 3)
        def _():
            RD.along(order[-4])

    df3[...] = qkv[:, QKV : 3 * D].reshape(df3.shape)
    YF.start()
    RO.bound(1)
    for j in range(n_mp):
        g = dot(hlt[...], qkv[:, j * plan.qkv : (j + 1) * plan.qkv]).astype(BF)
        gq[j, :, :, 0:R, 0 : plan.qkv] = g.reshape(n_z, 2, R, plan.qkv)
    for offset in order:
        RQ.to_sibling(offset)
    RO.bound(0)
    RD.along(order[-3])
    acc[...] = dot_nt(qkv[:, 0:QKV], wq[...])
    RD.along(order[-2])

    def first_back(at, rows):
        n1, inv = norm_stats(rows_of(x3, at, step)[...].astype(F32))
        dh = acc[rows, :]
        dr = norm_back(dh, n1, inv, row(G1))
        rows_of(dx3, at, step)[...] = (mid[rows, :] + dr).astype(BF)
        total = lambda a: jnp.sum(a, axis=0, keepdims=True)
        sums[G1 : G1 + 1, :] += total(dh * n1)
        sums[B1 : B1 + 1, :] += total(dh)
        sums[QB : QB + 1, :] += total(qkv[rows, 0:D].astype(F32))
        sums[V_BIAS : V_BIAS + 1, 0:VFRESH] += total(qkv[rows, 2 * D : QKV].astype(F32))

    blocks(step, first_back)
    RQ.far()
    RQ.free(0)
    RQ.free(1)

    def collect(g, e, owner):
        return dot_nt(jnp.where(owner == rowdev, g, 0.0).astype(BF), e)

    for v in WIDE:
        sv[v // plan.spr, :, lanes(v)] = collect(sums[v : v + 1, :], e24, tab[1:2, :])
    sv[V_BIAS // plan.spr, :, lanes(V_BIAS)] = collect(sums[V_BIAS : V_BIAS + 1, :], onehot(2, D), tab[3:4, :])
    got = collect(ubg[0:1, :], e96, tab[5:6, :C])
    for j in range(1, n_mp):
        got = got + collect(ubg[j : j + 1, :], e96, tab[5:6, :C] + j * n_dp)
    sv[UP_BIAS // plan.spr, :, lanes(UP_BIAS)] = got
    at8 = lax.broadcasted_iota(jnp.int32, (8, plan.qw), 0)
    for j in range(n_mp):
        for d in range(n_dp):
            at = j * n_dp + d
            value = jnp.zeros((8, plan.qw), F32)
            for r in range(plan.vec_rows):
                value = jnp.where(at8 == r, sv[r, at : at + 1, :], value)
            gq[j, d // 2, d % 2, R:, :] = value.astype(BF)
    for offset in order:
        RS.to_sibling(offset)
    RD.along(order[-1])
    RS.far()
    RS.free(0)
    RS.free(1)
    RO.nearer()
    RO.home()
    RU.nearer()
    RU.home()
    RS.bound(1)
    RS.bound(0)
    RS.nearer()
    RS.home()
    RD.end(order[-4])
    RD.far()
    RQ.bound(1)
    RS.along()
    RQ.bound(0)
    RO.along()
    o_s[...] = RS.finish()
    RD.end(order[-3])
    RD.free(1)
    RD.bound(1)
    RQ.nearer()
    RQ.home()
    YX.start()
    RD.end(order[-2])
    RD.free(0)
    RD.bound(0)
    o_o[...] = RO.finish()
    RU.along()
    RD.end(order[-1])
    RD.nearer()
    RQ.along()
    o_d[...] = RD.finish()
    o_u[...] = RU.finish()
    o_q[...] = RQ.finish()
    for r in (RU, RD, RO, RQ, RS):
        r.wait_sent()
    for r in (YO, YF, YX):
        r.wait_sent()
        r.wait_here()


def step(plan, w_qkv, w_out, w_up, w_down, tok, fv, cot, small):
    R, C, n_mp, n_z, n = plan.rows, plan.cols, plan.n_mp, plan.n_z, plan.n
    count = np.arange(D, dtype=np.int32)
    tab = np.zeros((8, D), np.int32)
    for at, width in ((0, D // n), (2, VFRESH // n), (4, FF // n)):
        tab[at], tab[at + 1] = count % width, count // width
    r = np.arange(n, dtype=np.int32)
    dev = np.tile(((r % plan.n_dp) * n_mp + r // plan.n_dp)[:, None], (1, 128))
    vm = pltpu.VMEM
    dma = pltpu.SemaphoreType.DMA
    wide = lambda t: vm((SEQ, D), t)
    tall = lambda t: vm((D, SEQ), t)
    panel = lambda rows, cols: vm((n_mp, n_z, 2, rows, cols), BF)

    def sums(rows, cols):
        ring = n_z // 2 + (plan.half - 1) * n_z
        return [
            vm((n_mp, n_z, rows, cols), BF),
            vm((2, ring, rows, cols), BF),
            vm((n_z - 1, rows, cols), BF),
        ]

    def ring_last(rows, cols):
        return [
            vm((n_mp, n_z, rows, cols), BF),
            vm((2, plan.half, rows, cols), BF),
            vm((n_mp, n_z - 1, rows, cols), BF),
        ]

    panel_z = [dma((n_mp, n_z - 1))] * 2
    gather_sems = [dma((n_z - 1,))] * 2 + [dma((2, plan.half))] * 2 + [dma((n_mp,))] * 2
    reduce_sems = [dma((n_mp,))] * 2 + [dma((2, plan.half + 1))] * 2 + [dma((n_z - 1,))] * 2
    shape = jax.ShapeDtypeStruct
    ins = (jnp.asarray(tab), jnp.asarray(dev), w_qkv, w_out, w_up, w_down, tok, fv, cot, *small)
    return pl.pallas_call(
        functools.partial(step_kernel, plan, len(ins)),
        name="step",
        out_shape=(
            shape(tok.shape, BF),
            shape(tok.shape, BF),
            shape(fv.shape, BF),
            shape((R, plan.qw), F32),
            shape((8, plan.qw), F32),
            shape((R // plan.parts, C), F32),
            shape((R, C), F32),
            shape((R, C), F32),
        ),
        in_specs=[IN_VMEM] * 6 + [ANY] * 3 + [IN_VMEM] * N_VEC,
        out_specs=(ANY,) * 3 + (IN_VMEM,) * 5,
        scratch_shapes=[
            panel(R + 8, plan.qw), panel(R // plan.parts, C), panel(R, C), panel(R, C),
            vm(tok.shape, BF), vm(fv.shape, BF), vm(cot.shape, BF),
            vm(tok.shape, BF),
            *sums(R, plan.qw), *sums(8, plan.qw), *sums(R // plan.parts, C), *sums(R, C), *ring_last(R, C),
            vm((D, QKV), BF), vm((D, D), BF),
            vm((plan.vec_rows, n, plan.qw), F32), vm((n, 16, 128), F32), vm((16, D), F32), vm((max(8, n_mp), C), F32),
            tall(BF), vm((SEQ, 3 * D), BF), tall(BF),
            vm((HEADS // 2, 8, SEQ), F32),
            wide(F32), wide(BF), tall(BF), tall(BF),
            wide(F32), wide(F32), vm((n_mp, SEQ, C), BF), vm((n_mp, SEQ, C), BF), wide(BF),
            vm((SEQ, 128), F32), vm((SEQ, 128), F32), vm((128, SEQ), F32),
            vm((16, D), F32), vm((max(8, n_mp), C), F32),
            *(gather_sems * 4),
            *(panel_z + gather_sems[2:]),
            *(reduce_sems * 4),
            *(reduce_sems[:4] + panel_z),
            *([dma((MICRO,))] * 12),
        ],
        compiler_params=pltpu.CompilerParams(
            collective_id=0, has_side_effects=True, vmem_limit_bytes=63 << 20
        ),
    )(*ins)


def unpack_kernel(plan, widths, *refs):
    (r1, r2, r3, t_q, t_s, t_o, t_u, t_d), outs, sem = refs[:8], refs[8:24], refs[24]
    moves = [pltpu.make_async_copy(src, dst, sem.at[k]) for k, (src, dst) in enumerate(zip((r1, r2, r3), outs[:3]))]
    for move in moves:
        move.start()
    outs[5][...] = t_q[:, 0 : plan.qkv]
    part = plan.rows // plan.parts
    for t in range(plan.parts):
        outs[8][t * part : (t + 1) * part, :] = t_o[:, t * plan.out : (t + 1) * plan.out]
    outs[12][...] = t_u[...]
    outs[14][...] = t_d[...]
    for v, at in enumerate((3, 4, 6, 7, 9, 10, 11, 13, 15)):
        row, lane = v // plan.spr, (v % plan.spr) * 128
        outs[at][...] = t_s[row, lane : lane + widths[v]]
    for move in moves:
        move.wait()


def unpack(plan, summed, widths):
    shape = lambda *dims: jax.ShapeDtypeStruct(dims, F32)
    vec = [shape(w) for w in widths]
    R, C = plan.rows, plan.cols
    out_shape = [jax.ShapeDtypeStruct(r.shape, BF) for r in summed[:3]]
    out_shape += [vec[0], vec[1], shape(R, plan.qkv), vec[2], vec[3], shape(R, plan.out)]
    out_shape += [vec[4], vec[5], vec[6], shape(R, C), vec[7], shape(R, C), vec[8]]
    return pl.pallas_call(
        functools.partial(unpack_kernel, plan, widths),
        name="unpack",
        out_shape=tuple(out_shape),
        in_specs=[IN_VMEM] * 3 + [IN_VMEM] * 5,
        out_specs=(ANY,) * 3 + (IN_VMEM,) * 13,
        scratch_shapes=[pltpu.SemaphoreType.DMA((3,))],
    )(*summed)


def shards(
    plan, tokens, first_values, out_cot, ln1_gain, ln1_bias, w_qkv, q_bias, v_bias, w_out, out_bias,
    ln2_gain, ln2_bias, w_up, up_bias, w_down, down_bias,
):
    small = (ln1_gain, ln1_bias, q_bias, v_bias, out_bias, ln2_gain, ln2_bias, up_bias, down_bias)
    assert tokens.shape[1] * plan.n_mp == SEQ
    summed = step(plan, w_qkv, w_out, w_up, w_down.T, tokens, first_values, out_cot, small)
    outs = unpack(plan, summed, [s.shape[0] for s in small])
    return (*outs[:14], outs[14].T, outs[15])


def layer_norm(inputs, gain_vec, shift_vec):
    average = jnp.mean(inputs, axis=-1, keepdims=True)
    centred = inputs - average
    variance = jnp.mean(centred * centred, axis=-1, keepdims=True)
    inv_std = lax.rsqrt(variance + EPS)
    scaled = centred * inv_std
    return (scaled * gain_vec + shift_vec, scaled, inv_std)


def norm_back_all(grad_out, scaled, inv_std, gain_vec):
    grad_scaled = grad_out * gain_vec
    first_term = jnp.mean(grad_scaled, axis=-1, keepdims=True)
    second_term = jnp.mean(grad_scaled * scaled, axis=-1, keepdims=True)
    grad_in = inv_std * (grad_scaled - first_term - scaled * second_term)
    return (grad_in, jnp.sum(grad_out * scaled, axis=0), jnp.sum(grad_out, axis=0))


def gelu_both(inputs):
    cubic_term = inputs + GELU_A * inputs * inputs * inputs
    tangent = jnp.tanh(GELU_C * cubic_term)
    gelu_out = 0.5 * inputs * (1.0 + tangent)
    gelu_slope = 0.5 * (1.0 + tangent) + 0.5 * inputs * (1.0 - tangent * tangent) * GELU_C * (
        1.0 + 3.0 * GELU_A * inputs * inputs
    )
    return (gelu_out, gelu_slope)


def split_heads(matrix):
    return matrix.reshape(matrix.shape[0], HEADS, HEAD)


def block_scores(query_heads, key_block, row_first, key_first):
    key_heads = split_heads(key_block)
    scores = jnp.einsum(
        "qhd,khd->hqk", query_heads, key_heads, preferred_element_type=jnp.float32
    ) * HEAD ** (-0.5)
    query_pos = row_first + jnp.arange(query_heads.shape[0], dtype=jnp.int32)
    key_pos = key_first + jnp.arange(key_block.shape[0], dtype=jnp.int32)
    allowed = key_pos[None, :] <= query_pos[:, None]
    return (jnp.where(allowed[None], scores, -BIG), allowed, key_heads)


def block_length():
    return 512


def fold_blocks(function, carried, key_block, value_block, key_first):
    row_count = key_block.shape[0]
    block_rows = block_length()
    if block_rows == row_count:
        return function(carried, key_block, value_block, key_first)
    key_parts = key_block.reshape(row_count // block_rows, block_rows, key_block.shape[1])
    value_parts = value_block.reshape(row_count // block_rows, block_rows, value_block.shape[1])
    offsets = key_first + jnp.arange(row_count // block_rows, dtype=jnp.int32) * block_rows

    def step_once(inner_state, element):
        return (function(inner_state, element[0], element[1], element[2]), None)

    result, ignored = lax.scan(step_once, carried, (key_parts, value_parts, offsets))
    return result


def map_blocks(function, key_block, value_block, key_first):
    row_count = key_block.shape[0]
    block_rows = block_length()
    if block_rows == row_count:
        return function(key_block, value_block, key_first)
    key_parts = key_block.reshape(row_count // block_rows, block_rows, key_block.shape[1])
    value_parts = value_block.reshape(row_count // block_rows, block_rows, value_block.shape[1])
    offsets = key_first + jnp.arange(row_count // block_rows, dtype=jnp.int32) * block_rows

    def apply_once(element):
        return function(element[0], element[1], element[2])

    outputs = lax.map(apply_once, (key_parts, value_parts, offsets))
    return outputs.reshape(row_count, outputs.shape[-1])


def attention_forward(queries, keys_low, values_low, row_first):
    query_heads = split_heads(queries)
    row_total = queries.shape[0]

    def online_step(fold_state, key_block, value_block, key_first):
        running_top, running_sum, running_acc = fold_state
        masked, allowed, ignored = block_scores(query_heads, key_block, row_first, key_first)
        new_top = jnp.maximum(running_top, jnp.max(masked, axis=-1))
        weights = jnp.exp(masked - new_top[:, :, None]) * allowed[None]
        shrink = jnp.exp(running_top - new_top)
        running_sum = running_sum * shrink + jnp.sum(weights, axis=-1)
        running_acc = running_acc * shrink[:, :, None] + jnp.einsum(
            "hqk,khd->hqd",
            weights.astype(jnp.bfloat16),
            split_heads(value_block),
            preferred_element_type=jnp.float32,
        )
        return (new_top, running_sum, running_acc)

    start_state = (
        jnp.full((HEADS, row_total), -BIG, jnp.float32),
        jnp.zeros((HEADS, row_total), jnp.float32),
        jnp.zeros((HEADS, row_total, HEAD), jnp.float32),
    )
    running_top, running_sum, running_acc = fold_blocks(
        online_step,
        start_state,
        lax.all_gather(keys_low, "mp", axis=0, tiled=True),
        lax.all_gather(values_low, "mp", axis=0, tiled=True),
        jnp.int32(0),
    )
    attended = (running_acc / running_sum[:, :, None]).transpose(1, 0, 2).reshape(row_total, D)
    return (attended, running_top + jnp.log(running_sum))


def attention_backward(queries, keys_low, values_low, grad_out, attended, log_total, row_first):
    query_heads = split_heads(queries)
    grad_heads = split_heads(grad_out)
    row_total = queries.shape[0]
    score_scale = HEAD ** (-0.5)
    row_delta = jnp.sum(grad_heads.astype(jnp.float32) * split_heads(attended), axis=-1).T
    keys_all, values_all = (
        lax.all_gather(keys_low, "mp", axis=0, tiled=True),
        lax.all_gather(values_low, "mp", axis=0, tiled=True),
    )

    def soft_grads(key_block, value_block, key_first):
        masked, allowed, key_heads = block_scores(query_heads, key_block, row_first, key_first)
        probabilities = jnp.exp(masked - log_total[:, :, None])
        grad_probs = jnp.einsum(
            "qhd,khd->hqk", grad_heads, split_heads(value_block), preferred_element_type=jnp.float32
        )
        grad_scores = (probabilities * (grad_probs - row_delta[:, :, None])).astype(jnp.bfloat16)
        return (probabilities, grad_scores, key_heads)

    def query_step(accum, key_block, value_block, key_first):
        probabilities, grad_scores, key_heads = soft_grads(key_block, value_block, key_first)
        return (
            accum
            + jnp.einsum("hqk,khd->qhd", grad_scores, key_heads, preferred_element_type=jnp.float32)
            * score_scale
        )

    grad_query = fold_blocks(
        query_step, jnp.zeros((row_total, HEADS, HEAD), jnp.float32), keys_all, values_all, 0
    )

    def key_step(key_block, value_block, key_first):
        probabilities, grad_scores, key_heads = soft_grads(key_block, value_block, key_first)
        grad_value = jnp.einsum(
            "hqk,qhd->khd",
            probabilities.astype(jnp.bfloat16),
            grad_heads,
            preferred_element_type=jnp.float32,
        )
        grad_key = (
            jnp.einsum("hqk,qhd->khd", grad_scores, query_heads, preferred_element_type=jnp.float32)
            * score_scale
        )
        return jnp.concatenate(
            [grad_key.reshape(key_block.shape[0], D), grad_value.reshape(key_block.shape[0], D)],
            axis=1,
        )

    key_block = keys_all
    value_block = values_all
    grad_kv = lax.psum_scatter(
        map_blocks(key_step, key_block, value_block, jnp.int32(0)).astype(jnp.bfloat16),
        "mp",
        scatter_dimension=0,
        tiled=True,
    ).astype(jnp.float32)
    return (grad_query.reshape(row_total, D), grad_kv)


def reduce_grads(local_grads):
    row_parts = (
        lax.psum_scatter(
            local_grads[0].astype(jnp.bfloat16), "dp", scatter_dimension=0, tiled=True
        ).astype(jnp.float32),
        lax.psum_scatter(
            local_grads[1].astype(jnp.bfloat16), "dp", scatter_dimension=0, tiled=True
        ).astype(jnp.float32),
        lax.psum_scatter(
            local_grads[2].astype(jnp.bfloat16), "dp", scatter_dimension=0, tiled=True
        ).astype(jnp.float32),
        lax.psum_scatter(
            local_grads[3].astype(jnp.bfloat16), "dp", scatter_dimension=0, tiled=True
        ).astype(jnp.float32),
        lax.psum_scatter(
            local_grads[4].astype(jnp.bfloat16), "dp", scatter_dimension=0, tiled=True
        ).astype(jnp.float32),
        lax.psum_scatter(
            local_grads[5].astype(jnp.bfloat16), "dp", scatter_dimension=0, tiled=True
        ).astype(jnp.float32),
        lax.psum_scatter(
            local_grads[6].astype(jnp.bfloat16), "dp", scatter_dimension=0, tiled=True
        ).astype(jnp.float32),
        lax.psum_scatter(
            local_grads[7].astype(jnp.bfloat16), "dp", scatter_dimension=0, tiled=True
        ).astype(jnp.float32),
        lax.psum_scatter(
            local_grads[8].astype(jnp.bfloat16), "dp", scatter_dimension=0, tiled=True
        ).astype(jnp.float32),
        lax.psum_scatter(
            local_grads[9].astype(jnp.bfloat16), "dp", scatter_dimension=0, tiled=True
        ).astype(jnp.float32),
        lax.psum_scatter(
            local_grads[10].astype(jnp.bfloat16), "dp", scatter_dimension=0, tiled=True
        ).astype(jnp.float32),
        lax.psum_scatter(
            local_grads[11].astype(jnp.bfloat16), "dp", scatter_dimension=1, tiled=True
        ).astype(jnp.float32),
        lax.psum_scatter(
            local_grads[12].astype(jnp.bfloat16), "dp", scatter_dimension=0, tiled=True
        ).astype(jnp.float32),
    )
    row_parts = tuple(row_parts)
    col_parts = tuple(
        (
            lax.psum_scatter(
                row_parts[0].astype(jnp.bfloat16), "mp", scatter_dimension=0, tiled=True
            ).astype(jnp.float32),
            lax.psum_scatter(
                row_parts[1].astype(jnp.bfloat16), "mp", scatter_dimension=0, tiled=True
            ).astype(jnp.float32),
            lax.psum_scatter(
                row_parts[2].astype(jnp.bfloat16), "mp", scatter_dimension=1, tiled=True
            ).astype(jnp.float32),
            lax.psum_scatter(
                row_parts[3].astype(jnp.bfloat16), "mp", scatter_dimension=0, tiled=True
            ).astype(jnp.float32),
            lax.psum_scatter(
                row_parts[4].astype(jnp.bfloat16), "mp", scatter_dimension=0, tiled=True
            ).astype(jnp.float32),
            lax.psum_scatter(
                row_parts[5].astype(jnp.bfloat16), "mp", scatter_dimension=1, tiled=True
            ).astype(jnp.float32),
            lax.psum_scatter(
                row_parts[6].astype(jnp.bfloat16), "mp", scatter_dimension=0, tiled=True
            ).astype(jnp.float32),
            lax.psum_scatter(
                row_parts[7].astype(jnp.bfloat16), "mp", scatter_dimension=0, tiled=True
            ).astype(jnp.float32),
            lax.psum_scatter(
                row_parts[8].astype(jnp.bfloat16), "mp", scatter_dimension=0, tiled=True
            ).astype(jnp.float32),
            lax.psum_scatter(
                row_parts[10].astype(jnp.bfloat16), "mp", scatter_dimension=0, tiled=True
            ).astype(jnp.float32),
            lax.psum_scatter(
                row_parts[12].astype(jnp.bfloat16), "mp", scatter_dimension=0, tiled=True
            ).astype(jnp.float32),
        )
    )
    return col_parts[:9] + (row_parts[9], col_parts[9], row_parts[11], col_parts[10])


def general_shards(
    tokens,
    first_values,
    out_cot,
    ln1_gain,
    ln1_bias,
    w_qkv,
    q_bias,
    v_bias,
    w_out,
    out_bias,
    ln2_gain,
    ln2_bias,
    w_up,
    up_bias,
    w_down,
    down_bias,
):
    near_blocks = tuple(
        (
            lax.all_gather(ln1_gain, "mp", axis=0, tiled=True),
            lax.all_gather(ln1_bias, "mp", axis=0, tiled=True),
            lax.all_gather(w_qkv, "mp", axis=1, tiled=True),
            lax.all_gather(q_bias, "mp", axis=0, tiled=True),
            lax.all_gather(v_bias, "mp", axis=0, tiled=True),
            lax.all_gather(w_out, "mp", axis=1, tiled=True),
            lax.all_gather(out_bias, "mp", axis=0, tiled=True),
            lax.all_gather(ln2_gain, "mp", axis=0, tiled=True),
            lax.all_gather(ln2_bias, "mp", axis=0, tiled=True),
            lax.all_gather(up_bias, "mp", axis=0, tiled=True),
            lax.all_gather(down_bias, "mp", axis=0, tiled=True),
        )
    )
    near_blocks = near_blocks[:9] + (w_up, near_blocks[9], w_down, near_blocks[10])
    params = tuple(
        (
            lax.all_gather(near_blocks[0], "dp", axis=0, tiled=True),
            lax.all_gather(near_blocks[1], "dp", axis=0, tiled=True),
            lax.all_gather(near_blocks[2], "dp", axis=0, tiled=True),
            lax.all_gather(near_blocks[3], "dp", axis=0, tiled=True),
            lax.all_gather(near_blocks[4], "dp", axis=0, tiled=True),
            lax.all_gather(near_blocks[5], "dp", axis=0, tiled=True),
            lax.all_gather(near_blocks[6], "dp", axis=0, tiled=True),
            lax.all_gather(near_blocks[7], "dp", axis=0, tiled=True),
            lax.all_gather(near_blocks[8], "dp", axis=0, tiled=True),
            lax.all_gather(near_blocks[9], "dp", axis=0, tiled=True),
            lax.all_gather(near_blocks[10], "dp", axis=0, tiled=True),
            lax.all_gather(near_blocks[11], "dp", axis=1, tiled=True),
            lax.all_gather(near_blocks[12], "dp", axis=0, tiled=True),
        )
    )
    gain_one = params[0].astype(jnp.float32)
    shift_one = params[1].astype(jnp.float32)
    qkv_full = params[2]
    query_shift = params[3].astype(jnp.float32)
    value_shift = params[4].astype(jnp.float32)
    out_full = params[5]
    out_shift = params[6].astype(jnp.float32)
    gain_two = params[7].astype(jnp.float32)
    shift_two = params[8].astype(jnp.float32)
    up_full = params[9]
    up_shift_all = params[10].astype(jnp.float32)
    down_full = params[11]
    down_shift = params[12].astype(jnp.float32)
    up_cols = up_full.shape[1]
    up_start = 0
    up_start = lax.axis_index("mp") * up_cols
    up_used = lax.dynamic_slice_in_dim(up_shift_all, up_start, up_cols, 0)
    row_total = tokens.shape[1]
    row_first = lax.axis_index("mp") * row_total
    fresh_cols = value_shift.shape[0]
    outputs = []
    grad_inputs = []
    grad_firsts = []
    summed = None
    for micro_index in range(MICRO):
        cot_low = out_cot[micro_index]
        inputs = tokens[micro_index].astype(jnp.float32)
        normed, scaled_one, inv_one = layer_norm(inputs, gain_one, shift_one)
        normed_low = normed.astype(jnp.bfloat16)
        mixed_proj = jnp.dot(normed_low, qkv_full, preferred_element_type=jnp.float32)
        queries = (mixed_proj[:, :D] + query_shift).astype(jnp.bfloat16)
        keys_low = mixed_proj[:, D : 2 * D].astype(jnp.bfloat16)
        values_low = jnp.concatenate(
            [
                (mixed_proj[:, 2 * D :] + value_shift).astype(jnp.bfloat16),
                first_values[micro_index],
            ],
            axis=1,
        )
        attended, log_total = attention_forward(queries, keys_low, values_low, row_first)
        attended_low = attended.astype(jnp.bfloat16)
        middle = inputs + (
            jnp.dot(attended_low, out_full, preferred_element_type=jnp.float32) + out_shift
        )
        normed_two, scaled_two, inv_two = layer_norm(middle, gain_two, shift_two)
        normed_two_low = normed_two.astype(jnp.bfloat16)
        cot_float = cot_low.astype(jnp.float32)
        row_piece = lax.all_gather(normed_two_low, "mp", axis=0, tiled=True)
        hidden = jnp.dot(row_piece, up_full, preferred_element_type=jnp.float32) + up_used
        gelu_out, gelu_slope = gelu_both(hidden)
        active_all = gelu_out.astype(jnp.bfloat16)
        down_part = lax.psum_scatter(
            jnp.dot(active_all, down_full, preferred_element_type=jnp.float32).astype(jnp.bfloat16),
            "mp",
            scatter_dimension=0,
            tiled=True,
        ).astype(jnp.float32)
        result = middle + (down_part + down_shift)
        back_row_piece = lax.all_gather(cot_low, "mp", axis=0, tiled=True)
        grad_active = jnp.einsum(
            "rd,fd->rf", back_row_piece, down_full, preferred_element_type=jnp.float32
        )
        back_gelu_out, back_gelu_slope = gelu_both(hidden)
        grad_hidden = (grad_active * back_gelu_slope).astype(jnp.bfloat16)
        grad_normed_two = lax.psum_scatter(
            jnp.einsum(
                "rf,df->rd", grad_hidden, up_full, preferred_element_type=jnp.float32
            ).astype(jnp.bfloat16),
            "mp",
            scatter_dimension=0,
            tiled=True,
        ).astype(jnp.float32)
        grad_down = jnp.einsum(
            "rf,rd->fd", active_all, back_row_piece, preferred_element_type=jnp.float32
        )
        grad_up = jnp.einsum(
            "rd,rf->df", row_piece, grad_hidden, preferred_element_type=jnp.float32
        )
        up_piece = jnp.sum(grad_hidden.astype(jnp.float32), axis=0)
        grad_up_shift = lax.dynamic_update_slice_in_dim(
            jnp.zeros((FF,), jnp.float32), up_piece, up_start, 0
        )
        grad_norm_two, grad_gain_two, grad_shift_two = norm_back_all(
            grad_normed_two, scaled_two, inv_two, gain_two
        )
        grad_middle = cot_float + grad_norm_two
        grad_branch = grad_middle.astype(jnp.bfloat16)
        grad_out_shift = jnp.sum(grad_branch.astype(jnp.float32), axis=0)
        grad_out_proj = jnp.einsum(
            "rd,re->de", attended_low, grad_branch, preferred_element_type=jnp.float32
        )
        grad_attended = jnp.einsum(
            "re,de->rd", grad_branch, out_full, preferred_element_type=jnp.float32
        ).astype(jnp.bfloat16)
        grad_query, grad_kv = attention_backward(
            queries, keys_low, values_low, grad_attended, attended, log_total, row_first
        )
        grad_query_low = grad_query.astype(jnp.bfloat16)
        grad_kv_low = grad_kv.astype(jnp.bfloat16)
        grad_mixed = jnp.concatenate([grad_query_low, grad_kv_low[:, : D + fresh_cols]], axis=1)
        grad_query_shift = jnp.sum(grad_query_low.astype(jnp.float32), axis=0)
        grad_value_shift = jnp.sum(grad_kv_low[:, D : D + fresh_cols].astype(jnp.float32), axis=0)
        grad_qkv = jnp.einsum(
            "rd,rc->dc", normed_low, grad_mixed, preferred_element_type=jnp.float32
        )
        grad_normed = jnp.einsum(
            "rc,dc->rd", grad_mixed, qkv_full, preferred_element_type=jnp.float32
        )
        grad_norm_one, grad_gain_one, grad_shift_one = norm_back_all(
            grad_normed, scaled_one, inv_one, gain_one
        )
        grad_input = grad_middle + grad_norm_one
        local_grads = (
            grad_gain_one,
            grad_shift_one,
            grad_qkv,
            grad_query_shift,
            grad_value_shift,
            grad_out_proj,
            grad_out_shift,
            grad_gain_two,
            grad_shift_two,
            grad_up,
            grad_up_shift,
            grad_down,
            jnp.sum(cot_float, axis=0),
        )
        result, grad_input, grad_first, local_grads = (
            result.astype(jnp.bfloat16),
            grad_input.astype(jnp.bfloat16),
            grad_kv_low[:, D + fresh_cols :],
            local_grads,
        )
        outputs.append(result)
        grad_inputs.append(grad_input)
        grad_firsts.append(grad_first)
        local_grads = reduce_grads(local_grads)
        summed = local_grads if summed is None else jax.tree.map(jnp.add, summed, local_grads)
    return (
        jnp.stack(outputs),
        jnp.stack(grad_inputs),
        jnp.stack(grad_firsts),
        summed[0],
        summed[1],
        summed[2],
        summed[3],
        summed[4],
        summed[5],
        summed[6],
        summed[7],
        summed[8],
        summed[9],
        summed[10],
        summed[11],
        summed[12],
    )


def solution(mesh):
    whole_sequences = mesh.shape["mp"] == MICRO
    body = functools.partial(shards, Plan(mesh)) if whole_sequences else general_shards
    line = P(("dp", "mp"))
    rows = P(None, ("dp", "mp"), None)
    block = P("dp", "mp")
    grads = (line, line, block, line, line, block, line, line, line, block, line, P("mp", "dp"), line)
    return jax.shard_map(
        body,
        mesh=mesh,
        in_specs=(rows, rows, rows) + grads,
        out_specs=(rows, rows, rows) + grads,
        check_vma=False,
    )
```

```python
import functools

import jax
import jax.numpy as jnp
import numpy as np
from jax import lax
from jax.experimental import pallas as pl
from jax.experimental.pallas import tpu as pltpu
from jax.sharding import PartitionSpec as P

D = 768
HEADS = 12
HEAD = 64
FF = 3072
MICRO = 4
QKV = 1920
SEQ = 512
VFRESH = 384

EPS = 1e-05
BIG = 1e30
GELU_C = 0.7978845608028654
GELU_A = 0.044715
MESH = pl.DeviceIdType.MESH
ANY = pl.BlockSpec(memory_space=pl.ANY)
IN_VMEM = pl.BlockSpec(memory_space=pltpu.VMEM)
BF, F32 = jnp.bfloat16, jnp.float32

WIDE = (0, 1, 2, 4, 5, 6, 8)
V_BIAS, UP_BIAS = 3, 7
G1, B1, QB, OB, G2, B2, DB = WIDE
N_VEC = 9
LANES = 32
UP_ROWS = (UP_BIAS, N_VEC, N_VEC + 1)


class Plan:
    def __init__(self, mesh):
        self.n_dp = mesh.shape["dp"]
        self.n_mp = mesh.shape["mp"]
        self.n = self.n_dp * self.n_mp
        self.n_z = self.n_dp // 2
        self.rows = D // self.n_dp
        self.cols = FF // self.n_mp
        self.qkv = QKV // self.n_mp
        self.out = D // self.n_mp
        self.qw = -(-self.qkv // 128) * 128
        self.parts = self.cols // self.out
        self.spr = self.qw // 128
        self.vec_rows = -(-N_VEC // self.spr)
        self.half = self.n_mp // 2
        self.per_seq = SEQ // (SEQ // MICRO)
        self.n_seq = self.n_mp // MICRO
        assert self.qkv + LANES <= self.qw and D // self.n <= LANES and FF // self.n <= 3 * LANES
        assert self.parts * self.out == self.cols and self.rows % (8 * self.parts) == 0 and self.vec_rows <= 8
        self.bits = self.n_z.bit_length() - 1
        assert self.n_seq * MICRO == self.n_mp and self.n_z == 1 << self.bits and self.bits > 0

    def ring_at(self, i):
        return i + (i // self.half) * (self.n_mp - 1 + self.half - 2 * i)

    def row_half(self, s, rows):
        middle = -(-rows // 32) * 16 if rows > 16 else 8
        return slice(middle, rows) if s else slice(0, middle)

    def slots(self, d):
        if d == self.half:
            return 0, self.n_z // 2
        return self.n_z // 2 + (d - 1) * self.n_z, self.n_z


def dot(a, b):
    return jnp.dot(a, b, preferred_element_type=F32)


def dot_nt(a, b):
    return lax.dot_general(a, b, (((1,), (1,)), ((), ())), preferred_element_type=F32)


def chunks(rows, step, body):
    @pl.loop(0, rows // step)
    def _(at):
        body(pl.ds(pl.multiple_of(at * step, step), step))


def norm_stats(r):
    average = jnp.mean(r, axis=-1, keepdims=True)
    centred = r - average
    variance = jnp.mean(centred * centred, axis=-1, keepdims=True)
    inv_std = lax.rsqrt(variance + EPS)
    return centred * inv_std, inv_std


def norm_back(grad_out, scaled, inv_std, gain):
    e = grad_out * gain
    first = jnp.mean(e, axis=-1, keepdims=True)
    second = jnp.mean(e * scaled, axis=-1, keepdims=True)
    return inv_std * (e - first - scaled * second)


class Exchange:
    def __init__(self, plan):
        self.plan = plan
        dp, i = lax.axis_index("dp"), lax.axis_index("mp")
        self.dp, self.i, self.c, self.z = dp, i, dp % 2, dp // 2
        self.sib = (dp + 1 - 2 * self.c, i)
        self.p = plan.ring_at(i)

    def at(self, pos):
        return self.plan.ring_at((pos + 2 * self.plan.n_mp) % self.plan.n_mp)

    def across(self, b):
        return self.z + (1 << b) * (1 - 2 * (self.z // (1 << b) % 2))

    def z_units(self, b, far):
        n_z = self.plan.n_z
        base = self.across(b) if far else self.z
        return [(base + m * (2 << b)) % n_z for m in range(n_z // (2 << b))]

    def z_slot(self, b, m):
        return self.plan.n_z // (2 << b) - 1 + m

    def z_device(self, b):
        return (self.across(b) * 2 + self.c, self.i)

    def greet(self):
        plan = self.plan
        barrier = pltpu.get_barrier_semaphore()
        partners = [self.sib]
        partners += [self.z_device(b) for b in range(plan.bits)]
        partners += [(self.dp, (self.i + k) % plan.n_mp) for k in range(1, plan.n_mp)]
        for partner in partners:
            pl.semaphore_signal(barrier, inc=1, device_id=partner, device_id_type=MESH)
        return lambda: pl.semaphore_wait(barrier, len(partners))

    def push(self, src, dst, send, recv, device):
        return pltpu.make_async_remote_copy(
            src_ref=src, dst_ref=dst, send_sem=send, recv_sem=recv, device_id=device, device_id_type=MESH
        )


class Gather:
    def __init__(self, ex, ref, sems, tile=slice(None)):
        self.ex, self.ref, self.tile = ex, ref, tile
        self.zs, self.zr, self.rs, self.rr, self.ss, self.sr = sems

    def z_copy(self, b, m):
        ex = self.ex
        view = self.ref.at[ex.i, ex.z_units(b, False)[m], ex.c, self.tile]
        at = ex.z_slot(b, m)
        return ex.push(view, view, self.zs.at[at], self.zr.at[at], ex.z_device(b))

    def ring_view(self, origin, s, d):
        n_z, half = self.ex.plan.n_z, self.ex.plan.half
        units = pl.ds(s * (n_z // 2), n_z // 2) if d == half else pl.ds(0, n_z)
        return self.ref.at[origin, units, self.ex.c, self.tile]

    def ring_copy(self, s, d):
        ex = self.ex
        sign = 1 - 2 * s
        view = self.ring_view(ex.at(ex.p - sign * (d - 1)), s, d)
        return ex.push(view, view, self.rs.at[s, d - 1], self.rr.at[s, d - 1], (ex.dp, ex.at(ex.p + sign)))

    def sib_copy(self, offset):
        ex = self.ex
        at = (offset + ex.plan.n_mp) % ex.plan.n_mp
        view = self.ref.at[ex.at(ex.p + offset), :, ex.c, self.tile]
        return ex.push(view, view, self.ss.at[at], self.sr.at[at], ex.sib)

    def start(self):
        for b in range(self.ex.plan.bits):
            self.z_copy(b, 0).start()

    def z_sizes(self):
        n_z = self.ex.plan.n_z
        return [(b, n_z // (2 << b)) for b in range(self.ex.plan.bits)]

    def spread(self):
        sizes = self.z_sizes()
        for b, count in reversed(sizes[:-1]):
            for m in range(sizes[b + 1][1]):
                self.z_copy(b + 1, m).wait_recv()
            for m in range(1, count):
                self.z_copy(b, m).start()

    def column(self):
        for m in range(self.z_sizes()[0][1]):
            self.z_copy(0, m).wait_recv()
        for s in range(2):
            self.ring_copy(s, 1).start()
        self.sib_copy(0).start()

    def hop(self, d):
        half = self.ex.plan.half
        for s in range(2):
            self.ring_copy(s, d).wait_recv()
            if d < half:
                self.ring_copy(s, d + 1).start()
                self.sib_copy(-d if s == 0 else d).start()
        if d == half:
            self.sib_copy(half).start()

    def wait_sib(self, offset):
        self.sib_copy(offset).wait_recv()

    def wait_sent(self, offset):
        half = self.ex.plan.half
        self.sib_copy(offset).wait_send()
        if offset == 0:
            for b, count in self.z_sizes():
                for m in range(count):
                    self.z_copy(b, m).wait_send()
            for s in range(2):
                self.ring_copy(s, 1).wait_send()
        elif abs(offset) < half:
            self.ring_copy(0 if offset < 0 else 1, abs(offset) + 1).wait_send()


class RingFirst(Gather):
    def ring_view(self, origin, s, d):
        ex = self.ex
        rows = ex.plan.row_half(s, self.ref.shape[3]) if d == ex.plan.half else slice(None)
        return self.ref.at[origin, ex.z, ex.c, rows]

    def panel_copy(self, offset, b, m):
        ex = self.ex
        view = self.ref.at[ex.at(ex.p + offset), ex.z_units(b, False)[m], ex.c]
        at = (offset + ex.plan.n_mp) % ex.plan.n_mp, ex.z_slot(b, m)
        return ex.push(view, view, self.zs.at[at], self.zr.at[at], ex.z_device(b))

    def begin(self, offset):
        for b in range(self.ex.plan.bits):
            self.panel_copy(offset, b, 0).start()

    def circle(self):
        for s in range(2):
            self.ring_copy(s, 1).start()

    def hop(self, d):
        half = self.ex.plan.half
        for s in range(2):
            self.ring_copy(s, d).wait_recv()
            if d < half:
                self.ring_copy(s, d + 1).start()
        if d < half:
            self.begin(-d)
            self.begin(d)
        else:
            self.begin(half)

    def spread(self, offset):
        sizes = self.z_sizes()
        for b, count in reversed(sizes[:-1]):
            for m in range(sizes[b + 1][1]):
                self.panel_copy(offset, b + 1, m).wait_recv()
            for m in range(1, count):
                self.panel_copy(offset, b, m).start()

    def column(self, offset):
        for m in range(self.z_sizes()[0][1]):
            self.panel_copy(offset, 0, m).wait_recv()
        self.sib_copy(offset).start()

    def wait_sent(self, offset):
        half = self.ex.plan.half
        self.sib_copy(offset).wait_send()
        for b, count in self.z_sizes():
            for m in range(count):
                self.panel_copy(offset, b, m).wait_send()
        if offset == 0:
            for s in range(2):
                self.ring_copy(s, 1).wait_send()
        elif abs(offset) < half:
            self.ring_copy(0 if offset < 0 else 1, abs(offset) + 1).wait_send()


class Reduce:
    def __init__(self, ex, ref, tile, other, ring, last, sems):
        self.ex, self.ref, self.tile = ex, ref, tile
        self.other, self.ring, self.last = other, ring, last
        self.ss, self.sr, self.rs, self.rr, self.zs, self.zr = sems

    def sib_copy(self, offset):
        ex = self.ex
        at = (offset + ex.plan.n_mp) % ex.plan.n_mp
        view = self.ref.at[ex.at(ex.p + offset), :, 1 - ex.c, self.tile]
        return ex.push(view, self.other.at[at], self.ss.at[at], self.sr.at[at], ex.sib)

    def ring_views(self, dest, s, d, part):
        plan = self.ex.plan
        at, count = plan.slots(d)
        first = 0
        if d == plan.half:
            first = s * count
        elif part is not None:
            count = plan.n_z // 2
            first, at = part * count, at + part * count
        return self.ref.at[dest, pl.ds(first, count), self.ex.c, self.tile], self.ring.at[s, pl.ds(at, count)]

    def ring_copy(self, s, d, part=None):
        ex = self.ex
        plan = ex.plan
        sign = 1 - 2 * s
        sem = d - 1 if part is None else plan.half - 2 + 2 * part
        view, there = self.ring_views(ex.at(ex.p + sign * d), s, d, part)
        return ex.push(view, there, self.rs.at[s, sem], self.rr.at[s, sem], (ex.dp, ex.at(ex.p + sign)))

    def ring_copies(self, s, d):
        if d == self.ex.plan.half - 1:
            return [self.ring_copy(s, d, part) for part in range(2)]
        return [self.ring_copy(s, d)]

    def z_copy(self, b, m):
        ex = self.ex
        view = self.ref.at[ex.i, ex.z_units(b, True)[m], ex.c, self.tile]
        at = ex.z_slot(b, m)
        return ex.push(view, self.last.at[at], self.zs.at[at], self.zr.at[at], ex.z_device(b))

    def z_sizes(self):
        n_z = self.ex.plan.n_z
        return [(b, n_z // (2 << b)) for b in range(self.ex.plan.bits)]

    def to_sibling(self, offset):
        self.sib_copy(offset).start()

    def add(self, offset, first, count, *terms):
        j = self.ex.at(self.ex.p + offset)

        @pl.loop(0, count)
        def _(u):
            value = self.ref[j, first + u, self.ex.c, self.tile, :].astype(F32)
            for buf, at in terms:
                value = value + buf(at + u).astype(F32)
            self.ref[j, first + u, self.ex.c, self.tile, :] = value.astype(BF)

    def from_sibling(self, offset):
        at = (offset + self.ex.plan.n_mp) % self.ex.plan.n_mp
        self.sib_copy(offset).wait_recv()
        self.add(offset, 0, self.ex.plan.n_z, (lambda u: self.other[at, u], 0))

    def far(self):
        half = self.ex.plan.half
        self.from_sibling(half)
        for s in range(2):
            self.ring_copy(s, half).start()

    def free(self, s):
        half = self.ex.plan.half
        self.from_sibling((1 - 2 * s) * (half - 1))
        self.ring_copy(s, half - 1, 1 - s).start()

    def bound(self, s):
        plan = self.ex.plan
        half = plan.half
        self.ring_copy(s, half).wait_recv()
        at, count = plan.slots(half)
        self.add((1 - 2 * s) * (half - 1), s * count, count, (lambda u: self.ring[s, u], at))
        self.ring_copy(s, half - 1, s).start()

    def wait_ring(self, s, d):
        for copy in self.ring_copies(s, d):
            copy.wait_recv()

    def nearer(self):
        plan = self.ex.plan
        for d in range(plan.half - 2, 0, -1):
            for s in range(2):
                offset = (1 - 2 * s) * d
                self.from_sibling(offset)
                self.wait_ring(s, d + 1)
                self.add(offset, 0, plan.n_z, (lambda u: self.ring[s, u], plan.slots(d + 1)[0]))
                self.ring_copy(s, d).start()

    def home(self):
        plan = self.ex.plan
        for s in range(2):
            self.wait_ring(s, 1)
        self.sib_copy(0).wait_recv()
        at = plan.slots(1)[0]
        self.add(
            0, 0, plan.n_z,
            (lambda u: self.other[0, u], 0),
            (lambda u: self.ring[0, u], at),
            (lambda u: self.ring[1, u], at),
        )
        for m in range(self.z_sizes()[0][1]):
            self.z_copy(0, m).start()

    def along(self):
        ex = self.ex
        for b, count in self.z_sizes()[:-1]:
            for m, unit in enumerate(ex.z_units(b, False)):
                self.z_copy(b, m).wait_recv()
                at = ex.z_slot(b, m)
                self.add(0, unit, 1, (lambda u: self.last[u], at))
            for m in range(count // 2):
                self.z_copy(b + 1, m).start()

    def finish(self):
        ex = self.ex
        self.z_copy(ex.plan.bits - 1, 0).wait_recv()
        return self.ref[ex.i, ex.z, ex.c, self.tile, :].astype(F32) + self.last[0].astype(F32)

    def wait_z_sent(self):
        for b, count in self.z_sizes():
            for m in range(count):
                self.z_copy(b, m).wait_send()

    def wait_sent(self):
        plan = self.ex.plan
        for offset in range(plan.n_mp):
            self.sib_copy(offset).wait_send()
        for s in range(2):
            for d in range(1, plan.half + 1):
                for copy in self.ring_copies(s, d):
                    copy.wait_send()
        self.wait_z_sent()


class RingLast(Reduce):
    def half_rows(self, s):
        return self.ex.plan.row_half(s, self.ref.shape[3])

    def panel_copy(self, offset, b, m):
        ex = self.ex
        view = self.ref.at[ex.at(ex.p + offset), ex.z_units(b, True)[m], ex.c, self.tile]
        at = (offset + ex.plan.n_mp) % ex.plan.n_mp, ex.z_slot(b, m)
        return ex.push(view, self.last.at[at], self.zs.at[at], self.zr.at[at], ex.z_device(b))

    def begin(self, offset):
        self.from_sibling(offset)
        for m in range(self.z_sizes()[0][1]):
            self.panel_copy(offset, 0, m).start()

    def take(self, offset, b):
        ex = self.ex
        q = (offset + ex.plan.n_mp) % ex.plan.n_mp
        for m, unit in enumerate(ex.z_units(b, False)):
            self.panel_copy(offset, b, m).wait_recv()
            self.add(offset, unit, 1, (lambda u: self.last[q, u], ex.z_slot(b, m)))

    def along(self, offset):
        for b, count in self.z_sizes()[:-1]:
            self.take(offset, b)
            for m in range(count // 2):
                self.panel_copy(offset, b + 1, m).start()

    def end(self, offset):
        self.take(offset, self.ex.plan.bits - 1)

    def ring_views(self, dest, s, d, part):
        ex = self.ex
        rows = slice(None)
        if d == ex.plan.half:
            rows = self.half_rows(s)
        elif part is not None:
            rows = self.half_rows(part)
        return self.ref.at[dest, ex.z, ex.c, rows], self.ring.at[s, d - 1, rows]

    def add_rows(self, offset, rows, *terms):
        ex = self.ex
        j = ex.at(ex.p + offset)
        value = self.ref[j, ex.z, ex.c, rows, :].astype(F32)
        for term in terms:
            value = value + term.astype(F32)
        self.ref[j, ex.z, ex.c, rows, :] = value.astype(BF)

    def far(self):
        for s in range(2):
            self.ring_copy(s, self.ex.plan.half).start()

    def free(self, s):
        self.ring_copy(s, self.ex.plan.half - 1, 1 - s).start()

    def bound(self, s):
        plan = self.ex.plan
        half = plan.half
        self.ring_copy(s, half).wait_recv()
        rows = self.half_rows(s)
        self.add_rows((1 - 2 * s) * (half - 1), rows, self.ring[s, half - 1, rows, :])
        self.ring_copy(s, half - 1, s).start()

    def nearer(self):
        for d in range(self.ex.plan.half - 2, 0, -1):
            for s in range(2):
                self.wait_ring(s, d + 1)
                self.add_rows((1 - 2 * s) * d, slice(None), self.ring[s, d])
                self.ring_copy(s, d).start()

    def finish(self):
        ex = self.ex
        for s in range(2):
            self.wait_ring(s, 1)
        value = self.ref[ex.i, ex.z, ex.c].astype(F32)
        return value + self.ring[0, 0].astype(F32) + self.ring[1, 0].astype(F32)

    def wait_z_sent(self):
        for offset in range(self.ex.plan.n_mp):
            for b, count in self.z_sizes():
                for m in range(count):
                    self.panel_copy(offset, b, m).wait_send()


class Rows:
    def __init__(self, ex, src, dst, send, recv, out):
        self.ex, self.src, self.dst, self.send, self.recv, self.out = ex, src, dst, send, recv, out

    def move(self, start):
        ex = self.ex
        plan, i = ex.plan, ex.i
        q = plan.per_seq
        for m in range(MICRO):
            if self.out:
                target, place = (i % plan.n_seq) * q + m, i // plan.n_seq
            else:
                target, place = m * plan.n_seq + i // q, i % q
            far = ex.push(self.src.at[m], self.dst.at[place], self.send.at[m], self.recv.at[place], (ex.dp, target))
            near = pltpu.make_async_copy(self.src.at[m], self.dst.at[place], self.send.at[m])

            @pl.when(target != i)
            def _():
                far.start() if start else far.wait_send()

            @pl.when(target == i)
            def _():
                near.start() if start else near.wait()

    def start(self):
        self.move(True)

    def wait_sent(self):
        self.move(False)

    def wait_here(self):
        ex = self.ex
        plan, i = ex.plan, ex.i
        q = plan.per_seq
        for m in range(MICRO):
            origin = m * plan.n_seq + i // q if self.out else (i % plan.n_seq) * q + m

            @pl.when(origin != i)
            def _():
                ex.push(self.dst.at[m], self.dst.at[m], self.send.at[0], self.recv.at[m], ex.sib).wait_recv()


def step_kernel(plan, n_in, *refs):
    (tab, dev, w_qkv, w_out, w_up, w_down, tok, fv, cot), small = refs[:9], refs[9:n_in]
    (o_out, o_dx, o_df, o_q, o_s, o_o, o_u, o_d) = refs[n_in : n_in + 8]
    (
        gq, go, gu, gd, x3, f3, y3, out3,
        q_other, q_ring, q_last, s_other, s_ring, s_last, o_other, o_ring, o_last, u_other, u_ring, u_last,
        d_other, d_ring, d_last,
        wq, wo, sv, tail, vec, ub, hlt, qkv, otb, lse, mid, h2, h2t, yt,
        big, acc, act, slope, du, dv, dk, dqt, sums, ubg,
    ) = refs[n_in + 8 : n_in + 8 + 47]
    sems = refs[n_in + 8 + 47 :]
    dx3, df3 = y3, f3
    R, C, n_mp, n_dp, n_z = plan.rows, plan.cols, plan.n_mp, plan.n_dp, plan.n_z
    step = 64
    part = R // plan.parts
    ex = Exchange(plan)
    i, z, c = ex.i, ex.z, ex.c
    Q = Gather(ex, gq, sems[0:6], slice(0, R))
    O = Gather(ex, go, sems[6:12])
    U1 = Gather(ex, gu, sems[12:18], plan.row_half(0, R))
    U2 = Gather(ex, gu, sems[18:24], plan.row_half(1, R))
    W = RingFirst(ex, gd, sems[24:30])
    RQ = Reduce(ex, gq, slice(0, R), q_other, q_ring, q_last, sems[30:36])
    RS = Reduce(ex, gq, slice(R, R + 8), s_other, s_ring, s_last, sems[36:42])
    RU = Reduce(ex, gu, slice(0, R), u_other, u_ring, u_last, sems[42:48])
    RO = Reduce(ex, go, slice(0, part), o_other, o_ring, o_last, sems[48:54])
    RD = RingLast(ex, gd, slice(0, R), d_other, d_ring, d_last, sems[54:60])
    a2a = sems[60:72]
    XT = Rows(ex, tok, x3, a2a[0], a2a[1], False)
    XF = Rows(ex, fv, f3, a2a[2], a2a[3], False)
    XY = Rows(ex, cot, y3, a2a[4], a2a[5], False)
    YO = Rows(ex, out3, o_out, a2a[6], a2a[7], True)
    YX = Rows(ex, dx3, o_dx, a2a[8], a2a[9], True)
    YF = Rows(ex, df3, o_df, a2a[10], a2a[11], True)
    near = range(-plan.half + 1, plan.half)

    all_here = ex.greet()
    gq[i, z, c, 0:R, 0 : plan.qkv] = w_qkv[...]
    sv[0, 0:16, 0:128] = jnp.zeros((16, 128), F32)
    sv[1, 0:1, 0 : 3 * LANES] = jnp.zeros((1, 3 * LANES), F32)
    sv[1, 0:1, 0 : small[UP_BIAS].shape[0]] = small[UP_BIAS][...].astype(F32)[None]
    for v in range(N_VEC):
        if v != UP_BIAS:
            sv[0, v : v + 1, 0 : small[v].shape[0]] = small[v][...].astype(F32)[None]
    for k, r in enumerate(UP_ROWS):
        sv[0, r : r + 1, 0:LANES] = sv[1, 0:1, k * LANES : (k + 1) * LANES]
    gq[i, z, c, 0:16, plan.qw - LANES :] = sv[0, 0:16, 0:LANES].astype(BF)
    def rows_of(ref3, at, step):
        part = SEQ // MICRO
        return ref3.at[at // (part // step), pl.ds(pl.multiple_of((at % (part // step)) * step, step), step)]

    def blocks(step, body):
        @pl.loop(0, SEQ // step)
        def _(at):
            body(at, pl.ds(pl.multiple_of(at * step, step), step))

    all_here()
    Q.start()
    XT.start()
    for t in range(plan.parts):
        go[i, z, c, :, t * plan.out : (t + 1) * plan.out] = w_out[t * part : (t + 1) * part, :]
    gu[i, z, c] = w_up[...]
    gd[i, z, c] = w_down[...]
    Q.spread()
    Q.column()
    W.circle()
    O.start()
    U1.start()
    U2.start()
    W.begin(0)
    XT.wait_here()
    XT.wait_sent()

    def first_stats(at, rows):
        acc[rows, :], _ = norm_stats(rows_of(x3, at, step)[...].astype(F32))

    blocks(step, first_stats)
    Q.hop(1)
    U1.spread()
    XF.start()
    U2.spread()
    W.spread(0)
    O.spread()
    U1.column()
    U2.column()
    O.column()
    W.column(0)
    W.hop(1)
    for d in range(2, plan.half + 1):
        Q.hop(d)

    rowdev = dev[:, 0:1]
    row = lambda v: vec[v : v + 1, :]
    lanes = lambda v: slice((v % plan.spr) * 128, (v % plan.spr) * 128 + 128)
    onehot = lambda t, width: (lax.broadcasted_iota(jnp.int32, (128, width), 0) == tab[t : t + 1, :width]).astype(BF)
    e24 = onehot(0, D)
    e96 = onehot(4, C)

    for offset in (*near, plan.half):
        Q.wait_sib(offset)

    for j in range(n_mp):
        for d in range(n_dp):
            rows = slice(d * R, (d + 1) * R)
            wq[rows, j * plan.qkv : (j + 1) * plan.qkv] = gq[j, d // 2, d % 2, 0:R, 0 : plan.qkv]
    for j in range(n_mp):
        for d in range(n_dp):
            tail[j * n_dp + d] = gq[j, d // 2, d % 2, 0:16, plan.qw - 128 :].astype(F32)
    skip = 128 - LANES
    shifted = lambda t, width, back: (
        lax.broadcasted_iota(jnp.int32, (128, width), 0) - skip == tab[t : t + 1, :width] - back
    ) & (lax.broadcasted_iota(jnp.int32, (128, width), 0) >= skip)

    def expand(r, e, owner):
        got = dot(tail[:, r, :].astype(BF), e.astype(BF))
        return jnp.sum(jnp.where(owner == rowdev, got, 0.0), axis=0, keepdims=True)

    for v in WIDE:
        vec[v : v + 1, :] = expand(v, shifted(0, D, 0), tab[1:2, :])
    vec[V_BIAS : V_BIAS + 1, :] = expand(V_BIAS, shifted(2, D, 0), tab[3:4, :])
    for j in range(n_mp):
        owner = tab[5:6, :C] + j * n_dp
        ub[j : j + 1, :] = sum(expand(r, shifted(4, C, k * LANES), owner) for k, r in enumerate(UP_ROWS))

    def first_norm(at, rows):
        rows_of(out3, at, step)[...] = (acc[rows, :] * row(G1) + row(B1)).astype(BF)

    blocks(step, first_norm)
    for d in range(2, plan.half + 1):
        W.hop(d)
    hl = out3[...].reshape(SEQ, D)
    hlt[...] = hl.T
    XF.wait_here()
    XF.wait_sent()

    q = dot(hl, wq[:, 0:D]) + row(QB)
    qkv[:, 0:D] = q.astype(BF) * 0.125
    qkv[:, D : 2 * D] = dot(hl, wq[:, D : 2 * D]).astype(BF)
    v = dot(hl, wq[:, 2 * D : QKV]) + row(V_BIAS)[:, :VFRESH]
    qkv[:, 2 * D : QKV] = v.astype(BF)
    qkv[:, QKV : 3 * D] = f3[...].reshape(SEQ, D // 2)

    B = 256
    head_of = lax.broadcasted_iota(jnp.int32, (1, 128), 1) // HEAD
    keep = lax.broadcasted_iota(jnp.int32, (B, B), 0) <= lax.broadcasted_iota(jnp.int32, (B, B), 1)

    def scores(k2, qm, at):
        s = dot_nt(k2, qm)
        last = jnp.where(keep, s[at * B :, :], -BIG)
        return last if at == 0 else jnp.concatenate([s[: at * B, :], last], axis=0)

    @pl.loop(0, HEADS // 2)
    def _(t):
        cols = lambda base: pl.ds(pl.multiple_of(base + t * 128, 128), 128)
        vt = qkv[:, cols(2 * D)].T
        for e in range(2):
            mask = (head_of == e).astype(BF)
            for at in range(SEQ // B):
                kk = (at + 1) * B
                span = slice(at * B, kk)
                s = scores(qkv[0:kk, cols(D)], qkv[span, cols(0)] * mask, at)
                top = jnp.max(s, axis=0, keepdims=True)
                ex_ = jnp.exp(s - top)
                total = jnp.sum(ex_, axis=0, keepdims=True)
                o = dot(vt[e * HEAD : (e + 1) * HEAD, 0:kk], ex_.astype(BF)) / total
                otb[pl.ds(pl.multiple_of(t * 128 + e * HEAD, HEAD), HEAD), span] = o.astype(BF)
                lse[t, e : e + 1, span] = top + jnp.log(total)

        @pl.when(t == 0)
        def _():
            for d in range(1, plan.half):
                O.hop(d)

        @pl.when(t == 1)
        def _():
            for d in range(1, plan.half):
                U1.hop(d)
                U2.hop(d)
            XY.start()
            for offset in near:
                if offset:
                    W.spread(offset)

        @pl.when(t == 3)
        def _():
            O.hop(plan.half)

        @pl.when(t == 5)
        def _():
            W.spread(plan.half)

    for offset in (*near, plan.half):
        O.wait_sib(offset)
    for j in range(n_mp):
        for d in range(n_dp):
            for t in range(plan.parts):
                rows = slice(d * R + t * part, d * R + (t + 1) * part)
                wo[rows, j * plan.out : (j + 1) * plan.out] = go[
                    j, d // 2, d % 2, :, t * plan.out : (t + 1) * plan.out
                ]
    du[:, 0:D] = otb[...].T

    acc[...] = dot(du[:, 0:D], wo[...]) + row(OB)

    def second_norm(at, rows):
        m = rows_of(x3, at, step)[...].astype(F32) + acc[rows, :]
        mid[rows, :] = m
        scaled, _ = norm_stats(m)
        h2[rows, :] = (scaled * row(G2) + row(B2)).astype(BF)

    blocks(step, second_norm)
    for offset in near:
        if offset:
            W.column(offset)
    h2t[...] = h2[...].T
    acc[...] = jnp.zeros_like(acc)
    big[...] = jnp.zeros_like(big)

    offset_of = lambda q: (q + 1) // 2 * (1 - 2 * (q % 2))

    @pl.loop(0, n_mp)
    def _(q):
        j = ex.at(ex.p + offset_of(q))
        for s in range(n_mp):
            offset = plan.half if s == n_mp - 1 else offset_of(s)

            @pl.when(q == s)
            def _():
                if s == 1:
                    W.column(plan.half)
                    U1.hop(plan.half)
                    U2.hop(plan.half)
                U1.wait_sib(offset)
                U2.wait_sib(offset)
                W.wait_sib(offset)

        u = dot(h2[...], gu[j].reshape(D, C)) + ub[pl.ds(j, 1), :]
        u2 = u * u
        tangent = jnp.tanh(GELU_C * (u + GELU_A * u2 * u))
        half = 0.5 * (1.0 + tangent)
        a = (u * half).astype(BF)
        act[j] = a
        slope[j] = (
            half + 0.5 * u * (1.0 - tangent * tangent) * GELU_C * (1.0 + 3.0 * GELU_A * u2)
        ).astype(BF)
        acc[...] += dot_nt(a, gd[j].reshape(D, C))

    def finish_out(at, rows):
        rows_of(out3, at, step)[...] = (mid[rows, :] + (acc[rows, :] + row(DB))).astype(BF)

    blocks(step, finish_out)
    YO.start()
    XY.wait_here()
    XY.wait_sent()
    yt[...] = y3[...].reshape(SEQ, D).T

    order = [plan.half]
    for d in range(plan.half - 1, 0, -1):
        order += [-d, d]
    order += [0]

    def nth(q):
        d = plan.half - (q + 1) // 2
        return jnp.where(q == 0, plan.half, jnp.where(q == n_mp - 1, 0, d * (1 - 2 * (q % 2))))

    def up_leaves(offset):
        if offset == plan.half:
            RU.far()
        elif abs(offset) == plan.half - 1:
            RU.free(0 if offset > 0 else 1)

    @pl.loop(0, n_mp)
    def _(q):
        j = ex.at(ex.p + nth(q))
        g = (dot(y3[...].reshape(SEQ, D), gd[j].reshape(D, C)) * slope[j].astype(F32)).astype(BF)
        du[:, 0:C] = g
        big[...] += dot_nt(g, gu[j].reshape(D, C))
        for s, offset in enumerate(order):

            @pl.when(q == s)
            def _():
                if s >= 1:
                    up_leaves(order[s - 1])
                if s >= 2:
                    RD.begin(order[s - 2])
                W.wait_sent(offset)
                U1.wait_sent(offset)
                U2.wait_sent(offset)

        gu[j] = dot(h2t[...], du[:, 0:C]).astype(BF).reshape(n_z, 2, R, C)
        for s, offset in enumerate(order):

            @pl.when(q == s)
            def _():
                RU.to_sibling(offset)

        gd[j] = dot(yt[...], act[j]).astype(BF).reshape(n_z, 2, R, C)
        ubg[pl.ds(j, 1), :] = jnp.sum(du[:, 0:C].astype(F32), axis=0, keepdims=True)
        for s, offset in enumerate(order):

            @pl.when(q == s)
            def _():
                RD.to_sibling(offset)

    RD.begin(order[-2])
    sums[...] = jnp.zeros_like(sums)

    def second_back(at, rows):
        dh = big[rows, :]
        dy = rows_of(y3, at, step)[...].astype(F32)
        scaled, inv = norm_stats(mid[rows, :])
        dr = norm_back(dh, scaled, inv, row(G2))
        dmid = dy + dr
        mid[rows, :] = dmid
        low = dmid.astype(BF)
        du[rows, 0:D] = low
        total = lambda a: jnp.sum(a, axis=0, keepdims=True)
        sums[G2 : G2 + 1, :] += total(dh * scaled)
        sums[B2 : B2 + 1, :] += total(dh)
        sums[OB : OB + 1, :] += total(low.astype(F32))
        sums[DB : DB + 1, :] += total(dy)

    blocks(step, second_back)
    for offset in order[:-4]:
        RD.along(offset)
        RD.end(offset)
    for offset in (*near, plan.half):
        O.wait_sent(offset)
        Q.wait_sent(offset)
    for j in range(n_mp):
        g = dot(otb[...], du[:, j * plan.out : (j + 1) * plan.out]).reshape(n_z, 2, plan.parts, part, plan.out)
        for t in range(plan.parts):
            go[j, :, :, :, t * plan.out : (t + 1) * plan.out] = g[:, :, t].astype(BF)
    for offset in order:
        RO.to_sibling(offset)
    do = h2
    do[...] = dot_nt(du[:, 0:D], wo[...]).astype(BF)
    RD.begin(0)
    RU.bound(0)
    RO.far()
    RO.free(0)
    RO.free(1)
    RU.bound(1)

    @pl.loop(0, HEADS // 2)
    def _(t):
        cols = lambda base: pl.ds(pl.multiple_of(base + t * 128, 128), 128)
        kt = qkv[:, cols(D)].T
        dot_ = do[:, cols(0)].astype(F32).T
        prod = dot_ * otb[cols(0), :].astype(F32)
        dv[...] = jnp.zeros_like(dv)
        dk[...] = jnp.zeros_like(dk)
        for e in range(2):
            mask = (head_of == e).astype(BF)
            delta = jnp.sum(prod[e * HEAD : (e + 1) * HEAD, :], axis=0, keepdims=True)
            for at in range(SEQ // B):
                kk = (at + 1) * B
                span = slice(at * B, kk)
                qm = qkv[span, cols(0)] * mask
                dom = do[span, cols(0)] * mask
                s = scores(qkv[0:kk, cols(D)], qm, at)
                p = jnp.exp(s - lse[t, e : e + 1, span])
                dp = dot_nt(qkv[0:kk, cols(2 * D)], dom)
                ds = (p * (dp - delta[:, span])).astype(BF)
                dv[0:kk, :] += dot(p.astype(BF), dom)
                dk[0:kk, :] += dot(ds, qm)
                dqt[e * HEAD : (e + 1) * HEAD, span] = dot(kt[e * HEAD : (e + 1) * HEAD, 0:kk], ds)
        qkv[:, cols(0)] = (dqt[...].T * 0.125).astype(BF)
        qkv[:, cols(D)] = dk[...].astype(BF)
        qkv[:, cols(2 * D)] = dv[...].astype(BF)

        @pl.when(t == 3)
        def _():
            RD.along(order[-4])

    df3[...] = qkv[:, QKV : 3 * D].reshape(df3.shape)
    YF.start()
    RO.bound(1)
    for j in range(n_mp):
        g = dot(hlt[...], qkv[:, j * plan.qkv : (j + 1) * plan.qkv]).astype(BF)
        gq[j, :, :, 0:R, 0 : plan.qkv] = g.reshape(n_z, 2, R, plan.qkv)
    for offset in order:
        RQ.to_sibling(offset)
    RO.bound(0)
    RD.along(order[-3])
    acc[...] = dot_nt(qkv[:, 0:QKV], wq[...])
    RD.along(order[-2])
    RQ.far()
    RQ.free(0)
    RQ.free(1)

    def first_back(at, rows):
        n1, inv = norm_stats(rows_of(x3, at, step)[...].astype(F32))
        dh = acc[rows, :]
        dr = norm_back(dh, n1, inv, row(G1))
        rows_of(dx3, at, step)[...] = (mid[rows, :] + dr).astype(BF)
        total = lambda a: jnp.sum(a, axis=0, keepdims=True)
        sums[G1 : G1 + 1, :] += total(dh * n1)
        sums[B1 : B1 + 1, :] += total(dh)
        sums[QB : QB + 1, :] += total(qkv[rows, 0:D].astype(F32))
        sums[V_BIAS : V_BIAS + 1, 0:VFRESH] += total(qkv[rows, 2 * D : QKV].astype(F32))

    blocks(step, first_back)

    def collect(g, e, owner):
        return dot_nt(jnp.where(owner == rowdev, g, 0.0).astype(BF), e)

    for v in WIDE:
        sv[v // plan.spr, :, lanes(v)] = collect(sums[v : v + 1, :], e24, tab[1:2, :])
    sv[V_BIAS // plan.spr, :, lanes(V_BIAS)] = collect(sums[V_BIAS : V_BIAS + 1, :], onehot(2, D), tab[3:4, :])
    got = collect(ubg[0:1, :], e96, tab[5:6, :C])
    for j in range(1, n_mp):
        got = got + collect(ubg[j : j + 1, :], e96, tab[5:6, :C] + j * n_dp)
    sv[UP_BIAS // plan.spr, :, lanes(UP_BIAS)] = got
    at8 = lax.broadcasted_iota(jnp.int32, (8, plan.qw), 0)
    for j in range(n_mp):
        for d in range(n_dp):
            at = j * n_dp + d
            value = jnp.zeros((8, plan.qw), F32)
            for r in range(plan.vec_rows):
                value = jnp.where(at8 == r, sv[r, at : at + 1, :], value)
            gq[j, d // 2, d % 2, R:, :] = value.astype(BF)
    for offset in order:
        RS.to_sibling(offset)
    RD.along(order[-1])
    RS.far()
    RS.free(0)
    RS.free(1)
    RO.nearer()
    RO.home()
    RU.nearer()
    RU.home()
    RS.bound(1)
    RS.bound(0)
    RS.nearer()
    RS.home()
    RD.end(order[-4])
    RD.far()
    RQ.bound(1)
    RS.along()
    RQ.bound(0)
    RO.along()
    o_s[...] = RS.finish()
    RD.end(order[-3])
    RD.free(1)
    RD.bound(1)
    RQ.nearer()
    RQ.home()
    YX.start()
    RD.end(order[-2])
    RD.free(0)
    RD.bound(0)
    o_o[...] = RO.finish()
    RU.along()
    RD.end(order[-1])
    RD.nearer()
    RQ.along()
    o_d[...] = RD.finish()
    o_u[...] = RU.finish()
    o_q[...] = RQ.finish()
    for r in (RU, RD, RO, RQ, RS):
        r.wait_sent()
    for r in (YO, YF, YX):
        r.wait_sent()
        r.wait_here()


def step(plan, w_qkv, w_out, w_up, w_down, tok, fv, cot, small):
    R, C, n_mp, n_z, n = plan.rows, plan.cols, plan.n_mp, plan.n_z, plan.n
    count = np.arange(D, dtype=np.int32)
    tab = np.zeros((8, D), np.int32)
    for at, width in ((0, D // n), (2, VFRESH // n), (4, FF // n)):
        tab[at], tab[at + 1] = count % width, count // width
    r = np.arange(n, dtype=np.int32)
    dev = np.tile(((r % plan.n_dp) * n_mp + r // plan.n_dp)[:, None], (1, 128))
    vm = pltpu.VMEM
    dma = pltpu.SemaphoreType.DMA
    wide = lambda t: vm((SEQ, D), t)
    tall = lambda t: vm((D, SEQ), t)
    panel = lambda rows, cols: vm((n_mp, n_z, 2, rows, cols), BF)

    def sums(rows, cols):
        ring = n_z // 2 + (plan.half - 1) * n_z
        return [
            vm((n_mp, n_z, rows, cols), BF),
            vm((2, ring, rows, cols), BF),
            vm((n_z - 1, rows, cols), BF),
        ]

    def ring_last(rows, cols):
        return [
            vm((n_mp, n_z, rows, cols), BF),
            vm((2, plan.half, rows, cols), BF),
            vm((n_mp, n_z - 1, rows, cols), BF),
        ]

    panel_z = [dma((n_mp, n_z - 1))] * 2
    gather_sems = [dma((n_z - 1,))] * 2 + [dma((2, plan.half))] * 2 + [dma((n_mp,))] * 2
    reduce_sems = [dma((n_mp,))] * 2 + [dma((2, plan.half + 1))] * 2 + [dma((n_z - 1,))] * 2
    shape = jax.ShapeDtypeStruct
    ins = (jnp.asarray(tab), jnp.asarray(dev), w_qkv, w_out, w_up, w_down, tok, fv, cot, *small)
    return pl.pallas_call(
        functools.partial(step_kernel, plan, len(ins)),
        name="step",
        out_shape=(
            shape(tok.shape, BF),
            shape(tok.shape, BF),
            shape(fv.shape, BF),
            shape((R, plan.qw), F32),
            shape((8, plan.qw), F32),
            shape((R // plan.parts, C), F32),
            shape((R, C), F32),
            shape((R, C), F32),
        ),
        in_specs=[IN_VMEM] * 6 + [ANY] * 3 + [IN_VMEM] * N_VEC,
        out_specs=(ANY,) * 3 + (IN_VMEM,) * 5,
        scratch_shapes=[
            panel(R + 8, plan.qw), panel(R // plan.parts, C), panel(R, C), panel(R, C),
            vm(tok.shape, BF), vm(fv.shape, BF), vm(cot.shape, BF),
            vm(tok.shape, BF),
            *sums(R, plan.qw), *sums(8, plan.qw), *sums(R // plan.parts, C), *sums(R, C), *ring_last(R, C),
            vm((D, QKV), BF), vm((D, D), BF),
            vm((plan.vec_rows, n, plan.qw), F32), vm((n, 16, 128), F32), vm((16, D), F32), vm((max(8, n_mp), C), F32),
            tall(BF), vm((SEQ, 3 * D), BF), tall(BF),
            vm((HEADS // 2, 8, SEQ), F32),
            wide(F32), wide(BF), tall(BF), tall(BF),
            wide(F32), wide(F32), vm((n_mp, SEQ, C), BF), vm((n_mp, SEQ, C), BF), wide(BF),
            vm((SEQ, 128), F32), vm((SEQ, 128), F32), vm((128, SEQ), F32),
            vm((16, D), F32), vm((max(8, n_mp), C), F32),
            *(gather_sems * 4),
            *(panel_z + gather_sems[2:]),
            *(reduce_sems * 4),
            *(reduce_sems[:4] + panel_z),
            *([dma((MICRO,))] * 12),
        ],
        compiler_params=pltpu.CompilerParams(
            collective_id=0, has_side_effects=True, vmem_limit_bytes=63 << 20
        ),
    )(*ins)


def unpack_kernel(plan, widths, *refs):
    (r1, r2, r3, t_q, t_s, t_o, t_u, t_d), outs, sem = refs[:8], refs[8:24], refs[24]
    moves = [pltpu.make_async_copy(src, dst, sem.at[k]) for k, (src, dst) in enumerate(zip((r1, r2, r3), outs[:3]))]
    for move in moves:
        move.start()
    outs[5][...] = t_q[:, 0 : plan.qkv]
    part = plan.rows // plan.parts
    for t in range(plan.parts):
        outs[8][t * part : (t + 1) * part, :] = t_o[:, t * plan.out : (t + 1) * plan.out]
    outs[12][...] = t_u[...]
    outs[14][...] = t_d[...]
    for v, at in enumerate((3, 4, 6, 7, 9, 10, 11, 13, 15)):
        row, lane = v // plan.spr, (v % plan.spr) * 128
        outs[at][...] = t_s[row, lane : lane + widths[v]]
    for move in moves:
        move.wait()


def unpack(plan, summed, widths):
    shape = lambda *dims: jax.ShapeDtypeStruct(dims, F32)
    vec = [shape(w) for w in widths]
    R, C = plan.rows, plan.cols
    out_shape = [jax.ShapeDtypeStruct(r.shape, BF) for r in summed[:3]]
    out_shape += [vec[0], vec[1], shape(R, plan.qkv), vec[2], vec[3], shape(R, plan.out)]
    out_shape += [vec[4], vec[5], vec[6], shape(R, C), vec[7], shape(R, C), vec[8]]
    return pl.pallas_call(
        functools.partial(unpack_kernel, plan, widths),
        name="unpack",
        out_shape=tuple(out_shape),
        in_specs=[IN_VMEM] * 3 + [IN_VMEM] * 5,
        out_specs=(ANY,) * 3 + (IN_VMEM,) * 13,
        scratch_shapes=[pltpu.SemaphoreType.DMA((3,))],
    )(*summed)


def shards(
    plan, tokens, first_values, out_cot, ln1_gain, ln1_bias, w_qkv, q_bias, v_bias, w_out, out_bias,
    ln2_gain, ln2_bias, w_up, up_bias, w_down, down_bias,
):
    small = (ln1_gain, ln1_bias, q_bias, v_bias, out_bias, ln2_gain, ln2_bias, up_bias, down_bias)
    assert tokens.shape[1] * plan.n_mp == SEQ
    summed = step(plan, w_qkv, w_out, w_up, w_down.T, tokens, first_values, out_cot, small)
    outs = unpack(plan, summed, [s.shape[0] for s in small])
    return (*outs[:14], outs[14].T, outs[15])


def layer_norm(inputs, gain_vec, shift_vec):
    average = jnp.mean(inputs, axis=-1, keepdims=True)
    centred = inputs - average
    variance = jnp.mean(centred * centred, axis=-1, keepdims=True)
    inv_std = lax.rsqrt(variance + EPS)
    scaled = centred * inv_std
    return (scaled * gain_vec + shift_vec, scaled, inv_std)


def norm_back_all(grad_out, scaled, inv_std, gain_vec):
    grad_scaled = grad_out * gain_vec
    first_term = jnp.mean(grad_scaled, axis=-1, keepdims=True)
    second_term = jnp.mean(grad_scaled * scaled, axis=-1, keepdims=True)
    grad_in = inv_std * (grad_scaled - first_term - scaled * second_term)
    return (grad_in, jnp.sum(grad_out * scaled, axis=0), jnp.sum(grad_out, axis=0))


def gelu_both(inputs):
    cubic_term = inputs + GELU_A * inputs * inputs * inputs
    tangent = jnp.tanh(GELU_C * cubic_term)
    gelu_out = 0.5 * inputs * (1.0 + tangent)
    gelu_slope = 0.5 * (1.0 + tangent) + 0.5 * inputs * (1.0 - tangent * tangent) * GELU_C * (
        1.0 + 3.0 * GELU_A * inputs * inputs
    )
    return (gelu_out, gelu_slope)


def split_heads(matrix):
    return matrix.reshape(matrix.shape[0], HEADS, HEAD)


def block_scores(query_heads, key_block, row_first, key_first):
    key_heads = split_heads(key_block)
    scores = jnp.einsum(
        "qhd,khd->hqk", query_heads, key_heads, preferred_element_type=jnp.float32
    ) * HEAD ** (-0.5)
    query_pos = row_first + jnp.arange(query_heads.shape[0], dtype=jnp.int32)
    key_pos = key_first + jnp.arange(key_block.shape[0], dtype=jnp.int32)
    allowed = key_pos[None, :] <= query_pos[:, None]
    return (jnp.where(allowed[None], scores, -BIG), allowed, key_heads)


def block_length():
    return 512


def fold_blocks(function, carried, key_block, value_block, key_first):
    row_count = key_block.shape[0]
    block_rows = block_length()
    if block_rows == row_count:
        return function(carried, key_block, value_block, key_first)
    key_parts = key_block.reshape(row_count // block_rows, block_rows, key_block.shape[1])
    value_parts = value_block.reshape(row_count // block_rows, block_rows, value_block.shape[1])
    offsets = key_first + jnp.arange(row_count // block_rows, dtype=jnp.int32) * block_rows

    def step_once(inner_state, element):
        return (function(inner_state, element[0], element[1], element[2]), None)

    result, ignored = lax.scan(step_once, carried, (key_parts, value_parts, offsets))
    return result


def map_blocks(function, key_block, value_block, key_first):
    row_count = key_block.shape[0]
    block_rows = block_length()
    if block_rows == row_count:
        return function(key_block, value_block, key_first)
    key_parts = key_block.reshape(row_count // block_rows, block_rows, key_block.shape[1])
    value_parts = value_block.reshape(row_count // block_rows, block_rows, value_block.shape[1])
    offsets = key_first + jnp.arange(row_count // block_rows, dtype=jnp.int32) * block_rows

    def apply_once(element):
        return function(element[0], element[1], element[2])

    outputs = lax.map(apply_once, (key_parts, value_parts, offsets))
    return outputs.reshape(row_count, outputs.shape[-1])


def attention_forward(queries, keys_low, values_low, row_first):
    query_heads = split_heads(queries)
    row_total = queries.shape[0]

    def online_step(fold_state, key_block, value_block, key_first):
        running_top, running_sum, running_acc = fold_state
        masked, allowed, ignored = block_scores(query_heads, key_block, row_first, key_first)
        new_top = jnp.maximum(running_top, jnp.max(masked, axis=-1))
        weights = jnp.exp(masked - new_top[:, :, None]) * allowed[None]
        shrink = jnp.exp(running_top - new_top)
        running_sum = running_sum * shrink + jnp.sum(weights, axis=-1)
        running_acc = running_acc * shrink[:, :, None] + jnp.einsum(
            "hqk,khd->hqd",
            weights.astype(jnp.bfloat16),
            split_heads(value_block),
            preferred_element_type=jnp.float32,
        )
        return (new_top, running_sum, running_acc)

    start_state = (
        jnp.full((HEADS, row_total), -BIG, jnp.float32),
        jnp.zeros((HEADS, row_total), jnp.float32),
        jnp.zeros((HEADS, row_total, HEAD), jnp.float32),
    )
    running_top, running_sum, running_acc = fold_blocks(
        online_step,
        start_state,
        lax.all_gather(keys_low, "mp", axis=0, tiled=True),
        lax.all_gather(values_low, "mp", axis=0, tiled=True),
        jnp.int32(0),
    )
    attended = (running_acc / running_sum[:, :, None]).transpose(1, 0, 2).reshape(row_total, D)
    return (attended, running_top + jnp.log(running_sum))


def attention_backward(queries, keys_low, values_low, grad_out, attended, log_total, row_first):
    query_heads = split_heads(queries)
    grad_heads = split_heads(grad_out)
    row_total = queries.shape[0]
    score_scale = HEAD ** (-0.5)
    row_delta = jnp.sum(grad_heads.astype(jnp.float32) * split_heads(attended), axis=-1).T
    keys_all, values_all = (
        lax.all_gather(keys_low, "mp", axis=0, tiled=True),
        lax.all_gather(values_low, "mp", axis=0, tiled=True),
    )

    def soft_grads(key_block, value_block, key_first):
        masked, allowed, key_heads = block_scores(query_heads, key_block, row_first, key_first)
        probabilities = jnp.exp(masked - log_total[:, :, None])
        grad_probs = jnp.einsum(
            "qhd,khd->hqk", grad_heads, split_heads(value_block), preferred_element_type=jnp.float32
        )
        grad_scores = (probabilities * (grad_probs - row_delta[:, :, None])).astype(jnp.bfloat16)
        return (probabilities, grad_scores, key_heads)

    def query_step(accum, key_block, value_block, key_first):
        probabilities, grad_scores, key_heads = soft_grads(key_block, value_block, key_first)
        return (
            accum
            + jnp.einsum("hqk,khd->qhd", grad_scores, key_heads, preferred_element_type=jnp.float32)
            * score_scale
        )

    grad_query = fold_blocks(
        query_step, jnp.zeros((row_total, HEADS, HEAD), jnp.float32), keys_all, values_all, 0
    )

    def key_step(key_block, value_block, key_first):
        probabilities, grad_scores, key_heads = soft_grads(key_block, value_block, key_first)
        grad_value = jnp.einsum(
            "hqk,qhd->khd",
            probabilities.astype(jnp.bfloat16),
            grad_heads,
            preferred_element_type=jnp.float32,
        )
        grad_key = (
            jnp.einsum("hqk,qhd->khd", grad_scores, query_heads, preferred_element_type=jnp.float32)
            * score_scale
        )
        return jnp.concatenate(
            [grad_key.reshape(key_block.shape[0], D), grad_value.reshape(key_block.shape[0], D)],
            axis=1,
        )

    key_block = keys_all
    value_block = values_all
    grad_kv = lax.psum_scatter(
        map_blocks(key_step, key_block, value_block, jnp.int32(0)).astype(jnp.bfloat16),
        "mp",
        scatter_dimension=0,
        tiled=True,
    ).astype(jnp.float32)
    return (grad_query.reshape(row_total, D), grad_kv)


def reduce_grads(local_grads):
    row_parts = (
        lax.psum_scatter(
            local_grads[0].astype(jnp.bfloat16), "dp", scatter_dimension=0, tiled=True
        ).astype(jnp.float32),
        lax.psum_scatter(
            local_grads[1].astype(jnp.bfloat16), "dp", scatter_dimension=0, tiled=True
        ).astype(jnp.float32),
        lax.psum_scatter(
            local_grads[2].astype(jnp.bfloat16), "dp", scatter_dimension=0, tiled=True
        ).astype(jnp.float32),
        lax.psum_scatter(
            local_grads[3].astype(jnp.bfloat16), "dp", scatter_dimension=0, tiled=True
        ).astype(jnp.float32),
        lax.psum_scatter(
            local_grads[4].astype(jnp.bfloat16), "dp", scatter_dimension=0, tiled=True
        ).astype(jnp.float32),
        lax.psum_scatter(
            local_grads[5].astype(jnp.bfloat16), "dp", scatter_dimension=0, tiled=True
        ).astype(jnp.float32),
        lax.psum_scatter(
            local_grads[6].astype(jnp.bfloat16), "dp", scatter_dimension=0, tiled=True
        ).astype(jnp.float32),
        lax.psum_scatter(
            local_grads[7].astype(jnp.bfloat16), "dp", scatter_dimension=0, tiled=True
        ).astype(jnp.float32),
        lax.psum_scatter(
            local_grads[8].astype(jnp.bfloat16), "dp", scatter_dimension=0, tiled=True
        ).astype(jnp.float32),
        lax.psum_scatter(
            local_grads[9].astype(jnp.bfloat16), "dp", scatter_dimension=0, tiled=True
        ).astype(jnp.float32),
        lax.psum_scatter(
            local_grads[10].astype(jnp.bfloat16), "dp", scatter_dimension=0, tiled=True
        ).astype(jnp.float32),
        lax.psum_scatter(
            local_grads[11].astype(jnp.bfloat16), "dp", scatter_dimension=1, tiled=True
        ).astype(jnp.float32),
        lax.psum_scatter(
            local_grads[12].astype(jnp.bfloat16), "dp", scatter_dimension=0, tiled=True
        ).astype(jnp.float32),
    )
    row_parts = tuple(row_parts)
    col_parts = tuple(
        (
            lax.psum_scatter(
                row_parts[0].astype(jnp.bfloat16), "mp", scatter_dimension=0, tiled=True
            ).astype(jnp.float32),
            lax.psum_scatter(
                row_parts[1].astype(jnp.bfloat16), "mp", scatter_dimension=0, tiled=True
            ).astype(jnp.float32),
            lax.psum_scatter(
                row_parts[2].astype(jnp.bfloat16), "mp", scatter_dimension=1, tiled=True
            ).astype(jnp.float32),
            lax.psum_scatter(
                row_parts[3].astype(jnp.bfloat16), "mp", scatter_dimension=0, tiled=True
            ).astype(jnp.float32),
            lax.psum_scatter(
                row_parts[4].astype(jnp.bfloat16), "mp", scatter_dimension=0, tiled=True
            ).astype(jnp.float32),
            lax.psum_scatter(
                row_parts[5].astype(jnp.bfloat16), "mp", scatter_dimension=1, tiled=True
            ).astype(jnp.float32),
            lax.psum_scatter(
                row_parts[6].astype(jnp.bfloat16), "mp", scatter_dimension=0, tiled=True
            ).astype(jnp.float32),
            lax.psum_scatter(
                row_parts[7].astype(jnp.bfloat16), "mp", scatter_dimension=0, tiled=True
            ).astype(jnp.float32),
            lax.psum_scatter(
                row_parts[8].astype(jnp.bfloat16), "mp", scatter_dimension=0, tiled=True
            ).astype(jnp.float32),
            lax.psum_scatter(
                row_parts[10].astype(jnp.bfloat16), "mp", scatter_dimension=0, tiled=True
            ).astype(jnp.float32),
            lax.psum_scatter(
                row_parts[12].astype(jnp.bfloat16), "mp", scatter_dimension=0, tiled=True
            ).astype(jnp.float32),
        )
    )
    return col_parts[:9] + (row_parts[9], col_parts[9], row_parts[11], col_parts[10])


def general_shards(
    tokens,
    first_values,
    out_cot,
    ln1_gain,
    ln1_bias,
    w_qkv,
    q_bias,
    v_bias,
    w_out,
    out_bias,
    ln2_gain,
    ln2_bias,
    w_up,
    up_bias,
    w_down,
    down_bias,
):
    near_blocks = tuple(
        (
            lax.all_gather(ln1_gain, "mp", axis=0, tiled=True),
            lax.all_gather(ln1_bias, "mp", axis=0, tiled=True),
            lax.all_gather(w_qkv, "mp", axis=1, tiled=True),
            lax.all_gather(q_bias, "mp", axis=0, tiled=True),
            lax.all_gather(v_bias, "mp", axis=0, tiled=True),
            lax.all_gather(w_out, "mp", axis=1, tiled=True),
            lax.all_gather(out_bias, "mp", axis=0, tiled=True),
            lax.all_gather(ln2_gain, "mp", axis=0, tiled=True),
            lax.all_gather(ln2_bias, "mp", axis=0, tiled=True),
            lax.all_gather(up_bias, "mp", axis=0, tiled=True),
            lax.all_gather(down_bias, "mp", axis=0, tiled=True),
        )
    )
    near_blocks = near_blocks[:9] + (w_up, near_blocks[9], w_down, near_blocks[10])
    params = tuple(
        (
            lax.all_gather(near_blocks[0], "dp", axis=0, tiled=True),
            lax.all_gather(near_blocks[1], "dp", axis=0, tiled=True),
            lax.all_gather(near_blocks[2], "dp", axis=0, tiled=True),
            lax.all_gather(near_blocks[3], "dp", axis=0, tiled=True),
            lax.all_gather(near_blocks[4], "dp", axis=0, tiled=True),
            lax.all_gather(near_blocks[5], "dp", axis=0, tiled=True),
            lax.all_gather(near_blocks[6], "dp", axis=0, tiled=True),
            lax.all_gather(near_blocks[7], "dp", axis=0, tiled=True),
            lax.all_gather(near_blocks[8], "dp", axis=0, tiled=True),
            lax.all_gather(near_blocks[9], "dp", axis=0, tiled=True),
            lax.all_gather(near_blocks[10], "dp", axis=0, tiled=True),
            lax.all_gather(near_blocks[11], "dp", axis=1, tiled=True),
            lax.all_gather(near_blocks[12], "dp", axis=0, tiled=True),
        )
    )
    gain_one = params[0].astype(jnp.float32)
    shift_one = params[1].astype(jnp.float32)
    qkv_full = params[2]
    query_shift = params[3].astype(jnp.float32)
    value_shift = params[4].astype(jnp.float32)
    out_full = params[5]
    out_shift = params[6].astype(jnp.float32)
    gain_two = params[7].astype(jnp.float32)
    shift_two = params[8].astype(jnp.float32)
    up_full = params[9]
    up_shift_all = params[10].astype(jnp.float32)
    down_full = params[11]
    down_shift = params[12].astype(jnp.float32)
    up_cols = up_full.shape[1]
    up_start = 0
    up_start = lax.axis_index("mp") * up_cols
    up_used = lax.dynamic_slice_in_dim(up_shift_all, up_start, up_cols, 0)
    row_total = tokens.shape[1]
    row_first = lax.axis_index("mp") * row_total
    fresh_cols = value_shift.shape[0]
    outputs = []
    grad_inputs = []
    grad_firsts = []
    summed = None
    for micro_index in range(MICRO):
        cot_low = out_cot[micro_index]
        inputs = tokens[micro_index].astype(jnp.float32)
        normed, scaled_one, inv_one = layer_norm(inputs, gain_one, shift_one)
        normed_low = normed.astype(jnp.bfloat16)
        mixed_proj = jnp.dot(normed_low, qkv_full, preferred_element_type=jnp.float32)
        queries = (mixed_proj[:, :D] + query_shift).astype(jnp.bfloat16)
        keys_low = mixed_proj[:, D : 2 * D].astype(jnp.bfloat16)
        values_low = jnp.concatenate(
            [
                (mixed_proj[:, 2 * D :] + value_shift).astype(jnp.bfloat16),
                first_values[micro_index],
            ],
            axis=1,
        )
        attended, log_total = attention_forward(queries, keys_low, values_low, row_first)
        attended_low = attended.astype(jnp.bfloat16)
        middle = inputs + (
            jnp.dot(attended_low, out_full, preferred_element_type=jnp.float32) + out_shift
        )
        normed_two, scaled_two, inv_two = layer_norm(middle, gain_two, shift_two)
        normed_two_low = normed_two.astype(jnp.bfloat16)
        cot_float = cot_low.astype(jnp.float32)
        row_piece = lax.all_gather(normed_two_low, "mp", axis=0, tiled=True)
        hidden = jnp.dot(row_piece, up_full, preferred_element_type=jnp.float32) + up_used
        gelu_out, gelu_slope = gelu_both(hidden)
        active_all = gelu_out.astype(jnp.bfloat16)
        down_part = lax.psum_scatter(
            jnp.dot(active_all, down_full, preferred_element_type=jnp.float32).astype(jnp.bfloat16),
            "mp",
            scatter_dimension=0,
            tiled=True,
        ).astype(jnp.float32)
        result = middle + (down_part + down_shift)
        back_row_piece = lax.all_gather(cot_low, "mp", axis=0, tiled=True)
        grad_active = jnp.einsum(
            "rd,fd->rf", back_row_piece, down_full, preferred_element_type=jnp.float32
        )
        back_gelu_out, back_gelu_slope = gelu_both(hidden)
        grad_hidden = (grad_active * back_gelu_slope).astype(jnp.bfloat16)
        grad_normed_two = lax.psum_scatter(
            jnp.einsum(
                "rf,df->rd", grad_hidden, up_full, preferred_element_type=jnp.float32
            ).astype(jnp.bfloat16),
            "mp",
            scatter_dimension=0,
            tiled=True,
        ).astype(jnp.float32)
        grad_down = jnp.einsum(
            "rf,rd->fd", active_all, back_row_piece, preferred_element_type=jnp.float32
        )
        grad_up = jnp.einsum(
            "rd,rf->df", row_piece, grad_hidden, preferred_element_type=jnp.float32
        )
        up_piece = jnp.sum(grad_hidden.astype(jnp.float32), axis=0)
        grad_up_shift = lax.dynamic_update_slice_in_dim(
            jnp.zeros((FF,), jnp.float32), up_piece, up_start, 0
        )
        grad_norm_two, grad_gain_two, grad_shift_two = norm_back_all(
            grad_normed_two, scaled_two, inv_two, gain_two
        )
        grad_middle = cot_float + grad_norm_two
        grad_branch = grad_middle.astype(jnp.bfloat16)
        grad_out_shift = jnp.sum(grad_branch.astype(jnp.float32), axis=0)
        grad_out_proj = jnp.einsum(
            "rd,re->de", attended_low, grad_branch, preferred_element_type=jnp.float32
        )
        grad_attended = jnp.einsum(
            "re,de->rd", grad_branch, out_full, preferred_element_type=jnp.float32
        ).astype(jnp.bfloat16)
        grad_query, grad_kv = attention_backward(
            queries, keys_low, values_low, grad_attended, attended, log_total, row_first
        )
        grad_query_low = grad_query.astype(jnp.bfloat16)
        grad_kv_low = grad_kv.astype(jnp.bfloat16)
        grad_mixed = jnp.concatenate([grad_query_low, grad_kv_low[:, : D + fresh_cols]], axis=1)
        grad_query_shift = jnp.sum(grad_query_low.astype(jnp.float32), axis=0)
        grad_value_shift = jnp.sum(grad_kv_low[:, D : D + fresh_cols].astype(jnp.float32), axis=0)
        grad_qkv = jnp.einsum(
            "rd,rc->dc", normed_low, grad_mixed, preferred_element_type=jnp.float32
        )
        grad_normed = jnp.einsum(
            "rc,dc->rd", grad_mixed, qkv_full, preferred_element_type=jnp.float32
        )
        grad_norm_one, grad_gain_one, grad_shift_one = norm_back_all(
            grad_normed, scaled_one, inv_one, gain_one
        )
        grad_input = grad_middle + grad_norm_one
        local_grads = (
            grad_gain_one,
            grad_shift_one,
            grad_qkv,
            grad_query_shift,
            grad_value_shift,
            grad_out_proj,
            grad_out_shift,
            grad_gain_two,
            grad_shift_two,
            grad_up,
            grad_up_shift,
            grad_down,
            jnp.sum(cot_float, axis=0),
        )
        result, grad_input, grad_first, local_grads = (
            result.astype(jnp.bfloat16),
            grad_input.astype(jnp.bfloat16),
            grad_kv_low[:, D + fresh_cols :],
            local_grads,
        )
        outputs.append(result)
        grad_inputs.append(grad_input)
        grad_firsts.append(grad_first)
        local_grads = reduce_grads(local_grads)
        summed = local_grads if summed is None else jax.tree.map(jnp.add, summed, local_grads)
    return (
        jnp.stack(outputs),
        jnp.stack(grad_inputs),
        jnp.stack(grad_firsts),
        summed[0],
        summed[1],
        summed[2],
        summed[3],
        summed[4],
        summed[5],
        summed[6],
        summed[7],
        summed[8],
        summed[9],
        summed[10],
        summed[11],
        summed[12],
    )


def solution(mesh):
    whole_sequences = mesh.shape["mp"] == MICRO
    body = functools.partial(shards, Plan(mesh)) if whole_sequences else general_shards
    line = P(("dp", "mp"))
    rows = P(None, ("dp", "mp"), None)
    block = P("dp", "mp")
    grads = (line, line, block, line, line, block, line, line, line, block, line, P("mp", "dp"), line)
    return jax.shard_map(
        body,
        mesh=mesh,
        in_specs=(rows, rows, rows) + grads,
        out_specs=(rows, rows, rows) + grads,
        check_vma=False,
    )
```
